32 devices in a mesh: fsdp: 8 (over z, y), seq: 4 (over x, core).
Axes of the slice: x: 2, y: 2, z: 4, core: 2. Of those that a mesh axis runs over, the one named last changes fastest.
Arguments:
- inputs: bfloat16 [48, 512, 768], P('fsdp', 'seq'), may hold values from -6 to 6
- lengths: int32 [48], P('fsdp'), may hold values from 40 to 512, as said below
- w_query: bfloat16 [768, 768], P('fsdp'), may hold values from -0.3125 to 0.3125
- b_query: bfloat16 [768], P('fsdp'), may hold values from -3 to 3
- w_key: bfloat16 [768, 768], P('fsdp'), may hold values from -0.3125 to 0.3125
- w_value: bfloat16 [768, 768], P('fsdp'), may hold values from -0.21875 to 0.21875
- b_value: bfloat16 [768], P('fsdp'), may hold values from -3 to 3
- w_out: bfloat16 [768, 768], P('fsdp'), may hold values from -0.875 to 0.875
- b_out: bfloat16 [768], P('fsdp'), may hold values from -3 to 3
- gain_one: bfloat16 [768], P('fsdp'), may hold values from 0.5 to 1.5
- shift_one: bfloat16 [768], P('fsdp'), may hold values from -3 to 3
- w_inner: bfloat16 [768, 3072], P('fsdp'), may hold values from -0.21875 to 0.21875
- b_inner: bfloat16 [3072], P('fsdp'), may hold values from -3 to 3
- w_outer: bfloat16 [3072, 768], P('fsdp'), may hold values from -0.15625 to 0.15625
- b_outer: bfloat16 [768], P('fsdp'), may hold values from -3 to 3
- gain_two: bfloat16 [768], P('fsdp'), may hold values from 0.5 to 1.5
- shift_two: bfloat16 [768], P('fsdp'), may hold values from -3 to 3
- cotangent: bfloat16 [48, 512, 768], P('fsdp', 'seq'), may hold values from -6 to 6
Outputs:
- output: bfloat16 [48, 512, 768], P('fsdp', 'seq')
- grad_inputs: float32 [48, 512, 768], P('fsdp', 'seq')
- grad_w_query: float32 [768, 768], P('fsdp')
- grad_b_query: float32 [768], P('fsdp')
- grad_w_key: float32 [768, 768], P('fsdp')
- grad_w_value: float32 [768, 768], P('fsdp')
- grad_b_value: float32 [768], P('fsdp')
- grad_w_out: float32 [768, 768], P('fsdp')
- grad_b_out: float32 [768], P('fsdp')
- grad_gain_one: float32 [768], P('fsdp')
- grad_shift_one: float32 [768], P('fsdp')
- grad_w_inner: float32 [768, 3072], P('fsdp')
- grad_b_inner: float32 [3072], P('fsdp')
- grad_w_outer: float32 [3072, 768], P('fsdp')
- grad_b_outer: float32 [768], P('fsdp')
- grad_gain_two: float32 [768], P('fsdp')
- grad_shift_two: float32 [768], P('fsdp')
The draws below stay inside these ranges and needn't reach their ends.
Inputs may be any that keep to these rules, and one draw needn't show every extreme that they name: `lengths`: real rows of each page; in every draw some page has exactly 512.
All inputs are finite; a program needn't handle non-finite values.
Results may differ from the reference program's by a relative error of at most 0.019.
Values may be sent and summed in bfloat16 or wider, within the bound.
A program may use at most 192 MiB of HBM per device.

```python
import math
import jax
import jax.numpy as jnp
from jax import lax

D = 768
HEADS = 12
HEAD_DIM = 64
FF = 3072
LEN = 512
MIN_LEN = 40
PAGES = 6
PAGES_ALL = 48
N_FSDP = 8


def draw_lengths(key, part):
    key_one = jax.random.fold_in(key, 11)
    key_two = jax.random.fold_in(key, 12)
    raw_lengths = jax.random.randint(key_one, (PAGES_ALL,), MIN_LEN, LEN + 1)
    longest = jax.random.randint(key_two, (), 0, PAGES_ALL)
    places = jnp.arange(PAGES_ALL).astype(jnp.int32)
    return jnp.where(places == longest, LEN, raw_lengths).astype(jnp.int32)


def shard_levels(key, shape, cuts, low, largest):
    def one(position, parts):
        heights = jax.random.uniform(jax.random.fold_in(jax.random.fold_in(key, 6), position), (parts,), jnp.float32, low / len(cuts), largest / len(cuts))
        return jnp.repeat(jnp.exp(heights), shape[position] // parts).reshape((-1,) + (1,) * (len(shape) - position - 1))

    factor_of = one(*cuts[0])
    for cut in cuts[1:]:
        factor_of = factor_of * one(*cut)
    return factor_of


def bell_draw(stream_key, shape, width, most, split=(), held_as=jnp.bfloat16):
    factor_of = shard_levels(stream_key, shape, split, -0.22, 0.18) if split else 1.0
    values = jax.random.normal(stream_key, shape, jnp.float32) * width * factor_of
    return jnp.minimum(jnp.maximum(values, -most), most).astype(held_as)


def setup_inputs(seed: int = 0) -> dict:
    key_list = jax.random.split(jax.random.key(seed), 19)
    return {
        "inputs": bell_draw(key_list[0], (PAGES_ALL, LEN, D), 1.0, 6.0, ((0, 8), (1, 4))),
        "lengths": draw_lengths(jax.random.fold_in(key_list[18], 71), 0),
        "w_query": bell_draw(key_list[2], (D, D), (D // 2) ** -0.5, 0.3125, ((0, 8),)),
        "b_query": bell_draw(key_list[3], (D,), 0.5, 3.0, ((0, 8),)),
        "w_key": bell_draw(key_list[4], (D, D), (D // 2) ** -0.5, 0.3125, ((0, 8),)),
        "w_value": bell_draw(key_list[5], (D, D), D ** -0.5, 0.21875, ((0, 8),)),
        "b_value": bell_draw(key_list[6], (D,), 0.5, 3.0, ((0, 8),)),
        "w_out": bell_draw(key_list[7], (D, D), (D // 16) ** -0.5, 0.875, ((0, 8),)),
        "b_out": bell_draw(key_list[8], (D,), 0.5, 3.0, ((0, 8),)),
        "gain_one": jnp.clip(1.0 + 0.1 * jax.random.normal(key_list[9], (D,), jnp.float32), 0.5, 1.5).astype(jnp.bfloat16),
        "shift_one": bell_draw(key_list[10], (D,), 0.5, 3.0, ((0, 8),)),
        "w_inner": bell_draw(key_list[11], (D, FF), D ** -0.5, 0.21875, ((0, 8),)),
        "b_inner": bell_draw(key_list[12], (FF,), 0.5, 3.0, ((0, 8),)),
        "w_outer": bell_draw(key_list[13], (FF, D), (FF // 2) ** -0.5, 0.15625, ((0, 8),)),
        "b_outer": bell_draw(key_list[14], (D,), 0.5, 3.0, ((0, 8),)),
        "gain_two": jnp.clip(1.0 + 0.1 * jax.random.normal(key_list[15], (D,), jnp.float32), 0.5, 1.5).astype(jnp.bfloat16),
        "shift_two": bell_draw(key_list[16], (D,), 0.5, 3.0, ((0, 8),)),
        "cotangent": bell_draw(key_list[17], (PAGES_ALL, LEN, D), 1.0, 6.0, ((0, 8), (1, 4))),
    }


@jax.custom_vjp
def low(v):
    return lax.optimization_barrier(v.astype(jnp.bfloat16)).astype(jnp.float32)

@jax.custom_vjp
def low_back(v):
    return v

def low_keep(v):
    return (low(v), None)

def low_pass(kept, grad):
    return (grad,)

def back_keep(v):
    return (v, None)

def back_low(kept, grad):
    return (low(grad),)
low.defvjp(low_keep, low_pass)
low_back.defvjp(back_keep, back_low)
negative_fill = -1e+30
norm_eps = 1e-12

def matmul(left_side, right_side):
    return jnp.dot(left_side, right_side, precision=lax.Precision.HIGHEST, preferred_element_type=jnp.float32)

def layer_norm(row_values, gain_vec, shift_vec):
    average = lax.optimization_barrier(jnp.mean(row_values, -1, keepdims=True))
    centered = row_values - average
    spread = lax.optimization_barrier(jnp.mean(centered * centered, -1, keepdims=True))
    return centered * lax.rsqrt(spread + norm_eps) * gain_vec + shift_vec

def forward(layer_in, key_valid, w_query, b_query, w_key, w_value, b_value, w_out, b_out, gain_one, shift_one, w_inner, b_inner, w_outer, b_outer, gain_two, shift_two):
    page_count = layer_in.shape[0]
    head_scale = 1.0 / math.sqrt(HEAD_DIM)
    query_rows = low(low_back(matmul(layer_in, w_query) + b_query)).reshape(page_count, LEN, HEADS, HEAD_DIM)
    key_rows = low(low_back(matmul(layer_in, w_key))).reshape(page_count, LEN, HEADS, HEAD_DIM)
    value_rows = low(low_back(matmul(layer_in, w_value) + b_value)).reshape(page_count, LEN, HEADS, HEAD_DIM)
    raw_scores = jnp.einsum('pqhd,pkhd->phqk', query_rows, key_rows, precision=lax.Precision.HIGHEST) * head_scale
    raw_scores = low_back(raw_scores)
    masked = jnp.where(key_valid[:, None, None, :], raw_scores, negative_fill)
    attn_probs = low(jax.nn.softmax(masked, axis=-1))
    context = jnp.einsum('phqk,pkhd->pqhd', attn_probs, value_rows, precision=lax.Precision.HIGHEST).reshape(page_count, LEN, D)
    context = low(low_back(context))
    attended = low_back(matmul(context, w_out) + b_out)
    hidden_one = layer_norm(layer_in + attended, gain_one, shift_one)
    inner_pre = low_back(matmul(low(hidden_one), w_inner) + b_inner)
    activated = low(jax.nn.gelu(inner_pre, approximate=False))
    outer_out = low_back(matmul(activated, w_outer) + b_outer)
    return layer_norm(hidden_one + outer_out, gain_two, shift_two)

def reference(inputs, lengths, w_query, b_query, w_key, w_value, b_value, w_out, b_out, gain_one, shift_one, w_inner, b_inner, w_outer, b_outer, gain_two, shift_two, cotangent):
    params = tuple((weight.astype(jnp.float32) for weight in (w_query, b_query, w_key, w_value, b_value, w_out, b_out, gain_one, shift_one, w_inner, b_inner, w_outer, b_outer, gain_two, shift_two)))
    grouped_in = inputs.astype(jnp.float32).reshape(N_FSDP, PAGES, LEN, D)
    grouped_len = lengths.astype(jnp.int32).reshape(N_FSDP, PAGES)
    grouped_cot = cotangent.astype(jnp.float32).reshape(N_FSDP, PAGES, LEN, D)
    positions = jnp.arange(LEN).astype(jnp.int32)

    def one_group(totals, pieces):
        page_in, page_len, page_cot = pieces
        key_valid = positions[None, :] < page_len[:, None]

        def apply_layer(layer_in, *weights):
            return forward(layer_in, key_valid, *weights)
        result, pullback = jax.vjp(apply_layer, page_in, *params)
        grad_list = pullback(page_cot)
        summed = tuple((run_total + each_grad for run_total, each_grad in zip(totals, grad_list[1:])))
        return (summed, (result.astype(jnp.bfloat16), grad_list[0]))
    zero_totals = tuple((jnp.zeros_like(weight) for weight in params))
    totals, (results, grad_in) = lax.scan(one_group, zero_totals, (grouped_in, grouped_len, grouped_cot))
    grad_w_query, grad_b_query, grad_w_key, grad_w_value, grad_b_value, grad_w_out, grad_b_out, grad_gain_one, grad_shift_one, grad_w_inner, grad_b_inner, grad_w_outer, grad_b_outer, grad_gain_two, grad_shift_two = totals
    return (results.reshape(PAGES_ALL, LEN, D), grad_in.reshape(PAGES_ALL, LEN, D), grad_w_query, grad_b_query, grad_w_key, grad_w_value, grad_b_value, grad_w_out, grad_b_out, grad_gain_one, grad_shift_one, grad_w_inner, grad_b_inner, grad_w_outer, grad_b_outer, grad_gain_two, grad_shift_two)
```

```python
import functools
import math

import jax
import jax.numpy as jnp
from jax import lax
from jax.experimental import pallas as pl
from jax.experimental.pallas import tpu as pltpu
from jax.sharding import PartitionSpec as P

HEADS = 12
HEAD_DIM = 64
PAIR = 2 * HEAD_DIM
NEG = -1e30
EPS = 1e-12
BF = jnp.bfloat16
F32 = jnp.float32
MESH = pl.DeviceIdType.MESH
ANY = pl.BlockSpec(memory_space=pl.ANY)
VM = pl.BlockSpec(memory_space=pltpu.VMEM)
CHUNK = 512
ROW = 96
VMEM_CAP = 60 << 20

NN = (((1,), (0,)), ((), ()))
NT = (((1,), (1,)), ((), ()))
TN = (((0,), (0,)), ((), ()))


def dot(a, b, dims=NN):
    return lax.dot_general(a, b, dims, preferred_element_type=F32)


def call(body, cost, **kw):
    flops, byts, trans = cost
    params = dict(vmem_limit_bytes=VMEM_CAP)
    params.update(kw.pop("params", {}))
    return pl.pallas_call(
        body,
        compiler_params=pltpu.CompilerParams(**params),
        cost_estimate=pl.CostEstimate(
            flops=int(flops), bytes_accessed=int(byts), transcendentals=int(trans)
        ),
        **kw,
    )


def attn_fwd_body(thr, xa, xb, xc, xd, wq, wk, wv, vec, q_o, k_o, v_o, p_o, c_o, bias):
    page = pl.program_id(0)
    x_all = jnp.concatenate([xa[0], xb[0], xc[0], xd[0]], axis=0)
    own = x_all.shape[0] // 2
    query = (dot(x_all[:own], wq[...]) + vec[0:1, :]).astype(BF)
    q_o[0] = query
    k_o[0] = dot(x_all, wk[...]).astype(BF)
    v_o[0] = (dot(x_all, wv[...]) + vec[1:2, :]).astype(BF)
    blk = xa.shape[1]
    place = lax.broadcasted_iota(jnp.int32, (blk, own), 0)
    for b in range(4):
        bias[b * blk : (b + 1) * blk, :] = jnp.where(place < thr[page, b], 0.0, NEG)
    low_lane = lax.broadcasted_iota(jnp.int32, (own, PAIR), 1) < HEAD_DIM

    def pair(i, carry):
        cols = pl.ds(pl.multiple_of(i * PAIR, PAIR), PAIR)
        qp = q_o[0, :, cols] * jnp.array(1.0 / math.sqrt(HEAD_DIM), BF)
        kp = k_o[0, :, cols]
        vt = v_o[0, :, cols].T
        outs = []
        for h in range(2):
            keep = low_lane if h == 0 else jnp.logical_not(low_lane)
            qh = jnp.where(keep, qp, jnp.zeros_like(qp))
            st = dot(kp, qh, NT) + bias[...]
            top = jnp.max(st, axis=0, keepdims=True)
            ex = jnp.exp(st - top)
            tot = jnp.sum(ex, axis=0, keepdims=True)
            pt = (ex * (1.0 / tot)).astype(BF)
            p_o[0, 2 * i + h] = pt
            outs.append(dot(vt[h * HEAD_DIM : (h + 1) * HEAD_DIM], pt))
        c_o[0, :, cols] = jnp.concatenate(outs, axis=0).T.astype(BF)
        return carry

    lax.fori_loop(0, HEADS // 2, pair, 0)


def attn_fwd(thr, xs, wq, wk, wv, vec):
    pages, blk, d = xs[0].shape
    own, rows = 2 * blk, 4 * blk
    const = lambda p, t: (0, 0)
    by_page = lambda p, t: (p, 0, 0)
    one = pl.Buffered(1)
    return call(
        attn_fwd_body,
        (
            pages * (2 * d * d * (own + 2 * rows) + 4 * own * rows * d),
            pages * rows * d * 2 * 4 + 6 * d * d + pages * HEADS * own * rows * 2,
            pages * HEADS * own * rows,
        ),
        grid_spec=pltpu.PrefetchScalarGridSpec(
            num_scalar_prefetch=1,
            grid=(pages,),
            in_specs=[pl.BlockSpec((1, blk, d), by_page)] * 4
            + [pl.BlockSpec((d, d), const, pipeline_mode=one)] * 3
            + [pl.BlockSpec((8, d), const)],
            out_specs=[
                pl.BlockSpec((1, own, d), by_page),
                pl.BlockSpec((1, rows, d), by_page),
                pl.BlockSpec((1, rows, d), by_page),
                pl.BlockSpec((1, HEADS, rows, own), lambda p, t: (p, 0, 0, 0)),
                pl.BlockSpec((1, own, d), by_page),
            ],
            scratch_shapes=[pltpu.VMEM((rows, own), F32)],
        ),
        out_shape=[
            jax.ShapeDtypeStruct((pages, own, d), BF),
            jax.ShapeDtypeStruct((pages, rows, d), BF),
            jax.ShapeDtypeStruct((pages, rows, d), BF),
            jax.ShapeDtypeStruct((pages, HEADS, rows, own), BF),
            jax.ShapeDtypeStruct((pages, own, d), BF),
        ],
        name="attn_fwd",
    )(thr, *xs, wq, wk, wv, vec)


def attn_bwd_body(q, k, v, p, ctx, dctx, dq_o, dk_own, dk_oth, dv_own, dv_oth):
    own = q.shape[1]
    low_lane = lax.broadcasted_iota(jnp.int32, (own, PAIR), 1) < HEAD_DIM
    scale = 1.0 / math.sqrt(HEAD_DIM)

    def pair(i, carry):
        cols = pl.ds(pl.multiple_of(i * PAIR, PAIR), PAIR)
        qp = q[0, :, cols] * jnp.array(scale, BF)
        kp = k[0, :, cols]
        kt = kp.T
        vp = v[0, :, cols]
        dc = dctx[0, :, cols]
        prod = (dc.astype(F32) * ctx[0, :, cols].astype(F32)).T
        dk = None
        dv = None
        dqs = []
        for h in range(2):
            keep = low_lane if h == 0 else jnp.logical_not(low_lane)
            feats = slice(h * HEAD_DIM, (h + 1) * HEAD_DIM)
            dch = jnp.where(keep, dc, jnp.zeros_like(dc))
            qh = jnp.where(keep, qp, jnp.zeros_like(qp))
            pt = p[0, 2 * i + h]
            delta = jnp.sum(prod[feats], axis=0, keepdims=True)
            dpt = dot(vp, dch, NT)
            dst = (pt.astype(F32) * (dpt - delta)).astype(BF)
            dvh = dot(pt, dch)
            dkh = dot(dst, qh)
            dk = dkh if dk is None else dk + dkh
            dv = dvh if dv is None else dv + dvh
            dqs.append(dot(kt[feats], dst))
        dq_o[0, :, cols] = (jnp.concatenate(dqs, axis=0) * scale).T.astype(BF)
        dk_own[0, :, cols] = dk[:own].astype(BF)
        dk_oth[0, :, cols] = dk[own:].astype(BF)
        dv_own[0, :, cols] = dv[:own].astype(BF)
        dv_oth[0, :, cols] = dv[own:].astype(BF)
        return carry

    lax.fori_loop(0, HEADS // 2, pair, 0)


def attn_bwd(q, k, v, p, ctx, dctx):
    pages, own, d = q.shape
    rows = k.shape[1]
    by_page = lambda i: (i, 0, 0)
    o = pl.BlockSpec((1, own, d), by_page)
    r = pl.BlockSpec((1, rows, d), by_page)
    return call(
        attn_bwd_body,
        (pages * 10 * own * rows * d, pages * (own * rows * HEADS * 2 + 10 * own * d * 2), 0),
        grid=(pages,),
        in_specs=[o, r, r, pl.BlockSpec((1, HEADS, rows, own), lambda i: (i, 0, 0, 0)), o, o],
        out_specs=[o] * 5,
        out_shape=[jax.ShapeDtypeStruct((pages, own, d), BF)] * 5,
        name="attn_bwd",
    )(q, k, v, p, ctx, dctx)


def normal_parts(v):
    bell = jnp.exp(v * v * -0.5)
    t = 1.0 / (1.0 + jnp.abs(v) * (0.3275911 / math.sqrt(2.0)))
    tail = t * (
        0.127414796 + t * (-0.142248368 + t * (0.7107068705 + t * (-0.7265760135 + t * 0.5307027145)))
    )
    tail = tail * bell
    return jnp.where(v >= 0.0, 1.0 - tail, tail), bell * (1.0 / math.sqrt(2.0 * math.pi))


def row_norm(v):
    centered = v - jnp.mean(v, -1, keepdims=True)
    inv = lax.rsqrt(jnp.mean(centered * centered, -1, keepdims=True) + EPS)
    return centered * inv, inv


def norm_back(e, n, inv):
    return inv * (e - jnp.mean(e, -1, keepdims=True) - n * jnp.mean(e * n, -1, keepdims=True))


def ffn_body(
    ctx, xa, xb, ca, cb, wo, wi, w2, vec, b_in,
    out_a, out_b, gm1_o, dctx_o, dwo_o, dwi_o, dw2_o, gvec, gbin,
    act, din, dgel, hid, gout, gatt, ctx_all,
):
    page = pl.program_id(0)
    blk = xa.shape[1]
    own = 2 * blk
    ff = wi.shape[1]
    here = pl.ds(pl.multiple_of(page * own, own), own)

    @pl.when(page == 0)
    def _():
        gvec[...] = jnp.zeros_like(gvec)
        gbin[...] = jnp.zeros_like(gbin)

    ctx_v = ctx[0]
    ctx_all[here, :] = ctx_v
    x_own = jnp.concatenate([xa[0], xb[0]], axis=0).astype(F32)
    mid_one = x_own + (dot(ctx_v, wo[...]) + vec[2:3, :])
    n1, r1 = row_norm(mid_one)
    h1 = n1 * vec[3:4, :] + vec[4:5, :]
    hl = h1.astype(BF)
    hid[here, :] = hl

    def up(j, acc):
        cols = pl.ds(pl.multiple_of(j * CHUNK, CHUNK), CHUNK)
        pre = dot(hl, wi[:, cols]) + b_in[:, cols]
        big, bell = normal_parts(pre)
        a = (pre * big).astype(BF)
        dgel[:, cols] = (big + pre * bell).astype(BF)
        act[here, cols] = a
        return acc + dot(a, w2[cols, :])

    outer = lax.fori_loop(0, ff // CHUNK, up, jnp.zeros((own, x_own.shape[1]), F32))
    mid_two = h1 + (outer + vec[5:6, :])
    n2, r2 = row_norm(mid_two)
    res = (n2 * vec[6:7, :] + vec[7:8, :]).astype(BF)
    out_a[0] = res[:blk]
    out_b[0] = res[blk:]
    cot = jnp.concatenate([ca[0], cb[0]], axis=0).astype(F32)
    gm2 = norm_back(cot * vec[6:7, :], n2, r2)
    go = gm2.astype(BF)
    gout[here, :] = go

    def down(j, acc):
        cols = pl.ds(pl.multiple_of(j * CHUNK, CHUNK), CHUNK)
        di = (dot(go, w2[cols, :], NT) * dgel[:, cols].astype(F32)).astype(BF)
        din[here, cols] = di
        gbin[:, cols] += jnp.sum(di.astype(F32), 0, keepdims=True)
        return acc + dot(di, wi[:, cols], NT)

    gh = gm2 + lax.fori_loop(0, ff // CHUNK, down, jnp.zeros_like(gm2))
    gm1 = norm_back(gh * vec[3:4, :], n1, r1)
    gm1_o[0] = gm1
    ga = gm1.astype(BF)
    gatt[here, :] = ga
    dctx_o[0] = dot(ga, wo[...], NT).astype(BF)

    def add(row, value):
        gvec[row : row + 1, :] += jnp.sum(value, 0, keepdims=True)

    add(2, ga.astype(F32))
    add(3, gh * n1)
    add(4, gh)
    add(5, go.astype(F32))
    add(6, cot * n2)
    add(7, cot)

    @pl.when(page == pl.num_programs(0) - 1)
    def _():
        go_all = gout[...]
        hid_t = hid[...].T

        def grads(j, carry):
            cols = pl.ds(pl.multiple_of(j * CHUNK, CHUNK), CHUNK)
            dw2_o[cols, :] = dot(act[:, cols], go_all, TN).astype(BF)
            dwi_o[:, cols] = dot(hid_t, din[:, cols]).astype(BF)
            return carry

        lax.fori_loop(0, ff // CHUNK, grads, 0)
        dwo_o[...] = dot(ctx_all[...], gatt[...], TN).astype(BF)


def ffn(ctx, xa, xb, ca, cb, wo, wi, w2, vec, b_in):
    pages, own, d = ctx.shape
    blk = own // 2
    ff = wi.shape[1]
    n = pages * own
    by_page = lambda p: (p, 0, 0)
    const = lambda p: (0, 0)
    one = pl.Buffered(1)
    half = pl.BlockSpec((1, blk, d), by_page)
    whole = pl.BlockSpec((1, own, d), by_page)

    def fixed(*shape):
        return pl.BlockSpec(shape, const, pipeline_mode=one)

    return call(
        ffn_body,
        (n * d * (12 * ff + 6 * d), 4 * d * ff * 2 + 12 * n * d * 2, n * ff),
        grid=(pages,),
        in_specs=[whole, half, half, half, half, fixed(d, d), fixed(d, ff), fixed(ff, d), fixed(8, d), fixed(1, ff)],
        out_specs=[half, half, whole, whole, fixed(d, d), fixed(d, ff), fixed(ff, d), fixed(8, d), fixed(1, ff)],
        out_shape=[
            jax.ShapeDtypeStruct((pages, blk, d), BF),
            jax.ShapeDtypeStruct((pages, blk, d), BF),
            jax.ShapeDtypeStruct((pages, own, d), F32),
            jax.ShapeDtypeStruct((pages, own, d), BF),
            jax.ShapeDtypeStruct((d, d), BF),
            jax.ShapeDtypeStruct((d, ff), BF),
            jax.ShapeDtypeStruct((ff, d), BF),
            jax.ShapeDtypeStruct((8, d), F32),
            jax.ShapeDtypeStruct((1, ff), F32),
        ],
        scratch_shapes=[
            pltpu.VMEM((n, ff), BF),
            pltpu.VMEM((n, ff), BF),
            pltpu.VMEM((own, ff), BF),
            pltpu.VMEM((n, d), BF),
            pltpu.VMEM((n, d), BF),
            pltpu.VMEM((n, d), BF),
            pltpu.VMEM((n, d), BF),
        ],
        name="ffn",
    )(ctx, xa, xb, ca, cb, wo, wi, w2, vec, b_in)


def proj_body(
    xa, xb, dq, dk, dkr, dv, dvr, gm1, wq, wk, wv,
    ga_o, gb_o, dwq_o, dwk_o, dwv_o, gvec, x_all, dq_all, dk_all, dv_all,
):
    page = pl.program_id(0)
    blk = xa.shape[1]
    own = 2 * blk
    here = pl.ds(pl.multiple_of(page * own, own), own)
    x_all[here, :] = jnp.concatenate([xa[0], xb[0]], axis=0)
    dq_v = dq[0]
    dk_v = (dk[0].astype(F32) + dkr[0].astype(F32)).astype(BF)
    dv_v = (dv[0].astype(F32) + dvr[0].astype(F32)).astype(BF)
    dq_all[here, :] = dq_v
    dk_all[here, :] = dk_v
    dv_all[here, :] = dv_v
    gx = gm1[0] + dot(dq_v, wq[...], NT) + dot(dk_v, wk[...], NT) + dot(dv_v, wv[...], NT)
    ga_o[0] = gx[:blk]
    gb_o[0] = gx[blk:].astype(BF)

    @pl.when(page == 0)
    def _():
        gvec[...] = jnp.zeros_like(gvec)

    gvec[0:1, :] += jnp.sum(dq_v.astype(F32), 0, keepdims=True)
    gvec[1:2, :] += jnp.sum(dv_v.astype(F32), 0, keepdims=True)

    @pl.when(page == pl.num_programs(0) - 1)
    def _():
        x_t = x_all[...].T
        dwq_o[...] = dot(x_t, dq_all[...]).astype(BF)
        dwk_o[...] = dot(x_t, dk_all[...]).astype(BF)
        dwv_o[...] = dot(x_t, dv_all[...]).astype(BF)


def proj(xa, xb, dq, dk, dkr, dv, dvr, gm1, wq, wk, wv):
    pages, own, d = dq.shape
    blk = own // 2
    n = pages * own
    by_page = lambda p: (p, 0, 0)
    const = lambda p: (0, 0)
    one = pl.Buffered(1)
    half = pl.BlockSpec((1, blk, d), by_page)
    whole = pl.BlockSpec((1, own, d), by_page)
    square = pl.BlockSpec((d, d), const, pipeline_mode=one)
    return call(
        proj_body,
        (12 * n * d * d, 12 * d * d + 16 * n * d, 0),
        grid=(pages,),
        in_specs=[half, half] + [whole] * 6 + [square] * 3,
        out_specs=[half, half] + [square] * 3 + [pl.BlockSpec((8, d), const)],
        out_shape=[
            jax.ShapeDtypeStruct((pages, blk, d), F32),
            jax.ShapeDtypeStruct((pages, blk, d), BF),
        ]
        + [jax.ShapeDtypeStruct((d, d), BF)] * 3
        + [jax.ShapeDtypeStruct((8, d), F32)],
        scratch_shapes=[pltpu.VMEM((n, d), BF)] * 4,
        name="proj_bwd",
    )(xa, xb, dq, dk, dkr, dv, dvr, gm1, wq, wk, wv)


def place():
    f, s = lax.axis_index("fsdp"), lax.axis_index("seq")
    return lax.div(f, 2), lax.rem(f, 2), lax.div(s, 2), lax.rem(s, 2)


def at(z, y, x, c):
    return {"fsdp": 2 * z + y, "seq": 2 * x + c}


def meet(others):
    barrier = pltpu.get_barrier_semaphore()
    for other in others:
        pl.semaphore_signal(barrier, inc=1, device_id=other, device_id_type=MESH)
    pl.semaphore_wait(barrier, len(others))


def remote(src, dst, send, recv, other):
    copy = pltpu.make_async_remote_copy(
        src_ref=src, dst_ref=dst, send_sem=send, recv_sem=recv,
        device_id=other, device_id_type=MESH,
    )
    copy.start()
    return copy


def neighbours(z, y, x, c):
    n_z = 4
    zs = [at(lax.rem(z + k, n_z), y, x, c) for k in range(1, n_z)]
    far = [at(lax.rem(z + k, n_z), 1 - y, x, c) for k in range(n_z)]
    return zs + far + [at(z, y, 1 - x, c), at(z, y, x, 1 - c)]


def piece_views(wq, wk, wv, wo, wi, w2, lead):
    views = []

    def add(ref, row0, col0):
        def view(sel, rows, cols):
            r0, nr = rows
            c0, nc = cols
            r = pl.ds(row0 + r0, nr)
            c = pl.ds(col0 + c0, nc)
            return ref.at[sel + (r, c)] if lead else ref.at[r, c]

        views.append(view)

    for ref in (wq, wk, wv, wo):
        add(ref, 0, 0)
    for j in range(4):
        add(wi, 0, 768 * j)
    for j in range(4):
        add(w2, ROW * j, 0)
    return views


ALL = slice(None)


def gather_body(
    x_in, cot, wq, wk, wv, wo, wi, w2, vec,
    gq, gk, gv, go, gi, g2, xa, xb, xc, xd, ca, cb, gvec,
    lsem, zs, zr, ys, yr, xs, xr, cs, cr, asend, arecv, aloc, vs, vr,
):
    z, y, x, c = place()
    f = 2 * z + y
    meet(neighbours(z, y, x, c))
    x_peer, c_peer, y_peer = at(z, y, 1 - x, c), at(z, y, x, 1 - c), at(z, 1 - y, x, c)
    own_pages, sent_pages = pl.ds(3 * x, 3), pl.ds(3 * (1 - x), 3)
    src = piece_views(wq, wk, wv, wo, wi, w2, False)
    dst = piece_views(gq, gk, gv, go, gi, g2, True)
    n = len(src)
    half_cols = (pl.multiple_of(c * 384, 128), 384)
    full = (0, ROW)
    mine = (pl.multiple_of(x * (ROW // 2), 16), ROW // 2)
    wide = [p % 2 == 0 for p in range(n)]

    to_b = remote(x_in.at[sent_pages], xb, asend.at[0], arecv.at[0], x_peer)
    to_c = remote(x_in.at[own_pages], xc, asend.at[1], arecv.at[1], c_peer)
    locals_ = [
        pltpu.make_async_copy(x_in.at[own_pages], xa, aloc.at[0]),
        pltpu.make_async_copy(cot.at[own_pages], ca, aloc.at[1]),
        pltpu.make_async_copy(vec, gvec.at[f], aloc.at[2]),
    ]
    for copy in locals_:
        copy.start()
    vecs = [
        remote(vec, gvec.at[f], vs.at[k], vr.at[k], {"fsdp": lax.rem(f + k + 1, 8)})
        for k in range(7)
    ]
    own = [
        pltpu.make_async_copy(
            src[p]((), full if wide[p] else mine, half_cols),
            dst[p]((z, y), full if wide[p] else mine, half_cols),
            lsem.at[p],
        )
        for p in range(n)
    ]
    for copy in own:
        copy.start()
    along_z, along_y, along_x, along_c = [], [], [], []
    to_d = None
    to_cb = None
    for t in range(n + 3):
        if t < n:
            rows = full if wide[t] else mine
            along_z.append(
                [
                    remote(
                        src[t]((), rows, half_cols), dst[t]((z, y), rows, half_cols),
                        zs.at[t, k], zr.at[t, k], at(lax.rem(z + k + 1, 4), y, x, c),
                    )
                    for k in range(3)
                ]
            )
        p = t - 1
        if 0 <= p < n:
            own[p].wait()
            for copy in along_z[p]:
                copy.wait_recv()
            view = dst[p]((ALL, y), mine, half_cols)
            along_y.append(remote(view, view, ys.at[p], yr.at[p], y_peer))
        p = t - 2
        if 0 <= p < n:
            along_y[p].wait_recv()
            view = dst[p]((ALL, 1 - y) if wide[p] else (ALL, ALL), mine, half_cols)
            along_x.append(remote(view, view, xs.at[p], xr.at[p], x_peer))
        p = t - 3
        if 0 <= p < n:
            along_x[p].wait_recv()
            view = dst[p]((ALL, ALL), full, half_cols)
            along_c.append(remote(view, view, cs.at[p], cr.at[p], c_peer))
        if t == 2:
            to_b.wait_recv()
            to_d = remote(xb, xd, asend.at[2], arecv.at[2], c_peer)
            to_cb = remote(cot.at[sent_pages], cb, asend.at[3], arecv.at[3], x_peer)
    for copy in along_c:
        copy.wait_recv()
    to_c.wait_recv()
    to_d.wait_recv()
    to_cb.wait_recv()
    for copy in vecs:
        copy.wait_recv()
    for group in along_z:
        for copy in group:
            copy.wait_send()
    for copy in along_y + along_x + along_c + vecs + [to_b, to_c, to_d, to_cb]:
        copy.wait_send()
    for copy in locals_:
        copy.wait()


def gather_all(x_in, cot, ws, vec):
    half = jax.ShapeDtypeStruct((3,) + x_in.shape[1:], BF)
    dma = pltpu.SemaphoreType.DMA
    n = 12
    outs = [jax.ShapeDtypeStruct((4, 2) + w.shape, BF) for w in ws]
    res = call(
        gather_body,
        (0, sum(16 * w.size for w in ws), 0),
        in_specs=[ANY] * 9,
        out_specs=[ANY] * 13,
        out_shape=outs + [half] * 6 + [jax.ShapeDtypeStruct((8,) + vec.shape, vec.dtype)],
        scratch_shapes=[
            dma((n,)), dma((n, 3)), dma((n, 3)), dma((n,)), dma((n,)), dma((n,)), dma((n,)),
            dma((n,)), dma((n,)), dma((4,)), dma((4,)), dma((3,)), dma((7,)), dma((7,)),
        ],
        params=dict(collective_id=0, has_side_effects=True),
        name="gather_all",
    )(x_in, cot, *ws, vec)
    full = [r.reshape(-1, r.shape[-1]) for r in res[:6]]
    return full, res[6:10], res[10:12], res[12]


def scatter_body(
    gq, gk, gv, go, gi, g2, out_a, out_b, gx_a, gx_b, gvec,
    oq, ok, ov, oo, oi, o2, out, gx, ovec,
    acc, rc, rx, ry, rz, fin, rf, rgx, vecin, vtot, vx,
    lsem, cs, cr, xs, xr, ys, yr, zs, zr, fs, fr, es, er, asend, arecv, aloc, vs, vr, us, ur,
):
    z, y, x, c = place()
    f = 2 * z + y
    meet(neighbours(z, y, x, c) + [at(z, y, 1 - x, 1 - c)])
    x_peer, c_peer, y_peer = at(z, y, 1 - x, c), at(z, y, x, 1 - c), at(z, 1 - y, x, c)
    own_pages = pl.ds(3 * x, 3)
    other_pages = pl.ds(3 * (1 - x), 3)
    src = piece_views(gq, gk, gv, go, gi, g2, True)
    dst = piece_views(oq, ok, ov, oo, oi, o2, False)
    n = len(src)
    hr = ROW // 2
    half_cols = (pl.multiple_of(c * 384, 128), 384)
    their_cols = (pl.multiple_of((1 - c) * 384, 128), 384)
    full = (0, ROW)
    mine = pl.ds(pl.multiple_of(x * hr, 16), hr)
    theirs = pl.ds(pl.multiple_of((1 - x) * hr, 16), hr)
    wide = [p % 2 == 0 for p in range(n)]

    back_x = remote(gx_b, rgx, asend.at[0], arecv.at[0], x_peer)
    vecs = []
    for k in range(7):
        to = lax.rem(f + k + 1, 8)
        vecs.append(remote(gvec.at[to], vecin.at[k], vs.at[k], vr.at[k], {"fsdp": to}))
    keep_out = pltpu.make_async_copy(out_a, out.at[own_pages], aloc.at[0])
    keep_out.start()
    mine_first = []
    to_core = []
    for p in range(n):
        copy = pltpu.make_async_copy(src[p]((ALL, ALL), full, half_cols), acc.at[p], lsem.at[p])
        copy.start()
        mine_first.append(copy)
        to_core.append(
            remote(src[p]((ALL, ALL), full, their_cols), rc.at[p], cs.at[p], cr.at[p], c_peer)
        )
    back_out = remote(out_b, out.at[own_pages], asend.at[1], arecv.at[1], x_peer)

    gx[own_pages] = gx_a[...]
    along_x, along_y, along_z, finals, ends = [], [], [], [], []
    vec_x = []
    for t in range(n + 5):
        p = t
        if p < n:
            mine_first[p].wait()
            to_core[p].wait_recv()
            acc[p] = (acc[p].astype(F32) + rc[p].astype(F32)).astype(BF)
            if wide[p]:
                along_x.append(
                    remote(acc.at[p, :, 1 - y, theirs, :], rx.at[p, :, 0], xs.at[p], xr.at[p], x_peer)
                )
            else:
                along_x.append(
                    remote(acc.at[p, :, :, theirs, :], rx.at[p], xs.at[p], xr.at[p], x_peer)
                )
        p = t - 1
        if 0 <= p < n:
            along_x[p].wait_recv()
            if wide[p]:
                acc[p, :, 1 - y, mine, :] = (
                    acc[p, :, 1 - y, mine, :].astype(F32) + rx[p, :, 0].astype(F32)
                ).astype(BF)
            else:
                acc[p, :, :, mine, :] = (
                    acc[p, :, :, mine, :].astype(F32) + rx[p].astype(F32)
                ).astype(BF)
            along_y.append(
                remote(acc.at[p, :, 1 - y, mine, :], ry.at[p], ys.at[p], yr.at[p], y_peer)
            )
        p = t - 2
        if 0 <= p < n:
            along_y[p].wait_recv()
            acc[p, :, y, mine, :] = (
                acc[p, :, y, mine, :].astype(F32) + ry[p].astype(F32)
            ).astype(BF)
            group = []
            for k in range(3):
                to = lax.rem(z + k + 1, 4)
                if wide[p]:
                    a, b = acc.at[p, to, y], rz.at[p, k]
                else:
                    a, b = acc.at[p, to, y, mine, :], rz.at[p, k, pl.ds(0, hr)]
                group.append(remote(a, b, zs.at[p, k], zr.at[p, k], at(to, y, x, c)))
            along_z.append(group)
        p = t - 3
        if 0 <= p < n:
            for copy in along_z[p]:
                copy.wait_recv()
            if wide[p]:
                total = acc[p, z, y].astype(F32)
                for k in range(3):
                    total = total + rz[p, k].astype(F32)
                fin[p] = total.astype(BF)
                finals.append(remote(fin.at[p], rf.at[p], fs.at[p], fr.at[p], x_peer))
            else:
                total = acc[p, z, y, mine, :].astype(F32)
                for k in range(3):
                    total = total + rz[p, k, :hr].astype(F32)
                fin[p, :hr] = total.astype(BF)
                finals.append(
                    remote(fin.at[p, pl.ds(0, hr)], rf.at[p, pl.ds(0, hr)], fs.at[p], fr.at[p], x_peer)
                )
        p = t - 4
        if 0 <= p < n:
            finals[p].wait_recv()
            if wide[p]:
                dst[p]((), full, half_cols)[...] = fin[p].astype(F32) + rf[p].astype(F32)
            else:
                dst[p]((), (pl.multiple_of(x * hr, 16), hr), half_cols)[...] = fin[p, :hr].astype(F32)
                dst[p]((), (pl.multiple_of((1 - x) * hr, 16), hr), half_cols)[...] = rf[p, :hr].astype(F32)
            view = dst[p]((), full, half_cols)
            ends.append(remote(view, view, es.at[p], er.at[p], c_peer))
        if t == 1:
            total = gvec[f]
            for copy in vecs:
                copy.wait_recv()
            for k in range(7):
                total = total + vecin[k]
            vtot[...] = total
            vec_x = [
                remote(vtot, vx.at[0], us.at[0], ur.at[0], x_peer),
            ]
        if t == 3:
            vec_x[0].wait_recv()
            vx[1] = vtot[...] + vx[0]
            vec_x.append(remote(vx.at[1], vx.at[2], us.at[1], ur.at[1], c_peer))
        if t == 5:
            back_x.wait_recv()
            gx[other_pages] = rgx[...].astype(F32)
    vec_x[1].wait_recv()
    ovec[...] = vx[1] + vx[2]
    for copy in ends:
        copy.wait_recv()
    back_out.wait_recv()
    keep_out.wait()
    for group in along_z:
        for copy in group:
            copy.wait_send()
    for copy in to_core + along_x + along_y + finals + ends + vecs + vec_x + [back_x, back_out]:
        copy.wait_send()


def scatter_all(grads, out_a, out_b, gx_a, gx_b, gvec, shards):
    dma = pltpu.SemaphoreType.DMA
    n = 12
    pages, blk, d = out_a.shape
    views = [g.reshape((4, 2) + shape) for g, shape in zip(grads, shards)]
    vmem = pltpu.VMEM
    res = call(
        scatter_body,
        (0, sum(16 * g.size for g in grads), 0),
        in_specs=[ANY] * 6 + [ANY, ANY, VM, ANY, VM],
        out_specs=[VM] * 6 + [ANY, VM, VM],
        out_shape=[jax.ShapeDtypeStruct(shape, F32) for shape in shards]
        + [
            jax.ShapeDtypeStruct((2 * pages, blk, d), BF),
            jax.ShapeDtypeStruct((2 * pages, blk, d), F32),
            jax.ShapeDtypeStruct(gvec.shape[1:], F32),
        ],
        scratch_shapes=[
            vmem((n, 4, 2, ROW, 384), BF),
            vmem((n, 4, 2, ROW, 384), BF),
            vmem((n, 4, 2, ROW // 2, 384), BF),
            vmem((n, 4, ROW // 2, 384), BF),
            vmem((n, 3, ROW, 384), BF),
            vmem((n, ROW, 384), BF),
            vmem((n, ROW, 384), BF),
            vmem((pages, blk, d), BF),
            vmem((7,) + gvec.shape[1:], F32),
            vmem(gvec.shape[1:], F32),
            vmem((3,) + gvec.shape[1:], F32),
            dma((n,)), dma((n,)), dma((n,)), dma((n,)), dma((n,)), dma((n,)), dma((n,)),
            dma((n, 3)), dma((n, 3)), dma((n,)), dma((n,)), dma((n,)), dma((n,)),
            dma((2,)), dma((2,)), dma((1,)), dma((7,)), dma((7,)), dma((2,)), dma((2,)),
        ],
        params=dict(collective_id=1, has_side_effects=True),
        name="scatter_all",
    )(*views, out_a, out_b, gx_a, gx_b, gvec)
    return res[:6], res[6], res[7], res[8]


SWAP_X = [(0, 2), (2, 0), (1, 3), (3, 1)]
SWAP_C = [(0, 1), (1, 0), (2, 3), (3, 2)]


def swap(value, pairs):
    return lax.ppermute(value, "seq", pairs)


def per_device(
    fsdp, inputs, lengths, w_query, b_query, w_key, w_value, b_value, w_out, b_out,
    gain_one, shift_one, w_inner, b_inner, w_outer, b_outer, gain_two, shift_two, cotangent,
):
    pages_all, blk, d = inputs.shape
    pages = pages_all // 2
    s = lax.axis_index("seq")
    x_at = lax.div(s, 2)
    direct = fsdp == 8
    ws = (w_query, w_key, w_value, w_out, w_inner, w_outer)
    shards = [w.shape for w in ws]
    width = b_query.shape[0]
    names = (b_query, b_value, b_out, gain_one, shift_one, b_outer, gain_two, shift_two)
    vec = jnp.concatenate(names + (b_inner,)).reshape(12, width)

    def pages_of(array, side):
        return lax.dynamic_slice_in_dim(array, side * pages, pages, 0)

    if direct:
        padded = jnp.pad(vec, ((0, 4), (0, 128 - width)))
        full, xs, cots, gvec = gather_all(inputs, cotangent, ws, padded)
        gvec = gvec[:, :12, :width]
        xa, xb, xc, xd = xs
        ca, cb = cots
    else:
        full = [lax.all_gather(w, "fsdp", axis=0, tiled=True) for w in ws]
        gvec = lax.all_gather(vec, "fsdp", axis=0)
        xa, ca = pages_of(inputs, x_at), pages_of(cotangent, x_at)
        xb = swap(pages_of(inputs, 1 - x_at), SWAP_X)
        cb = swap(pages_of(cotangent, 1 - x_at), SWAP_X)
        xc, xd = swap(xa, SWAP_C), swap(xb, SWAP_C)
    wq, wk, wv, wo, wi, w2 = full
    vec_full = jnp.swapaxes(gvec[:, :8], 0, 1).reshape(8, d).astype(F32)
    bin_full = gvec[:, 8:].reshape(1, -1).astype(F32)

    order = jnp.stack([s, s ^ 2, s ^ 1, s ^ 3]).astype(jnp.int32)
    thr = pages_of(lengths, x_at).astype(jnp.int32)[:, None] - order[None, :] * blk

    q, k, v, p, ctx = attn_fwd(thr, (xa, xb, xc, xd), wq, wk, wv, vec_full)
    out_a, out_b, gm1, dctx, dwo, dwi, dw2, gv_ffn, gbin = ffn(
        ctx, xa, xb, ca, cb, wo, wi, w2, vec_full, bin_full
    )
    dq, dk, dk_send, dv, dv_send = attn_bwd(q, k, v, p, ctx, dctx)
    dkr, dvr = swap(dk_send, SWAP_C), swap(dv_send, SWAP_C)
    gx_a, gx_b, dwq, dwk, dwv, gv_proj = proj(xa, xb, dq, dk, dkr, dv, dvr, gm1, wq, wk, wv)

    gv = jnp.concatenate([gv_proj[:2], gv_ffn[2:]], axis=0)
    grads = (dwq, dwk, dwv, dwo, dwi, dw2)
    by_owner = jnp.concatenate(
        [jnp.swapaxes(gv.reshape(8, fsdp, width), 0, 1), gbin.reshape(fsdp, 4, width)], axis=1
    )
    if direct:
        padded = jnp.pad(by_owner, ((0, 0), (0, 4), (0, 128 - width)))
        tot, output, grad_inputs, tvec = scatter_all(grads, out_a, out_b, gx_a, gx_b, padded, shards)
        tvec = tvec[:12, :width]
    else:
        tot = [
            lax.psum(lax.psum_scatter(g, "fsdp", scatter_dimension=0, tiled=True), "seq").astype(F32)
            for g in grads
        ]
        tvec = lax.psum(lax.psum_scatter(by_owner, "fsdp", scatter_dimension=0, tiled=True)[0], "seq")

        def joined(mine, other):
            here = lax.dynamic_update_slice_in_dim(
                jnp.zeros((pages_all, blk, d), mine.dtype), mine, x_at * pages, 0
            )
            return lax.dynamic_update_slice_in_dim(here, other, (1 - x_at) * pages, 0)

        output = joined(out_a, swap(out_b, SWAP_X))
        grad_inputs = joined(gx_a, swap(gx_b, SWAP_X).astype(F32))
    small = [tvec[i] for i in range(8)]
    g_bq, g_bv, g_bo, g_g1, g_s1, g_bo2, g_g2, g_s2 = small
    g_bi = tvec[8:].reshape(-1)
    t_q, t_k, t_v, t_o, t_i, t_2 = tot
    return (
        output, grad_inputs, t_q, g_bq, t_k, t_v, g_bv, t_o, g_bo, g_g1, g_s1,
        t_i, g_bi, t_2, g_bo2, g_g2, g_s2,
    )


def solution(mesh):
    vec, mat, act = P("fsdp"), P("fsdp", None), P("fsdp", "seq", None)
    return jax.shard_map(
        functools.partial(per_device, mesh.shape["fsdp"]),
        mesh=mesh,
        in_specs=(act, vec, mat, vec, mat, mat, vec, mat, vec, vec, vec, mat, vec, mat, vec, vec, vec, act),
        out_specs=(act, act, mat, vec, mat, mat, vec, mat, vec, vec, vec, mat, vec, mat, vec, vec, vec),
        check_vma=False,
    )
```

```python
import functools
import math

import jax
import jax.numpy as jnp
from jax import lax
from jax.experimental import pallas as pl
from jax.experimental.pallas import tpu as pltpu
from jax.sharding import PartitionSpec as P

HEADS = 12
HEAD_DIM = 64
PAIR = 2 * HEAD_DIM
NEG = -1e30
EPS = 1e-12
BF = jnp.bfloat16
F32 = jnp.float32
MESH = pl.DeviceIdType.MESH
ANY = pl.BlockSpec(memory_space=pl.ANY)
VM = pl.BlockSpec(memory_space=pltpu.VMEM)
CHUNK = 1024
ROW = 96
VMEM_CAP = 60 << 20

NN = (((1,), (0,)), ((), ()))
NT = (((1,), (1,)), ((), ()))
TN = (((0,), (0,)), ((), ()))


def dot(a, b, dims=NN):
    return lax.dot_general(a, b, dims, preferred_element_type=F32)


def call(body, cost, **kw):
    flops, byts, trans = cost
    params = dict(vmem_limit_bytes=VMEM_CAP)
    params.update(kw.pop("params", {}))
    return pl.pallas_call(
        body,
        compiler_params=pltpu.CompilerParams(**params),
        cost_estimate=pl.CostEstimate(
            flops=int(flops), bytes_accessed=int(byts), transcendentals=int(trans)
        ),
        **kw,
    )


def attn_fwd_body(thr, xall, wq, wk, wv, vec, q_o, k_o, v_o, p_o, c_o, bias):
    page = pl.program_id(0)
    x_all = xall[0]
    own = x_all.shape[0] // 2
    query = (dot(x_all[:own], wq[...]) + vec[0:1, :]).astype(BF)
    q_o[0] = query
    k_o[0] = dot(x_all, wk[...]).astype(BF)
    v_o[0] = (dot(x_all, wv[...]) + vec[1:2, :]).astype(BF)
    blk = x_all.shape[0] // 4
    place = lax.broadcasted_iota(jnp.int32, (blk, own), 0)
    for b in range(4):
        bias[b * blk : (b + 1) * blk, :] = jnp.where(place < thr[page, b], 0.0, NEG)
    low_lane = lax.broadcasted_iota(jnp.int32, (own, PAIR), 1) < HEAD_DIM

    def pair(i, carry):
        cols = pl.ds(pl.multiple_of(i * PAIR, PAIR), PAIR)
        qp = q_o[0, :, cols] * jnp.array(1.0 / math.sqrt(HEAD_DIM), BF)
        kp = k_o[0, :, cols]
        vt = v_o[0, :, cols].T
        outs = []
        for h in range(2):
            keep = low_lane if h == 0 else jnp.logical_not(low_lane)
            qh = jnp.where(keep, qp, jnp.zeros_like(qp))
            st = dot(kp, qh, NT) + bias[...]
            top = jnp.max(st, axis=0, keepdims=True)
            ex = jnp.exp(st - top)
            tot = jnp.sum(ex, axis=0, keepdims=True)
            pt = (ex * (1.0 / tot)).astype(BF)
            p_o[0, 2 * i + h] = pt
            outs.append(dot(vt[h * HEAD_DIM : (h + 1) * HEAD_DIM], pt))
        c_o[0, :, cols] = jnp.concatenate(outs, axis=0).T.astype(BF)
        return carry

    lax.fori_loop(0, HEADS // 2, pair, 0)


def attn_fwd(thr, xall, wq, wk, wv, vec):
    pages, rows, d = xall.shape
    own = rows // 2
    const = lambda p, t: (0, 0)
    by_page = lambda p, t: (p, 0, 0)
    one = pl.Buffered(1)
    return call(
        attn_fwd_body,
        (
            pages * (2 * d * d * (own + 2 * rows) + 4 * own * rows * d),
            pages * rows * d * 2 * 4 + 6 * d * d + pages * HEADS * own * rows * 2,
            pages * HEADS * own * rows,
        ),
        grid_spec=pltpu.PrefetchScalarGridSpec(
            num_scalar_prefetch=1,
            grid=(pages,),
            in_specs=[pl.BlockSpec((1, rows, d), by_page)]
            + [pl.BlockSpec((d, d), const, pipeline_mode=one)] * 3
            + [pl.BlockSpec((8, d), const)],
            out_specs=[
                pl.BlockSpec((1, own, d), by_page),
                pl.BlockSpec((1, rows, d), by_page),
                pl.BlockSpec((1, rows, d), by_page),
                pl.BlockSpec((1, HEADS, rows, own), lambda p, t: (p, 0, 0, 0)),
                pl.BlockSpec((1, own, d), by_page),
            ],
            scratch_shapes=[pltpu.VMEM((rows, own), F32)],
        ),
        out_shape=[
            jax.ShapeDtypeStruct((pages, own, d), BF),
            jax.ShapeDtypeStruct((pages, rows, d), BF),
            jax.ShapeDtypeStruct((pages, rows, d), BF),
            jax.ShapeDtypeStruct((pages, HEADS, rows, own), BF),
            jax.ShapeDtypeStruct((pages, own, d), BF),
        ],
        name="attn_fwd",
    )(thr, xall, wq, wk, wv, vec)


def attn_bwd_body(q, k, v, p, ctx, dctx, dq_o, dk_own, dk_oth, dv_own, dv_oth):
    own = q.shape[1]
    low_lane = lax.broadcasted_iota(jnp.int32, (own, PAIR), 1) < HEAD_DIM
    scale = 1.0 / math.sqrt(HEAD_DIM)

    def pair(i, carry):
        cols = pl.ds(pl.multiple_of(i * PAIR, PAIR), PAIR)
        qp = q[0, :, cols] * jnp.array(scale, BF)
        kp = k[0, :, cols]
        kt = kp.T
        vp = v[0, :, cols]
        dc = dctx[0, :, cols]
        prod = (dc.astype(F32) * ctx[0, :, cols].astype(F32)).T
        dk = None
        dv = None
        dqs = []
        for h in range(2):
            keep = low_lane if h == 0 else jnp.logical_not(low_lane)
            feats = slice(h * HEAD_DIM, (h + 1) * HEAD_DIM)
            dch = jnp.where(keep, dc, jnp.zeros_like(dc))
            qh = jnp.where(keep, qp, jnp.zeros_like(qp))
            pt = p[0, 2 * i + h]
            delta = jnp.sum(prod[feats], axis=0, keepdims=True)
            dpt = dot(vp, dch, NT)
            dst = (pt.astype(F32) * (dpt - delta)).astype(BF)
            dvh = dot(pt, dch)
            dkh = dot(dst, qh)
            dk = dkh if dk is None else dk + dkh
            dv = dvh if dv is None else dv + dvh
            dqs.append(dot(kt[feats], dst))
        dq_o[0, :, cols] = (jnp.concatenate(dqs, axis=0) * scale).T.astype(BF)
        dk_own[0, :, cols] = dk[:own].astype(BF)
        dk_oth[0, :, cols] = dk[own:].astype(BF)
        dv_own[0, :, cols] = dv[:own].astype(BF)
        dv_oth[0, :, cols] = dv[own:].astype(BF)
        return carry

    lax.fori_loop(0, HEADS // 2, pair, 0)


def attn_bwd(q, k, v, p, ctx, dctx):
    pages, own, d = q.shape
    rows = k.shape[1]
    by_page = lambda i: (i, 0, 0)
    o = pl.BlockSpec((1, own, d), by_page)
    r = pl.BlockSpec((1, rows, d), by_page)
    return call(
        attn_bwd_body,
        (pages * 10 * own * rows * d, pages * (own * rows * HEADS * 2 + 10 * own * d * 2), 0),
        grid=(pages,),
        in_specs=[o, r, r, pl.BlockSpec((1, HEADS, rows, own), lambda i: (i, 0, 0, 0)), o, o],
        out_specs=[o] * 5,
        out_shape=[jax.ShapeDtypeStruct((pages, own, d), BF)] * 5,
        name="attn_bwd",
    )(q, k, v, p, ctx, dctx)


def normal_parts(v):
    bell = jnp.exp(v * v * -0.5)
    t = 1.0 / (1.0 + jnp.abs(v) * (0.3275911 / math.sqrt(2.0)))
    tail = t * (
        0.127414796 + t * (-0.142248368 + t * (0.7107068705 + t * (-0.7265760135 + t * 0.5307027145)))
    )
    tail = tail * bell
    return jnp.where(v >= 0.0, 1.0 - tail, tail), bell * (1.0 / math.sqrt(2.0 * math.pi))


def row_norm(v):
    centered = v - jnp.mean(v, -1, keepdims=True)
    inv = lax.rsqrt(jnp.mean(centered * centered, -1, keepdims=True) + EPS)
    return centered * inv, inv


def norm_back(e, n, inv):
    return inv * (e - jnp.mean(e, -1, keepdims=True) - n * jnp.mean(e * n, -1, keepdims=True))


def ffn_body(
    ctx, xall, cown, wo, wi_h, w2_h, vec, b_in,
    out, gm1_o, dctx_o, dwo_o, dwi_h, dw2_h, gvec, gbin,
    wi, w2, act, din, dgel, hid, gout, gatt, n1s, h1s, accs, r1s, dwi, dw2, lsem, osem,
):
    n, ff = act.shape
    pages, own, d = ctx.shape

    def cols_of(j):
        return pl.ds(pl.multiple_of(j * CHUNK, CHUNK), CHUNK)

    def loads(j):
        cols = cols_of(j)
        return (
            pltpu.make_async_copy(wi_h.at[:, cols], wi.at[:, cols], lsem.at[0, j]),
            pltpu.make_async_copy(w2_h.at[cols, :], w2.at[cols, :], lsem.at[1, j]),
        )

    def store_w2(j):
        return pltpu.make_async_copy(dw2.at[cols_of(j), :], dw2_h.at[cols_of(j), :], osem.at[0, j])

    def store_wi(j):
        return pltpu.make_async_copy(dwi.at[:, cols_of(j)], dwi_h.at[:, cols_of(j)], osem.at[1, j])

    n_chunks = ff // CHUNK
    for j in range(n_chunks):
        for copy in loads(j):
            copy.start()
    gvec[...] = jnp.zeros_like(gvec)

    def add(row, value):
        gvec[row : row + 1, :] += jnp.sum(value, 0, keepdims=True)

    for p in range(pages):
        r = slice(p * own, (p + 1) * own)
        mid = xall[p].astype(F32) + (dot(ctx[p], wo[...]) + vec[2:3, :])
        n1, r1 = row_norm(mid)
        n1s[r, :] = n1
        r1s[r, :] = jnp.broadcast_to(r1, (own, 128))
        h1 = n1 * vec[3:4, :] + vec[4:5, :]
        h1s[r, :] = h1
        hid[r, :] = h1.astype(BF)
    accs[...] = jnp.zeros_like(accs)

    def up(j, carry):
        cols = cols_of(j)
        for copy in loads(j):
            copy.wait()
        pre = dot(hid[...], wi[:, cols]) + b_in[:, cols]
        big, bell = normal_parts(pre)
        a = (pre * big).astype(BF)
        dgel[:, cols] = (big + pre * bell).astype(BF)
        act[:, cols] = a
        accs[...] += dot(a, w2[cols, :])
        return carry

    lax.fori_loop(0, n_chunks, up, 0)
    for p in range(pages):
        r = slice(p * own, (p + 1) * own)
        mid = h1s[r, :] + (accs[r, :] + vec[5:6, :])
        n2, r2 = row_norm(mid)
        out[p] = (n2 * vec[6:7, :] + vec[7:8, :]).astype(BF)
        cot = cown[p].astype(F32)
        gm2 = norm_back(cot * vec[6:7, :], n2, r2)
        go = gm2.astype(BF)
        gout[r, :] = go
        accs[r, :] = gm2
        add(5, go.astype(F32))
        add(6, cot * n2)
        add(7, cot)

    def down(j, carry):
        cols = cols_of(j)
        di = (dot(gout[...], w2[cols, :], NT) * dgel[:, cols].astype(F32)).astype(BF)
        din[:, cols] = di
        accs[...] += dot(di, wi[:, cols], NT)
        gbin[:, cols] = jnp.sum(di.astype(F32), 0, keepdims=True)
        dw2[cols, :] = dot(act[:, cols], gout[...], TN).astype(BF)
        store_w2(j).start()
        return carry

    lax.fori_loop(0, n_chunks, down, 0)
    for p in range(pages):
        r = slice(p * own, (p + 1) * own)
        gh = accs[r, :]
        n1 = n1s[r, :]
        gm1 = norm_back(gh * vec[3:4, :], n1, r1s[r, 0:1])
        gm1_o[p] = gm1
        ga = gm1.astype(BF)
        gatt[r, :] = ga
        dctx_o[p] = dot(ga, wo[...], NT).astype(BF)
        add(2, ga.astype(F32))
        add(3, gh * n1)
        add(4, gh)
    hid_t = hid[...].T

    def grads(j, carry):
        cols = cols_of(j)
        dwi[:, cols] = dot(hid_t, din[:, cols]).astype(BF)
        store_wi(j).start()
        return carry

    lax.fori_loop(0, n_chunks, grads, 0)
    dwo_o[...] = dot(ctx[...].reshape(n, d), gatt[...], TN).astype(BF)
    for j in range(n_chunks):
        store_w2(j).wait()
        store_wi(j).wait()


def ffn(ctx, xall, cown, wo, wi, w2, vec, b_in):
    pages, own, d = ctx.shape
    ff = wi.shape[1]
    n = pages * own
    sds = jax.ShapeDtypeStruct
    vm = pltpu.VMEM
    dma = pltpu.SemaphoreType.DMA
    return call(
        ffn_body,
        (n * d * (12 * ff + 6 * d), 4 * d * ff * 2 + 12 * n * d * 2, n * ff),
        grid=(1,),
        in_specs=[
            pl.BlockSpec((pages, own, d), lambda i: (0, 0, 0)),
            pl.BlockSpec((pages, own, d), lambda i: (0, 0, 0)),
            VM, VM, ANY, ANY, VM, VM,
        ],
        out_specs=[VM] * 4 + [ANY, ANY, VM, VM],
        out_shape=[
            sds((pages, own, d), BF), sds((pages, own, d), F32), sds((pages, own, d), BF),
            sds((d, d), BF), sds((d, ff), BF), sds((ff, d), BF), sds((8, d), F32), sds((1, ff), F32),
        ],
        scratch_shapes=[
            vm((d, ff), BF), vm((ff, d), BF), vm((n, ff), BF), vm((n, ff), BF), vm((n, ff), BF),
            vm((n, d), BF), vm((n, d), BF), vm((n, d), BF), vm((n, d), F32), vm((n, d), F32),
            vm((n, d), F32), vm((n, 128), F32), vm((d, ff), BF), vm((ff, d), BF),
            dma((2, ff // CHUNK)), dma((2, ff // CHUNK)),
        ],
        params=dict(vmem_limit_bytes=63 << 20),
        name="ffn",
    )(ctx, xall, cown, wo, wi, w2, vec, b_in)


def proj_body(
    xall, dq, dk, dkr, dv, dvr, gm1, wq, wk, wv,
    ga_o, gb_o, dwq_o, dwk_o, dwv_o, gvec, x_all, dq_all, dk_all, dv_all,
):
    page = pl.program_id(0)
    own = xall.shape[1]
    blk = own // 2
    here = pl.ds(pl.multiple_of(page * own, own), own)
    x_all[here, :] = xall[0]
    dq_v = dq[0]
    dk_v = (dk[0].astype(F32) + dkr[0].astype(F32)).astype(BF)
    dv_v = (dv[0].astype(F32) + dvr[0].astype(F32)).astype(BF)
    dq_all[here, :] = dq_v
    dk_all[here, :] = dk_v
    dv_all[here, :] = dv_v
    gx = gm1[0] + dot(dq_v, wq[...], NT) + dot(dk_v, wk[...], NT) + dot(dv_v, wv[...], NT)
    ga_o[0] = gx[:blk]
    gb_o[0] = gx[blk:].astype(BF)

    @pl.when(page == 0)
    def _():
        gvec[...] = jnp.zeros_like(gvec)

    gvec[0:1, :] += jnp.sum(dq_v.astype(F32), 0, keepdims=True)
    gvec[1:2, :] += jnp.sum(dv_v.astype(F32), 0, keepdims=True)

    @pl.when(page == pl.num_programs(0) - 1)
    def _():
        x_t = x_all[...].T
        dwq_o[...] = dot(x_t, dq_all[...]).astype(BF)
        dwk_o[...] = dot(x_t, dk_all[...]).astype(BF)
        dwv_o[...] = dot(x_t, dv_all[...]).astype(BF)


def proj(xall, dq, dk, dkr, dv, dvr, gm1, wq, wk, wv):
    pages, own, d = dq.shape
    blk = own // 2
    n = pages * own
    by_page = lambda p: (p, 0, 0)
    const = lambda p: (0, 0)
    one = pl.Buffered(1)
    half = pl.BlockSpec((1, blk, d), by_page)
    whole = pl.BlockSpec((1, own, d), by_page)
    square = pl.BlockSpec((d, d), const, pipeline_mode=one)
    return call(
        proj_body,
        (12 * n * d * d, 12 * d * d + 16 * n * d, 0),
        grid=(pages,),
        in_specs=[whole] * 7 + [square] * 3,
        out_specs=[half, half] + [square] * 3 + [pl.BlockSpec((8, d), const)],
        out_shape=[
            jax.ShapeDtypeStruct((pages, blk, d), F32),
            jax.ShapeDtypeStruct((pages, blk, d), BF),
        ]
        + [jax.ShapeDtypeStruct((d, d), BF)] * 3
        + [jax.ShapeDtypeStruct((8, d), F32)],
        scratch_shapes=[pltpu.VMEM((n, d), BF)] * 4,
        name="proj_bwd",
    )(xall, dq, dk, dkr, dv, dvr, gm1, wq, wk, wv)


def place():
    f, s = lax.axis_index("fsdp"), lax.axis_index("seq")
    return lax.div(f, 2), lax.rem(f, 2), lax.div(s, 2), lax.rem(s, 2)


def at(z, y, x, c):
    return {"fsdp": 2 * z + y, "seq": 2 * x + c}


def meet(others):
    barrier = pltpu.get_barrier_semaphore()
    for other in others:
        pl.semaphore_signal(barrier, inc=1, device_id=other, device_id_type=MESH)
    pl.semaphore_wait(barrier, len(others))


def remote(src, dst, send, recv, other):
    return pltpu.make_async_remote_copy(
        src_ref=src, dst_ref=dst, send_sem=send, recv_sem=recv,
        device_id=other, device_id_type=MESH,
    )


def begin(copy):
    copy.start()
    return copy


class Spread:
    def __init__(self, where, src, dst, row0, col0, width, sems, key):
        self.z, self.y, self.x, self.c = where
        z, y, x, c = where
        zs, zr, fs, ys, yr, xs, xr, cs, cr, lo = sems
        k = key
        cols = pl.ds(pl.multiple_of(col0 + width * c, 128), width)
        full = pl.ds(row0, ROW)
        mine = pl.ds(pl.multiple_of(row0 + (ROW // 2) * x, 16), ROW // 2)
        near, far, across = z + 1 - 2 * lax.rem(z, 2), lax.rem(z + 2, 4), 3 - z
        self.inner = jnp.logical_or(z == 1, z == 2)
        self.local = lambda: pltpu.make_async_copy(src.at[full, cols], dst.at[z, y, full, cols], lo.at[k])

        def send(block, n, target, sem):
            from_ref = src.at[full, cols] if block is None else dst.at[block, y, full, cols]
            b = z if block is None else block
            return remote(from_ref, dst.at[b, y, full, cols], sem, zr.at[k + (n,)], at(target, y, x, c))

        self.a = lambda: send(None, 0, near, zs.at[k + (0,)])
        self.b = lambda: send(None, 1, far, zs.at[k + (1,)])
        self.d = lambda: send(None, 2, across, zs.at[k + (2,)])
        self.fwd = lambda: send(far, 2, near, fs.at[k])
        yv = lambda: dst.at[:, y, mine, cols]
        self.ycopy = lambda: remote(yv(), yv(), ys.at[k], yr.at[k], at(z, 1 - y, x, c))
        xv = lambda: dst.at[:, 1 - y, mine, cols]
        self.xcopy = lambda: remote(xv(), xv(), xs.at[k], xr.at[k], at(z, y, 1 - x, c))
        cv = lambda: dst.at[:, :, full, cols]
        self.ccopy = lambda: remote(cv(), cv(), cs.at[k], cr.at[k], at(z, y, x, 1 - c))

    def along_z(self):
        self.local().start()
        self.b().start()
        self.a().start()

        @pl.when(self.inner)
        def _():
            self.d().start()

    def forward(self):
        self.b().wait_recv()

        @pl.when(self.inner)
        def _():
            self.fwd().start()

    def along_y(self):
        self.a().wait_recv()
        self.d().wait_recv()
        self.local().wait()
        self.ycopy().start()

    def along_x(self):
        self.ycopy().wait_recv()
        self.xcopy().start()

    def to_core(self):
        self.xcopy().wait_recv()
        self.ccopy().start()

    def arrive(self):
        self.ccopy().wait_recv()

    def drain(self):
        self.a().wait_send()
        self.b().wait_send()

        @pl.when(self.inner)
        def _():
            self.d().wait_send()
            self.fwd().wait_send()

        self.ycopy().wait_send()
        self.xcopy().wait_send()
        self.ccopy().wait_send()


def spread_sems(*lead):
    dma = pltpu.SemaphoreType.DMA
    return [dma(lead + (3,)), dma(lead + (3,))] + [dma(lead)] * 8


GROUPS = 3
GCOLS = 256
REST = 9


def fwd_body(
    thr, x_in, cot, wq, wk, wv, wo, wi, w2, *refs,
):
    smalls = refs[:9]
    (gq, gk, gv, go, gi, g2, xall, cown, q_o, k_o, v_o, c_o, p_o, vec, b_in) = refs[9:24]
    bias, pbuf, vpk, gvec = refs[24:28]
    qs, rs = refs[28:38], refs[38:48]
    asend, arecv, aloc, vs, vr, ps = refs[48:]
    z, y, x, c = where = place()
    f = 2 * z + y
    pages, rows = xall.shape[0], xall.shape[1]
    own, blk = rows // 2, rows // 4
    width = smalls[0].shape[-1]
    for i in range(8):
        vpk[i : i + 1, :width] = smalls[i][...].astype(F32).reshape(1, width)
    for i in range(3):
        vpk[8 + i : 9 + i, :] = smalls[8][:, 128 * i : 128 * (i + 1)].astype(F32).reshape(1, 128)
    gvec[f] = vpk[...]
    x_peer, c_peer = at(z, y, 1 - x, c), at(z, y, x, 1 - c)
    meet([{"fsdp": lax.rem(f + k + 1, 8)} for k in range(7)] + [x_peer, c_peer])

    groups = [
        [Spread(where, src, dst, 0, GCOLS * g, GCOLS // 2, qs, (g, w)) for w, (src, dst) in enumerate(((wq, gq), (wk, gk), (wv, gv)))]
        for g in range(GROUPS)
    ]

    def each(g, step):
        for part in groups[g]:
            getattr(part, step)()

    mine, sent = pl.ds(pages * x, pages), pl.ds(pages * (1 - x), pages)

    def band(b):
        return xall.at[:, pl.ds(blk * b, blk), :]

    to_b = remote(x_in.at[sent], band(1), asend.at[0], arecv.at[0], x_peer)
    to_c = remote(x_in.at[mine], band(2), asend.at[1], arecv.at[1], c_peer)
    to_d = remote(band(1), band(3), asend.at[2], arecv.at[2], c_peer)
    cot_b = remote(cot.at[sent], cown.at[:, pl.ds(blk, blk), :], asend.at[3], arecv.at[3], x_peer)
    keep_x = pltpu.make_async_copy(x_in.at[mine], band(0), aloc.at[0])
    keep_c = pltpu.make_async_copy(cot.at[mine], cown.at[:, pl.ds(0, blk), :], aloc.at[1])
    vecs = [
        remote(vpk, gvec.at[f], vs.at[k], vr.at[k], {"fsdp": lax.rem(f + k + 1, 8)}) for k in range(7)
    ]
    each(0, "along_z")
    to_b.start()
    keep_x.start()
    to_c.start()
    for copy in vecs:
        copy.start()
    each(1, "along_z")
    place_row = lax.broadcasted_iota(jnp.int32, (blk, own), 0)
    for page in range(pages):
        for b in range(4):
            bias[page, b * blk : (b + 1) * blk, :] = jnp.where(place_row < thr[page, b], 0.0, NEG)
    each(0, "forward")
    each(0, "along_y")
    each(2, "along_z")
    each(1, "forward")
    each(1, "along_y")
    each(0, "along_x")
    each(2, "forward")
    each(2, "along_y")
    to_b.wait_recv()
    to_d.start()
    each(1, "along_x")
    for copy in vecs:
        copy.wait_recv()
    for i in range(8):
        vec[i : i + 1, :] = jnp.concatenate([gvec[j, i : i + 1, :width] for j in range(8)], axis=1)
    for j in range(8):
        for i in range(3):
            b_in[:, (3 * j + i) * 128 : (3 * j + i + 1) * 128] = gvec[j, 8 + i : 9 + i, :]
    each(0, "to_core")
    keep_c.start()
    keep_x.wait()
    to_c.wait_recv()
    to_d.wait_recv()
    each(0, "arrive")

    def rest(p, step):
        def run(src, dst, row0, col0):
            getattr(Spread(where, src, dst, row0, col0, 384, rs, (p,)), step)()

        @pl.when(p == 0)
        def _():
            run(wo, go, 0, 0)

        @pl.when(jnp.logical_and(p >= 1, p < 5))
        def _():
            run(wi, gi, 0, 768 * (p - 1))

        @pl.when(jnp.logical_and(p >= 5, p < REST))
        def _():
            run(w2, g2, ROW * (p - 5), 0)

    low_lane = lax.broadcasted_iota(jnp.int32, (own, PAIR), 1) < HEAD_DIM
    lags = (("forward", 2), ("along_y", 3), ("along_x", 6), ("to_core", 9))

    def tick(t):
        @pl.when(t < REST)
        def _():
            rest(t, "along_z")

        for step, lag in lags:
            rest(t - lag, step)

    def p_copy(page, pair, slot):
        return pltpu.make_async_copy(pbuf.at[slot], p_o.at[page, pl.ds(2 * pair, 2)], ps.at[slot])

    def unit(it, carry):
        g, page = lax.div(it, pages), lax.rem(it, pages)

        @pl.when(it == 0)
        def _():
            each(2, "along_x")
            each(1, "to_core")

        @pl.when(it == 1)
        def _():
            each(2, "to_core")
            cot_b.start()

        @pl.when(it == pages)
        def _():
            each(1, "arrive")

        @pl.when(it == 2 * pages)
        def _():
            each(2, "arrive")

        gcols = pl.ds(pl.multiple_of(g * GCOLS, GCOLS), GCOLS)
        x_all = xall[page]
        d = x_all.shape[1]
        query = (dot(x_all[:own], gq[:, :, :, gcols].reshape(d, GCOLS)) + vec[0:1, gcols]).astype(BF)
        keys = dot(x_all, gk[:, :, :, gcols].reshape(d, GCOLS)).astype(BF)
        vals = (dot(x_all, gv[:, :, :, gcols].reshape(d, GCOLS)) + vec[1:2, gcols]).astype(BF)
        q_o[page, :, gcols] = query
        k_o[page, :, gcols] = keys
        v_o[page, :, gcols] = vals
        for half in range(2):
            lanes = slice(half * PAIR, (half + 1) * PAIR)
            pair = 2 * g + half

            @pl.when(it > 0)
            def _():
                p_copy(page, pair, half).wait()

            qp = query[:, lanes] * jnp.array(1.0 / math.sqrt(HEAD_DIM), BF)
            kp = keys[:, lanes]
            vt = vals[:, lanes].T
            outs = []
            for h in range(2):
                keep = low_lane if h == 0 else jnp.logical_not(low_lane)
                qh = jnp.where(keep, qp, jnp.zeros_like(qp))
                st = dot(kp, qh, NT) + bias[page]
                top = jnp.max(st, axis=0, keepdims=True)
                ex = jnp.exp(st - top)
                tot = jnp.sum(ex, axis=0, keepdims=True)
                pt = (ex * (1.0 / tot)).astype(BF)
                pbuf[half, h] = pt
                outs.append(dot(vt[h * HEAD_DIM : (h + 1) * HEAD_DIM], pt))
            p_copy(page, pair, half).start()
            cols = pl.ds(pl.multiple_of(pair * PAIR, PAIR), PAIR)
            c_o[page, :, cols] = jnp.concatenate(outs, axis=0).T.astype(BF)
            tick(2 * it + half)
        return carry

    lax.fori_loop(0, GROUPS * pages, unit, 0)
    n_ticks = 2 * GROUPS * pages
    lax.fori_loop(n_ticks, REST + lags[-1][1], lambda t, carry: (tick(t), carry)[1], 0)
    for half in range(2):
        p_copy(0, 0, half).wait()

    def finish(p, carry):
        rest(p, "arrive")
        rest(p, "drain")
        return carry

    lax.fori_loop(0, REST, finish, 0)
    for g in range(GROUPS):
        each(g, "drain")
    cot_b.wait_recv()
    for copy in vecs + [to_b, to_c, to_d, cot_b]:
        copy.wait_send()
    keep_c.wait()


def fwd(thr, x_in, cot, ws, smalls):
    pages_all, blk, d = x_in.shape
    pages, own, rows = pages_all // 2, 2 * blk, 4 * blk
    dma = pltpu.SemaphoreType.DMA
    sds = jax.ShapeDtypeStruct
    shapes = [(4, 2) + w.shape for w in ws]
    ff = ws[4].shape[1]
    res = call(
        fwd_body,
        (pages * 2 * d * d * (own + 2 * rows), sum(16 * w.size for w in ws), pages * HEADS * own * rows),
        in_specs=[pl.BlockSpec(memory_space=pltpu.SMEM)] + [ANY] * 8 + [VM] * 9,
        out_specs=[VM] * 3 + [ANY] * 3 + [VM, ANY, VM, VM, VM, VM, ANY, VM, VM],
        out_shape=[sds(s, BF) for s in shapes]
        + [
            sds((pages, rows, d), BF), sds((pages, own, d), BF),
            sds((pages, own, d), BF), sds((pages, rows, d), BF), sds((pages, rows, d), BF),
            sds((pages, own, d), BF), sds((pages, HEADS, rows, own), BF),
            sds((8, d), F32), sds((1, ff), F32),
        ],
        scratch_shapes=[
            pltpu.VMEM((pages, rows, own), F32),
            pltpu.VMEM((2, 2, rows, own), BF),
            pltpu.VMEM((16, 128), F32),
            pltpu.VMEM((8, 16, 128), F32),
        ]
        + spread_sems(GROUPS, 3)
        + spread_sems(REST)
        + [dma((4,)), dma((4,)), dma((2,)), dma((7,)), dma((7,)), dma((2,))],
        params=dict(collective_id=0, has_side_effects=True),
        name="gather_attention",
    )(thr, x_in, cot, *ws, *smalls)
    full = [r.reshape(-1, r.shape[-1]) for r in res[:6]]
    return full, res[6:]


def neighbours(z, y, x, c):
    n_z = 4
    zs = [at(lax.rem(z + k, n_z), y, x, c) for k in range(1, n_z)]
    far = [at(lax.rem(z + k, n_z), 1 - y, x, c) for k in range(n_z)]
    return zs + far + [at(z, y, 1 - x, c), at(z, y, x, 1 - c)]


def piece_views(wq, wk, wv, wo, wi, w2, lead):
    views = []

    def add(ref, row0, col0):
        def view(sel, rows, cols):
            r0, nr = rows
            c0, nc = cols
            r = pl.ds(row0 + r0, nr)
            c = pl.ds(col0 + c0, nc)
            return ref.at[sel + (r, c)] if lead else ref.at[r, c]

        views.append(view)

    for ref in (wq, wk, wv, wo):
        add(ref, 0, 0)
    for j in range(4):
        add(wi, 0, 768 * j)
    for j in range(4):
        add(w2, ROW * j, 0)
    return views


ALL = slice(None)


def rstart(*a):
    return begin(remote(*a))


def scatter_body(
    gq, gk, gv, go, gi, g2, res, gx_a, gx_b, gvec,
    oq, ok, ov, oo, oi, o2, fin_out, gx, ovec,
    acc, rc, rx, ry, rz, fin, rf, rgx, vecin, vtot, vx,
    lsem, cs, cr, xs, xr, ys, yr, zs, zr, fs, fr, es, er, asend, arecv, aloc, vs, vr, us, ur,
):
    z, y, x, c = place()
    f = 2 * z + y
    meet(neighbours(z, y, x, c) + [at(z, y, 1 - x, 1 - c)])
    x_peer, c_peer, y_peer = at(z, y, 1 - x, c), at(z, y, x, 1 - c), at(z, 1 - y, x, c)
    own_pages = pl.ds(3 * x, 3)
    other_pages = pl.ds(3 * (1 - x), 3)
    src = piece_views(gq, gk, gv, go, gi, g2, True)
    dst = piece_views(oq, ok, ov, oo, oi, o2, False)
    n = len(src)
    hr = ROW // 2
    half_cols = (pl.multiple_of(c * 384, 128), 384)
    their_cols = (pl.multiple_of((1 - c) * 384, 128), 384)
    full = (0, ROW)
    mine = pl.ds(pl.multiple_of(x * hr, 16), hr)
    theirs = pl.ds(pl.multiple_of((1 - x) * hr, 16), hr)
    wide = [p % 2 == 0 for p in range(n)]

    back_x = rstart(gx_b, rgx, asend.at[0], arecv.at[0], x_peer)
    vecs = []
    for k in range(7):
        to = lax.rem(f + k + 1, 8)
        vecs.append(rstart(gvec.at[to], vecin.at[k], vs.at[k], vr.at[k], {"fsdp": to}))
    keep_out = pltpu.make_async_copy(res.at[:, pl.ds(0, 128), :], fin_out.at[own_pages], aloc.at[0])
    keep_out.start()
    mine_first = []
    to_core = []
    for p in range(n):
        copy = pltpu.make_async_copy(src[p]((ALL, ALL), full, half_cols), acc.at[p], lsem.at[p])
        copy.start()
        mine_first.append(copy)
        to_core.append(
            rstart(src[p]((ALL, ALL), full, their_cols), rc.at[p], cs.at[p], cr.at[p], c_peer)
        )
    back_out = rstart(res.at[:, pl.ds(128, 128), :], fin_out.at[own_pages], asend.at[1], arecv.at[1], x_peer)

    gx[own_pages] = gx_a[...]
    along_x, along_y, along_z, finals, ends = [], [], [], [], []
    vec_x = []
    for t in range(n + 5):
        p = t
        if p < n:
            mine_first[p].wait()
            to_core[p].wait_recv()
            acc[p] = (acc[p].astype(F32) + rc[p].astype(F32)).astype(BF)
            if wide[p]:
                along_x.append(
                    rstart(acc.at[p, :, 1 - y, theirs, :], rx.at[p, :, 0], xs.at[p], xr.at[p], x_peer)
                )
            else:
                along_x.append(
                    rstart(acc.at[p, :, :, theirs, :], rx.at[p], xs.at[p], xr.at[p], x_peer)
                )
        p = t - 1
        if 0 <= p < n:
            along_x[p].wait_recv()
            if wide[p]:
                acc[p, :, 1 - y, mine, :] = (
                    acc[p, :, 1 - y, mine, :].astype(F32) + rx[p, :, 0].astype(F32)
                ).astype(BF)
            else:
                acc[p, :, :, mine, :] = (
                    acc[p, :, :, mine, :].astype(F32) + rx[p].astype(F32)
                ).astype(BF)
            along_y.append(
                rstart(acc.at[p, :, 1 - y, mine, :], ry.at[p], ys.at[p], yr.at[p], y_peer)
            )
        p = t - 2
        if 0 <= p < n:
            along_y[p].wait_recv()
            acc[p, :, y, mine, :] = (
                acc[p, :, y, mine, :].astype(F32) + ry[p].astype(F32)
            ).astype(BF)
            group = []
            for k in range(3):
                to = lax.rem(z + k + 1, 4)
                if wide[p]:
                    a, b = acc.at[p, to, y], rz.at[p, k]
                else:
                    a, b = acc.at[p, to, y, mine, :], rz.at[p, k, pl.ds(0, hr)]
                group.append(rstart(a, b, zs.at[p, k], zr.at[p, k], at(to, y, x, c)))
            along_z.append(group)
        p = t - 3
        if 0 <= p < n:
            for copy in along_z[p]:
                copy.wait_recv()
            if wide[p]:
                total = acc[p, z, y].astype(F32)
                for k in range(3):
                    total = total + rz[p, k].astype(F32)
                fin[p] = total.astype(BF)
                finals.append(rstart(fin.at[p], rf.at[p], fs.at[p], fr.at[p], x_peer))
            else:
                total = acc[p, z, y, mine, :].astype(F32)
                for k in range(3):
                    total = total + rz[p, k, :hr].astype(F32)
                fin[p, :hr] = total.astype(BF)
                finals.append(
                    rstart(fin.at[p, pl.ds(0, hr)], rf.at[p, pl.ds(0, hr)], fs.at[p], fr.at[p], x_peer)
                )
        p = t - 4
        if 0 <= p < n:
            finals[p].wait_recv()
            if wide[p]:
                dst[p]((), full, half_cols)[...] = fin[p].astype(F32) + rf[p].astype(F32)
            else:
                dst[p]((), (pl.multiple_of(x * hr, 16), hr), half_cols)[...] = fin[p, :hr].astype(F32)
                dst[p]((), (pl.multiple_of((1 - x) * hr, 16), hr), half_cols)[...] = rf[p, :hr].astype(F32)
            view = dst[p]((), full, half_cols)
            ends.append(rstart(view, view, es.at[p], er.at[p], c_peer))
        if t == 1:
            total = gvec[f]
            for copy in vecs:
                copy.wait_recv()
            for k in range(7):
                total = total + vecin[k]
            vtot[...] = total
            vec_x = [
                rstart(vtot, vx.at[0], us.at[0], ur.at[0], x_peer),
            ]
        if t == 3:
            vec_x[0].wait_recv()
            vx[1] = vtot[...] + vx[0]
            vec_x.append(rstart(vx.at[1], vx.at[2], us.at[1], ur.at[1], c_peer))
        if t == 5:
            back_x.wait_recv()
            gx[other_pages] = rgx[...].astype(F32)
    vec_x[1].wait_recv()
    ovec[...] = vx[1] + vx[2]
    for copy in ends:
        copy.wait_recv()
    back_out.wait_recv()
    keep_out.wait()
    for group in along_z:
        for copy in group:
            copy.wait_send()
    for copy in to_core + along_x + along_y + finals + ends + vecs + vec_x + [back_x, back_out]:
        copy.wait_send()


def scatter_all(grads, out, gx_a, gx_b, gvec, shards):
    dma = pltpu.SemaphoreType.DMA
    n = 12
    pages, own, d = out.shape
    blk = own // 2
    views = [g.reshape((4, 2) + shape) for g, shape in zip(grads, shards)]
    vmem = pltpu.VMEM
    res = call(
        scatter_body,
        (0, sum(16 * g.size for g in grads), 0),
        in_specs=[ANY] * 6 + [ANY, VM, ANY, VM],
        out_specs=[VM] * 6 + [ANY, VM, VM],
        out_shape=[jax.ShapeDtypeStruct(shape, F32) for shape in shards]
        + [
            jax.ShapeDtypeStruct((2 * pages, blk, d), BF),
            jax.ShapeDtypeStruct((2 * pages, blk, d), F32),
            jax.ShapeDtypeStruct(gvec.shape[1:], F32),
        ],
        scratch_shapes=[
            vmem((n, 4, 2, ROW, 384), BF),
            vmem((n, 4, 2, ROW, 384), BF),
            vmem((n, 4, 2, ROW // 2, 384), BF),
            vmem((n, 4, ROW // 2, 384), BF),
            vmem((n, 3, ROW, 384), BF),
            vmem((n, ROW, 384), BF),
            vmem((n, ROW, 384), BF),
            vmem((pages, blk, d), BF),
            vmem((7,) + gvec.shape[1:], F32),
            vmem(gvec.shape[1:], F32),
            vmem((3,) + gvec.shape[1:], F32),
            dma((n,)), dma((n,)), dma((n,)), dma((n,)), dma((n,)), dma((n,)), dma((n,)),
            dma((n, 3)), dma((n, 3)), dma((n,)), dma((n,)), dma((n,)), dma((n,)),
            dma((2,)), dma((2,)), dma((1,)), dma((7,)), dma((7,)), dma((2,)), dma((2,)),
        ],
        params=dict(collective_id=1, has_side_effects=True),
        name="scatter_all",
    )(*views, out, gx_a, gx_b, gvec)
    return res[:6], res[6], res[7], res[8]


SWAP_X = [(0, 2), (2, 0), (1, 3), (3, 1)]
SWAP_C = [(0, 1), (1, 0), (2, 3), (3, 2)]


def swap(value, pairs):
    return lax.ppermute(value, "seq", pairs)


def per_device(
    fsdp, inputs, lengths, w_query, b_query, w_key, w_value, b_value, w_out, b_out,
    gain_one, shift_one, w_inner, b_inner, w_outer, b_outer, gain_two, shift_two, cotangent,
):
    pages_all, blk, d = inputs.shape
    pages = pages_all // 2
    s = lax.axis_index("seq")
    x_at = lax.div(s, 2)
    direct = fsdp == 8
    ws = (w_query, w_key, w_value, w_out, w_inner, w_outer)
    shards = [w.shape for w in ws]
    width = b_query.shape[0]
    names = (b_query, b_value, b_out, gain_one, shift_one, b_outer, gain_two, shift_two)

    def pages_of(array, side):
        return lax.dynamic_slice_in_dim(array, side * pages, pages, 0)

    order = jnp.stack([s, s ^ 2, s ^ 1, s ^ 3]).astype(jnp.int32)
    thr = pages_of(lengths, x_at).astype(jnp.int32)[:, None] - order[None, :] * blk
    if direct:
        lanes = tuple(v.reshape(1, -1) for v in names + (b_inner,))
        full, rest = fwd(thr, inputs, cotangent, ws, lanes)
        wq, wk, wv, wo, wi, w2 = full
        xall, cown, q, k, v, ctx, p, vec_full, bin_full = rest
    else:
        wq, wk, wv, wo, wi, w2 = [lax.all_gather(w, "fsdp", axis=0, tiled=True) for w in ws]
        vec = jnp.concatenate(names + (b_inner,)).reshape(12, width)
        gvec = lax.all_gather(vec, "fsdp", axis=0)
        vec_full = jnp.swapaxes(gvec[:, :8], 0, 1).reshape(8, d).astype(F32)
        bin_full = gvec[:, 8:].reshape(1, -1).astype(F32)

        def own_rows(array):
            other = swap(pages_of(array, 1 - x_at), SWAP_X)
            return jnp.concatenate([pages_of(array, x_at), other], axis=1)

        xown, cown = own_rows(inputs), own_rows(cotangent)
        xall = jnp.concatenate([xown, swap(xown, SWAP_C)], axis=1)
        q, k, v, p, ctx = attn_fwd(thr, xall, wq, wk, wv, vec_full)
    out, gm1, dctx, dwo, dwi, dw2, gv_ffn, gbin = ffn(ctx, xall, cown, wo, wi, w2, vec_full, bin_full)
    dq, dk, dk_send, dv, dv_send = attn_bwd(q, k, v, p, ctx, dctx)
    dkr, dvr = swap(dk_send, SWAP_C), swap(dv_send, SWAP_C)
    gx_a, gx_b, dwq, dwk, dwv, gv_proj = proj(xall, dq, dk, dkr, dv, dvr, gm1, wq, wk, wv)

    gv = jnp.concatenate([gv_proj[:2], gv_ffn[2:]], axis=0)
    grads = (dwq, dwk, dwv, dwo, dwi, dw2)
    by_owner = jnp.concatenate(
        [jnp.swapaxes(gv.reshape(8, fsdp, width), 0, 1), gbin.reshape(fsdp, 4, width)], axis=1
    )
    if direct:
        padded = jnp.pad(by_owner, ((0, 0), (0, 4), (0, 128 - width)))
        tot, output, grad_inputs, tvec = scatter_all(grads, out, gx_a, gx_b, padded, shards)
        tvec = tvec[:12, :width]
    else:
        tot = [
            lax.psum(lax.psum_scatter(g, "fsdp", scatter_dimension=0, tiled=True), "seq").astype(F32)
            for g in grads
        ]
        tvec = lax.psum(lax.psum_scatter(by_owner, "fsdp", scatter_dimension=0, tiled=True)[0], "seq")

        def joined(mine, other):
            here = lax.dynamic_update_slice_in_dim(
                jnp.zeros((pages_all, blk, d), mine.dtype), mine, x_at * pages, 0
            )
            return lax.dynamic_update_slice_in_dim(here, other, (1 - x_at) * pages, 0)

        output = joined(out[:, :blk], swap(out[:, blk:], SWAP_X))
        grad_inputs = joined(gx_a, swap(gx_b, SWAP_X).astype(F32))
    small = [tvec[i] for i in range(8)]
    g_bq, g_bv, g_bo, g_g1, g_s1, g_bo2, g_g2, g_s2 = small
    g_bi = tvec[8:].reshape(-1)
    t_q, t_k, t_v, t_o, t_i, t_2 = tot
    return (
        output, grad_inputs, t_q, g_bq, t_k, t_v, g_bv, t_o, g_bo, g_g1, g_s1,
        t_i, g_bi, t_2, g_bo2, g_g2, g_s2,
    )


def solution(mesh):
    vec, mat, act = P("fsdp"), P("fsdp", None), P("fsdp", "seq", None)
    return jax.shard_map(
        functools.partial(per_device, mesh.shape["fsdp"]),
        mesh=mesh,
        in_specs=(act, vec, mat, vec, mat, mat, vec, mat, vec, vec, vec, mat, vec, mat, vec, vec, vec, act),
        out_specs=(act, act, mat, vec, mat, mat, vec, mat, vec, vec, vec, mat, vec, mat, vec, vec, vec),
        check_vma=False,
    )
```

```python
import functools
import math

import jax
import jax.numpy as jnp
from jax import lax
from jax.experimental import pallas as pl
from jax.experimental.pallas import tpu as pltpu
from jax.sharding import PartitionSpec as P

HEADS = 12
HEAD_DIM = 64
PAIR = 2 * HEAD_DIM
NEG = -1e30
EPS = 1e-12
BF = jnp.bfloat16
F32 = jnp.float32
MESH = pl.DeviceIdType.MESH
ANY = pl.BlockSpec(memory_space=pl.ANY)
VM = pl.BlockSpec(memory_space=pltpu.VMEM)
CHUNK = 1024
ROW = 96
VMEM_CAP = 60 << 20

NN = (((1,), (0,)), ((), ()))
NT = (((1,), (1,)), ((), ()))
TN = (((0,), (0,)), ((), ()))


def dot(a, b, dims=NN):
    return lax.dot_general(a, b, dims, preferred_element_type=F32)


def call(body, cost, **kw):
    flops, byts, trans = cost
    params = dict(vmem_limit_bytes=VMEM_CAP)
    params.update(kw.pop("params", {}))
    return pl.pallas_call(
        body,
        compiler_params=pltpu.CompilerParams(**params),
        cost_estimate=pl.CostEstimate(
            flops=int(flops), bytes_accessed=int(byts), transcendentals=int(trans)
        ),
        **kw,
    )


def attn_fwd_body(thr, xall, wq, wk, wv, vec, q_o, k_o, v_o, p_o, c_o, bias):
    page = pl.program_id(0)
    x_all = xall[0]
    own = x_all.shape[0] // 2
    query = (dot(x_all[:own], wq[...]) + vec[0:1, :]).astype(BF)
    q_o[0] = query
    k_o[0] = dot(x_all, wk[...]).astype(BF)
    v_o[0] = (dot(x_all, wv[...]) + vec[1:2, :]).astype(BF)
    blk = x_all.shape[0] // 4
    place = lax.broadcasted_iota(jnp.int32, (blk, own), 0)
    for b in range(4):
        bias[b * blk : (b + 1) * blk, :] = jnp.where(place < thr[page, b], 0.0, NEG)
    low_lane = lax.broadcasted_iota(jnp.int32, (own, PAIR), 1) < HEAD_DIM

    def pair(i, carry):
        cols = pl.ds(pl.multiple_of(i * PAIR, PAIR), PAIR)
        qp = q_o[0, :, cols] * jnp.array(1.0 / math.sqrt(HEAD_DIM), BF)
        kp = k_o[0, :, cols]
        vt = v_o[0, :, cols].T
        outs = []
        for h in range(2):
            keep = low_lane if h == 0 else jnp.logical_not(low_lane)
            qh = jnp.where(keep, qp, jnp.zeros_like(qp))
            st = dot(kp, qh, NT) + bias[...]
            top = jnp.max(st, axis=0, keepdims=True)
            ex = jnp.exp(st - top)
            tot = jnp.sum(ex, axis=0, keepdims=True)
            pt = (ex * (1.0 / tot)).astype(BF)
            p_o[0, 2 * i + h] = pt
            outs.append(dot(vt[h * HEAD_DIM : (h + 1) * HEAD_DIM], pt))
        c_o[0, :, cols] = jnp.concatenate(outs, axis=0).T.astype(BF)
        return carry

    lax.fori_loop(0, HEADS // 2, pair, 0)


def attn_fwd(thr, xall, wq, wk, wv, vec):
    pages, rows, d = xall.shape
    own = rows // 2
    const = lambda p, t: (0, 0)
    by_page = lambda p, t: (p, 0, 0)
    one = pl.Buffered(1)
    return call(
        attn_fwd_body,
        (
            pages * (2 * d * d * (own + 2 * rows) + 4 * own * rows * d),
            pages * rows * d * 2 * 4 + 6 * d * d + pages * HEADS * own * rows * 2,
            pages * HEADS * own * rows,
        ),
        grid_spec=pltpu.PrefetchScalarGridSpec(
            num_scalar_prefetch=1,
            grid=(pages,),
            in_specs=[pl.BlockSpec((1, rows, d), by_page)]
            + [pl.BlockSpec((d, d), const, pipeline_mode=one)] * 3
            + [pl.BlockSpec((8, d), const)],
            out_specs=[
                pl.BlockSpec((1, own, d), by_page),
                pl.BlockSpec((1, rows, d), by_page),
                pl.BlockSpec((1, rows, d), by_page),
                pl.BlockSpec((1, HEADS, rows, own), lambda p, t: (p, 0, 0, 0)),
                pl.BlockSpec((1, own, d), by_page),
            ],
            scratch_shapes=[pltpu.VMEM((rows, own), F32)],
        ),
        out_shape=[
            jax.ShapeDtypeStruct((pages, own, d), BF),
            jax.ShapeDtypeStruct((pages, rows, d), BF),
            jax.ShapeDtypeStruct((pages, rows, d), BF),
            jax.ShapeDtypeStruct((pages, HEADS, rows, own), BF),
            jax.ShapeDtypeStruct((pages, own, d), BF),
        ],
        name="attn_fwd",
    )(thr, xall, wq, wk, wv, vec)


def attn_bwd_body(q, k, v, p, ctx, dctx, dq_o, dk_own, dk_oth, dv_own, dv_oth):
    own = q.shape[1]
    low_lane = lax.broadcasted_iota(jnp.int32, (own, PAIR), 1) < HEAD_DIM
    scale = 1.0 / math.sqrt(HEAD_DIM)

    def pair(i, carry):
        cols = pl.ds(pl.multiple_of(i * PAIR, PAIR), PAIR)
        qp = q[0, :, cols] * jnp.array(scale, BF)
        kp = k[0, :, cols]
        kt = kp.T
        vp = v[0, :, cols]
        dc = dctx[0, :, cols]
        prod = (dc.astype(F32) * ctx[0, :, cols].astype(F32)).T
        dk = None
        dv = None
        dqs = []
        for h in range(2):
            keep = low_lane if h == 0 else jnp.logical_not(low_lane)
            feats = slice(h * HEAD_DIM, (h + 1) * HEAD_DIM)
            dch = jnp.where(keep, dc, jnp.zeros_like(dc))
            qh = jnp.where(keep, qp, jnp.zeros_like(qp))
            pt = p[0, 2 * i + h]
            delta = jnp.sum(prod[feats], axis=0, keepdims=True)
            dpt = dot(vp, dch, NT)
            dst = (pt.astype(F32) * (dpt - delta)).astype(BF)
            dvh = dot(pt, dch)
            dkh = dot(dst, qh)
            dk = dkh if dk is None else dk + dkh
            dv = dvh if dv is None else dv + dvh
            dqs.append(dot(kt[feats], dst))
        dq_o[0, :, cols] = (jnp.concatenate(dqs, axis=0) * scale).T.astype(BF)
        dk_own[0, :, cols] = dk[:own].astype(BF)
        dk_oth[0, :, cols] = dk[own:].astype(BF)
        dv_own[0, :, cols] = dv[:own].astype(BF)
        dv_oth[0, :, cols] = dv[own:].astype(BF)
        return carry

    lax.fori_loop(0, HEADS // 2, pair, 0)


def attn_bwd(q, k, v, p, ctx, dctx):
    pages, own, d = q.shape
    rows = k.shape[1]
    by_page = lambda i: (i, 0, 0)
    o = pl.BlockSpec((1, own, d), by_page)
    r = pl.BlockSpec((1, rows, d), by_page)
    return call(
        attn_bwd_body,
        (pages * 10 * own * rows * d, pages * (own * rows * HEADS * 2 + 10 * own * d * 2), 0),
        grid=(pages,),
        in_specs=[o, r, r, pl.BlockSpec((1, HEADS, rows, own), lambda i: (i, 0, 0, 0)), o, o],
        out_specs=[o] * 5,
        out_shape=[jax.ShapeDtypeStruct((pages, own, d), BF)] * 5,
        name="attn_bwd",
    )(q, k, v, p, ctx, dctx)


def normal_parts(v):
    bell = jnp.exp(v * v * -0.5)
    t = 1.0 / (1.0 + jnp.abs(v) * (0.3275911 / math.sqrt(2.0)))
    tail = t * (
        0.127414796 + t * (-0.142248368 + t * (0.7107068705 + t * (-0.7265760135 + t * 0.5307027145)))
    )
    tail = tail * bell
    return jnp.where(v >= 0.0, 1.0 - tail, tail), bell * (1.0 / math.sqrt(2.0 * math.pi))


def row_norm(v):
    centered = v - jnp.mean(v, -1, keepdims=True)
    inv = lax.rsqrt(jnp.mean(centered * centered, -1, keepdims=True) + EPS)
    return centered * inv, inv


def norm_back(e, n, inv):
    return inv * (e - jnp.mean(e, -1, keepdims=True) - n * jnp.mean(e * n, -1, keepdims=True))


def ffn_body(
    ctx, xall, cown, wo, wi_h, w2_h, vec, b_in,
    out, gm1_o, dctx_o, dwo_o, dwi_h, dw2_h, gvec, gbin,
    wi, w2, act, din, dgel, hid, gout, gatt, n1s, h1s, accs, r1s, dwi, dw2, lsem, osem,
):
    n, ff = act.shape
    pages, own, d = ctx.shape

    def cols_of(j):
        return pl.ds(pl.multiple_of(j * CHUNK, CHUNK), CHUNK)

    def loads(j):
        cols = cols_of(j)
        return (
            pltpu.make_async_copy(wi_h.at[:, cols], wi.at[:, cols], lsem.at[0, j]),
            pltpu.make_async_copy(w2_h.at[cols, :], w2.at[cols, :], lsem.at[1, j]),
        )

    def store_w2(j):
        return pltpu.make_async_copy(dw2.at[cols_of(j), :], dw2_h.at[cols_of(j), :], osem.at[0, j])

    def store_wi(j):
        return pltpu.make_async_copy(dwi.at[:, cols_of(j)], dwi_h.at[:, cols_of(j)], osem.at[1, j])

    n_chunks = ff // CHUNK
    for j in range(n_chunks):
        for copy in loads(j):
            copy.start()
    gvec[...] = jnp.zeros_like(gvec)

    def add(row, value):
        gvec[row : row + 1, :] += jnp.sum(value, 0, keepdims=True)

    for p in range(pages):
        r = slice(p * own, (p + 1) * own)
        mid = xall[p].astype(F32) + (dot(ctx[p], wo[...]) + vec[2:3, :])
        n1, r1 = row_norm(mid)
        n1s[r, :] = n1
        r1s[r, :] = jnp.broadcast_to(r1, (own, 128))
        h1 = n1 * vec[3:4, :] + vec[4:5, :]
        h1s[r, :] = h1
        hid[r, :] = h1.astype(BF)
    accs[...] = jnp.zeros_like(accs)

    def up(j, carry):
        cols = cols_of(j)
        for copy in loads(j):
            copy.wait()
        pre = dot(hid[...], wi[:, cols]) + b_in[:, cols]
        big, bell = normal_parts(pre)
        a = (pre * big).astype(BF)
        dgel[:, cols] = (big + pre * bell).astype(BF)
        act[:, cols] = a
        accs[...] += dot(a, w2[cols, :])
        return carry

    lax.fori_loop(0, n_chunks, up, 0)
    for p in range(pages):
        r = slice(p * own, (p + 1) * own)
        mid = h1s[r, :] + (accs[r, :] + vec[5:6, :])
        n2, r2 = row_norm(mid)
        out[p] = (n2 * vec[6:7, :] + vec[7:8, :]).astype(BF)
        cot = cown[p].astype(F32)
        gm2 = norm_back(cot * vec[6:7, :], n2, r2)
        go = gm2.astype(BF)
        gout[r, :] = go
        accs[r, :] = gm2
        add(5, go.astype(F32))
        add(6, cot * n2)
        add(7, cot)

    def down(j, carry):
        cols = cols_of(j)
        di = (dot(gout[...], w2[cols, :], NT) * dgel[:, cols].astype(F32)).astype(BF)
        din[:, cols] = di
        accs[...] += dot(di, wi[:, cols], NT)
        gbin[:, cols] = jnp.sum(di.astype(F32), 0, keepdims=True)
        dw2[cols, :] = dot(act[:, cols], gout[...], TN).astype(BF)
        store_w2(j).start()
        return carry

    lax.fori_loop(0, n_chunks, down, 0)
    for p in range(pages):
        r = slice(p * own, (p + 1) * own)
        gh = accs[r, :]
        n1 = n1s[r, :]
        gm1 = norm_back(gh * vec[3:4, :], n1, r1s[r, 0:1])
        gm1_o[p] = gm1
        ga = gm1.astype(BF)
        gatt[r, :] = ga
        dctx_o[p] = dot(ga, wo[...], NT).astype(BF)
        add(2, ga.astype(F32))
        add(3, gh * n1)
        add(4, gh)
    hid_t = hid[...].T

    def grads(j, carry):
        cols = cols_of(j)
        dwi[:, cols] = dot(hid_t, din[:, cols]).astype(BF)
        store_wi(j).start()
        return carry

    lax.fori_loop(0, n_chunks, grads, 0)
    dwo_o[...] = dot(ctx[...].reshape(n, d), gatt[...], TN).astype(BF)
    for j in range(n_chunks):
        store_w2(j).wait()
        store_wi(j).wait()


def ffn(ctx, xall, cown, wo, wi, w2, vec, b_in):
    pages, own, d = ctx.shape
    ff = wi.shape[1]
    n = pages * own
    sds = jax.ShapeDtypeStruct
    vm = pltpu.VMEM
    dma = pltpu.SemaphoreType.DMA
    return call(
        ffn_body,
        (n * d * (12 * ff + 6 * d), 4 * d * ff * 2 + 12 * n * d * 2, n * ff),
        grid=(1,),
        in_specs=[
            pl.BlockSpec((pages, own, d), lambda i: (0, 0, 0)),
            pl.BlockSpec((pages, own, d), lambda i: (0, 0, 0)),
            VM, VM, ANY, ANY, VM, VM,
        ],
        out_specs=[VM] * 4 + [ANY, ANY, VM, VM],
        out_shape=[
            sds((pages, own, d), BF), sds((pages, own, d), F32), sds((pages, own, d), BF),
            sds((d, d), BF), sds((d, ff), BF), sds((ff, d), BF), sds((8, d), F32), sds((1, ff), F32),
        ],
        scratch_shapes=[
            vm((d, ff), BF), vm((ff, d), BF), vm((n, ff), BF), vm((n, ff), BF), vm((n, ff), BF),
            vm((n, d), BF), vm((n, d), BF), vm((n, d), BF), vm((n, d), F32), vm((n, d), F32),
            vm((n, d), F32), vm((n, 128), F32), vm((d, ff), BF), vm((ff, d), BF),
            dma((2, ff // CHUNK)), dma((2, ff // CHUNK)),
        ],
        params=dict(vmem_limit_bytes=63 << 20),
        name="ffn",
    )(ctx, xall, cown, wo, wi, w2, vec, b_in)


def proj_body(
    xall, dq, dk, dkr, dv, dvr, gm1, wq, wk, wv,
    ga_o, gb_o, dwq_o, dwk_o, dwv_o, gvec, x_all, dq_all, dk_all, dv_all,
):
    page = pl.program_id(0)
    own = xall.shape[1]
    blk = own // 2
    here = pl.ds(pl.multiple_of(page * own, own), own)
    x_all[here, :] = xall[0]
    dq_v = dq[0]
    dk_v = (dk[0].astype(F32) + dkr[0].astype(F32)).astype(BF)
    dv_v = (dv[0].astype(F32) + dvr[0].astype(F32)).astype(BF)
    dq_all[here, :] = dq_v
    dk_all[here, :] = dk_v
    dv_all[here, :] = dv_v
    gx = gm1[0] + dot(dq_v, wq[...], NT) + dot(dk_v, wk[...], NT) + dot(dv_v, wv[...], NT)
    ga_o[0] = gx[:blk]
    gb_o[0] = gx[blk:].astype(BF)

    @pl.when(page == 0)
    def _():
        gvec[...] = jnp.zeros_like(gvec)

    gvec[0:1, :] += jnp.sum(dq_v.astype(F32), 0, keepdims=True)
    gvec[1:2, :] += jnp.sum(dv_v.astype(F32), 0, keepdims=True)

    @pl.when(page == pl.num_programs(0) - 1)
    def _():
        x_t = x_all[...].T
        dwq_o[...] = dot(x_t, dq_all[...]).astype(BF)
        dwk_o[...] = dot(x_t, dk_all[...]).astype(BF)
        dwv_o[...] = dot(x_t, dv_all[...]).astype(BF)


def proj(xall, dq, dk, dkr, dv, dvr, gm1, wq, wk, wv):
    pages, own, d = dq.shape
    blk = own // 2
    n = pages * own
    by_page = lambda p: (p, 0, 0)
    const = lambda p: (0, 0)
    one = pl.Buffered(1)
    half = pl.BlockSpec((1, blk, d), by_page)
    whole = pl.BlockSpec((1, own, d), by_page)
    square = pl.BlockSpec((d, d), const, pipeline_mode=one)
    return call(
        proj_body,
        (12 * n * d * d, 12 * d * d + 16 * n * d, 0),
        grid=(pages,),
        in_specs=[whole] * 7 + [square] * 3,
        out_specs=[half, half] + [square] * 3 + [pl.BlockSpec((8, d), const)],
        out_shape=[
            jax.ShapeDtypeStruct((pages, blk, d), F32),
            jax.ShapeDtypeStruct((pages, blk, d), BF),
        ]
        + [jax.ShapeDtypeStruct((d, d), BF)] * 3
        + [jax.ShapeDtypeStruct((8, d), F32)],
        scratch_shapes=[pltpu.VMEM((n, d), BF)] * 4,
        name="proj_bwd",
    )(xall, dq, dk, dkr, dv, dvr, gm1, wq, wk, wv)


def place():
    f, s = lax.axis_index("fsdp"), lax.axis_index("seq")
    return lax.div(f, 2), lax.rem(f, 2), lax.div(s, 2), lax.rem(s, 2)


def at(z, y, x, c):
    return {"fsdp": 2 * z + y, "seq": 2 * x + c}


def meet(others):
    barrier = pltpu.get_barrier_semaphore()
    for other in others:
        pl.semaphore_signal(barrier, inc=1, device_id=other, device_id_type=MESH)
    pl.semaphore_wait(barrier, len(others))


def remote(src, dst, send, recv, other):
    return pltpu.make_async_remote_copy(
        src_ref=src, dst_ref=dst, send_sem=send, recv_sem=recv,
        device_id=other, device_id_type=MESH,
    )


def begin(copy):
    copy.start()
    return copy


class Spread:
    def __init__(self, where, src, dst, row0, col0, width, sems, key):
        self.z, self.y, self.x, self.c = where
        z, y, x, c = where
        zs, zr, fs, ys, yr, xs, xr, cs, cr, lo = sems
        k = key
        cols = pl.ds(pl.multiple_of(col0 + width * c, 128), width)
        full = pl.ds(row0, ROW)
        mine = pl.ds(pl.multiple_of(row0 + (ROW // 2) * x, 16), ROW // 2)
        near, far, across = z + 1 - 2 * lax.rem(z, 2), lax.rem(z + 2, 4), 3 - z
        self.inner = jnp.logical_or(z == 1, z == 2)
        self.local = lambda: pltpu.make_async_copy(src.at[full, cols], dst.at[z, y, full, cols], lo.at[k])

        def send(block, n, target, sem):
            from_ref = src.at[full, cols] if block is None else dst.at[block, y, full, cols]
            b = z if block is None else block
            return remote(from_ref, dst.at[b, y, full, cols], sem, zr.at[k + (n,)], at(target, y, x, c))

        self.a = lambda: send(None, 0, near, zs.at[k + (0,)])
        self.b = lambda: send(None, 1, far, zs.at[k + (1,)])
        self.d = lambda: send(None, 2, across, zs.at[k + (2,)])
        self.fwd = lambda: send(far, 2, near, fs.at[k])
        yv = lambda: dst.at[:, y, mine, cols]
        self.ycopy = lambda: remote(yv(), yv(), ys.at[k], yr.at[k], at(z, 1 - y, x, c))
        xv = lambda: dst.at[:, 1 - y, mine, cols]
        self.xcopy = lambda: remote(xv(), xv(), xs.at[k], xr.at[k], at(z, y, 1 - x, c))
        cv = lambda: dst.at[:, :, full, cols]
        self.ccopy = lambda: remote(cv(), cv(), cs.at[k], cr.at[k], at(z, y, x, 1 - c))

    def along_z(self):
        self.local().start()
        self.b().start()
        self.a().start()

        @pl.when(self.inner)
        def _():
            self.d().start()

    def forward(self):
        self.b().wait_recv()

        @pl.when(self.inner)
        def _():
            self.fwd().start()

    def along_y(self):
        self.a().wait_recv()
        self.d().wait_recv()
        self.local().wait()
        self.ycopy().start()

    def along_x(self):
        self.ycopy().wait_recv()
        self.xcopy().start()

    def to_core(self):
        self.xcopy().wait_recv()
        self.ccopy().start()

    def arrive(self):
        self.ccopy().wait_recv()

    def drain(self):
        self.a().wait_send()
        self.b().wait_send()

        @pl.when(self.inner)
        def _():
            self.d().wait_send()
            self.fwd().wait_send()

        self.ycopy().wait_send()
        self.xcopy().wait_send()
        self.ccopy().wait_send()


def spread_sems(*lead):
    dma = pltpu.SemaphoreType.DMA
    return [dma(lead + (3,)), dma(lead + (3,))] + [dma(lead)] * 8


GROUPS = 3
GCOLS = 256
REST = 9


def fwd_body(
    thr, x_in, cot, wq, wk, wv, wo, wi, w2, *refs,
):
    smalls = refs[:9]
    (gq, gk, gv, go, gi, g2, xall, cown, q_o, k_o, v_o, c_o, p_o, vec, b_in) = refs[9:24]
    bias, pbuf, vpk, gvec = refs[24:28]
    qs, rs = refs[28:38], refs[38:48]
    asend, arecv, aloc, vs, vr, ps = refs[48:]
    z, y, x, c = where = place()
    f = 2 * z + y
    pages, rows = xall.shape[0], xall.shape[1]
    own, blk = rows // 2, rows // 4
    width = smalls[0].shape[-1]
    for i in range(8):
        vpk[i : i + 1, :width] = smalls[i][...].astype(F32).reshape(1, width)
    for i in range(3):
        vpk[8 + i : 9 + i, :] = smalls[8][:, 128 * i : 128 * (i + 1)].astype(F32).reshape(1, 128)
    gvec[f] = vpk[...]
    x_peer, c_peer = at(z, y, 1 - x, c), at(z, y, x, 1 - c)
    meet([{"fsdp": lax.rem(f + k + 1, 8)} for k in range(7)] + [x_peer, c_peer])

    groups = [
        [Spread(where, src, dst, 0, GCOLS * g, GCOLS // 2, qs, (g, w)) for w, (src, dst) in enumerate(((wq, gq), (wk, gk), (wv, gv)))]
        for g in range(GROUPS)
    ]

    def each(g, step):
        for part in groups[g]:
            getattr(part, step)()

    mine, sent = pl.ds(pages * x, pages), pl.ds(pages * (1 - x), pages)

    def band(b):
        return xall.at[:, pl.ds(blk * b, blk), :]

    to_b = remote(x_in.at[sent], band(1), asend.at[0], arecv.at[0], x_peer)
    to_c = remote(x_in.at[mine], band(2), asend.at[1], arecv.at[1], c_peer)
    to_d = remote(band(1), band(3), asend.at[2], arecv.at[2], c_peer)
    cot_b = remote(cot.at[sent], cown.at[:, pl.ds(blk, blk), :], asend.at[3], arecv.at[3], x_peer)
    keep_x = pltpu.make_async_copy(x_in.at[mine], band(0), aloc.at[0])
    keep_c = pltpu.make_async_copy(cot.at[mine], cown.at[:, pl.ds(0, blk), :], aloc.at[1])
    vecs = [
        remote(vpk, gvec.at[f], vs.at[k], vr.at[k], {"fsdp": lax.rem(f + k + 1, 8)}) for k in range(7)
    ]
    each(0, "along_z")
    to_b.start()
    keep_x.start()
    to_c.start()
    for copy in vecs:
        copy.start()
    each(1, "along_z")
    place_row = lax.broadcasted_iota(jnp.int32, (blk, own), 0)
    for page in range(pages):
        for b in range(4):
            bias[page, b * blk : (b + 1) * blk, :] = jnp.where(place_row < thr[page, b], 0.0, NEG)
    each(0, "forward")
    each(0, "along_y")
    each(2, "along_z")
    each(1, "forward")
    each(1, "along_y")
    each(0, "along_x")
    each(2, "forward")
    each(2, "along_y")
    to_b.wait_recv()
    to_d.start()
    each(1, "along_x")
    for copy in vecs:
        copy.wait_recv()
    for i in range(8):
        vec[i : i + 1, :] = jnp.concatenate([gvec[j, i : i + 1, :width] for j in range(8)], axis=1)
    for j in range(8):
        for i in range(3):
            b_in[:, (3 * j + i) * 128 : (3 * j + i + 1) * 128] = gvec[j, 8 + i : 9 + i, :]
    each(0, "to_core")
    keep_c.start()
    keep_x.wait()
    to_c.wait_recv()
    to_d.wait_recv()
    each(0, "arrive")

    def rest(p, step):
        def run(src, dst, row0, col0):
            getattr(Spread(where, src, dst, row0, col0, 384, rs, (p,)), step)()

        @pl.when(p == 0)
        def _():
            run(wo, go, 0, 0)

        @pl.when(jnp.logical_and(p >= 1, p < 5))
        def _():
            run(wi, gi, 0, 768 * (p - 1))

        @pl.when(jnp.logical_and(p >= 5, p < REST))
        def _():
            run(w2, g2, ROW * (p - 5), 0)

    low_lane = lax.broadcasted_iota(jnp.int32, (own, PAIR), 1) < HEAD_DIM
    lags = (("forward", 2), ("along_y", 3), ("along_x", 6), ("to_core", 9))

    def tick(t):
        @pl.when(t < REST)
        def _():
            rest(t, "along_z")

        for step, lag in lags:
            rest(t - lag, step)

    def p_copy(page, pair, slot):
        return pltpu.make_async_copy(pbuf.at[slot], p_o.at[page, pl.ds(2 * pair, 2)], ps.at[slot])

    def unit(it, carry):
        g, page = lax.div(it, pages), lax.rem(it, pages)

        @pl.when(it == 0)
        def _():
            each(2, "along_x")
            each(1, "to_core")

        @pl.when(it == 1)
        def _():
            each(2, "to_core")
            cot_b.start()

        @pl.when(it == pages)
        def _():
            each(1, "arrive")

        @pl.when(it == 2 * pages)
        def _():
            each(2, "arrive")

        gcols = pl.ds(pl.multiple_of(g * GCOLS, GCOLS), GCOLS)
        x_all = xall[page]
        d = x_all.shape[1]
        query = (dot(x_all[:own], gq[:, :, :, gcols].reshape(d, GCOLS)) + vec[0:1, gcols]).astype(BF)
        keys = dot(x_all, gk[:, :, :, gcols].reshape(d, GCOLS)).astype(BF)
        vals = (dot(x_all, gv[:, :, :, gcols].reshape(d, GCOLS)) + vec[1:2, gcols]).astype(BF)
        q_o[page, :, gcols] = query
        k_o[page, :, gcols] = keys
        v_o[page, :, gcols] = vals
        for half in range(2):
            lanes = slice(half * PAIR, (half + 1) * PAIR)
            pair = 2 * g + half

            @pl.when(it > 0)
            def _():
                p_copy(page, pair, half).wait()

            qp = query[:, lanes] * jnp.array(1.0 / math.sqrt(HEAD_DIM), BF)
            kp = keys[:, lanes]
            vt = vals[:, lanes].T
            outs = []
            for h in range(2):
                keep = low_lane if h == 0 else jnp.logical_not(low_lane)
                qh = jnp.where(keep, qp, jnp.zeros_like(qp))
                st = dot(kp, qh, NT) + bias[page]
                top = jnp.max(st, axis=0, keepdims=True)
                ex = jnp.exp(st - top)
                tot = jnp.sum(ex, axis=0, keepdims=True)
                pt = (ex * (1.0 / tot)).astype(BF)
                pbuf[half, h] = pt
                outs.append(dot(vt[h * HEAD_DIM : (h + 1) * HEAD_DIM], pt))
            p_copy(page, pair, half).start()
            cols = pl.ds(pl.multiple_of(pair * PAIR, PAIR), PAIR)
            c_o[page, :, cols] = jnp.concatenate(outs, axis=0).T.astype(BF)
            tick(2 * it + half)
        return carry

    lax.fori_loop(0, GROUPS * pages, unit, 0)
    n_ticks = 2 * GROUPS * pages
    lax.fori_loop(n_ticks, REST + lags[-1][1], lambda t, carry: (tick(t), carry)[1], 0)
    for half in range(2):
        p_copy(0, 0, half).wait()

    def finish(p, carry):
        rest(p, "arrive")
        rest(p, "drain")
        return carry

    lax.fori_loop(0, REST, finish, 0)
    for g in range(GROUPS):
        each(g, "drain")
    cot_b.wait_recv()
    for copy in vecs + [to_b, to_c, to_d, cot_b]:
        copy.wait_send()
    keep_c.wait()


def fwd(thr, x_in, cot, ws, smalls):
    pages_all, blk, d = x_in.shape
    pages, own, rows = pages_all // 2, 2 * blk, 4 * blk
    dma = pltpu.SemaphoreType.DMA
    sds = jax.ShapeDtypeStruct
    shapes = [(4, 2) + w.shape for w in ws]
    ff = ws[4].shape[1]
    res = call(
        fwd_body,
        (pages * 2 * d * d * (own + 2 * rows), sum(16 * w.size for w in ws), pages * HEADS * own * rows),
        in_specs=[pl.BlockSpec(memory_space=pltpu.SMEM)] + [ANY] * 8 + [VM] * 9,
        out_specs=[VM] * 3 + [ANY] * 3 + [VM, ANY, VM, VM, VM, VM, ANY, VM, VM],
        out_shape=[sds(s, BF) for s in shapes]
        + [
            sds((pages, rows, d), BF), sds((pages, own, d), BF),
            sds((pages, own, d), BF), sds((pages, rows, d), BF), sds((pages, rows, d), BF),
            sds((pages, own, d), BF), sds((pages, HEADS, rows, own), BF),
            sds((8, d), F32), sds((1, ff), F32),
        ],
        scratch_shapes=[
            pltpu.VMEM((pages, rows, own), F32),
            pltpu.VMEM((2, 2, rows, own), BF),
            pltpu.VMEM((16, 128), F32),
            pltpu.VMEM((8, 16, 128), F32),
        ]
        + spread_sems(GROUPS, 3)
        + spread_sems(REST)
        + [dma((4,)), dma((4,)), dma((2,)), dma((7,)), dma((7,)), dma((2,))],
        params=dict(collective_id=0, has_side_effects=True),
        name="gather_attention",
    )(thr, x_in, cot, *ws, *smalls)
    full = [r.reshape(-1, r.shape[-1]) for r in res[:6]]
    return full, res[6:]


class Fold:
    def __init__(self, where, acc, bufs, sems, key):
        self.z, self.y, self.x, self.c = where
        self.acc, self.key = acc, key
        self.rc, self.rx, self.ry, self.rz, self.fin, self.rf = [b.at[key] for b in bufs]
        self.cs, self.cr, self.xs, self.xr, self.ys, self.yr, self.zs, self.zr, self.fs, self.fr, self.es, self.er = sems
        z = self.z
        self.near, self.far, self.across = z + 1 - 2 * lax.rem(z, 2), lax.rem(z + 2, 4), 3 - z
        self.inner = jnp.logical_or(z == 1, z == 2)
        self.outer = jnp.logical_not(self.inner)
        self.keep = pl.ds(pl.multiple_of(32 * self.x, 32), 64)
        self.give = pl.ds(pl.multiple_of(64 * (1 - self.x), 32), 32)
        self.gain = pl.ds(pl.multiple_of(64 * self.x, 32), 32)

    def part(self, *sel):
        return self.acc(sel)

    def xcopy(self):
        return remote(
            self.part(ALL, 1 - self.y, self.give), self.rx, self.xs.at[self.key], self.xr.at[self.key],
            at(self.z, self.y, 1 - self.x, self.c),
        )

    def ycopy(self):
        return remote(
            self.part(ALL, 1 - self.y, self.keep), self.ry, self.ys.at[self.key], self.yr.at[self.key],
            at(self.z, 1 - self.y, self.x, self.c),
        )

    def zcopy(self, block, target, slot):
        return remote(
            self.part(block, self.y, ALL), self.rz.at[slot], self.zs.at[self.key + (slot,)],
            self.zr.at[self.key + (slot,)], at(target, self.y, self.x, self.c),
        )

    def a(self):
        return self.zcopy(self.near, self.near, 0)

    def b(self):
        return self.zcopy(self.far, self.far, 1)

    def d(self):
        return self.zcopy(self.across, self.across, 2)

    def f(self):
        return self.zcopy(self.across, self.near, 3)

    def fcopy(self):
        return remote(
            self.fin, self.rf, self.fs.at[self.key], self.fr.at[self.key],
            at(self.z, self.y, 1 - self.x, self.c),
        )

    def over_x(self, first):
        first.wait_recv()
        whole = self.part(ALL, ALL, ALL)
        whole[...] = whole[...] + self.rc[...]
        self.xcopy().start()

    def over_y(self):
        self.xcopy().wait_recv()
        rows = self.part(ALL, 1 - self.y, self.gain)
        rows[...] = rows[...] + self.rx[...]
        self.ycopy().start()

    def over_z(self):
        self.ycopy().wait_recv()
        rows = self.part(ALL, self.y, self.keep)
        rows[...] = rows[...] + self.ry[...]
        self.a().start()

        @pl.when(self.outer)
        def _():
            self.f().start()
            self.b().start()

        @pl.when(self.inner)
        def _():
            self.d().start()

    def inside(self):
        @pl.when(self.inner)
        def _():
            self.f().wait_recv()
            rows = self.part(self.far, self.y, ALL)
            rows[...] = rows[...] + self.rz[3]
            self.b().start()

    def total(self):
        self.a().wait_recv()
        self.b().wait_recv()
        own = self.part(self.z, self.y, ALL)

        @pl.when(self.outer)
        def _():
            self.fin[...] = (own[...].astype(F32) + self.rz[0].astype(F32) + self.rz[1].astype(F32)).astype(BF)

        @pl.when(self.inner)
        def _():
            self.d().wait_recv()
            self.fin[...] = (
                own[...].astype(F32) + self.rz[0].astype(F32) + self.rz[1].astype(F32) + self.rz[2].astype(F32)
            ).astype(BF)

        self.fcopy().start()

    def ecopy(self, view):
        return remote(view, view, self.es.at[self.key], self.er.at[self.key], at(self.z, self.y, self.x, 1 - self.c))

    def write(self, view):
        self.fcopy().wait_recv()
        view[...] = self.fin[...].astype(F32) + self.rf[...].astype(F32)
        self.ecopy(view).start()

    def drain(self, first, view):
        self.ecopy(view).wait_recv()
        first.wait_send()
        self.xcopy().wait_send()
        self.ycopy().wait_send()
        self.a().wait_send()
        self.b().wait_send()

        @pl.when(self.outer)
        def _():
            self.f().wait_send()

        @pl.when(self.inner)
        def _():
            self.d().wait_send()

        self.fcopy().wait_send()
        self.ecopy(view).wait_send()


ALL = slice(None)


def fold_sems(*lead):
    dma = pltpu.SemaphoreType.DMA
    return [dma(lead)] * 6 + [dma(lead + (4,))] * 2 + [dma(lead)] * 4


def fold_bufs(width, *lead):
    return [
        pltpu.VMEM(lead + shape, BF)
        for shape in (
            (4, 2, ROW, width), (4, 32, width), (4, 64, width), (4, ROW, width), (ROW, width), (ROW, width),
        )
    ]


def bwd_body(
    q_h, k_h, v_h, c_h, dc_h, g1_h, x_h, gq_h, gk_h, gv_h, p_h, dwo, dwi, dw2, res, gvf, gbin,
    oq, ok, ov, oo, oi, o2, fin_out, gx, ovec,
    *refs,
):
    q_v, k_v, v_v, c_v, dc_v, g1_v, x_v, gq_v, gk_v, gv_v = refs[:10]
    (acc, dwg, dq_all, dk_all, dv_all, rk, rv, sk, sv, pbuf, x_t, gxs, rgx, pack, vecin, vtot, vx, brow) = refs[10:28]
    fb, gb = refs[28:34], refs[34:40]
    fsem, gsem = refs[40:52], refs[52:64]
    lsem, csem, ps, ks, kr, gs, gr, osem, orem, oloc, vs, vr, us, ur = refs[64:]
    z, y, x, c = where = place()
    f = 2 * z + y
    pages, own, d = q_h.shape
    blk = own // 2
    rows = k_h.shape[1]
    x_peer, c_peer = at(z, y, 1 - x, c), at(z, y, x, 1 - c)
    meet([{"fsdp": lax.rem(f + k + 1, 8)} for k in range(7)] + [x_peer, c_peer])

    def first_of(p):
        def run(src, row0, col0, go):
            rr = pl.ds(row0, ROW)
            mine = src.at[:, :, rr, pl.ds(pl.multiple_of(col0 + 384 * c, 128), 384)]
            other = src.at[:, :, rr, pl.ds(pl.multiple_of(col0 + 384 * (1 - c), 128), 384)]
            copy = pltpu.make_async_copy(mine, acc.at[p], csem.at[p])
            send = remote(other, fb[0].at[p], fsem[0].at[p], fsem[1].at[p], c_peer)
            if go:
                copy.start()
                send.start()
            return copy, send

        return run

    def rest_src(p, run):
        @pl.when(p < 4)
        def _():
            run(dw2, ROW * p, 0)

        @pl.when(jnp.logical_and(p >= 4, p < 8))
        def _():
            run(dwi, 0, 768 * (p - 4))

        @pl.when(p == 8)
        def _():
            run(dwo, 0, 0)

    def rest_out(p, run):
        @pl.when(p < 4)
        def _():
            run(o2.at[pl.ds(pl.multiple_of(ROW * p, 32), ROW), pl.ds(pl.multiple_of(384 * c, 128), 384)])

        @pl.when(jnp.logical_and(p >= 4, p < 8))
        def _():
            run(oi.at[:, pl.ds(pl.multiple_of(768 * (p - 4) + 384 * c, 128), 384)])

        @pl.when(p == 8)
        def _():
            run(oo.at[:, pl.ds(pl.multiple_of(384 * c, 128), 384)])

    def fold(p):
        return Fold(where, lambda sel: acc.at[(p,) + sel], fb, fsem, (p,))

    def any_first(p):
        return remote(fb[0].at[p], fb[0].at[p], fsem[0].at[p], fsem[1].at[p], c_peer)

    def step(p, name):
        ok_p = jnp.logical_and(p >= 0, p < REST)

        @pl.when(ok_p)
        def _():
            if name == "start":
                rest_src(p, lambda src, r0, c0: first_of(p)(src, r0, c0, True) and None)
            elif name == "over_x":
                pltpu.make_async_copy(acc.at[p], acc.at[p], csem.at[p]).wait()
                fold(p).over_x(any_first(p))
            elif name == "write":
                rest_out(p, lambda view: fold(p).write(view))
            elif name == "drain":
                rest_out(p, lambda view: fold(p).drain(any_first(p), view))
            else:
                getattr(fold(p), name)()

    lags = (("over_x", 1), ("over_y", 3), ("over_z", 5), ("inside", 8), ("total", 9), ("write", 11))

    def tick(t):
        step(t, "start")
        for name, lag in lags:
            step(t - lag, name)

    def gfold(g, w):
        cols = pl.ds(pl.multiple_of(128 * c, 128), 128)
        return Fold(where, lambda sel: dwg.at[(g, w) + sel + (cols,)], gb, gsem, (g, w))

    def gfirst(g, w):
        cols = pl.ds(pl.multiple_of(128 * (1 - c), 128), 128)
        return remote(dwg.at[g, w, :, :, :, cols], gb[0].at[g, w], gsem[0].at[g, w], gsem[1].at[g, w], c_peer)

    def gstep(g, name):
        for w, o in enumerate((oq, ok, ov)):
            view = o.at[:, pl.ds(pl.multiple_of(GCOLS * g + 128 * c, 128), 128)]
            if name == "start":
                gfirst(g, w).start()
            elif name == "over_x":
                gfold(g, w).over_x(gfirst(g, w))
            elif name == "write":
                gfold(g, w).write(view)
            elif name == "drain":
                gfold(g, w).drain(gfirst(g, w), view)
            else:
                getattr(gfold(g, w), name)()

    glags = (("over_x", 1), ("over_y", 2), ("over_z", 3), ("inside", 4), ("total", 5), ("write", 6))

    loads = [
        pltpu.make_async_copy(src, dst, lsem.at[i])
        for i, (src, dst) in enumerate(
            (
                (q_h, q_v), (k_h, k_v), (v_h, v_v), (c_h, c_v), (dc_h, dc_v), (x_h.at[:, pl.ds(0, own), :], x_v),
                (g1_h, g1_v), (gq_h, gq_v), (gk_h, gk_v), (gv_h, gv_v),
            )
        )
    ]

    def p_copy(it, half):
        g, page = lax.div(it, pages), lax.rem(it, pages)
        return pltpu.make_async_copy(p_h.at[page, pl.ds(4 * g + 2 * half, 2)], pbuf.at[half], ps.at[half])

    tick(0)
    for half in range(2):
        p_copy(0, half).start()
    for copy in loads:
        copy.start()
    mine, sent = pl.ds(pages * x, pages), pl.ds(pages * (1 - x), pages)
    keep_out = pltpu.make_async_copy(res.at[:, pl.ds(0, blk), :], fin_out.at[mine], oloc.at[0])
    back_out = remote(res.at[:, pl.ds(blk, blk), :], fin_out.at[mine], osem.at[0], orem.at[0], x_peer)
    keep_out.start()
    tick(1)
    for copy in loads[:5]:
        copy.wait()

    low_lane = lax.broadcasted_iota(jnp.int32, (own, PAIR), 1) < HEAD_DIM
    scale = 1.0 / math.sqrt(HEAD_DIM)

    def kv_send(it):
        g, page = lax.div(it, pages), lax.rem(it, pages)
        gcols = pl.ds(pl.multiple_of(g * GCOLS, GCOLS), GCOLS)
        return [
            remote(s_ref.at[page, :, gcols], r_ref.at[page, :, gcols], ks.at[g, page, i], kr.at[g, page, i], c_peer)
            for i, (s_ref, r_ref) in enumerate(((sk, rk), (sv, rv)))
        ]

    def attend(it, half):
        g, page = lax.div(it, pages), lax.rem(it, pages)
        here = pl.ds(pl.multiple_of(page * own, own), own)
        p_copy(it, half).wait()
        cols = pl.ds(pl.multiple_of(g * GCOLS + half * PAIR, PAIR), PAIR)
        qp = q_v[page, :, cols] * jnp.array(scale, BF)
        kp = k_v[page, :, cols]
        kt = kp.T
        vp = v_v[page, :, cols]
        dc = dc_v[page, :, cols]
        prod = (dc.astype(F32) * c_v[page, :, cols].astype(F32)).T
        dk = None
        dv = None
        dqs = []
        for h in range(2):
            keep = low_lane if h == 0 else jnp.logical_not(low_lane)
            feats = slice(h * HEAD_DIM, (h + 1) * HEAD_DIM)
            dch = jnp.where(keep, dc, jnp.zeros_like(dc))
            qh = jnp.where(keep, qp, jnp.zeros_like(qp))
            pt = pbuf[half, h]
            delta = jnp.sum(prod[feats], axis=0, keepdims=True)
            dpt = dot(vp, dch, NT)
            dst = (pt.astype(F32) * (dpt - delta)).astype(BF)
            dvh = dot(pt, dch)
            dkh = dot(dst, qh)
            dk = dkh if dk is None else dk + dkh
            dv = dvh if dv is None else dv + dvh
            dqs.append(dot(kt[feats], dst))
        dq_all[here, cols] = (jnp.concatenate(dqs, axis=0) * scale).T.astype(BF)
        dk_all[here, cols] = dk[:own].astype(BF)
        sk[page, :, cols] = dk[own:].astype(BF)
        dv_all[here, cols] = dv[:own].astype(BF)
        sv[page, :, cols] = dv[own:].astype(BF)

        @pl.when(it + 1 < GROUPS * pages)
        def _():
            p_copy(it + 1, half).start()

    def group_grads(g):
        gcols = pl.ds(pl.multiple_of(g * GCOLS, GCOLS), GCOLS)
        for page in range(pages):
            here = pl.ds(page * own, own)
            for copy in kv_send(g * pages + page):
                copy.wait_recv()
            dk_all[here, gcols] = dk_all[here, gcols] + rk[page, :, gcols]
            dv_all[here, gcols] = dv_all[here, gcols] + rv[page, :, gcols]
        for w, grad in enumerate((dq_all, dk_all, dv_all)):
            value = grad[:, gcols]
            dwg[g, w] = dot(x_t[...], value).astype(BF).reshape(4, 2, ROW, GCOLS)
            if w != 1:
                brow[w : w + 1, gcols] = jnp.sum(value.astype(F32), 0, keepdims=True)
        gstep(g, "start")

    def gx_send(page):
        return remote(gxs.at[page], rgx.at[page], gs.at[page], gr.at[page], x_peer)

    def input_grads(page):
        here = pl.ds(pl.multiple_of(page * own, own), own)
        total = g1_v[page]
        for grad, w in ((dq_all, gq_v), (dk_all, gk_v), (dv_all, gv_v)):
            total = total + dot(grad[here, :], w[...], NT)
        gx[pages * x + page] = total[:blk]
        gxs[page] = total[blk:].astype(BF)
        gx_send(page).start()

    n_it = GROUPS * pages

    def unit(it, carry):
        for half in range(2):

            @pl.when(it < n_it)
            def _():
                attend(it, half)

            if half == 1:

                @pl.when(it < n_it)
                def _():
                    for copy in kv_send(it):
                        copy.start()

            tick(2 * it + 2 + half)

        @pl.when(it == 0)
        def _():
            for copy in loads[5:]:
                copy.wait()
            x_t[...] = x_v[...].reshape(pages * own, d).T
            back_out.start()

        done = it - pages + 1

        for name, lag in glags[::-1]:
            t = it - pages - lag + 1

            @pl.when(jnp.logical_and(t >= 0, jnp.logical_and(lax.rem(t + pages * 10, pages) == 0, t < n_it)))
            def _():
                gstep(lax.div(t, pages), name)

        @pl.when(jnp.logical_and(done >= 0, jnp.logical_and(lax.rem(done + pages, pages) == 0, done < n_it)))
        def _():
            group_grads(lax.div(done, pages))

        page = it - n_it + 1

        @pl.when(jnp.logical_and(page >= 0, page < pages))
        def _():
            input_grads(page)

        return carry

    lax.fori_loop(0, n_it, unit, 0)
    for i in range(8):
        row = brow[0:1, :] if i == 0 else brow[2:3, :] if i == 1 else gvf[i : i + 1, :]
        for j in range(8):
            pack[j, i : i + 1, :ROW] = row[:, ROW * j : ROW * (j + 1)]
    for j in range(8):
        for i in range(3):
            pack[j, 8 + i : 9 + i, :] = gbin[:, (3 * j + i) * 128 : (3 * j + i + 1) * 128]

    def vec_send(k):
        to = lax.rem(f + k + 1, 8)
        return remote(pack.at[to], vecin.at[k], vs.at[k], vr.at[k], {"fsdp": to})

    for k in range(7):
        vec_send(k).start()
    lax.fori_loop(n_it, n_it + 2, unit, 0)
    total = pack[f]
    for k in range(7):
        vec_send(k).wait_recv()
        total = total + vecin[k]
    vtot[...] = total
    vec_x = remote(vtot, vx.at[0], us.at[0], ur.at[0], x_peer)
    vec_x.start()
    lax.fori_loop(n_it + 2, n_it + 4, unit, 0)
    vec_x.wait_recv()
    vx[1] = vtot[...] + vx[0]
    vec_c = remote(vx.at[1], vx.at[2], us.at[1], ur.at[1], c_peer)
    vec_c.start()
    for page in range(pages):
        gx_send(page).wait_recv()
        gx[pages * (1 - x) + page] = rgx[page].astype(F32)
    lax.fori_loop(n_it + 4, n_it + 6, unit, 0)
    vec_c.wait_recv()
    ovec[...] = vx[1] + vx[2]

    def finish(p, carry):
        step(p, "drain")
        return carry

    lax.fori_loop(0, REST, finish, 0)
    for g in range(GROUPS):
        gstep(g, "drain")
    for it in range(n_it):
        for copy in kv_send(it):
            copy.wait_send()
    for page in range(pages):
        gx_send(page).wait_send()
    for k in range(7):
        vec_send(k).wait_send()
    vec_x.wait_send()
    vec_c.wait_send()
    back_out.wait()
    keep_out.wait()


def bwd(q, k, v, ctx, dctx, gm1, xall, ws, p, grads, out, gvf, gbin, shards):
    pages, own, d = q.shape
    rows, blk = k.shape[1], own // 2
    n = pages * own
    dma = pltpu.SemaphoreType.DMA
    vm = pltpu.VMEM
    sds = jax.ShapeDtypeStruct
    views = [g.reshape((4, 2) + shape) for g, shape in zip(grads, shards[3:])]
    res = call(
        bwd_body,
        (12 * n * d * d + pages * 10 * own * rows * d, sum(16 * g.size for g in grads), 0),
        in_specs=[ANY] * 15 + [VM, VM],
        out_specs=[VM] * 6 + [ANY, VM, VM],
        out_shape=[sds(shape, F32) for shape in shards]
        + [sds((2 * pages, blk, d), BF), sds((2 * pages, blk, d), F32), sds((16, 128), F32)],
        scratch_shapes=[
            vm((pages, own, d), BF), vm((pages, rows, d), BF), vm((pages, rows, d), BF),
            vm((pages, own, d), BF), vm((pages, own, d), BF), vm((pages, own, d), F32), vm((pages, own, d), BF),
            vm((d, d), BF), vm((d, d), BF), vm((d, d), BF),
            vm((REST, 4, 2, ROW, 384), BF), vm((GROUPS, 3, 4, 2, ROW, GCOLS), BF),
            vm((n, d), BF), vm((n, d), BF), vm((n, d), BF),
            vm((pages, own, d), BF), vm((pages, own, d), BF), vm((pages, own, d), BF), vm((pages, own, d), BF),
            vm((2, 2, rows, own), BF), vm((d, n), BF), vm((pages, blk, d), BF), vm((pages, blk, d), BF),
            vm((8, 16, 128), F32), vm((7, 16, 128), F32), vm((16, 128), F32), vm((3, 16, 128), F32), vm((8, d), F32),
        ]
        + fold_bufs(384, REST)
        + fold_bufs(128, GROUPS, 3)
        + fold_sems(REST)
        + fold_sems(GROUPS, 3)
        + [
            dma((10,)), dma((REST,)), dma((2,)), dma((GROUPS, pages, 2)), dma((GROUPS, pages, 2)),
            dma((pages,)), dma((pages,)), dma((1,)), dma((1,)), dma((1,)), dma((7,)), dma((7,)), dma((2,)), dma((2,)),
        ],
        params=dict(collective_id=1, has_side_effects=True, vmem_limit_bytes=64 << 20),
        name="attention_reduce",
    )(q, k, v, ctx, dctx, gm1, xall, *ws, p, *views, out, gvf, gbin)
    return res[:6], res[6], res[7], res[8]


SWAP_X = [(0, 2), (2, 0), (1, 3), (3, 1)]
SWAP_C = [(0, 1), (1, 0), (2, 3), (3, 2)]


def swap(value, pairs):
    return lax.ppermute(value, "seq", pairs)


def per_device(
    fsdp, inputs, lengths, w_query, b_query, w_key, w_value, b_value, w_out, b_out,
    gain_one, shift_one, w_inner, b_inner, w_outer, b_outer, gain_two, shift_two, cotangent,
):
    pages_all, blk, d = inputs.shape
    pages = pages_all // 2
    s = lax.axis_index("seq")
    x_at = lax.div(s, 2)
    direct = fsdp == 8
    ws = (w_query, w_key, w_value, w_out, w_inner, w_outer)
    shards = [w.shape for w in ws]
    width = b_query.shape[0]
    names = (b_query, b_value, b_out, gain_one, shift_one, b_outer, gain_two, shift_two)

    def pages_of(array, side):
        return lax.dynamic_slice_in_dim(array, side * pages, pages, 0)

    order = jnp.stack([s, s ^ 2, s ^ 1, s ^ 3]).astype(jnp.int32)
    thr = pages_of(lengths, x_at).astype(jnp.int32)[:, None] - order[None, :] * blk
    if direct:
        lanes = tuple(v.reshape(1, -1) for v in names + (b_inner,))
        full, rest = fwd(thr, inputs, cotangent, ws, lanes)
        wq, wk, wv, wo, wi, w2 = full
        xall, cown, q, k, v, ctx, p, vec_full, bin_full = rest
    else:
        wq, wk, wv, wo, wi, w2 = [lax.all_gather(w, "fsdp", axis=0, tiled=True) for w in ws]
        vec = jnp.concatenate(names + (b_inner,)).reshape(12, width)
        gvec = lax.all_gather(vec, "fsdp", axis=0)
        vec_full = jnp.swapaxes(gvec[:, :8], 0, 1).reshape(8, d).astype(F32)
        bin_full = gvec[:, 8:].reshape(1, -1).astype(F32)

        def own_rows(array):
            other = swap(pages_of(array, 1 - x_at), SWAP_X)
            return jnp.concatenate([pages_of(array, x_at), other], axis=1)

        xown, cown = own_rows(inputs), own_rows(cotangent)
        xall = jnp.concatenate([xown, swap(xown, SWAP_C)], axis=1)
        q, k, v, p, ctx = attn_fwd(thr, xall, wq, wk, wv, vec_full)
    out, gm1, dctx, dwo, dwi, dw2, gv_ffn, gbin = ffn(ctx, xall, cown, wo, wi, w2, vec_full, bin_full)
    if direct:
        tot, output, grad_inputs, tvec = bwd(
            q, k, v, ctx, dctx, gm1, xall, (wq, wk, wv), p, (dwo, dwi, dw2), out, gv_ffn, gbin, shards
        )
        small = [tvec[i, :width] for i in range(8)]
        g_bi = tvec[8:11].reshape(-1)
    else:
        dq, dk, dk_send, dv, dv_send = attn_bwd(q, k, v, p, ctx, dctx)
        dkr, dvr = swap(dk_send, SWAP_C), swap(dv_send, SWAP_C)
        gx_a, gx_b, dwq, dwk, dwv, gv_proj = proj(xall, dq, dk, dkr, dv, dvr, gm1, wq, wk, wv)
        gv = jnp.concatenate([gv_proj[:2], gv_ffn[2:]], axis=0)
        by_owner = jnp.concatenate(
            [jnp.swapaxes(gv.reshape(8, fsdp, width), 0, 1), gbin.reshape(fsdp, 4, width)], axis=1
        )
        tot = [
            lax.psum(lax.psum_scatter(g, "fsdp", scatter_dimension=0, tiled=True), "seq").astype(F32)
            for g in (dwq, dwk, dwv, dwo, dwi, dw2)
        ]
        tvec = lax.psum(lax.psum_scatter(by_owner, "fsdp", scatter_dimension=0, tiled=True)[0], "seq")

        def joined(mine, other):
            here = lax.dynamic_update_slice_in_dim(
                jnp.zeros((pages_all, blk, d), mine.dtype), mine, x_at * pages, 0
            )
            return lax.dynamic_update_slice_in_dim(here, other, (1 - x_at) * pages, 0)

        output = joined(out[:, :blk], swap(out[:, blk:], SWAP_X))
        grad_inputs = joined(gx_a, swap(gx_b, SWAP_X).astype(F32))
        small = [tvec[i] for i in range(8)]
        g_bi = tvec[8:].reshape(-1)
    g_bq, g_bv, g_bo, g_g1, g_s1, g_bo2, g_g2, g_s2 = small
    t_q, t_k, t_v, t_o, t_i, t_2 = tot
    return (
        output, grad_inputs, t_q, g_bq, t_k, t_v, g_bv, t_o, g_bo, g_g1, g_s1,
        t_i, g_bi, t_2, g_bo2, g_g2, g_s2,
    )


def solution(mesh):
    vec, mat, act = P("fsdp"), P("fsdp", None), P("fsdp", "seq", None)
    return jax.shard_map(
        functools.partial(per_device, mesh.shape["fsdp"]),
        mesh=mesh,
        in_specs=(act, vec, mat, vec, mat, mat, vec, mat, vec, vec, vec, mat, vec, mat, vec, vec, vec, act),
        out_specs=(act, act, mat, vec, mat, mat, vec, mat, vec, vec, vec, mat, vec, mat, vec, vec, vec),
        check_vma=False,
    )
```

```python
import functools
import math

import jax
import jax.numpy as jnp
from jax import lax
from jax.experimental import pallas as pl
from jax.experimental.pallas import tpu as pltpu
from jax.sharding import PartitionSpec as P

HEADS = 12
HEAD_DIM = 64
PAIR = 2 * HEAD_DIM
NEG = -1e30
EPS = 1e-12
BF = jnp.bfloat16
F32 = jnp.float32
MESH = pl.DeviceIdType.MESH
ANY = pl.BlockSpec(memory_space=pl.ANY)
VM = pl.BlockSpec(memory_space=pltpu.VMEM)
CHUNK = 1024
ROW = 96
VMEM_CAP = 60 << 20

NN = (((1,), (0,)), ((), ()))
NT = (((1,), (1,)), ((), ()))
TN = (((0,), (0,)), ((), ()))


def dot(a, b, dims=NN):
    return lax.dot_general(a, b, dims, preferred_element_type=F32)


def call(body, cost, **kw):
    flops, byts, trans = cost
    params = dict(vmem_limit_bytes=VMEM_CAP)
    params.update(kw.pop("params", {}))
    return pl.pallas_call(
        body,
        compiler_params=pltpu.CompilerParams(**params),
        cost_estimate=pl.CostEstimate(
            flops=int(flops), bytes_accessed=int(byts), transcendentals=int(trans)
        ),
        **kw,
    )


def attn_fwd_body(thr, xall, wq, wk, wv, vec, q_o, k_o, v_o, p_o, c_o, bias):
    page = pl.program_id(0)
    x_all = xall[0]
    own = x_all.shape[0] // 2
    query = (dot(x_all[:own], wq[...]) + vec[0:1, :]).astype(BF)
    q_o[0] = query
    k_o[0] = dot(x_all, wk[...]).astype(BF)
    v_o[0] = (dot(x_all, wv[...]) + vec[1:2, :]).astype(BF)
    blk = x_all.shape[0] // 4
    place = lax.broadcasted_iota(jnp.int32, (blk, own), 0)
    for b in range(4):
        bias[b * blk : (b + 1) * blk, :] = jnp.where(place < thr[page, b], 0.0, NEG)
    low_lane = lax.broadcasted_iota(jnp.int32, (own, PAIR), 1) < HEAD_DIM

    def pair(i, carry):
        cols = pl.ds(pl.multiple_of(i * PAIR, PAIR), PAIR)
        qp = q_o[0, :, cols] * jnp.array(1.0 / math.sqrt(HEAD_DIM), BF)
        kp = k_o[0, :, cols]
        vt = v_o[0, :, cols].T
        outs = []
        for h in range(2):
            keep = low_lane if h == 0 else jnp.logical_not(low_lane)
            qh = jnp.where(keep, qp, jnp.zeros_like(qp))
            st = dot(kp, qh, NT) + bias[...]
            top = jnp.max(st, axis=0, keepdims=True)
            ex = jnp.exp(st - top)
            tot = jnp.sum(ex, axis=0, keepdims=True)
            pt = (ex * (1.0 / tot)).astype(BF)
            p_o[0, 2 * i + h] = pt
            outs.append(dot(vt[h * HEAD_DIM : (h + 1) * HEAD_DIM], pt))
        c_o[0, :, cols] = jnp.concatenate(outs, axis=0).T.astype(BF)
        return carry

    lax.fori_loop(0, HEADS // 2, pair, 0)


def attn_fwd(thr, xall, wq, wk, wv, vec):
    pages, rows, d = xall.shape
    own = rows // 2
    const = lambda p, t: (0, 0)
    by_page = lambda p, t: (p, 0, 0)
    one = pl.Buffered(1)
    return call(
        attn_fwd_body,
        (
            pages * (2 * d * d * (own + 2 * rows) + 4 * own * rows * d),
            pages * rows * d * 2 * 4 + 6 * d * d + pages * HEADS * own * rows * 2,
            pages * HEADS * own * rows,
        ),
        grid_spec=pltpu.PrefetchScalarGridSpec(
            num_scalar_prefetch=1,
            grid=(pages,),
            in_specs=[pl.BlockSpec((1, rows, d), by_page)]
            + [pl.BlockSpec((d, d), const, pipeline_mode=one)] * 3
            + [pl.BlockSpec((8, d), const)],
            out_specs=[
                pl.BlockSpec((1, own, d), by_page),
                pl.BlockSpec((1, rows, d), by_page),
                pl.BlockSpec((1, rows, d), by_page),
                pl.BlockSpec((1, HEADS, rows, own), lambda p, t: (p, 0, 0, 0)),
                pl.BlockSpec((1, own, d), by_page),
            ],
            scratch_shapes=[pltpu.VMEM((rows, own), F32)],
        ),
        out_shape=[
            jax.ShapeDtypeStruct((pages, own, d), BF),
            jax.ShapeDtypeStruct((pages, rows, d), BF),
            jax.ShapeDtypeStruct((pages, rows, d), BF),
            jax.ShapeDtypeStruct((pages, HEADS, rows, own), BF),
            jax.ShapeDtypeStruct((pages, own, d), BF),
        ],
        name="attn_fwd",
    )(thr, xall, wq, wk, wv, vec)


def attn_bwd_body(q, k, v, p, ctx, dctx, dq_o, dk_own, dk_oth, dv_own, dv_oth):
    own = q.shape[1]
    low_lane = lax.broadcasted_iota(jnp.int32, (own, PAIR), 1) < HEAD_DIM
    scale = 1.0 / math.sqrt(HEAD_DIM)

    def pair(i, carry):
        cols = pl.ds(pl.multiple_of(i * PAIR, PAIR), PAIR)
        qp = q[0, :, cols] * jnp.array(scale, BF)
        kp = k[0, :, cols]
        kt = kp.T
        vp = v[0, :, cols]
        dc = dctx[0, :, cols]
        prod = (dc.astype(F32) * ctx[0, :, cols].astype(F32)).T
        dk = None
        dv = None
        dqs = []
        for h in range(2):
            keep = low_lane if h == 0 else jnp.logical_not(low_lane)
            feats = slice(h * HEAD_DIM, (h + 1) * HEAD_DIM)
            dch = jnp.where(keep, dc, jnp.zeros_like(dc))
            qh = jnp.where(keep, qp, jnp.zeros_like(qp))
            pt = p[0, 2 * i + h]
            delta = jnp.sum(prod[feats], axis=0, keepdims=True)
            dpt = dot(vp, dch, NT)
            dst = (pt.astype(F32) * (dpt - delta)).astype(BF)
            dvh = dot(pt, dch)
            dkh = dot(dst, qh)
            dk = dkh if dk is None else dk + dkh
            dv = dvh if dv is None else dv + dvh
            dqs.append(dot(kt[feats], dst))
        dq_o[0, :, cols] = (jnp.concatenate(dqs, axis=0) * scale).T.astype(BF)
        dk_own[0, :, cols] = dk[:own].astype(BF)
        dk_oth[0, :, cols] = dk[own:].astype(BF)
        dv_own[0, :, cols] = dv[:own].astype(BF)
        dv_oth[0, :, cols] = dv[own:].astype(BF)
        return carry

    lax.fori_loop(0, HEADS // 2, pair, 0)


def attn_bwd(q, k, v, p, ctx, dctx):
    pages, own, d = q.shape
    rows = k.shape[1]
    by_page = lambda i: (i, 0, 0)
    o = pl.BlockSpec((1, own, d), by_page)
    r = pl.BlockSpec((1, rows, d), by_page)
    return call(
        attn_bwd_body,
        (pages * 10 * own * rows * d, pages * (own * rows * HEADS * 2 + 10 * own * d * 2), 0),
        grid=(pages,),
        in_specs=[o, r, r, pl.BlockSpec((1, HEADS, rows, own), lambda i: (i, 0, 0, 0)), o, o],
        out_specs=[o] * 5,
        out_shape=[jax.ShapeDtypeStruct((pages, own, d), BF)] * 5,
        name="attn_bwd",
    )(q, k, v, p, ctx, dctx)


def normal_parts(v):
    bell = jnp.exp(v * v * -0.5)
    t = 1.0 / (1.0 + jnp.abs(v) * (0.3275911 / math.sqrt(2.0)))
    tail = t * (
        0.127414796 + t * (-0.142248368 + t * (0.7107068705 + t * (-0.7265760135 + t * 0.5307027145)))
    )
    tail = tail * bell
    return jnp.where(v >= 0.0, 1.0 - tail, tail), bell * (1.0 / math.sqrt(2.0 * math.pi))


def row_norm(v):
    centered = v - jnp.mean(v, -1, keepdims=True)
    inv = lax.rsqrt(jnp.mean(centered * centered, -1, keepdims=True) + EPS)
    return centered * inv, inv


def norm_back(e, n, inv):
    return inv * (e - jnp.mean(e, -1, keepdims=True) - n * jnp.mean(e * n, -1, keepdims=True))


def ffn_body(
    ctx, xall, cown, wo, wi_h, w2_h, vec, b_in,
    out, gm1_o, dctx_o, dwo_o, dwi_h, dw2_h, gvec, gbin,
    wi, w2, act, din, dgel, hid, gout, gatt, n1s, h1s, accs, r1s, dwi, dw2, lsem, osem,
):
    n, ff = act.shape
    pages, own, d = ctx.shape

    def cols_of(j):
        return pl.ds(pl.multiple_of(j * CHUNK, CHUNK), CHUNK)

    def loads(j):
        cols = cols_of(j)
        return (
            pltpu.make_async_copy(wi_h.at[:, cols], wi.at[:, cols], lsem.at[0, j]),
            pltpu.make_async_copy(w2_h.at[cols, :], w2.at[cols, :], lsem.at[1, j]),
        )

    def store_w2(j):
        return pltpu.make_async_copy(dw2.at[cols_of(j), :], dw2_h.at[cols_of(j), :], osem.at[0, j])

    def store_wi(j):
        return pltpu.make_async_copy(dwi.at[:, cols_of(j)], dwi_h.at[:, cols_of(j)], osem.at[1, j])

    n_chunks = ff // CHUNK
    for j in range(n_chunks):
        for copy in loads(j):
            copy.start()
    gvec[...] = jnp.zeros_like(gvec)

    def add(row, value):
        gvec[row : row + 1, :] += jnp.sum(value, 0, keepdims=True)

    for p in range(pages):
        r = slice(p * own, (p + 1) * own)
        mid = xall[p].astype(F32) + (dot(ctx[p], wo[...]) + vec[2:3, :])
        n1, r1 = row_norm(mid)
        n1s[r, :] = n1
        r1s[r, :] = jnp.broadcast_to(r1, (own, 128))
        h1 = n1 * vec[3:4, :] + vec[4:5, :]
        h1s[r, :] = h1
        hid[r, :] = h1.astype(BF)
    accs[...] = jnp.zeros_like(accs)

    def up(j, carry):
        cols = cols_of(j)
        for copy in loads(j):
            copy.wait()
        pre = dot(hid[...], wi[:, cols]) + b_in[:, cols]
        big, bell = normal_parts(pre)
        a = (pre * big).astype(BF)
        dgel[:, cols] = (big + pre * bell).astype(BF)
        act[:, cols] = a
        accs[...] += dot(a, w2[cols, :])
        return carry

    lax.fori_loop(0, n_chunks, up, 0)
    for p in range(pages):
        r = slice(p * own, (p + 1) * own)
        mid = h1s[r, :] + (accs[r, :] + vec[5:6, :])
        n2, r2 = row_norm(mid)
        out[p] = (n2 * vec[6:7, :] + vec[7:8, :]).astype(BF)
        cot = cown[p].astype(F32)
        gm2 = norm_back(cot * vec[6:7, :], n2, r2)
        go = gm2.astype(BF)
        gout[r, :] = go
        accs[r, :] = gm2
        add(5, go.astype(F32))
        add(6, cot * n2)
        add(7, cot)

    def down(j, carry):
        cols = cols_of(j)
        di = (dot(gout[...], w2[cols, :], NT) * dgel[:, cols].astype(F32)).astype(BF)
        din[:, cols] = di
        accs[...] += dot(di, wi[:, cols], NT)
        gbin[:, cols] = jnp.sum(di.astype(F32), 0, keepdims=True)
        dw2[cols, :] = dot(act[:, cols], gout[...], TN).astype(BF)
        store_w2(j).start()
        return carry

    lax.fori_loop(0, n_chunks, down, 0)
    for p in range(pages):
        r = slice(p * own, (p + 1) * own)
        gh = accs[r, :]
        n1 = n1s[r, :]
        gm1 = norm_back(gh * vec[3:4, :], n1, r1s[r, 0:1])
        gm1_o[p] = gm1
        ga = gm1.astype(BF)
        gatt[r, :] = ga
        dctx_o[p] = dot(ga, wo[...], NT).astype(BF)
        add(2, ga.astype(F32))
        add(3, gh * n1)
        add(4, gh)
    hid_t = hid[...].T

    def grads(j, carry):
        cols = cols_of(j)
        dwi[:, cols] = dot(hid_t, din[:, cols]).astype(BF)
        store_wi(j).start()
        return carry

    lax.fori_loop(0, n_chunks, grads, 0)
    dwo_o[...] = dot(ctx[...].reshape(n, d), gatt[...], TN).astype(BF)
    for j in range(n_chunks):
        store_w2(j).wait()
        store_wi(j).wait()


def ffn(ctx, xall, cown, wo, wi, w2, vec, b_in):
    pages, own, d = ctx.shape
    ff = wi.shape[1]
    n = pages * own
    sds = jax.ShapeDtypeStruct
    vm = pltpu.VMEM
    dma = pltpu.SemaphoreType.DMA
    return call(
        ffn_body,
        (n * d * (12 * ff + 6 * d), 4 * d * ff * 2 + 12 * n * d * 2, n * ff),
        grid=(1,),
        in_specs=[
            pl.BlockSpec((pages, own, d), lambda i: (0, 0, 0)),
            pl.BlockSpec((pages, own, d), lambda i: (0, 0, 0)),
            VM, VM, ANY, ANY, VM, VM,
        ],
        out_specs=[VM] * 4 + [ANY, ANY, VM, VM],
        out_shape=[
            sds((pages, own, d), BF), sds((pages, own, d), F32), sds((pages, own, d), BF),
            sds((d, d), BF), sds((d, ff), BF), sds((ff, d), BF), sds((8, d), F32), sds((1, ff), F32),
        ],
        scratch_shapes=[
            vm((d, ff), BF), vm((ff, d), BF), vm((n, ff), BF), vm((n, ff), BF), vm((n, ff), BF),
            vm((n, d), BF), vm((n, d), BF), vm((n, d), BF), vm((n, d), F32), vm((n, d), F32),
            vm((n, d), F32), vm((n, 128), F32), vm((d, ff), BF), vm((ff, d), BF),
            dma((2, ff // CHUNK)), dma((2, ff // CHUNK)),
        ],
        params=dict(vmem_limit_bytes=63 << 20),
        name="ffn",
    )(ctx, xall, cown, wo, wi, w2, vec, b_in)


def proj_body(
    xall, dq, dk, dkr, dv, dvr, gm1, wq, wk, wv,
    ga_o, gb_o, dwq_o, dwk_o, dwv_o, gvec, x_all, dq_all, dk_all, dv_all,
):
    page = pl.program_id(0)
    own = xall.shape[1]
    blk = own // 2
    here = pl.ds(pl.multiple_of(page * own, own), own)
    x_all[here, :] = xall[0]
    dq_v = dq[0]
    dk_v = (dk[0].astype(F32) + dkr[0].astype(F32)).astype(BF)
    dv_v = (dv[0].astype(F32) + dvr[0].astype(F32)).astype(BF)
    dq_all[here, :] = dq_v
    dk_all[here, :] = dk_v
    dv_all[here, :] = dv_v
    gx = gm1[0] + dot(dq_v, wq[...], NT) + dot(dk_v, wk[...], NT) + dot(dv_v, wv[...], NT)
    ga_o[0] = gx[:blk]
    gb_o[0] = gx[blk:].astype(BF)

    @pl.when(page == 0)
    def _():
        gvec[...] = jnp.zeros_like(gvec)

    gvec[0:1, :] += jnp.sum(dq_v.astype(F32), 0, keepdims=True)
    gvec[1:2, :] += jnp.sum(dv_v.astype(F32), 0, keepdims=True)

    @pl.when(page == pl.num_programs(0) - 1)
    def _():
        x_t = x_all[...].T
        dwq_o[...] = dot(x_t, dq_all[...]).astype(BF)
        dwk_o[...] = dot(x_t, dk_all[...]).astype(BF)
        dwv_o[...] = dot(x_t, dv_all[...]).astype(BF)


def proj(xall, dq, dk, dkr, dv, dvr, gm1, wq, wk, wv):
    pages, own, d = dq.shape
    blk = own // 2
    n = pages * own
    by_page = lambda p: (p, 0, 0)
    const = lambda p: (0, 0)
    one = pl.Buffered(1)
    half = pl.BlockSpec((1, blk, d), by_page)
    whole = pl.BlockSpec((1, own, d), by_page)
    square = pl.BlockSpec((d, d), const, pipeline_mode=one)
    return call(
        proj_body,
        (12 * n * d * d, 12 * d * d + 16 * n * d, 0),
        grid=(pages,),
        in_specs=[whole] * 7 + [square] * 3,
        out_specs=[half, half] + [square] * 3 + [pl.BlockSpec((8, d), const)],
        out_shape=[
            jax.ShapeDtypeStruct((pages, blk, d), F32),
            jax.ShapeDtypeStruct((pages, blk, d), BF),
        ]
        + [jax.ShapeDtypeStruct((d, d), BF)] * 3
        + [jax.ShapeDtypeStruct((8, d), F32)],
        scratch_shapes=[pltpu.VMEM((n, d), BF)] * 4,
        name="proj_bwd",
    )(xall, dq, dk, dkr, dv, dvr, gm1, wq, wk, wv)


def place():
    f, s = lax.axis_index("fsdp"), lax.axis_index("seq")
    return lax.div(f, 2), lax.rem(f, 2), lax.div(s, 2), lax.rem(s, 2)


def at(z, y, x, c):
    return {"fsdp": 2 * z + y, "seq": 2 * x + c}


def meet(others):
    barrier = pltpu.get_barrier_semaphore()
    for other in others:
        pl.semaphore_signal(barrier, inc=1, device_id=other, device_id_type=MESH)
    pl.semaphore_wait(barrier, len(others))


def remote(src, dst, send, recv, other):
    return pltpu.make_async_remote_copy(
        src_ref=src, dst_ref=dst, send_sem=send, recv_sem=recv,
        device_id=other, device_id_type=MESH,
    )


def begin(copy):
    copy.start()
    return copy


class Spread:
    def __init__(self, where, src, dst, row0, col0, width, sems, key, from0=None):
        self.z, self.y, self.x, self.c = where
        z, y, x, c = where
        zs, zr, fs, ys, yr, xs, xr, cs, cr, lo = sems
        k = key
        cols = pl.ds(pl.multiple_of(col0 + width * c, 128), width)
        origin = pl.ds(pl.multiple_of((col0 if from0 is None else from0) + width * c, 128), width)
        full = pl.ds(row0, ROW)
        mine = pl.ds(pl.multiple_of(row0 + (ROW - YROWS) * x, 16), YROWS)
        lacks = pl.ds(pl.multiple_of(row0 + YROWS * x, 16), ROW - YROWS)
        near, far, across = z + 1 - 2 * lax.rem(z, 2), lax.rem(z + 2, 4), 3 - z
        self.inner = jnp.logical_or(z == 1, z == 2)
        self.local = lambda: pltpu.make_async_copy(src.at[full, origin], dst.at[z, y, full, cols], lo.at[k])

        def send(block, n, target, sem):
            from_ref = src.at[full, origin] if block is None else dst.at[block, y, full, cols]
            b = z if block is None else block
            return remote(from_ref, dst.at[b, y, full, cols], sem, zr.at[k + (n,)], at(target, y, x, c))

        self.a = lambda: send(None, 0, near, zs.at[k + (0,)])
        self.b = lambda: send(None, 1, far, zs.at[k + (1,)])
        self.d = lambda: send(None, 2, across, zs.at[k + (2,)])
        self.fwd = lambda: send(far, 2, near, fs.at[k])
        yv = lambda: dst.at[:, y, mine, cols]
        self.ycopy = lambda: remote(yv(), yv(), ys.at[k], yr.at[k], at(z, 1 - y, x, c))
        xv = lambda: dst.at[:, 1 - y, lacks, cols]
        self.xcopy = lambda: remote(xv(), xv(), xs.at[k], xr.at[k], at(z, y, 1 - x, c))
        cv = lambda: dst.at[:, :, full, cols]
        self.ccopy = lambda: remote(cv(), cv(), cs.at[k], cr.at[k], at(z, y, x, 1 - c))

    def along_z(self):
        self.local().start()
        self.b().start()
        self.a().start()

        @pl.when(self.inner)
        def _():
            self.d().start()

    def forward(self):
        self.b().wait_recv()

        @pl.when(self.inner)
        def _():
            self.fwd().start()

    def along_y(self):
        self.a().wait_recv()
        self.d().wait_recv()
        self.local().wait()
        self.ycopy().start()

    def along_x(self):
        self.ycopy().wait_recv()
        self.xcopy().start()

    def to_core(self):
        self.xcopy().wait_recv()
        self.ccopy().start()

    def arrive(self):
        self.ccopy().wait_recv()

    def drain(self):
        self.a().wait_send()
        self.b().wait_send()

        @pl.when(self.inner)
        def _():
            self.d().wait_send()
            self.fwd().wait_send()

        self.ycopy().wait_send()
        self.xcopy().wait_send()
        self.ccopy().wait_send()


def spread_sems(*lead):
    dma = pltpu.SemaphoreType.DMA
    return [dma(lead + (3,)), dma(lead + (3,))] + [dma(lead)] * 8


GROUPS = 3
GCOLS = 256
REST = 9
EARLY = 3
YROWS = 64


def fwd_body(
    thr, x_in, cot, wq, wk, wv, wo, wi, w2, *refs,
):
    smalls = refs[:9]
    (
        gq_h, gk_h, gv_h, xall_h, q_h, k_h, v_h, c_h, p_o, dctx_h, gm1_h, dwo_h, dwi_h, dw2_h, fin_out, gvs, gbin,
    ) = refs[9:26]
    (
        gq, gk, gv, go, gi, g2, xall, q_o, k_o, v_o, c_o, cown, bias, pbuf, vpk, gvec, vec, b_in,
        act, dd, hid, gout, gatt, dctx, n1s, accs, r1s, dw2_s, dwi_s,
    ) = refs[26:55]
    qs, rs = refs[55:65], refs[65:75]
    asend, arecv, aloc, vs, vr, ps, outs_sem, grad_sem = refs[75:]
    z, y, x, c = where = place()
    f = 2 * z + y
    pages, rows = xall.shape[0], xall.shape[1]
    own, blk = rows // 2, rows // 4
    width = smalls[0].shape[-1]
    for i in range(8):
        vpk[i : i + 1, :width] = smalls[i][...].astype(F32).reshape(1, width)
    for i in range(3):
        vpk[8 + i : 9 + i, :] = smalls[8][:, 128 * i : 128 * (i + 1)].astype(F32).reshape(1, 128)
    gvec[f] = vpk[...]
    x_peer, c_peer = at(z, y, 1 - x, c), at(z, y, x, 1 - c)
    meet([{"fsdp": lax.rem(f + k + 1, 8)} for k in range(7)] + [x_peer, c_peer])

    groups = [
        [Spread(where, src, dst, 0, GCOLS * g, GCOLS // 2, qs, (g, w)) for w, (src, dst) in enumerate(((wq, gq), (wk, gk), (wv, gv)))]
        for g in range(GROUPS)
    ]

    def each(g, step):
        for part in groups[g]:
            getattr(part, step)()

    mine, sent = pl.ds(pages * x, pages), pl.ds(pages * (1 - x), pages)

    def band(b):
        return xall.at[:, pl.ds(blk * b, blk), :]

    to_b = remote(x_in.at[sent], band(1), asend.at[0], arecv.at[0], x_peer)
    to_c = remote(x_in.at[mine], band(2), asend.at[1], arecv.at[1], c_peer)
    to_d = remote(band(1), band(3), asend.at[2], arecv.at[2], c_peer)
    cot_b = remote(cot.at[sent], cown.at[:, pl.ds(blk, blk), :], asend.at[3], arecv.at[3], x_peer)
    keep_x = pltpu.make_async_copy(x_in.at[mine], band(0), aloc.at[0])
    keep_c = pltpu.make_async_copy(cot.at[mine], cown.at[:, pl.ds(0, blk), :], aloc.at[1])
    vecs = [
        remote(vpk, gvec.at[f], vs.at[k], vr.at[k], {"fsdp": lax.rem(f + k + 1, 8)}) for k in range(7)
    ]
    def rest(p, step):
        def run(src, dst, row0, col0, from0=None):
            getattr(Spread(where, src, dst, row0, col0, 384, rs, (p,), from0), step)()

        @pl.when(p == 0)
        def _():
            run(wo, go, 0, 0)

        @pl.when(jnp.logical_and(p >= 1, p < 5))
        def _():
            run(wi, gi.at[p - 1], 0, 0, 768 * (p - 1))

        @pl.when(jnp.logical_and(p >= 5, p < REST))
        def _():
            run(w2, g2, ROW * (p - 5), 0)

    to_b.start()
    each(0, "along_z")
    keep_x.start()
    to_c.start()
    for copy in vecs:
        copy.start()
    place_row = lax.broadcasted_iota(jnp.int32, (blk, own), 0)
    for page in range(pages):
        for b in range(4):
            bias[page, b * blk : (b + 1) * blk, :] = jnp.where(place_row < thr[page, b], 0.0, NEG)
    each(0, "forward")
    each(1, "along_z")
    each(0, "along_y")
    each(1, "forward")
    each(2, "along_z")
    each(1, "along_y")
    each(0, "along_x")
    each(2, "forward")
    for p in range(EARLY):
        rest(p, "along_z")
    each(2, "along_y")
    to_b.wait_recv()
    to_d.start()
    each(0, "to_core")
    each(1, "along_x")
    for copy in vecs:
        copy.wait_recv()
    for i in range(8):
        vec[i : i + 1, :] = jnp.concatenate([gvec[j, i : i + 1, :width] for j in range(8)], axis=1)
    for j in range(8):
        for i in range(3):
            b_in[:, (3 * j + i) * 128 : (3 * j + i + 1) * 128] = gvec[j, 8 + i : 9 + i, :]
    keep_c.start()
    keep_x.wait()
    to_c.wait_recv()
    to_d.wait_recv()
    each(0, "arrive")

    low_lane = lax.broadcasted_iota(jnp.int32, (own, PAIR), 1) < HEAD_DIM
    stages = (("along_z", 1 - 8 * EARLY // 3), ("forward", 0), ("along_y", 2), ("along_x", 5), ("to_core", 8))

    def tick(t):
        for step, late in stages:
            n = t - late
            p = lax.div(3 * n + 7, 8)

            @pl.when(jnp.logical_and(n >= 0, lax.div(8 * p, 3) == n))
            def _():
                if step == "along_z":
                    pl.when(p >= EARLY)(lambda: rest(p, step))
                else:
                    rest(p, step)

    def p_copy(page, pair, slot):
        return pltpu.make_async_copy(pbuf.at[slot], p_o.at[page, pl.ds(2 * pair, 2)], ps.at[slot])

    def unit(it, carry):
        g, page = lax.div(it, pages), lax.rem(it, pages)

        @pl.when(it == 0)
        def _():
            each(2, "along_x")
            each(1, "to_core")

        @pl.when(it == 1)
        def _():
            each(2, "to_core")
            cot_b.start()

        @pl.when(it == pages)
        def _():
            each(1, "arrive")

        @pl.when(it == 2 * pages)
        def _():
            each(2, "arrive")

        gcols = pl.ds(pl.multiple_of(g * GCOLS, GCOLS), GCOLS)
        x_all = xall[page]
        d = x_all.shape[1]
        query = (dot(x_all[:own], gq[:, :, :, gcols].reshape(d, GCOLS)) + vec[0:1, gcols]).astype(BF)
        keys = dot(x_all, gk[:, :, :, gcols].reshape(d, GCOLS)).astype(BF)
        vals = (dot(x_all, gv[:, :, :, gcols].reshape(d, GCOLS)) + vec[1:2, gcols]).astype(BF)
        q_o[page, :, gcols] = query
        k_o[page, :, gcols] = keys
        v_o[page, :, gcols] = vals
        for half in range(2):
            lanes = slice(half * PAIR, (half + 1) * PAIR)
            pair = 2 * g + half

            @pl.when(it > 0)
            def _():
                p_copy(page, pair, half).wait()

            qp = query[:, lanes] * jnp.array(1.0 / math.sqrt(HEAD_DIM), BF)
            kp = keys[:, lanes]
            vt = vals[:, lanes].T
            outs = []
            for h in range(2):
                keep = low_lane if h == 0 else jnp.logical_not(low_lane)
                qh = jnp.where(keep, qp, jnp.zeros_like(qp))
                st = dot(kp, qh, NT) + bias[page]
                top = jnp.max(st, axis=0, keepdims=True)
                ex = jnp.exp(st - top)
                tot = jnp.sum(ex, axis=0, keepdims=True)
                pt = (ex * (1.0 / tot)).astype(BF)
                pbuf[half, h] = pt
                outs.append(dot(vt[h * HEAD_DIM : (h + 1) * HEAD_DIM], pt))
            p_copy(page, pair, half).start()
            cols = pl.ds(pl.multiple_of(pair * PAIR, PAIR), PAIR)
            c_o[page, :, cols] = jnp.concatenate(outs, axis=0).T.astype(BF)
            tick(2 * it + half)
        return carry

    lax.fori_loop(0, GROUPS * pages, unit, 0)
    n_ticks = 2 * GROUPS * pages
    stores = [
        pltpu.make_async_copy(src, dst, outs_sem.at[i])
        for i, (src, dst) in enumerate(
            ((q_o, q_h), (k_o, k_h), (v_o, v_h), (c_o, c_h), (xall, xall_h), (gq, gq_h), (gk, gk_h), (gv, gv_h))
        )
    ]
    for copy in stores:
        copy.start()
    for half in range(2):
        p_copy(0, 0, half).wait()

    d = xall.shape[2]
    n_chunks = gi.shape[0]
    last = 8 * (REST - 1) // 3 + stages[-1][1] + 1
    gvs[...] = jnp.zeros_like(gvs)

    def add(row, value):
        gvs[row : row + 1, :] += jnp.sum(value, 0, keepdims=True)

    def square(ref):
        return ref[...].reshape(d, d)

    rest(0, "arrive")
    for page in range(pages):
        r = slice(page * own, (page + 1) * own)
        mid = xall[page, :own].astype(F32) + (dot(c_o[page], square(go)) + vec[2:3, :])
        n1, r1 = row_norm(mid)
        n1s[r, :] = n1
        r1s[r, :] = jnp.broadcast_to(r1, (own, 128))
        hid[r, :] = (n1 * vec[3:4, :] + vec[4:5, :]).astype(BF)

    def ticks(lo, hi):
        lax.fori_loop(lo, hi, lambda t, carry: (tick(t), carry)[1], 0)

    def up(j, carry):
        ticks(n_ticks + 3 * j, jnp.minimum(n_ticks + 3 * j + 3, last))
        rest(j + 1, "arrive")
        cols = pl.ds(pl.multiple_of(j * d, d), d)
        pre = dot(hid[...], gi[j].reshape(d, d)) + b_in[:, cols]
        big, bell = normal_parts(pre)
        act[:, cols] = (pre * big).astype(BF)
        dd[:, cols] = (big + pre * bell).astype(BF)
        return carry

    lax.fori_loop(0, n_chunks, up, 0)
    ticks(n_ticks + 3 * n_chunks, last)
    for p in range(5, REST):
        rest(p, "arrive")
    keep_c.wait()
    cot_b.wait_recv()
    stores[0].wait()

    def w2_rows(j):
        return g2[j].reshape(d, d)

    accs[...] = jnp.zeros_like(accs)

    def outer(j, carry):
        cols = pl.ds(pl.multiple_of(j * d, d), d)
        accs[...] += dot(act[:, cols], w2_rows(j))
        return carry

    lax.fori_loop(0, n_chunks, outer, 0)
    for page in range(pages):
        r = slice(page * own, (page + 1) * own)
        h1 = n1s[r, :] * vec[3:4, :] + vec[4:5, :]
        mid = h1 + (accs[r, :] + vec[5:6, :])
        n2, r2 = row_norm(mid)
        q_o[page] = (n2 * vec[6:7, :] + vec[7:8, :]).astype(BF)
        ct = cown[page].astype(F32)
        gm2 = norm_back(ct * vec[6:7, :], n2, r2)
        gob = gm2.astype(BF)
        gout[r, :] = gob
        accs[r, :] = gm2
        add(5, gob.astype(F32))
        add(6, ct * n2)
        add(7, ct)
    keep_out = pltpu.make_async_copy(q_o.at[:, pl.ds(0, blk), :], fin_out.at[mine], aloc.at[2])
    back_out = remote(q_o.at[:, pl.ds(blk, blk), :], fin_out.at[mine], asend.at[4], arecv.at[4], x_peer)
    keep_out.start()
    back_out.start()

    def grad_store(j, i):
        slot = lax.rem(j, 2)
        return pltpu.make_async_copy((dw2_s, dwi_s)[i].at[slot], (dw2_h, dwi_h)[i].at[j], grad_sem.at[i, slot])

    def down(j, carry):
        cols = pl.ds(pl.multiple_of(j * d, d), d)
        di = (dot(gout[...], w2_rows(j), NT) * dd[:, cols].astype(F32)).astype(BF)
        dd[:, cols] = di
        accs[...] += dot(di, gi[j].reshape(d, d), NT)
        gbin[:, cols] = jnp.sum(di.astype(F32), 0, keepdims=True)

        @pl.when(j >= 2)
        def _():
            grad_store(j, 0).wait()
            grad_store(j, 1).wait()

        slot = lax.rem(j, 2)
        dw2_s[slot] = dot(act[:, cols], gout[...], TN).astype(BF)
        dwi_s[slot] = dot(hid[...], di, TN).astype(BF)
        grad_store(j, 0).start()
        grad_store(j, 1).start()
        return carry

    lax.fori_loop(0, n_chunks, down, 0)
    for page in range(pages):
        r = slice(page * own, (page + 1) * own)
        gh = accs[r, :]
        n1 = n1s[r, :]
        gm1 = norm_back(gh * vec[3:4, :], n1, r1s[r, 0:1])
        accs[r, :] = gm1
        ga = gm1.astype(BF)
        gatt[r, :] = ga
        dctx[page] = dot(ga, square(go), NT).astype(BF)
        add(2, ga.astype(F32))
        add(3, gh * n1)
        add(4, gh)
    tail = [
        pltpu.make_async_copy(accs, gm1_h, outs_sem.at[8]),
        pltpu.make_async_copy(dctx, dctx_h, outs_sem.at[9]),
        pltpu.make_async_copy(hid, dwo_h, outs_sem.at[10]),
    ]
    tail[0].start()
    tail[1].start()
    hid[...] = dot(c_o[...].reshape(pages * own, d), gatt[...], TN).astype(BF)
    tail[2].start()
    for j in range(n_chunks - 2, n_chunks):
        grad_store(j, 0).wait()
        grad_store(j, 1).wait()

    def finish(p, carry):
        rest(p, "drain")
        return carry

    lax.fori_loop(0, REST, finish, 0)
    for g in range(GROUPS):
        each(g, "drain")
    for copy in vecs + [to_b, to_c, to_d, cot_b]:
        copy.wait_send()
    for copy in stores[1:] + tail + [keep_out]:
        copy.wait()
    back_out.wait()


def fwd(thr, x_in, cot, ws, smalls):
    pages_all, blk, d = x_in.shape
    pages, own, rows = pages_all // 2, 2 * blk, 4 * blk
    n = pages * own
    dma = pltpu.SemaphoreType.DMA
    sds = jax.ShapeDtypeStruct
    vm = pltpu.VMEM
    ff = ws[4].shape[1]
    quarter = (4, 2, ROW, d)
    res = call(
        fwd_body,
        (n * d * (12 * ff + 12 * d), sum(16 * w.size for w in ws), pages * HEADS * own * rows),
        in_specs=[pl.BlockSpec(memory_space=pltpu.SMEM)] + [ANY] * 5 + [VM] * 12,
        out_specs=[ANY] * 15 + [VM, VM],
        out_shape=[sds(quarter, BF)] * 3
        + [
            sds((pages, rows, d), BF),
            sds((pages, own, d), BF), sds((pages, rows, d), BF), sds((pages, rows, d), BF), sds((pages, own, d), BF),
            sds((pages, HEADS, rows, own), BF),
            sds((pages, own, d), BF), sds((n, d), F32), sds((d, d), BF),
            sds((ff // d, d, d), BF), sds((ff // d, d, d), BF), sds((pages_all, blk, d), BF),
            sds((8, d), F32), sds((1, ff), F32),
        ],
        scratch_shapes=[
            vm(quarter, BF), vm(quarter, BF), vm(quarter, BF), vm(quarter, BF),
            vm((ff // d,) + quarter, BF), vm((4, 2, ff // 8, d), BF),
            vm((pages, rows, d), BF), vm((pages, own, d), BF), vm((pages, rows, d), BF), vm((pages, rows, d), BF),
            vm((pages, own, d), BF), vm((pages, own, d), BF), vm((pages, rows, own), F32), vm((2, 2, rows, own), BF),
            vm((16, 128), F32), vm((8, 16, 128), F32), vm((8, d), F32), vm((1, ff), F32),
            vm((n, ff), BF), vm((n, ff), BF), vm((n, d), BF), vm((n, d), BF), vm((n, d), BF), vm((pages, own, d), BF),
            vm((n, d), F32), vm((n, d), F32), vm((n, 128), F32), vm((2, d, d), BF), vm((2, d, d), BF),
        ]
        + spread_sems(GROUPS, 3)
        + spread_sems(REST)
        + [dma((5,)), dma((5,)), dma((3,)), dma((7,)), dma((7,)), dma((2,)), dma((11,)), dma((2, 2))],
        params=dict(collective_id=0, has_side_effects=True, vmem_limit_bytes=64 << 20),
        name="gather_forward",
    )(thr, x_in, cot, *ws, *smalls)
    full = [r.reshape(d, d) for r in res[:3]]
    return full, res[3:]


class Fold:
    def __init__(self, where, acc, bufs, sems, key, keep):
        self.z, self.y, self.x, self.c = where
        self.acc, self.key = acc, key
        give = ROW - keep
        self.rc, self.rx, self.ry, self.rz, self.fin, self.rf = [b.at[key] for b in bufs]
        self.cs, self.cr, self.xs, self.xr, self.ys, self.yr, self.zs, self.zr, self.fs, self.fr, self.es, self.er = sems
        z = self.z
        self.near, self.far, self.across = z + 1 - 2 * lax.rem(z, 2), lax.rem(z + 2, 4), 3 - z
        self.inner = jnp.logical_or(z == 1, z == 2)
        self.outer = jnp.logical_not(self.inner)
        self.keep = pl.ds(pl.multiple_of(give * self.x, 16), keep)
        self.give = pl.ds(pl.multiple_of(keep * (1 - self.x), 16), give)
        self.gain = pl.ds(pl.multiple_of(keep * self.x, 16), give)

    def part(self, *sel):
        return self.acc(sel)

    def xcopy(self):
        return remote(
            self.part(ALL, 1 - self.y, self.give), self.rx, self.xs.at[self.key], self.xr.at[self.key],
            at(self.z, self.y, 1 - self.x, self.c),
        )

    def ycopy(self):
        return remote(
            self.part(ALL, 1 - self.y, self.keep), self.ry, self.ys.at[self.key], self.yr.at[self.key],
            at(self.z, 1 - self.y, self.x, self.c),
        )

    def zcopy(self, block, target, slot):
        return remote(
            self.part(block, self.y, ALL), self.rz.at[slot], self.zs.at[self.key + (slot,)],
            self.zr.at[self.key + (slot,)], at(target, self.y, self.x, self.c),
        )

    def a(self):
        return self.zcopy(self.near, self.near, 0)

    def b(self):
        return self.zcopy(self.far, self.far, 1)

    def d(self):
        return self.zcopy(self.across, self.across, 2)

    def f(self):
        return self.zcopy(self.across, self.near, 3)

    def fcopy(self):
        return remote(
            self.fin, self.rf, self.fs.at[self.key], self.fr.at[self.key],
            at(self.z, self.y, 1 - self.x, self.c),
        )

    def over_x(self, first):
        first.wait_recv()
        whole = self.part(ALL, ALL, ALL)
        whole[...] = whole[...] + self.rc[...]
        self.xcopy().start()

    def over_y(self):
        self.xcopy().wait_recv()
        rows = self.part(ALL, 1 - self.y, self.gain)
        rows[...] = rows[...] + self.rx[...]
        self.ycopy().start()

    def over_z(self):
        self.ycopy().wait_recv()
        rows = self.part(ALL, self.y, self.keep)
        rows[...] = rows[...] + self.ry[...]
        self.a().start()

        @pl.when(self.outer)
        def _():
            self.f().start()
            self.b().start()

        @pl.when(self.inner)
        def _():
            self.d().start()

    def inside(self):
        @pl.when(self.inner)
        def _():
            self.f().wait_recv()
            rows = self.part(self.far, self.y, ALL)
            rows[...] = rows[...] + self.rz[3]
            self.b().start()

    def total(self):
        self.a().wait_recv()
        self.b().wait_recv()
        own = self.part(self.z, self.y, ALL)

        @pl.when(self.outer)
        def _():
            self.fin[...] = (own[...].astype(F32) + self.rz[0].astype(F32) + self.rz[1].astype(F32)).astype(BF)

        @pl.when(self.inner)
        def _():
            self.d().wait_recv()
            self.fin[...] = (
                own[...].astype(F32) + self.rz[0].astype(F32) + self.rz[1].astype(F32) + self.rz[2].astype(F32)
            ).astype(BF)

        self.fcopy().start()

    def ecopy(self, view):
        return remote(view, view, self.es.at[self.key], self.er.at[self.key], at(self.z, self.y, self.x, 1 - self.c))

    def write(self, view):
        self.fcopy().wait_recv()
        view[...] = self.fin[...].astype(F32) + self.rf[...].astype(F32)
        self.ecopy(view).start()

    def drain(self, first, view):
        self.ecopy(view).wait_recv()
        first.wait_send()
        self.xcopy().wait_send()
        self.ycopy().wait_send()
        self.a().wait_send()
        self.b().wait_send()

        @pl.when(self.outer)
        def _():
            self.f().wait_send()

        @pl.when(self.inner)
        def _():
            self.d().wait_send()

        self.fcopy().wait_send()
        self.ecopy(view).wait_send()


ALL = slice(None)
KEEP_REST = 64
KEEP_GROUP = 80


def fold_sems(*lead):
    dma = pltpu.SemaphoreType.DMA
    return [dma(lead)] * 6 + [dma(lead + (4,))] * 2 + [dma(lead)] * 4


def fold_bufs(width, keep, *lead):
    return [
        pltpu.VMEM(lead + shape, BF)
        for shape in (
            (4, 2, ROW, width), (4, ROW - keep, width), (4, keep, width), (4, ROW, width), (ROW, width), (ROW, width),
        )
    ]


def bwd_body(
    q_h, k_h, v_h, c_h, dc_h, g1_h, x_h, gq_h, gk_h, gv_h, p_h, dwo, dwi, dw2, gvf, gbin,
    oq, ok, ov, oo, oi, o2, gx, ovec,
    *refs,
):
    q_v, k_v, v_v, c_v, dc_v, g1_v, x_v, gq_v, gk_v, gv_v = refs[:10]
    (acc, dwg, dq_all, dk_all, dv_all, rk, rv, sk, sv, pbuf, x_t, gxs, rgx, pack, vecin, vtot, vx, brow) = refs[10:28]
    fb, gb = refs[28:34], refs[34:40]
    fsem, gsem = refs[40:52], refs[52:64]
    lsem, csem, ps, ks, kr, gs, gr, vs, vr, us, ur = refs[64:]
    z, y, x, c = where = place()
    f = 2 * z + y
    pages, own, d = q_h.shape
    blk = own // 2
    rows = k_h.shape[1]
    x_peer, c_peer = at(z, y, 1 - x, c), at(z, y, x, 1 - c)
    meet([{"fsdp": lax.rem(f + k + 1, 8)} for k in range(7)] + [x_peer, c_peer])

    def first_of(p):
        def run(src, row0, col0, go):
            rr = pl.ds(row0, ROW)
            mine = src.at[:, :, rr, pl.ds(pl.multiple_of(col0 + 384 * c, 128), 384)]
            other = src.at[:, :, rr, pl.ds(pl.multiple_of(col0 + 384 * (1 - c), 128), 384)]
            copy = pltpu.make_async_copy(mine, acc.at[p], csem.at[p])
            send = remote(other, fb[0].at[p], fsem[0].at[p], fsem[1].at[p], c_peer)
            if go:
                copy.start()
                send.start()
            return copy, send

        return run

    def rest_src(p, run):
        @pl.when(p < 4)
        def _():
            run(dw2, ROW * p, 0)

        @pl.when(jnp.logical_and(p >= 4, p < 8))
        def _():
            run(dwi.at[p - 4], 0, 0)

        @pl.when(p == 8)
        def _():
            run(dwo, 0, 0)

    def rest_out(p, run):
        @pl.when(p < 4)
        def _():
            run(o2.at[pl.ds(pl.multiple_of(ROW * p, 32), ROW), pl.ds(pl.multiple_of(384 * c, 128), 384)])

        @pl.when(jnp.logical_and(p >= 4, p < 8))
        def _():
            run(oi.at[:, pl.ds(pl.multiple_of(768 * (p - 4) + 384 * c, 128), 384)])

        @pl.when(p == 8)
        def _():
            run(oo.at[:, pl.ds(pl.multiple_of(384 * c, 128), 384)])

    def fold(p):
        return Fold(where, lambda sel: acc.at[(p,) + sel], fb, fsem, (p,), KEEP_REST)

    def any_first(p):
        return remote(fb[0].at[p], fb[0].at[p], fsem[0].at[p], fsem[1].at[p], c_peer)

    def step(p, name):
        ok_p = jnp.logical_and(p >= 0, p < REST)

        @pl.when(ok_p)
        def _():
            if name == "start":
                rest_src(p, lambda src, r0, c0: first_of(p)(src, r0, c0, True) and None)
            elif name == "over_x":
                pltpu.make_async_copy(acc.at[p], acc.at[p], csem.at[p]).wait()
                fold(p).over_x(any_first(p))
            elif name == "write":
                rest_out(p, lambda view: fold(p).write(view))
            elif name == "drain":
                rest_out(p, lambda view: fold(p).drain(any_first(p), view))
            else:
                getattr(fold(p), name)()

    def gfold(g, w):
        cols = pl.ds(pl.multiple_of(128 * c, 128), 128)
        return Fold(where, lambda sel: dwg.at[(g, w) + sel + (cols,)], gb, gsem, (g, w), KEEP_GROUP)

    def gfirst(g, w):
        cols = pl.ds(pl.multiple_of(128 * (1 - c), 128), 128)
        return remote(dwg.at[g, w, :, :, :, cols], gb[0].at[g, w], gsem[0].at[g, w], gsem[1].at[g, w], c_peer)

    def gstep(g, name):
        for w, o in enumerate((oq, ok, ov)):
            view = o.at[:, pl.ds(pl.multiple_of(GCOLS * g + 128 * c, 128), 128)]
            if name == "start":
                gfirst(g, w).start()
            elif name == "over_x":
                gfold(g, w).over_x(gfirst(g, w))
            elif name == "write":
                gfold(g, w).write(view)
            elif name == "drain":
                gfold(g, w).drain(gfirst(g, w), view)
            else:
                getattr(gfold(g, w), name)()

    stages = (("over_x", 0), ("over_y", 6), ("over_z", 14), ("inside", 19), ("total", 23), ("write", 28))
    pace = 3
    last = pace * (REST + GROUPS - 1) + stages[-1][1] + 1

    def tick(t):
        for name, late in stages:
            n = t - late
            p = lax.div(n, pace)

            @pl.when(jnp.logical_and(n >= 0, jnp.logical_and(lax.rem(n, pace) == 0, p < REST + GROUPS)))
            def _():
                step(p, name)

                @pl.when(p >= REST)
                def _():
                    gstep(p - REST, name)

    loads = [
        pltpu.make_async_copy(src, dst, lsem.at[i])
        for i, (src, dst) in enumerate(
            (
                (q_h, q_v), (k_h, k_v), (v_h, v_v), (c_h, c_v), (dc_h, dc_v), (x_h.at[:, pl.ds(0, own), :], x_v),
                (g1_h, g1_v), (gq_h, gq_v), (gk_h, gk_v), (gv_h, gv_v),
            )
        )
    ]

    def p_copy(it, half):
        g, page = lax.div(it, pages), lax.rem(it, pages)
        return pltpu.make_async_copy(p_h.at[page, pl.ds(4 * g + 2 * half, 2)], pbuf.at[half], ps.at[half])

    for half in range(2):
        p_copy(0, half).start()
    for copy in loads[:5]:
        copy.start()
    for p in range(REST):
        step(p, "start")
    for copy in loads[5:]:
        copy.start()
    for copy in loads[:5]:
        copy.wait()

    low_lane = lax.broadcasted_iota(jnp.int32, (own, PAIR), 1) < HEAD_DIM
    scale = 1.0 / math.sqrt(HEAD_DIM)

    def kv_send(it):
        g, page = lax.div(it, pages), lax.rem(it, pages)
        gcols = pl.ds(pl.multiple_of(g * GCOLS, GCOLS), GCOLS)
        return [
            remote(s_ref.at[page, :, gcols], r_ref.at[page, :, gcols], ks.at[g, page, i], kr.at[g, page, i], c_peer)
            for i, (s_ref, r_ref) in enumerate(((sk, rk), (sv, rv)))
        ]

    def attend(it, half):
        g, page = lax.div(it, pages), lax.rem(it, pages)
        here = pl.ds(pl.multiple_of(page * own, own), own)
        p_copy(it, half).wait()
        cols = pl.ds(pl.multiple_of(g * GCOLS + half * PAIR, PAIR), PAIR)
        qp = q_v[page, :, cols] * jnp.array(scale, BF)
        kp = k_v[page, :, cols]
        kt = kp.T
        vp = v_v[page, :, cols]
        dc = dc_v[page, :, cols]
        prod = (dc.astype(F32) * c_v[page, :, cols].astype(F32)).T
        dk = None
        dv = None
        dqs = []
        for h in range(2):
            keep = low_lane if h == 0 else jnp.logical_not(low_lane)
            feats = slice(h * HEAD_DIM, (h + 1) * HEAD_DIM)
            dch = jnp.where(keep, dc, jnp.zeros_like(dc))
            qh = jnp.where(keep, qp, jnp.zeros_like(qp))
            pt = pbuf[half, h]
            delta = jnp.sum(prod[feats], axis=0, keepdims=True)
            dpt = dot(vp, dch, NT)
            dst = (pt.astype(F32) * (dpt - delta)).astype(BF)
            dvh = dot(pt, dch)
            dkh = dot(dst, qh)
            dk = dkh if dk is None else dk + dkh
            dv = dvh if dv is None else dv + dvh
            dqs.append(dot(kt[feats], dst))
        dq_all[here, cols] = (jnp.concatenate(dqs, axis=0) * scale).T.astype(BF)
        dk_all[here, cols] = dk[:own].astype(BF)
        sk[page, :, cols] = dk[own:].astype(BF)
        dv_all[here, cols] = dv[:own].astype(BF)
        sv[page, :, cols] = dv[own:].astype(BF)

        @pl.when(it + 1 < GROUPS * pages)
        def _():
            p_copy(it + 1, half).start()

    def group_grads(g):
        gcols = pl.ds(pl.multiple_of(g * GCOLS, GCOLS), GCOLS)
        for page in range(pages):
            here = pl.ds(page * own, own)
            for copy in kv_send(g * pages + page):
                copy.wait_recv()
            dk_all[here, gcols] = dk_all[here, gcols] + rk[page, :, gcols]
            dv_all[here, gcols] = dv_all[here, gcols] + rv[page, :, gcols]
        for w, grad in enumerate((dq_all, dk_all, dv_all)):
            value = grad[:, gcols]
            dwg[g, w] = dot(x_t[...], value).astype(BF).reshape(4, 2, ROW, GCOLS)
            if w != 1:
                brow[w : w + 1, gcols] = jnp.sum(value.astype(F32), 0, keepdims=True)
        gstep(g, "start")

    def gx_send(page):
        return remote(gxs.at[page], rgx.at[page], gs.at[page], gr.at[page], x_peer)

    def input_grads(page):
        here = pl.ds(pl.multiple_of(page * own, own), own)
        total = g1_v[page]
        for grad, w in ((dq_all, gq_v), (dk_all, gk_v), (dv_all, gv_v)):
            total = total + dot(grad[here, :], w[...], NT)
        gx[pages * x + page] = total[:blk]
        gxs[page] = total[blk:].astype(BF)
        gx_send(page).start()

    n_it = GROUPS * pages

    def unit(it, carry):
        for half in range(2):

            @pl.when(it < n_it)
            def _():
                attend(it, half)

            if half == 1:

                @pl.when(it < n_it)
                def _():
                    for copy in kv_send(it):
                        copy.start()

            tick(2 * it + half)

        @pl.when(it == 0)
        def _():
            for copy in loads[5:]:
                copy.wait()
            x_t[...] = x_v[...].reshape(pages * own, d).T

        @pl.when(jnp.logical_and(it > 0, jnp.logical_and(lax.rem(it, pages) == 0, it <= n_it)))
        def _():
            group_grads(lax.div(it, pages) - 1)

        page = it - n_it

        @pl.when(jnp.logical_and(page >= 0, page < pages))
        def _():
            input_grads(page)

        return carry

    def vec_send(k):
        to = lax.rem(f + k + 1, 8)
        return remote(pack.at[to], vecin.at[k], vs.at[k], vr.at[k], {"fsdp": to})

    vec_x = lambda: remote(vtot, vx.at[0], us.at[0], ur.at[0], x_peer)
    vec_c = lambda: remote(vx.at[1], vx.at[2], us.at[1], ur.at[1], c_peer)

    def small_pack():
        for i in range(8):
            row = brow[0:1, :] if i == 0 else brow[2:3, :] if i == 1 else gvf[i : i + 1, :]
            for j in range(8):
                pack[j, i : i + 1, :ROW] = row[:, ROW * j : ROW * (j + 1)]
        for j in range(8):
            for i in range(3):
                pack[j, 8 + i : 9 + i, :] = gbin[:, (3 * j + i) * 128 : (3 * j + i + 1) * 128]
        for k in range(7):
            vec_send(k).start()

    def small_sum():
        total = pack[f]
        for k in range(7):
            vec_send(k).wait_recv()
            total = total + vecin[k]
        vtot[...] = total
        vec_x().start()

    def small_pair():
        vec_x().wait_recv()
        vx[1] = vtot[...] + vx[0]
        vec_c().start()

    def all_steps(it, carry):
        unit(it, carry)
        for when, run in ((n_it, small_pack), (n_it + 3, small_sum), (n_it + 6, small_pair)):
            pl.when(it == when)(run)
        return carry

    lax.fori_loop(0, (last + 1) // 2, all_steps, 0)
    for page in range(pages):
        gx_send(page).wait_recv()
        gx[pages * (1 - x) + page] = rgx[page].astype(F32)
    vec_c().wait_recv()
    ovec[...] = vx[1] + vx[2]

    def finish(p, carry):
        step(p, "drain")
        return carry

    lax.fori_loop(0, REST, finish, 0)
    for g in range(GROUPS):
        gstep(g, "drain")
    for it in range(n_it):
        for copy in kv_send(it):
            copy.wait_send()
    for page in range(pages):
        gx_send(page).wait_send()
    for k in range(7):
        vec_send(k).wait_send()
    vec_x().wait_send()
    vec_c().wait_send()


def bwd(q, k, v, ctx, dctx, gm1, xall, ws, p, grads, gvf, gbin, shards):
    pages, own, d = q.shape
    rows, blk = k.shape[1], own // 2
    n = pages * own
    dma = pltpu.SemaphoreType.DMA
    vm = pltpu.VMEM
    sds = jax.ShapeDtypeStruct
    dwo, dwi, dw2 = grads
    views = [dwo.reshape(4, 2, ROW, d), dwi.reshape(-1, 4, 2, ROW, d), dw2.reshape((4, 2) + shards[5])]
    res = call(
        bwd_body,
        (12 * n * d * d + pages * 10 * own * rows * d, sum(16 * g.size for g in grads), 0),
        in_specs=[ANY] * 14 + [VM, VM],
        out_specs=[VM] * 8,
        out_shape=[sds(shape, F32) for shape in shards]
        + [sds((2 * pages, blk, d), F32), sds((16, 128), F32)],
        scratch_shapes=[
            vm((pages, own, d), BF), vm((pages, rows, d), BF), vm((pages, rows, d), BF),
            vm((pages, own, d), BF), vm((pages, own, d), BF), vm((pages, own, d), F32), vm((pages, own, d), BF),
            vm((d, d), BF), vm((d, d), BF), vm((d, d), BF),
            vm((REST, 4, 2, ROW, 384), BF), vm((GROUPS, 3, 4, 2, ROW, GCOLS), BF),
            vm((n, d), BF), vm((n, d), BF), vm((n, d), BF),
            vm((pages, own, d), BF), vm((pages, own, d), BF), vm((pages, own, d), BF), vm((pages, own, d), BF),
            vm((2, 2, rows, own), BF), vm((d, n), BF), vm((pages, blk, d), BF), vm((pages, blk, d), BF),
            vm((8, 16, 128), F32), vm((7, 16, 128), F32), vm((16, 128), F32), vm((3, 16, 128), F32), vm((8, d), F32),
        ]
        + fold_bufs(384, KEEP_REST, REST)
        + fold_bufs(128, KEEP_GROUP, GROUPS, 3)
        + fold_sems(REST)
        + fold_sems(GROUPS, 3)
        + [
            dma((10,)), dma((REST,)), dma((2,)), dma((GROUPS, pages, 2)), dma((GROUPS, pages, 2)),
            dma((pages,)), dma((pages,)), dma((7,)), dma((7,)), dma((2,)), dma((2,)),
        ],
        params=dict(collective_id=1, has_side_effects=True, vmem_limit_bytes=64 << 20),
        name="attention_reduce",
    )(q, k, v, ctx, dctx, gm1, xall, *ws, p, *views, gvf, gbin)
    return res[:6], res[6], res[7]


SWAP_X = [(0, 2), (2, 0), (1, 3), (3, 1)]
SWAP_C = [(0, 1), (1, 0), (2, 3), (3, 2)]


def swap(value, pairs):
    return lax.ppermute(value, "seq", pairs)


def per_device(
    fsdp, inputs, lengths, w_query, b_query, w_key, w_value, b_value, w_out, b_out,
    gain_one, shift_one, w_inner, b_inner, w_outer, b_outer, gain_two, shift_two, cotangent,
):
    pages_all, blk, d = inputs.shape
    pages = pages_all // 2
    s = lax.axis_index("seq")
    x_at = lax.div(s, 2)
    direct = fsdp == 8
    ws = (w_query, w_key, w_value, w_out, w_inner, w_outer)
    shards = [w.shape for w in ws]
    width = b_query.shape[0]
    names = (b_query, b_value, b_out, gain_one, shift_one, b_outer, gain_two, shift_two)

    def pages_of(array, side):
        return lax.dynamic_slice_in_dim(array, side * pages, pages, 0)

    order = jnp.stack([s, s ^ 2, s ^ 1, s ^ 3]).astype(jnp.int32)
    thr = pages_of(lengths, x_at).astype(jnp.int32)[:, None] - order[None, :] * blk
    if direct:
        lanes = tuple(v.reshape(1, -1) for v in names + (b_inner,))
        full, rest = fwd(thr, inputs, cotangent, ws, lanes)
        xall, q, k, v, ctx, p, dctx, gm1, dwo, dwi, dw2, output, gv_ffn, gbin = rest
    else:
        wq, wk, wv, wo, wi, w2 = [lax.all_gather(w, "fsdp", axis=0, tiled=True) for w in ws]
        vec = jnp.concatenate(names + (b_inner,)).reshape(12, width)
        gvec = lax.all_gather(vec, "fsdp", axis=0)
        vec_full = jnp.swapaxes(gvec[:, :8], 0, 1).reshape(8, d).astype(F32)
        bin_full = gvec[:, 8:].reshape(1, -1).astype(F32)

        def own_rows(array):
            other = swap(pages_of(array, 1 - x_at), SWAP_X)
            return jnp.concatenate([pages_of(array, x_at), other], axis=1)

        xown, cown = own_rows(inputs), own_rows(cotangent)
        xall = jnp.concatenate([xown, swap(xown, SWAP_C)], axis=1)
        q, k, v, p, ctx = attn_fwd(thr, xall, wq, wk, wv, vec_full)
    if direct:
        tot, grad_inputs, tvec = bwd(
            q, k, v, ctx, dctx, gm1.reshape(pages, 2 * blk, d), xall, full, p, (dwo, dwi, dw2), gv_ffn, gbin, shards
        )
        small = [tvec[i, :width] for i in range(8)]
        g_bi = tvec[8:11].reshape(-1)
    else:
        out, gm1, dctx, dwo, dwi, dw2, gv_ffn, gbin = ffn(ctx, xall, cown, wo, wi, w2, vec_full, bin_full)
        dq, dk, dk_send, dv, dv_send = attn_bwd(q, k, v, p, ctx, dctx)
        dkr, dvr = swap(dk_send, SWAP_C), swap(dv_send, SWAP_C)
        gx_a, gx_b, dwq, dwk, dwv, gv_proj = proj(xall, dq, dk, dkr, dv, dvr, gm1, wq, wk, wv)
        gv = jnp.concatenate([gv_proj[:2], gv_ffn[2:]], axis=0)
        by_owner = jnp.concatenate(
            [jnp.swapaxes(gv.reshape(8, fsdp, width), 0, 1), gbin.reshape(fsdp, 4, width)], axis=1
        )
        tot = [
            lax.psum(lax.psum_scatter(g, "fsdp", scatter_dimension=0, tiled=True), "seq").astype(F32)
            for g in (dwq, dwk, dwv, dwo, dwi, dw2)
        ]
        tvec = lax.psum(lax.psum_scatter(by_owner, "fsdp", scatter_dimension=0, tiled=True)[0], "seq")

        def joined(mine, other):
            here = lax.dynamic_update_slice_in_dim(
                jnp.zeros((pages_all, blk, d), mine.dtype), mine, x_at * pages, 0
            )
            return lax.dynamic_update_slice_in_dim(here, other, (1 - x_at) * pages, 0)

        output = joined(out[:, :blk], swap(out[:, blk:], SWAP_X))
        grad_inputs = joined(gx_a, swap(gx_b, SWAP_X).astype(F32))
        small = [tvec[i] for i in range(8)]
        g_bi = tvec[8:].reshape(-1)
    g_bq, g_bv, g_bo, g_g1, g_s1, g_bo2, g_g2, g_s2 = small
    t_q, t_k, t_v, t_o, t_i, t_2 = tot
    return (
        output, grad_inputs, t_q, g_bq, t_k, t_v, g_bv, t_o, g_bo, g_g1, g_s1,
        t_i, g_bi, t_2, g_bo2, g_g2, g_s2,
    )


def solution(mesh):
    vec, mat, act = P("fsdp"), P("fsdp", None), P("fsdp", "seq", None)
    return jax.shard_map(
        functools.partial(per_device, mesh.shape["fsdp"]),
        mesh=mesh,
        in_specs=(act, vec, mat, vec, mat, mat, vec, mat, vec, vec, vec, mat, vec, mat, vec, vec, vec, act),
        out_specs=(act, act, mat, vec, mat, mat, vec, mat, vec, vec, vec, mat, vec, mat, vec, vec, vec),
        check_vma=False,
    )
```

```python
import functools
import math

import jax
import jax.numpy as jnp
from jax import lax
from jax.experimental import pallas as pl
from jax.experimental.pallas import tpu as pltpu
from jax.sharding import PartitionSpec as P

HEADS = 12
HEAD_DIM = 64
PAIR = 2 * HEAD_DIM
NEG = -1e30
EPS = 1e-12
BF = jnp.bfloat16
F32 = jnp.float32
MESH = pl.DeviceIdType.MESH
ANY = pl.BlockSpec(memory_space=pl.ANY)
VM = pl.BlockSpec(memory_space=pltpu.VMEM)
CHUNK = 1024
ROW = 96
VMEM_CAP = 60 << 20

NN = (((1,), (0,)), ((), ()))
NT = (((1,), (1,)), ((), ()))
TN = (((0,), (0,)), ((), ()))


def dot(a, b, dims=NN):
    return lax.dot_general(a, b, dims, preferred_element_type=F32)


def call(body, cost, **kw):
    flops, byts, trans = cost
    params = dict(vmem_limit_bytes=VMEM_CAP)
    params.update(kw.pop("params", {}))
    return pl.pallas_call(
        body,
        compiler_params=pltpu.CompilerParams(**params),
        cost_estimate=pl.CostEstimate(
            flops=int(flops), bytes_accessed=int(byts), transcendentals=int(trans)
        ),
        **kw,
    )


def attn_fwd_body(thr, xall, wq, wk, wv, vec, q_o, k_o, v_o, p_o, c_o, bias):
    page = pl.program_id(0)
    x_all = xall[0]
    own = x_all.shape[0] // 2
    query = (dot(x_all[:own], wq[...]) + vec[0:1, :]).astype(BF)
    q_o[0] = query
    k_o[0] = dot(x_all, wk[...]).astype(BF)
    v_o[0] = (dot(x_all, wv[...]) + vec[1:2, :]).astype(BF)
    blk = x_all.shape[0] // 4
    place = lax.broadcasted_iota(jnp.int32, (blk, own), 0)
    for b in range(4):
        bias[b * blk : (b + 1) * blk, :] = jnp.where(place < thr[page, b], 0.0, NEG)
    low_lane = lax.broadcasted_iota(jnp.int32, (own, PAIR), 1) < HEAD_DIM

    def pair(i, carry):
        cols = pl.ds(pl.multiple_of(i * PAIR, PAIR), PAIR)
        qp = q_o[0, :, cols] * jnp.array(1.0 / math.sqrt(HEAD_DIM), BF)
        kp = k_o[0, :, cols]
        vt = v_o[0, :, cols].T
        outs = []
        for h in range(2):
            keep = low_lane if h == 0 else jnp.logical_not(low_lane)
            qh = jnp.where(keep, qp, jnp.zeros_like(qp))
            st = dot(kp, qh, NT) + bias[...]
            top = jnp.max(st, axis=0, keepdims=True)
            ex = jnp.exp(st - top)
            tot = jnp.sum(ex, axis=0, keepdims=True)
            pt = (ex * (1.0 / tot)).astype(BF)
            p_o[0, 2 * i + h] = pt
            outs.append(dot(vt[h * HEAD_DIM : (h + 1) * HEAD_DIM], pt))
        c_o[0, :, cols] = jnp.concatenate(outs, axis=0).T.astype(BF)
        return carry

    lax.fori_loop(0, HEADS // 2, pair, 0)


def attn_fwd(thr, xall, wq, wk, wv, vec):
    pages, rows, d = xall.shape
    own = rows // 2
    const = lambda p, t: (0, 0)
    by_page = lambda p, t: (p, 0, 0)
    one = pl.Buffered(1)
    return call(
        attn_fwd_body,
        (
            pages * (2 * d * d * (own + 2 * rows) + 4 * own * rows * d),
            pages * rows * d * 2 * 4 + 6 * d * d + pages * HEADS * own * rows * 2,
            pages * HEADS * own * rows,
        ),
        grid_spec=pltpu.PrefetchScalarGridSpec(
            num_scalar_prefetch=1,
            grid=(pages,),
            in_specs=[pl.BlockSpec((1, rows, d), by_page)]
            + [pl.BlockSpec((d, d), const, pipeline_mode=one)] * 3
            + [pl.BlockSpec((8, d), const)],
            out_specs=[
                pl.BlockSpec((1, own, d), by_page),
                pl.BlockSpec((1, rows, d), by_page),
                pl.BlockSpec((1, rows, d), by_page),
                pl.BlockSpec((1, HEADS, rows, own), lambda p, t: (p, 0, 0, 0)),
                pl.BlockSpec((1, own, d), by_page),
            ],
            scratch_shapes=[pltpu.VMEM((rows, own), F32)],
        ),
        out_shape=[
            jax.ShapeDtypeStruct((pages, own, d), BF),
            jax.ShapeDtypeStruct((pages, rows, d), BF),
            jax.ShapeDtypeStruct((pages, rows, d), BF),
            jax.ShapeDtypeStruct((pages, HEADS, rows, own), BF),
            jax.ShapeDtypeStruct((pages, own, d), BF),
        ],
        name="attn_fwd",
    )(thr, xall, wq, wk, wv, vec)


def attn_bwd_body(q, k, v, p, ctx, dctx, dq_o, dk_own, dk_oth, dv_own, dv_oth):
    own = q.shape[1]
    low_lane = lax.broadcasted_iota(jnp.int32, (own, PAIR), 1) < HEAD_DIM
    scale = 1.0 / math.sqrt(HEAD_DIM)

    def pair(i, carry):
        cols = pl.ds(pl.multiple_of(i * PAIR, PAIR), PAIR)
        qp = q[0, :, cols] * jnp.array(scale, BF)
        kp = k[0, :, cols]
        kt = kp.T
        vp = v[0, :, cols]
        dc = dctx[0, :, cols]
        prod = (dc.astype(F32) * ctx[0, :, cols].astype(F32)).T
        dk = None
        dv = None
        dqs = []
        for h in range(2):
            keep = low_lane if h == 0 else jnp.logical_not(low_lane)
            feats = slice(h * HEAD_DIM, (h + 1) * HEAD_DIM)
            dch = jnp.where(keep, dc, jnp.zeros_like(dc))
            qh = jnp.where(keep, qp, jnp.zeros_like(qp))
            pt = p[0, 2 * i + h]
            delta = jnp.sum(prod[feats], axis=0, keepdims=True)
            dpt = dot(vp, dch, NT)
            dst = (pt.astype(F32) * (dpt - delta)).astype(BF)
            dvh = dot(pt, dch)
            dkh = dot(dst, qh)
            dk = dkh if dk is None else dk + dkh
            dv = dvh if dv is None else dv + dvh
            dqs.append(dot(kt[feats], dst))
        dq_o[0, :, cols] = (jnp.concatenate(dqs, axis=0) * scale).T.astype(BF)
        dk_own[0, :, cols] = dk[:own].astype(BF)
        dk_oth[0, :, cols] = dk[own:].astype(BF)
        dv_own[0, :, cols] = dv[:own].astype(BF)
        dv_oth[0, :, cols] = dv[own:].astype(BF)
        return carry

    lax.fori_loop(0, HEADS // 2, pair, 0)


def attn_bwd(q, k, v, p, ctx, dctx):
    pages, own, d = q.shape
    rows = k.shape[1]
    by_page = lambda i: (i, 0, 0)
    o = pl.BlockSpec((1, own, d), by_page)
    r = pl.BlockSpec((1, rows, d), by_page)
    return call(
        attn_bwd_body,
        (pages * 10 * own * rows * d, pages * (own * rows * HEADS * 2 + 10 * own * d * 2), 0),
        grid=(pages,),
        in_specs=[o, r, r, pl.BlockSpec((1, HEADS, rows, own), lambda i: (i, 0, 0, 0)), o, o],
        out_specs=[o] * 5,
        out_shape=[jax.ShapeDtypeStruct((pages, own, d), BF)] * 5,
        name="attn_bwd",
    )(q, k, v, p, ctx, dctx)


def normal_parts(v):
    bell = jnp.exp(v * v * -0.5)
    t = 1.0 / (1.0 + jnp.abs(v) * (0.3275911 / math.sqrt(2.0)))
    tail = t * (
        0.127414796 + t * (-0.142248368 + t * (0.7107068705 + t * (-0.7265760135 + t * 0.5307027145)))
    )
    tail = tail * bell
    return jnp.where(v >= 0.0, 1.0 - tail, tail), bell * (1.0 / math.sqrt(2.0 * math.pi))


def row_norm(v):
    centered = v - jnp.mean(v, -1, keepdims=True)
    inv = lax.rsqrt(jnp.mean(centered * centered, -1, keepdims=True) + EPS)
    return centered * inv, inv


def norm_back(e, n, inv):
    return inv * (e - jnp.mean(e, -1, keepdims=True) - n * jnp.mean(e * n, -1, keepdims=True))


def ffn_body(
    ctx, xall, cown, wo, wi_h, w2_h, vec, b_in,
    out, gm1_o, dctx_o, dwo_o, dwi_h, dw2_h, gvec, gbin,
    wi, w2, act, din, dgel, hid, gout, gatt, n1s, h1s, accs, r1s, dwi, dw2, lsem, osem,
):
    n, ff = act.shape
    pages, own, d = ctx.shape

    def cols_of(j):
        return pl.ds(pl.multiple_of(j * CHUNK, CHUNK), CHUNK)

    def loads(j):
        cols = cols_of(j)
        return (
            pltpu.make_async_copy(wi_h.at[:, cols], wi.at[:, cols], lsem.at[0, j]),
            pltpu.make_async_copy(w2_h.at[cols, :], w2.at[cols, :], lsem.at[1, j]),
        )

    def store_w2(j):
        return pltpu.make_async_copy(dw2.at[cols_of(j), :], dw2_h.at[cols_of(j), :], osem.at[0, j])

    def store_wi(j):
        return pltpu.make_async_copy(dwi.at[:, cols_of(j)], dwi_h.at[:, cols_of(j)], osem.at[1, j])

    n_chunks = ff // CHUNK
    for j in range(n_chunks):
        for copy in loads(j):
            copy.start()
    gvec[...] = jnp.zeros_like(gvec)

    def add(row, value):
        gvec[row : row + 1, :] += jnp.sum(value, 0, keepdims=True)

    for p in range(pages):
        r = slice(p * own, (p + 1) * own)
        mid = xall[p].astype(F32) + (dot(ctx[p], wo[...]) + vec[2:3, :])
        n1, r1 = row_norm(mid)
        n1s[r, :] = n1
        r1s[r, :] = jnp.broadcast_to(r1, (own, 128))
        h1 = n1 * vec[3:4, :] + vec[4:5, :]
        h1s[r, :] = h1
        hid[r, :] = h1.astype(BF)
    accs[...] = jnp.zeros_like(accs)

    def up(j, carry):
        cols = cols_of(j)
        for copy in loads(j):
            copy.wait()
        pre = dot(hid[...], wi[:, cols]) + b_in[:, cols]
        big, bell = normal_parts(pre)
        a = (pre * big).astype(BF)
        dgel[:, cols] = (big + pre * bell).astype(BF)
        act[:, cols] = a
        accs[...] += dot(a, w2[cols, :])
        return carry

    lax.fori_loop(0, n_chunks, up, 0)
    for p in range(pages):
        r = slice(p * own, (p + 1) * own)
        mid = h1s[r, :] + (accs[r, :] + vec[5:6, :])
        n2, r2 = row_norm(mid)
        out[p] = (n2 * vec[6:7, :] + vec[7:8, :]).astype(BF)
        cot = cown[p].astype(F32)
        gm2 = norm_back(cot * vec[6:7, :], n2, r2)
        go = gm2.astype(BF)
        gout[r, :] = go
        accs[r, :] = gm2
        add(5, go.astype(F32))
        add(6, cot * n2)
        add(7, cot)

    def down(j, carry):
        cols = cols_of(j)
        di = (dot(gout[...], w2[cols, :], NT) * dgel[:, cols].astype(F32)).astype(BF)
        din[:, cols] = di
        accs[...] += dot(di, wi[:, cols], NT)
        gbin[:, cols] = jnp.sum(di.astype(F32), 0, keepdims=True)
        dw2[cols, :] = dot(act[:, cols], gout[...], TN).astype(BF)
        store_w2(j).start()
        return carry

    lax.fori_loop(0, n_chunks, down, 0)
    for p in range(pages):
        r = slice(p * own, (p + 1) * own)
        gh = accs[r, :]
        n1 = n1s[r, :]
        gm1 = norm_back(gh * vec[3:4, :], n1, r1s[r, 0:1])
        gm1_o[p] = gm1
        ga = gm1.astype(BF)
        gatt[r, :] = ga
        dctx_o[p] = dot(ga, wo[...], NT).astype(BF)
        add(2, ga.astype(F32))
        add(3, gh * n1)
        add(4, gh)
    hid_t = hid[...].T

    def grads(j, carry):
        cols = cols_of(j)
        dwi[:, cols] = dot(hid_t, din[:, cols]).astype(BF)
        store_wi(j).start()
        return carry

    lax.fori_loop(0, n_chunks, grads, 0)
    dwo_o[...] = dot(ctx[...].reshape(n, d), gatt[...], TN).astype(BF)
    for j in range(n_chunks):
        store_w2(j).wait()
        store_wi(j).wait()


def ffn(ctx, xall, cown, wo, wi, w2, vec, b_in):
    pages, own, d = ctx.shape
    ff = wi.shape[1]
    n = pages * own
    sds = jax.ShapeDtypeStruct
    vm = pltpu.VMEM
    dma = pltpu.SemaphoreType.DMA
    return call(
        ffn_body,
        (n * d * (12 * ff + 6 * d), 4 * d * ff * 2 + 12 * n * d * 2, n * ff),
        grid=(1,),
        in_specs=[
            pl.BlockSpec((pages, own, d), lambda i: (0, 0, 0)),
            pl.BlockSpec((pages, own, d), lambda i: (0, 0, 0)),
            VM, VM, ANY, ANY, VM, VM,
        ],
        out_specs=[VM] * 4 + [ANY, ANY, VM, VM],
        out_shape=[
            sds((pages, own, d), BF), sds((pages, own, d), F32), sds((pages, own, d), BF),
            sds((d, d), BF), sds((d, ff), BF), sds((ff, d), BF), sds((8, d), F32), sds((1, ff), F32),
        ],
        scratch_shapes=[
            vm((d, ff), BF), vm((ff, d), BF), vm((n, ff), BF), vm((n, ff), BF), vm((n, ff), BF),
            vm((n, d), BF), vm((n, d), BF), vm((n, d), BF), vm((n, d), F32), vm((n, d), F32),
            vm((n, d), F32), vm((n, 128), F32), vm((d, ff), BF), vm((ff, d), BF),
            dma((2, ff // CHUNK)), dma((2, ff // CHUNK)),
        ],
        params=dict(vmem_limit_bytes=63 << 20),
        name="ffn",
    )(ctx, xall, cown, wo, wi, w2, vec, b_in)


def proj_body(
    xall, dq, dk, dkr, dv, dvr, gm1, wq, wk, wv,
    ga_o, gb_o, dwq_o, dwk_o, dwv_o, gvec, x_all, dq_all, dk_all, dv_all,
):
    page = pl.program_id(0)
    own = xall.shape[1]
    blk = own // 2
    here = pl.ds(pl.multiple_of(page * own, own), own)
    x_all[here, :] = xall[0]
    dq_v = dq[0]
    dk_v = (dk[0].astype(F32) + dkr[0].astype(F32)).astype(BF)
    dv_v = (dv[0].astype(F32) + dvr[0].astype(F32)).astype(BF)
    dq_all[here, :] = dq_v
    dk_all[here, :] = dk_v
    dv_all[here, :] = dv_v
    gx = gm1[0] + dot(dq_v, wq[...], NT) + dot(dk_v, wk[...], NT) + dot(dv_v, wv[...], NT)
    ga_o[0] = gx[:blk]
    gb_o[0] = gx[blk:].astype(BF)

    @pl.when(page == 0)
    def _():
        gvec[...] = jnp.zeros_like(gvec)

    gvec[0:1, :] += jnp.sum(dq_v.astype(F32), 0, keepdims=True)
    gvec[1:2, :] += jnp.sum(dv_v.astype(F32), 0, keepdims=True)

    @pl.when(page == pl.num_programs(0) - 1)
    def _():
        x_t = x_all[...].T
        dwq_o[...] = dot(x_t, dq_all[...]).astype(BF)
        dwk_o[...] = dot(x_t, dk_all[...]).astype(BF)
        dwv_o[...] = dot(x_t, dv_all[...]).astype(BF)


def proj(xall, dq, dk, dkr, dv, dvr, gm1, wq, wk, wv):
    pages, own, d = dq.shape
    blk = own // 2
    n = pages * own
    by_page = lambda p: (p, 0, 0)
    const = lambda p: (0, 0)
    one = pl.Buffered(1)
    half = pl.BlockSpec((1, blk, d), by_page)
    whole = pl.BlockSpec((1, own, d), by_page)
    square = pl.BlockSpec((d, d), const, pipeline_mode=one)
    return call(
        proj_body,
        (12 * n * d * d, 12 * d * d + 16 * n * d, 0),
        grid=(pages,),
        in_specs=[whole] * 7 + [square] * 3,
        out_specs=[half, half] + [square] * 3 + [pl.BlockSpec((8, d), const)],
        out_shape=[
            jax.ShapeDtypeStruct((pages, blk, d), F32),
            jax.ShapeDtypeStruct((pages, blk, d), BF),
        ]
        + [jax.ShapeDtypeStruct((d, d), BF)] * 3
        + [jax.ShapeDtypeStruct((8, d), F32)],
        scratch_shapes=[pltpu.VMEM((n, d), BF)] * 4,
        name="proj_bwd",
    )(xall, dq, dk, dkr, dv, dvr, gm1, wq, wk, wv)


def place():
    f, s = lax.axis_index("fsdp"), lax.axis_index("seq")
    return lax.div(f, 2), lax.rem(f, 2), lax.div(s, 2), lax.rem(s, 2)


def at(z, y, x, c):
    return {"fsdp": 2 * z + y, "seq": 2 * x + c}


def meet(others):
    barrier = pltpu.get_barrier_semaphore()
    for other in others:
        pl.semaphore_signal(barrier, inc=1, device_id=other, device_id_type=MESH)
    pl.semaphore_wait(barrier, len(others))


def remote(src, dst, send, recv, other):
    return pltpu.make_async_remote_copy(
        src_ref=src, dst_ref=dst, send_sem=send, recv_sem=recv,
        device_id=other, device_id_type=MESH,
    )


def begin(copy):
    copy.start()
    return copy


class Spread:
    def __init__(self, where, src, dst, row0, col0, width, sems, key, from0=None):
        self.z, self.y, self.x, self.c = where
        z, y, x, c = where
        zs, zr, fs, ys, yr, xs, xr, cs, cr, lo = sems
        k = key
        cols = pl.ds(pl.multiple_of(col0 + width * c, 128), width)
        origin = pl.ds(pl.multiple_of((col0 if from0 is None else from0) + width * c, 128), width)
        full = pl.ds(row0, ROW)
        mine = pl.ds(pl.multiple_of(row0 + (ROW - YROWS) * x, 16), YROWS)
        lacks = pl.ds(pl.multiple_of(row0 + YROWS * x, 16), ROW - YROWS)
        near, far, across = z + 1 - 2 * lax.rem(z, 2), lax.rem(z + 2, 4), 3 - z
        self.inner = jnp.logical_or(z == 1, z == 2)
        self.local = lambda: pltpu.make_async_copy(src.at[full, origin], dst.at[z, y, full, cols], lo.at[k])

        def send(block, n, target, sem):
            from_ref = src.at[full, origin] if block is None else dst.at[block, y, full, cols]
            b = z if block is None else block
            return remote(from_ref, dst.at[b, y, full, cols], sem, zr.at[k + (n,)], at(target, y, x, c))

        self.a = lambda: send(None, 0, near, zs.at[k + (0,)])
        self.b = lambda: send(None, 1, far, zs.at[k + (1,)])
        self.d = lambda: send(None, 2, across, zs.at[k + (2,)])
        self.fwd = lambda: send(far, 2, near, fs.at[k])
        yv = lambda: dst.at[:, y, mine, cols]
        self.ycopy = lambda: remote(yv(), yv(), ys.at[k], yr.at[k], at(z, 1 - y, x, c))
        xv = lambda: dst.at[:, 1 - y, lacks, cols]
        self.xcopy = lambda: remote(xv(), xv(), xs.at[k], xr.at[k], at(z, y, 1 - x, c))
        cv = lambda: dst.at[:, :, full, cols]
        self.ccopy = lambda: remote(cv(), cv(), cs.at[k], cr.at[k], at(z, y, x, 1 - c))

    def along_z(self):
        self.local().start()
        self.b().start()
        self.a().start()

        @pl.when(self.inner)
        def _():
            self.d().start()

    def forward(self):
        self.b().wait_recv()

        @pl.when(self.inner)
        def _():
            self.fwd().start()

    def along_y(self):
        self.a().wait_recv()
        self.d().wait_recv()
        self.local().wait()
        self.ycopy().start()

    def along_x(self):
        self.ycopy().wait_recv()
        self.xcopy().start()

    def to_core(self):
        self.xcopy().wait_recv()
        self.ccopy().start()

    def arrive(self):
        self.ccopy().wait_recv()

    def drain(self):
        self.a().wait_send()
        self.b().wait_send()

        @pl.when(self.inner)
        def _():
            self.d().wait_send()
            self.fwd().wait_send()

        self.ycopy().wait_send()
        self.xcopy().wait_send()
        self.ccopy().wait_send()


def spread_sems(*lead):
    dma = pltpu.SemaphoreType.DMA
    return [dma(lead + (3,)), dma(lead + (3,))] + [dma(lead)] * 8


GROUPS = 3
GCOLS = 256
REST = 9
EARLY = 3
YROWS = 64


def fwd_body(
    lens, x_in, cot, wq, wk, wv, wo, wi, w2, *refs,
):
    smalls = refs[:9]
    (
        gq_h, gk_h, gv_h, xall_h, q_h, k_h, v_h, c_h, p_o, dctx_h, gm1_h, dwo_h, dwi_h, dw2_h, fin_out, gvs, gbin,
    ) = refs[9:26]
    (
        gq, gk, gv, go, gi, g2, xall, q_o, k_o, v_o, c_o, cown, bias, pbuf, vpk, gvec, vec, b_in,
        act, dd, hid, gout, gatt, dctx, n1s, accs, r1s, dw2_s, dwi_s,
    ) = refs[26:55]
    qs, rs = refs[55:65], refs[65:75]
    asend, arecv, aloc, vs, vr, ps, outs_sem, grad_sem = refs[75:]
    z, y, x, c = where = place()
    f = 2 * z + y
    pages, rows = xall.shape[0], xall.shape[1]
    own, blk = rows // 2, rows // 4
    width = smalls[0].shape[-1]
    for i in range(8):
        vpk[i : i + 1, :width] = smalls[i][...].astype(F32).reshape(1, width)
    for i in range(3):
        vpk[8 + i : 9 + i, :] = smalls[8][128 * i : 128 * (i + 1)].astype(F32).reshape(1, 128)
    gvec[f] = vpk[...]
    x_peer, c_peer = at(z, y, 1 - x, c), at(z, y, x, 1 - c)
    meet([{"fsdp": lax.rem(f + k + 1, 8)} for k in range(7)] + [x_peer, c_peer])

    groups = [
        [Spread(where, src, dst, 0, GCOLS * g, GCOLS // 2, qs, (g, w)) for w, (src, dst) in enumerate(((wq, gq), (wk, gk), (wv, gv)))]
        for g in range(GROUPS)
    ]

    def each(g, step):
        for part in groups[g]:
            getattr(part, step)()

    mine, sent = pl.ds(pages * x, pages), pl.ds(pages * (1 - x), pages)

    def band(b):
        return xall.at[:, pl.ds(blk * b, blk), :]

    to_b = remote(x_in.at[sent], band(1), asend.at[0], arecv.at[0], x_peer)
    to_c = remote(x_in.at[mine], band(2), asend.at[1], arecv.at[1], c_peer)
    to_d = remote(band(1), band(3), asend.at[2], arecv.at[2], c_peer)
    cot_b = remote(cot.at[sent], cown.at[:, pl.ds(blk, blk), :], asend.at[3], arecv.at[3], x_peer)
    keep_x = pltpu.make_async_copy(x_in.at[mine], band(0), aloc.at[0])
    keep_c = pltpu.make_async_copy(cot.at[mine], cown.at[:, pl.ds(0, blk), :], aloc.at[1])
    vecs = [
        remote(vpk, gvec.at[f], vs.at[k], vr.at[k], {"fsdp": lax.rem(f + k + 1, 8)}) for k in range(7)
    ]
    def rest(p, step):
        def run(src, dst, row0, col0, from0=None):
            getattr(Spread(where, src, dst, row0, col0, 384, rs, (p,), from0), step)()

        @pl.when(p == 0)
        def _():
            run(wo, go, 0, 0)

        @pl.when(jnp.logical_and(p >= 1, p < 5))
        def _():
            run(wi, gi.at[p - 1], 0, 0, 768 * (p - 1))

        @pl.when(jnp.logical_and(p >= 5, p < REST))
        def _():
            run(w2, g2, ROW * (p - 5), 0)

    to_b.start()
    each(0, "along_z")
    keep_x.start()
    to_c.start()
    for copy in vecs:
        copy.start()
    place_row = lax.broadcasted_iota(jnp.int32, (blk, own), 0)
    for page in range(pages):
        for b in range(4):
            side = x if b % 2 == 0 else 1 - x
            core = c if b < 2 else 1 - c
            limit = lens[pages * x + page] - (2 * side + core) * blk
            bias[page, b * blk : (b + 1) * blk, :] = jnp.where(place_row < limit, 0.0, NEG)
    each(0, "forward")
    each(1, "along_z")
    each(0, "along_y")
    each(1, "forward")
    each(2, "along_z")
    each(1, "along_y")
    each(0, "along_x")
    each(2, "forward")
    for p in range(EARLY):
        rest(p, "along_z")
    each(2, "along_y")
    to_b.wait_recv()
    to_d.start()
    each(0, "to_core")
    each(1, "along_x")
    for copy in vecs:
        copy.wait_recv()
    for i in range(8):
        vec[i : i + 1, :] = jnp.concatenate([gvec[j, i : i + 1, :width] for j in range(8)], axis=1)
    for j in range(8):
        for i in range(3):
            b_in[:, (3 * j + i) * 128 : (3 * j + i + 1) * 128] = gvec[j, 8 + i : 9 + i, :]
    keep_c.start()
    keep_x.wait()
    to_c.wait_recv()
    to_d.wait_recv()
    each(0, "arrive")

    low_lane = lax.broadcasted_iota(jnp.int32, (own, PAIR), 1) < HEAD_DIM
    stages = (("along_z", 1 - 8 * EARLY // 3), ("forward", 0), ("along_y", 3), ("along_x", 8), ("to_core", 13))

    def tick(t):
        for step, late in stages:
            n = t - late
            p = lax.div(3 * n + 7, 8)

            @pl.when(jnp.logical_and(n >= 0, lax.div(8 * p, 3) == n))
            def _():
                if step == "along_z":
                    pl.when(p >= EARLY)(lambda: rest(p, step))
                else:
                    rest(p, step)

    def p_copy(page, pair, slot):
        return pltpu.make_async_copy(pbuf.at[slot], p_o.at[page, pl.ds(2 * pair, 2)], ps.at[slot])

    def unit(it, carry):
        g, page = lax.div(it, pages), lax.rem(it, pages)

        @pl.when(it == 0)
        def _():
            each(2, "along_x")
            each(1, "to_core")

        @pl.when(it == 1)
        def _():
            each(2, "to_core")
            cot_b.start()

        @pl.when(it == pages)
        def _():
            each(1, "arrive")

        @pl.when(it == 2 * pages)
        def _():
            each(2, "arrive")

        gcols = pl.ds(pl.multiple_of(g * GCOLS, GCOLS), GCOLS)
        x_all = xall[page]
        d = x_all.shape[1]
        query = (dot(x_all[:own], gq[:, :, :, gcols].reshape(d, GCOLS)) + vec[0:1, gcols]).astype(BF)
        keys = dot(x_all, gk[:, :, :, gcols].reshape(d, GCOLS)).astype(BF)
        vals = (dot(x_all, gv[:, :, :, gcols].reshape(d, GCOLS)) + vec[1:2, gcols]).astype(BF)
        q_o[page, :, gcols] = query
        k_o[page, :, gcols] = keys
        v_o[page, :, gcols] = vals
        for half in range(2):
            lanes = slice(half * PAIR, (half + 1) * PAIR)
            pair = 2 * g + half

            @pl.when(it > 0)
            def _():
                p_copy(page, pair, half).wait()

            qp = query[:, lanes] * jnp.array(1.0 / math.sqrt(HEAD_DIM), BF)
            kp = keys[:, lanes]
            vt = vals[:, lanes].T
            outs = []
            for h in range(2):
                keep = low_lane if h == 0 else jnp.logical_not(low_lane)
                qh = jnp.where(keep, qp, jnp.zeros_like(qp))
                st = dot(kp, qh, NT) + bias[page]
                top = jnp.max(st, axis=0, keepdims=True)
                ex = jnp.exp(st - top)
                tot = jnp.sum(ex, axis=0, keepdims=True)
                pt = (ex * (1.0 / tot)).astype(BF)
                pbuf[half, h] = pt
                outs.append(dot(vt[h * HEAD_DIM : (h + 1) * HEAD_DIM], pt))
            p_copy(page, pair, half).start()
            cols = pl.ds(pl.multiple_of(pair * PAIR, PAIR), PAIR)
            c_o[page, :, cols] = jnp.concatenate(outs, axis=0).T.astype(BF)
            tick(2 * it + half)
        return carry

    lax.fori_loop(0, GROUPS * pages, unit, 0)
    n_ticks = 2 * GROUPS * pages
    stores = [
        pltpu.make_async_copy(src, dst, outs_sem.at[i])
        for i, (src, dst) in enumerate(
            ((q_o, q_h), (k_o, k_h), (v_o, v_h), (c_o, c_h), (xall, xall_h), (gq, gq_h), (gk, gk_h), (gv, gv_h))
        )
    ]
    for copy in stores:
        copy.start()
    for half in range(2):
        p_copy(0, 0, half).wait()

    d = xall.shape[2]
    n_chunks = gi.shape[0]
    last = 8 * (REST - 1) // 3 + stages[-1][1] + 1
    gvs[...] = jnp.zeros_like(gvs)

    def add(row, value):
        gvs[row : row + 1, :] += jnp.sum(value, 0, keepdims=True)

    def square(ref):
        return ref[...].reshape(d, d)

    rest(0, "arrive")
    for page in range(pages):
        r = slice(page * own, (page + 1) * own)
        mid = xall[page, :own].astype(F32) + (dot(c_o[page], square(go)) + vec[2:3, :])
        n1, r1 = row_norm(mid)
        n1s[r, :] = n1
        r1s[r, :] = jnp.broadcast_to(r1, (own, 128))
        hid[r, :] = (n1 * vec[3:4, :] + vec[4:5, :]).astype(BF)

    def ticks(lo, hi):
        lax.fori_loop(lo, hi, lambda t, carry: (tick(t), carry)[1], 0)

    def up(j, carry):
        ticks(n_ticks + 3 * j, jnp.minimum(n_ticks + 3 * j + 3, last))
        rest(j + 1, "arrive")
        cols = pl.ds(pl.multiple_of(j * d, d), d)
        pre = dot(hid[...], gi[j].reshape(d, d)) + b_in[:, cols]
        big, bell = normal_parts(pre)
        act[:, cols] = (pre * big).astype(BF)
        dd[:, cols] = (big + pre * bell).astype(BF)
        return carry

    lax.fori_loop(0, n_chunks, up, 0)
    ticks(n_ticks + 3 * n_chunks, last)
    for p in range(5, REST):
        rest(p, "arrive")
    keep_c.wait()
    cot_b.wait_recv()
    stores[0].wait()

    def w2_rows(j):
        return g2[j].reshape(d, d)

    accs[...] = jnp.zeros_like(accs)

    def outer(j, carry):
        cols = pl.ds(pl.multiple_of(j * d, d), d)
        accs[...] += dot(act[:, cols], w2_rows(j))
        return carry

    lax.fori_loop(0, n_chunks, outer, 0)
    for page in range(pages):
        r = slice(page * own, (page + 1) * own)
        h1 = n1s[r, :] * vec[3:4, :] + vec[4:5, :]
        mid = h1 + (accs[r, :] + vec[5:6, :])
        n2, r2 = row_norm(mid)
        q_o[page] = (n2 * vec[6:7, :] + vec[7:8, :]).astype(BF)
        ct = cown[page].astype(F32)
        gm2 = norm_back(ct * vec[6:7, :], n2, r2)
        gob = gm2.astype(BF)
        gout[r, :] = gob
        accs[r, :] = gm2
        add(5, gob.astype(F32))
        add(6, ct * n2)
        add(7, ct)
    keep_out = pltpu.make_async_copy(q_o.at[:, pl.ds(0, blk), :], fin_out.at[mine], aloc.at[2])
    back_out = remote(q_o.at[:, pl.ds(blk, blk), :], fin_out.at[mine], asend.at[4], arecv.at[4], x_peer)
    keep_out.start()
    back_out.start()

    def grad_store(j, i):
        slot = lax.rem(j, 2)
        return pltpu.make_async_copy((dw2_s, dwi_s)[i].at[slot], (dw2_h, dwi_h)[i].at[j], grad_sem.at[i, slot])

    def down(j, carry):
        cols = pl.ds(pl.multiple_of(j * d, d), d)
        di = (dot(gout[...], w2_rows(j), NT) * dd[:, cols].astype(F32)).astype(BF)
        dd[:, cols] = di
        accs[...] += dot(di, gi[j].reshape(d, d), NT)
        gbin[:, cols] = jnp.sum(di.astype(F32), 0, keepdims=True)

        @pl.when(j >= 2)
        def _():
            grad_store(j, 0).wait()
            grad_store(j, 1).wait()

        slot = lax.rem(j, 2)
        dw2_s[slot] = dot(act[:, cols], gout[...], TN).astype(BF)
        dwi_s[slot] = dot(hid[...], di, TN).astype(BF)
        grad_store(j, 0).start()
        grad_store(j, 1).start()
        return carry

    lax.fori_loop(0, n_chunks, down, 0)
    for page in range(pages):
        r = slice(page * own, (page + 1) * own)
        gh = accs[r, :]
        n1 = n1s[r, :]
        gm1 = norm_back(gh * vec[3:4, :], n1, r1s[r, 0:1])
        accs[r, :] = gm1
        ga = gm1.astype(BF)
        gatt[r, :] = ga
        dctx[page] = dot(ga, square(go), NT).astype(BF)
        add(2, ga.astype(F32))
        add(3, gh * n1)
        add(4, gh)
    tail = [
        pltpu.make_async_copy(accs, gm1_h, outs_sem.at[8]),
        pltpu.make_async_copy(dctx, dctx_h, outs_sem.at[9]),
        pltpu.make_async_copy(hid, dwo_h, outs_sem.at[10]),
    ]
    tail[0].start()
    tail[1].start()
    hid[...] = dot(c_o[...].reshape(pages * own, d), gatt[...], TN).astype(BF)
    tail[2].start()
    for j in range(n_chunks - 2, n_chunks):
        grad_store(j, 0).wait()
        grad_store(j, 1).wait()

    def finish(p, carry):
        rest(p, "drain")
        return carry

    lax.fori_loop(0, REST, finish, 0)
    for g in range(GROUPS):
        each(g, "drain")
    for copy in vecs + [to_b, to_c, to_d, cot_b]:
        copy.wait_send()
    for copy in stores[1:] + tail + [keep_out]:
        copy.wait()
    back_out.wait()


def fwd(lens, x_in, cot, ws, smalls):
    pages_all, blk, d = x_in.shape
    pages, own, rows = pages_all // 2, 2 * blk, 4 * blk
    n = pages * own
    dma = pltpu.SemaphoreType.DMA
    sds = jax.ShapeDtypeStruct
    vm = pltpu.VMEM
    ff = ws[4].shape[1]
    quarter = (4, 2, ROW, d)
    res = call(
        fwd_body,
        (n * d * (12 * ff + 12 * d), sum(16 * w.size for w in ws), pages * HEADS * own * rows),
        in_specs=[pl.BlockSpec(memory_space=pltpu.SMEM)] + [ANY] * 5 + [VM] * 12,
        out_specs=[ANY] * 15 + [VM, VM],
        out_shape=[sds(quarter, BF)] * 3
        + [
            sds((pages, rows, d), BF),
            sds((pages, own, d), BF), sds((pages, rows, d), BF), sds((pages, rows, d), BF), sds((pages, own, d), BF),
            sds((pages, HEADS, rows, own), BF),
            sds((pages, own, d), BF), sds((n, d), F32), sds((d, d), BF),
            sds((ff // d, d, d), BF), sds((ff // d, d, d), BF), sds((pages_all, blk, d), BF),
            sds((8, d), F32), sds((1, ff), F32),
        ],
        scratch_shapes=[
            vm(quarter, BF), vm(quarter, BF), vm(quarter, BF), vm(quarter, BF),
            vm((ff // d,) + quarter, BF), vm((4, 2, ff // 8, d), BF),
            vm((pages, rows, d), BF), vm((pages, own, d), BF), vm((pages, rows, d), BF), vm((pages, rows, d), BF),
            vm((pages, own, d), BF), vm((pages, own, d), BF), vm((pages, rows, own), F32), vm((2, 2, rows, own), BF),
            vm((16, 128), F32), vm((8, 16, 128), F32), vm((8, d), F32), vm((1, ff), F32),
            vm((n, ff), BF), vm((n, ff), BF), vm((n, d), BF), vm((n, d), BF), vm((n, d), BF), vm((pages, own, d), BF),
            vm((n, d), F32), vm((n, d), F32), vm((n, 128), F32), vm((2, d, d), BF), vm((2, d, d), BF),
        ]
        + spread_sems(GROUPS, 3)
        + spread_sems(REST)
        + [dma((5,)), dma((5,)), dma((3,)), dma((7,)), dma((7,)), dma((2,)), dma((11,)), dma((2, 2))],
        params=dict(collective_id=0, has_side_effects=True, vmem_limit_bytes=64 << 20),
        name="gather_forward",
    )(lens, x_in, cot, *ws, *smalls)
    full = [r.reshape(d, d) for r in res[:3]]
    return full, res[3:]


class Fold:
    def __init__(self, where, acc, bufs, sems, key, keep):
        self.z, self.y, self.x, self.c = where
        self.acc, self.key = acc, key
        give = ROW - keep
        self.rc, self.rx, self.ry, self.rz, self.fin, self.rf = [b.at[key] for b in bufs]
        self.cs, self.cr, self.xs, self.xr, self.ys, self.yr, self.zs, self.zr, self.fs, self.fr, self.es, self.er = sems
        z = self.z
        self.near, self.far, self.across = z + 1 - 2 * lax.rem(z, 2), lax.rem(z + 2, 4), 3 - z
        self.inner = jnp.logical_or(z == 1, z == 2)
        self.outer = jnp.logical_not(self.inner)
        self.keep = pl.ds(pl.multiple_of(give * self.x, 16), keep)
        self.give = pl.ds(pl.multiple_of(keep * (1 - self.x), 16), give)
        self.gain = pl.ds(pl.multiple_of(keep * self.x, 16), give)

    def part(self, *sel):
        return self.acc(sel)

    def xcopy(self):
        return remote(
            self.part(ALL, 1 - self.y, self.give), self.rx, self.xs.at[self.key], self.xr.at[self.key],
            at(self.z, self.y, 1 - self.x, self.c),
        )

    def ycopy(self):
        return remote(
            self.part(ALL, 1 - self.y, self.keep), self.ry, self.ys.at[self.key], self.yr.at[self.key],
            at(self.z, 1 - self.y, self.x, self.c),
        )

    def zcopy(self, block, target, slot):
        return remote(
            self.part(block, self.y, ALL), self.rz.at[slot], self.zs.at[self.key + (slot,)],
            self.zr.at[self.key + (slot,)], at(target, self.y, self.x, self.c),
        )

    def a(self):
        return self.zcopy(self.near, self.near, 0)

    def b(self):
        return self.zcopy(self.far, self.far, 1)

    def d(self):
        return self.zcopy(self.across, self.across, 2)

    def f(self):
        return self.zcopy(self.across, self.near, 3)

    def fcopy(self):
        return remote(
            self.fin, self.rf, self.fs.at[self.key], self.fr.at[self.key],
            at(self.z, self.y, 1 - self.x, self.c),
        )

    def over_x(self, first):
        first.wait_recv()
        whole = self.part(ALL, ALL, ALL)
        whole[...] = whole[...] + self.rc[...]
        self.xcopy().start()

    def over_y(self):
        self.xcopy().wait_recv()
        rows = self.part(ALL, 1 - self.y, self.gain)
        rows[...] = rows[...] + self.rx[...]
        self.ycopy().start()

    def over_z(self):
        self.ycopy().wait_recv()
        rows = self.part(ALL, self.y, self.keep)
        rows[...] = rows[...] + self.ry[...]
        self.a().start()

        @pl.when(self.outer)
        def _():
            self.f().start()
            self.b().start()

        @pl.when(self.inner)
        def _():
            self.d().start()

    def inside(self):
        @pl.when(self.inner)
        def _():
            self.f().wait_recv()
            rows = self.part(self.far, self.y, ALL)
            rows[...] = rows[...] + self.rz[3]
            self.b().start()

    def total(self):
        self.a().wait_recv()
        self.b().wait_recv()
        own = self.part(self.z, self.y, ALL)

        @pl.when(self.outer)
        def _():
            self.fin[...] = (own[...].astype(F32) + self.rz[0].astype(F32) + self.rz[1].astype(F32)).astype(BF)

        @pl.when(self.inner)
        def _():
            self.d().wait_recv()
            self.fin[...] = (
                own[...].astype(F32) + self.rz[0].astype(F32) + self.rz[1].astype(F32) + self.rz[2].astype(F32)
            ).astype(BF)

        self.fcopy().start()

    def ecopy(self, view):
        return remote(view, view, self.es.at[self.key], self.er.at[self.key], at(self.z, self.y, self.x, 1 - self.c))

    def write(self, view):
        self.fcopy().wait_recv()
        view[...] = self.fin[...].astype(F32) + self.rf[...].astype(F32)
        self.ecopy(view).start()

    def drain(self, first, view):
        self.ecopy(view).wait_recv()
        first.wait_send()
        self.xcopy().wait_send()
        self.ycopy().wait_send()
        self.a().wait_send()
        self.b().wait_send()

        @pl.when(self.outer)
        def _():
            self.f().wait_send()

        @pl.when(self.inner)
        def _():
            self.d().wait_send()

        self.fcopy().wait_send()
        self.ecopy(view).wait_send()


ALL = slice(None)
KEEP_REST = 64
KEEP_GROUP = 80


def fold_sems(*lead):
    dma = pltpu.SemaphoreType.DMA
    return [dma(lead)] * 6 + [dma(lead + (4,))] * 2 + [dma(lead)] * 4


def fold_bufs(width, keep, *lead):
    return [
        pltpu.VMEM(lead + shape, BF)
        for shape in (
            (4, 2, ROW, width), (4, ROW - keep, width), (4, keep, width), (4, ROW, width), (ROW, width), (ROW, width),
        )
    ]


def bwd_body(
    q_h, k_h, v_h, c_h, dc_h, g1_h, x_h, gq_h, gk_h, gv_h, p_h, dwo, dwi, dw2, gvf, gbin,
    oq, ok, ov, oo, oi, o2, gx, ovec,
    *refs,
):
    q_v, k_v, v_v, c_v, dc_v, g1_v, x_v, gq_v, gk_v, gv_v = refs[:10]
    (acc, dwg, dq_all, dk_all, dv_all, rk, rv, sk, sv, pbuf, x_t, gxs, rgx, pack, vecin, vtot, vx, brow) = refs[10:28]
    fb, gb = refs[28:34], refs[34:40]
    fsem, gsem = refs[40:52], refs[52:64]
    lsem, csem, ps, ks, kr, gs, gr, vs, vr, us, ur = refs[64:]
    z, y, x, c = where = place()
    f = 2 * z + y
    pages, own, d = q_h.shape
    blk = own // 2
    rows = k_h.shape[1]
    x_peer, c_peer = at(z, y, 1 - x, c), at(z, y, x, 1 - c)
    meet([{"fsdp": lax.rem(f + k + 1, 8)} for k in range(7)] + [x_peer, c_peer])

    def first_of(p):
        def run(src, row0, col0, go):
            rr = pl.ds(row0, ROW)
            mine = src.at[:, :, rr, pl.ds(pl.multiple_of(col0 + 384 * c, 128), 384)]
            other = src.at[:, :, rr, pl.ds(pl.multiple_of(col0 + 384 * (1 - c), 128), 384)]
            copy = pltpu.make_async_copy(mine, acc.at[p], csem.at[p])
            send = remote(other, fb[0].at[p], fsem[0].at[p], fsem[1].at[p], c_peer)
            if go:
                copy.start()
                send.start()
            return copy, send

        return run

    def rest_src(p, run):
        @pl.when(p < 4)
        def _():
            run(dw2, ROW * p, 0)

        @pl.when(jnp.logical_and(p >= 4, p < 8))
        def _():
            run(dwi.at[p - 4], 0, 0)

        @pl.when(p == 8)
        def _():
            run(dwo, 0, 0)

    def rest_out(p, run):
        @pl.when(p < 4)
        def _():
            run(o2.at[pl.ds(pl.multiple_of(ROW * p, 32), ROW), pl.ds(pl.multiple_of(384 * c, 128), 384)])

        @pl.when(jnp.logical_and(p >= 4, p < 8))
        def _():
            run(oi.at[:, pl.ds(pl.multiple_of(768 * (p - 4) + 384 * c, 128), 384)])

        @pl.when(p == 8)
        def _():
            run(oo.at[:, pl.ds(pl.multiple_of(384 * c, 128), 384)])

    def fold(p):
        return Fold(where, lambda sel: acc.at[(p,) + sel], fb, fsem, (p,), KEEP_REST)

    def any_first(p):
        return remote(fb[0].at[p], fb[0].at[p], fsem[0].at[p], fsem[1].at[p], c_peer)

    def step(p, name):
        ok_p = jnp.logical_and(p >= 0, p < REST)

        @pl.when(ok_p)
        def _():
            if name == "start":
                rest_src(p, lambda src, r0, c0: first_of(p)(src, r0, c0, True) and None)
            elif name == "over_x":
                pltpu.make_async_copy(acc.at[p], acc.at[p], csem.at[p]).wait()
                fold(p).over_x(any_first(p))
            elif name == "write":
                rest_out(p, lambda view: fold(p).write(view))
            elif name == "drain":
                rest_out(p, lambda view: fold(p).drain(any_first(p), view))
            else:
                getattr(fold(p), name)()

    def gfold(g, w):
        cols = pl.ds(pl.multiple_of(128 * c, 128), 128)
        return Fold(where, lambda sel: dwg.at[(g, w) + sel + (cols,)], gb, gsem, (g, w), KEEP_GROUP)

    def gfirst(g, w):
        cols = pl.ds(pl.multiple_of(128 * (1 - c), 128), 128)
        return remote(dwg.at[g, w, :, :, :, cols], gb[0].at[g, w], gsem[0].at[g, w], gsem[1].at[g, w], c_peer)

    def gstep(g, name):
        for w, o in enumerate((oq, ok, ov)):
            view = o.at[:, pl.ds(pl.multiple_of(GCOLS * g + 128 * c, 128), 128)]
            if name == "start":
                gfirst(g, w).start()
            elif name == "over_x":
                gfold(g, w).over_x(gfirst(g, w))
            elif name == "write":
                gfold(g, w).write(view)
            elif name == "drain":
                gfold(g, w).drain(gfirst(g, w), view)
            else:
                getattr(gfold(g, w), name)()

    stages = (("over_x", 0), ("over_y", 3), ("over_z", 7), ("inside", 10), ("total", 13), ("write", 16))
    pace = 2
    last = pace * (REST + GROUPS - 1) + stages[-1][1] + 1

    def tick(t):
        for name, late in stages:
            n = t - late
            p = lax.div(n, pace)

            @pl.when(jnp.logical_and(n >= 0, jnp.logical_and(lax.rem(n, pace) == 0, p < REST + GROUPS)))
            def _():
                step(p, name)

                @pl.when(p >= REST)
                def _():
                    gstep(p - REST, name)

    loads = [
        pltpu.make_async_copy(src, dst, lsem.at[i])
        for i, (src, dst) in enumerate(
            (
                (q_h, q_v), (k_h, k_v), (v_h, v_v), (c_h, c_v), (dc_h, dc_v), (x_h.at[:, pl.ds(0, own), :], x_v),
                (g1_h, g1_v), (gq_h, gq_v), (gk_h, gk_v), (gv_h, gv_v),
            )
        )
    ]

    def p_copy(it, half):
        g, page = lax.div(it, pages), lax.rem(it, pages)
        return pltpu.make_async_copy(p_h.at[page, pl.ds(4 * g + 2 * half, 2)], pbuf.at[half], ps.at[half])

    for half in range(2):
        p_copy(0, half).start()
    for copy in loads[:5]:
        copy.start()
    for p in range(REST):
        step(p, "start")
    for copy in loads[5:]:
        copy.start()
    for copy in loads[:5]:
        copy.wait()

    low_lane = lax.broadcasted_iota(jnp.int32, (own, PAIR), 1) < HEAD_DIM
    scale = 1.0 / math.sqrt(HEAD_DIM)

    def kv_send(it):
        g, page = lax.div(it, pages), lax.rem(it, pages)
        gcols = pl.ds(pl.multiple_of(g * GCOLS, GCOLS), GCOLS)
        return [
            remote(s_ref.at[page, :, gcols], r_ref.at[page, :, gcols], ks.at[g, page, i], kr.at[g, page, i], c_peer)
            for i, (s_ref, r_ref) in enumerate(((sk, rk), (sv, rv)))
        ]

    def attend(it, half):
        g, page = lax.div(it, pages), lax.rem(it, pages)
        here = pl.ds(pl.multiple_of(page * own, own), own)
        p_copy(it, half).wait()
        cols = pl.ds(pl.multiple_of(g * GCOLS + half * PAIR, PAIR), PAIR)
        qp = q_v[page, :, cols] * jnp.array(scale, BF)
        kp = k_v[page, :, cols]
        kt = kp.T
        vp = v_v[page, :, cols]
        dc = dc_v[page, :, cols]
        prod = (dc.astype(F32) * c_v[page, :, cols].astype(F32)).T
        dk = None
        dv = None
        dqs = []
        for h in range(2):
            keep = low_lane if h == 0 else jnp.logical_not(low_lane)
            feats = slice(h * HEAD_DIM, (h + 1) * HEAD_DIM)
            dch = jnp.where(keep, dc, jnp.zeros_like(dc))
            qh = jnp.where(keep, qp, jnp.zeros_like(qp))
            pt = pbuf[half, h]
            delta = jnp.sum(prod[feats], axis=0, keepdims=True)
            dpt = dot(vp, dch, NT)
            dst = (pt.astype(F32) * (dpt - delta)).astype(BF)
            dvh = dot(pt, dch)
            dkh = dot(dst, qh)
            dk = dkh if dk is None else dk + dkh
            dv = dvh if dv is None else dv + dvh
            dqs.append(dot(kt[feats], dst))
        dq_all[here, cols] = (jnp.concatenate(dqs, axis=0) * scale).T.astype(BF)
        dk_all[here, cols] = dk[:own].astype(BF)
        sk[page, :, cols] = dk[own:].astype(BF)
        dv_all[here, cols] = dv[:own].astype(BF)
        sv[page, :, cols] = dv[own:].astype(BF)

        @pl.when(it + 1 < GROUPS * pages)
        def _():
            p_copy(it + 1, half).start()

    def group_grads(g):
        gcols = pl.ds(pl.multiple_of(g * GCOLS, GCOLS), GCOLS)
        for page in range(pages):
            here = pl.ds(page * own, own)
            for copy in kv_send(g * pages + page):
                copy.wait_recv()
            dk_all[here, gcols] = dk_all[here, gcols] + rk[page, :, gcols]
            dv_all[here, gcols] = dv_all[here, gcols] + rv[page, :, gcols]
        for w, grad in enumerate((dq_all, dk_all, dv_all)):
            value = grad[:, gcols]
            dwg[g, w] = dot(x_t[...], value).astype(BF).reshape(4, 2, ROW, GCOLS)
            if w != 1:
                brow[w : w + 1, gcols] = jnp.sum(value.astype(F32), 0, keepdims=True)
        gstep(g, "start")

    def gx_send(page):
        return remote(gxs.at[page], rgx.at[page], gs.at[page], gr.at[page], x_peer)

    def input_grads(page):
        here = pl.ds(pl.multiple_of(page * own, own), own)
        total = g1_v[page]
        for grad, w in ((dq_all, gq_v), (dk_all, gk_v), (dv_all, gv_v)):
            total = total + dot(grad[here, :], w[...], NT)
        gx[pages * x + page] = total[:blk]
        gxs[page] = total[blk:].astype(BF)
        gx_send(page).start()

    n_it = GROUPS * pages

    def unit(it, carry):
        for half in range(2):

            @pl.when(it < n_it)
            def _():
                attend(it, half)

            if half == 1:

                @pl.when(it < n_it)
                def _():
                    for copy in kv_send(it):
                        copy.start()

            tick(2 * it + half)

        @pl.when(it == 0)
        def _():
            for copy in loads[5:]:
                copy.wait()
            x_t[...] = x_v[...].reshape(pages * own, d).T

        @pl.when(jnp.logical_and(it > 0, jnp.logical_and(lax.rem(it, pages) == 0, it <= n_it)))
        def _():
            group_grads(lax.div(it, pages) - 1)

        page = it - n_it

        @pl.when(jnp.logical_and(page >= 0, page < pages))
        def _():
            input_grads(page)

        return carry

    def vec_send(k):
        to = lax.rem(f + k + 1, 8)
        return remote(pack.at[to], vecin.at[k], vs.at[k], vr.at[k], {"fsdp": to})

    vec_x = lambda: remote(vtot, vx.at[0], us.at[0], ur.at[0], x_peer)
    vec_c = lambda: remote(vx.at[1], vx.at[2], us.at[1], ur.at[1], c_peer)

    def small_pack():
        for i in range(8):
            row = brow[0:1, :] if i == 0 else brow[2:3, :] if i == 1 else gvf[i : i + 1, :]
            for j in range(8):
                pack[j, i : i + 1, :ROW] = row[:, ROW * j : ROW * (j + 1)]
        for j in range(8):
            for i in range(3):
                pack[j, 8 + i : 9 + i, :] = gbin[:, (3 * j + i) * 128 : (3 * j + i + 1) * 128]
        for k in range(7):
            vec_send(k).start()

    def small_sum():
        total = pack[f]
        for k in range(7):
            vec_send(k).wait_recv()
            total = total + vecin[k]
        vtot[...] = total
        vec_x().start()

    def small_pair():
        vec_x().wait_recv()
        vx[1] = vtot[...] + vx[0]
        vec_c().start()

    def all_steps(it, carry):
        unit(it, carry)
        for when, run in ((n_it, small_pack), (n_it + 3, small_sum), (n_it + 6, small_pair)):
            pl.when(it == when)(run)
        return carry

    lax.fori_loop(0, (last + 1) // 2, all_steps, 0)
    for page in range(pages):
        gx_send(page).wait_recv()
        gx[pages * (1 - x) + page] = rgx[page].astype(F32)
    vec_c().wait_recv()
    ovec[...] = vx[1] + vx[2]

    def finish(p, carry):
        step(p, "drain")
        return carry

    lax.fori_loop(0, REST, finish, 0)
    for g in range(GROUPS):
        gstep(g, "drain")
    for it in range(n_it):
        for copy in kv_send(it):
            copy.wait_send()
    for page in range(pages):
        gx_send(page).wait_send()
    for k in range(7):
        vec_send(k).wait_send()
    vec_x().wait_send()
    vec_c().wait_send()


def bwd(q, k, v, ctx, dctx, gm1, xall, ws, p, grads, gvf, gbin, shards):
    pages, own, d = q.shape
    rows, blk = k.shape[1], own // 2
    n = pages * own
    dma = pltpu.SemaphoreType.DMA
    vm = pltpu.VMEM
    sds = jax.ShapeDtypeStruct
    dwo, dwi, dw2 = grads
    views = [dwo.reshape(4, 2, ROW, d), dwi.reshape(-1, 4, 2, ROW, d), dw2.reshape((4, 2) + shards[5])]
    res = call(
        bwd_body,
        (12 * n * d * d + pages * 10 * own * rows * d, sum(16 * g.size for g in grads), 0),
        in_specs=[ANY] * 14 + [VM, VM],
        out_specs=[VM] * 8,
        out_shape=[sds(shape, F32) for shape in shards]
        + [sds((2 * pages, blk, d), F32), sds((16, 128), F32)],
        scratch_shapes=[
            vm((pages, own, d), BF), vm((pages, rows, d), BF), vm((pages, rows, d), BF),
            vm((pages, own, d), BF), vm((pages, own, d), BF), vm((pages, own, d), F32), vm((pages, own, d), BF),
            vm((d, d), BF), vm((d, d), BF), vm((d, d), BF),
            vm((REST, 4, 2, ROW, 384), BF), vm((GROUPS, 3, 4, 2, ROW, GCOLS), BF),
            vm((n, d), BF), vm((n, d), BF), vm((n, d), BF),
            vm((pages, own, d), BF), vm((pages, own, d), BF), vm((pages, own, d), BF), vm((pages, own, d), BF),
            vm((2, 2, rows, own), BF), vm((d, n), BF), vm((pages, blk, d), BF), vm((pages, blk, d), BF),
            vm((8, 16, 128), F32), vm((7, 16, 128), F32), vm((16, 128), F32), vm((3, 16, 128), F32), vm((8, d), F32),
        ]
        + fold_bufs(384, KEEP_REST, REST)
        + fold_bufs(128, KEEP_GROUP, GROUPS, 3)
        + fold_sems(REST)
        + fold_sems(GROUPS, 3)
        + [
            dma((10,)), dma((REST,)), dma((2,)), dma((GROUPS, pages, 2)), dma((GROUPS, pages, 2)),
            dma((pages,)), dma((pages,)), dma((7,)), dma((7,)), dma((2,)), dma((2,)),
        ],
        params=dict(collective_id=1, has_side_effects=True, vmem_limit_bytes=64 << 20),
        name="attention_reduce",
    )(q, k, v, ctx, dctx, gm1, xall, *ws, p, *views, gvf, gbin)
    return res[:6], res[6], res[7]


def finish_body(*refs):
    n = 8
    src, small, dst, lows = refs[:n], refs[n], refs[n + 1 : 2 * n + 1], refs[2 * n + 1 : 2 * n + 10]
    held, sem_in, sem_out = refs[2 * n + 10 : 3 * n + 10], refs[-2], refs[-1]
    loads = [pltpu.make_async_copy(src[i], held[i], sem_in.at[i]) for i in range(n)]
    stores = [pltpu.make_async_copy(held[i], dst[i], sem_out.at[i]) for i in range(n)]
    for copy in loads:
        copy.start()
    width = lows[0].shape[0]
    for i in range(8):
        lows[i][...] = small[i, :width]
    for i in range(3):
        lows[8][128 * i : 128 * (i + 1)] = small[8 + i, :]
    for load, store in zip(loads, stores):
        load.wait()
        store.start()
    for copy in stores:
        copy.wait()


def finish(arrays, small, width, wide):
    sds = jax.ShapeDtypeStruct
    dma = pltpu.SemaphoreType.DMA
    n = len(arrays)
    return call(
        finish_body,
        (0, 2 * sum(a.size * a.dtype.itemsize for a in arrays), 0),
        in_specs=[ANY] * n + [VM],
        out_specs=[ANY] * n + [VM] * 9,
        out_shape=[sds(a.shape, a.dtype) for a in arrays] + [sds((width,), F32)] * 8 + [sds((wide,), F32)],
        scratch_shapes=[pltpu.VMEM(a.shape, a.dtype) for a in arrays] + [dma((n,)), dma((n,))],
        name="finish",
    )(*arrays, small)


SWAP_X = [(0, 2), (2, 0), (1, 3), (3, 1)]
SWAP_C = [(0, 1), (1, 0), (2, 3), (3, 2)]


def swap(value, pairs):
    return lax.ppermute(value, "seq", pairs)


def per_device(
    fsdp, inputs, lengths, w_query, b_query, w_key, w_value, b_value, w_out, b_out,
    gain_one, shift_one, w_inner, b_inner, w_outer, b_outer, gain_two, shift_two, cotangent,
):
    pages_all, blk, d = inputs.shape
    pages = pages_all // 2
    s = lax.axis_index("seq")
    x_at = lax.div(s, 2)
    direct = fsdp == 8
    ws = (w_query, w_key, w_value, w_out, w_inner, w_outer)
    shards = [w.shape for w in ws]
    width = b_query.shape[0]
    names = (b_query, b_value, b_out, gain_one, shift_one, b_outer, gain_two, shift_two)

    def pages_of(array, side):
        return lax.dynamic_slice_in_dim(array, side * pages, pages, 0)

    order = jnp.stack([s, s ^ 2, s ^ 1, s ^ 3]).astype(jnp.int32)
    thr = pages_of(lengths, x_at).astype(jnp.int32)[:, None] - order[None, :] * blk
    if direct:
        full, rest = fwd(lengths.astype(jnp.int32), inputs, cotangent, ws, names + (b_inner,))
        xall, q, k, v, ctx, p, dctx, gm1, dwo, dwi, dw2, output, gv_ffn, gbin = rest
    else:
        wq, wk, wv, wo, wi, w2 = [lax.all_gather(w, "fsdp", axis=0, tiled=True) for w in ws]
        vec = jnp.concatenate(names + (b_inner,)).reshape(12, width)
        gvec = lax.all_gather(vec, "fsdp", axis=0)
        vec_full = jnp.swapaxes(gvec[:, :8], 0, 1).reshape(8, d).astype(F32)
        bin_full = gvec[:, 8:].reshape(1, -1).astype(F32)

        def own_rows(array):
            other = swap(pages_of(array, 1 - x_at), SWAP_X)
            return jnp.concatenate([pages_of(array, x_at), other], axis=1)

        xown, cown = own_rows(inputs), own_rows(cotangent)
        xall = jnp.concatenate([xown, swap(xown, SWAP_C)], axis=1)
        q, k, v, p, ctx = attn_fwd(thr, xall, wq, wk, wv, vec_full)
    if direct:
        tot, grad_inputs, tvec = bwd(
            q, k, v, ctx, dctx, gm1.reshape(pages, 2 * blk, d), xall, full, p, (dwo, dwi, dw2), gv_ffn, gbin, shards
        )
        res = finish((output, grad_inputs) + tuple(tot), tvec, width, b_inner.shape[0])
        output, grad_inputs, tot, small, g_bi = res[0], res[1], res[2:8], res[8:16], res[16]
    else:
        out, gm1, dctx, dwo, dwi, dw2, gv_ffn, gbin = ffn(ctx, xall, cown, wo, wi, w2, vec_full, bin_full)
        dq, dk, dk_send, dv, dv_send = attn_bwd(q, k, v, p, ctx, dctx)
        dkr, dvr = swap(dk_send, SWAP_C), swap(dv_send, SWAP_C)
        gx_a, gx_b, dwq, dwk, dwv, gv_proj = proj(xall, dq, dk, dkr, dv, dvr, gm1, wq, wk, wv)
        gv = jnp.concatenate([gv_proj[:2], gv_ffn[2:]], axis=0)
        by_owner = jnp.concatenate(
            [jnp.swapaxes(gv.reshape(8, fsdp, width), 0, 1), gbin.reshape(fsdp, 4, width)], axis=1
        )
        tot = [
            lax.psum(lax.psum_scatter(g, "fsdp", scatter_dimension=0, tiled=True), "seq").astype(F32)
            for g in (dwq, dwk, dwv, dwo, dwi, dw2)
        ]
        tvec = lax.psum(lax.psum_scatter(by_owner, "fsdp", scatter_dimension=0, tiled=True)[0], "seq")

        def joined(mine, other):
            here = lax.dynamic_update_slice_in_dim(
                jnp.zeros((pages_all, blk, d), mine.dtype), mine, x_at * pages, 0
            )
            return lax.dynamic_update_slice_in_dim(here, other, (1 - x_at) * pages, 0)

        output = joined(out[:, :blk], swap(out[:, blk:], SWAP_X))
        grad_inputs = joined(gx_a, swap(gx_b, SWAP_X).astype(F32))
        small = [tvec[i] for i in range(8)]
        g_bi = tvec[8:].reshape(-1)
    g_bq, g_bv, g_bo, g_g1, g_s1, g_bo2, g_g2, g_s2 = small
    t_q, t_k, t_v, t_o, t_i, t_2 = tot
    return (
        output, grad_inputs, t_q, g_bq, t_k, t_v, g_bv, t_o, g_bo, g_g1, g_s1,
        t_i, g_bi, t_2, g_bo2, g_g2, g_s2,
    )


def solution(mesh):
    vec, mat, act = P("fsdp"), P("fsdp", None), P("fsdp", "seq", None)
    return jax.shard_map(
        functools.partial(per_device, mesh.shape["fsdp"]),
        mesh=mesh,
        in_specs=(act, vec, mat, vec, mat, mat, vec, mat, vec, vec, vec, mat, vec, mat, vec, vec, vec, act),
        out_specs=(act, act, mat, vec, mat, mat, vec, mat, vec, vec, vec, mat, vec, mat, vec, vec, vec),
        check_vma=False,
    )
```

```python
import functools
import math

import jax
import jax.numpy as jnp
from jax import lax
from jax.experimental import pallas as pl
from jax.experimental.pallas import tpu as pltpu
from jax.sharding import PartitionSpec as P

HEADS = 12
HEAD_DIM = 64
PAIR = 2 * HEAD_DIM
NEG = -1e30
EPS = 1e-12
BF = jnp.bfloat16
F32 = jnp.float32
MESH = pl.DeviceIdType.MESH
ANY = pl.BlockSpec(memory_space=pl.ANY)
VM = pl.BlockSpec(memory_space=pltpu.VMEM)
CHUNK = 1024
ROW = 96
VMEM_CAP = 60 << 20

NN = (((1,), (0,)), ((), ()))
NT = (((1,), (1,)), ((), ()))
TN = (((0,), (0,)), ((), ()))


def dot(a, b, dims=NN):
    return lax.dot_general(a, b, dims, preferred_element_type=F32)


def call(body, cost, **kw):
    flops, byts, trans = cost
    params = dict(vmem_limit_bytes=VMEM_CAP)
    params.update(kw.pop("params", {}))
    return pl.pallas_call(
        body,
        compiler_params=pltpu.CompilerParams(**params),
        cost_estimate=pl.CostEstimate(
            flops=int(flops), bytes_accessed=int(byts), transcendentals=int(trans)
        ),
        **kw,
    )


def attn_fwd_body(thr, xall, wq, wk, wv, vec, q_o, k_o, v_o, p_o, c_o, bias):
    page = pl.program_id(0)
    x_all = xall[0]
    own = x_all.shape[0] // 2
    query = (dot(x_all[:own], wq[...]) + vec[0:1, :]).astype(BF)
    q_o[0] = query
    k_o[0] = dot(x_all, wk[...]).astype(BF)
    v_o[0] = (dot(x_all, wv[...]) + vec[1:2, :]).astype(BF)
    blk = x_all.shape[0] // 4
    place = lax.broadcasted_iota(jnp.int32, (blk, own), 0)
    for b in range(4):
        bias[b * blk : (b + 1) * blk, :] = jnp.where(place < thr[page, b], 0.0, NEG)
    low_lane = lax.broadcasted_iota(jnp.int32, (own, PAIR), 1) < HEAD_DIM

    def pair(i, carry):
        cols = pl.ds(pl.multiple_of(i * PAIR, PAIR), PAIR)
        qp = q_o[0, :, cols] * jnp.array(1.0 / math.sqrt(HEAD_DIM), BF)
        kp = k_o[0, :, cols]
        vt = v_o[0, :, cols].T
        outs = []
        for h in range(2):
            keep = low_lane if h == 0 else jnp.logical_not(low_lane)
            qh = jnp.where(keep, qp, jnp.zeros_like(qp))
            st = dot(kp, qh, NT) + bias[...]
            top = jnp.max(st, axis=0, keepdims=True)
            ex = jnp.exp(st - top)
            tot = jnp.sum(ex, axis=0, keepdims=True)
            pt = (ex * (1.0 / tot)).astype(BF)
            p_o[0, 2 * i + h] = pt
            outs.append(dot(vt[h * HEAD_DIM : (h + 1) * HEAD_DIM], pt))
        c_o[0, :, cols] = jnp.concatenate(outs, axis=0).T.astype(BF)
        return carry

    lax.fori_loop(0, HEADS // 2, pair, 0)


def attn_fwd(thr, xall, wq, wk, wv, vec):
    pages, rows, d = xall.shape
    own = rows // 2
    const = lambda p, t: (0, 0)
    by_page = lambda p, t: (p, 0, 0)
    one = pl.Buffered(1)
    return call(
        attn_fwd_body,
        (
            pages * (2 * d * d * (own + 2 * rows) + 4 * own * rows * d),
            pages * rows * d * 2 * 4 + 6 * d * d + pages * HEADS * own * rows * 2,
            pages * HEADS * own * rows,
        ),
        grid_spec=pltpu.PrefetchScalarGridSpec(
            num_scalar_prefetch=1,
            grid=(pages,),
            in_specs=[pl.BlockSpec((1, rows, d), by_page)]
            + [pl.BlockSpec((d, d), const, pipeline_mode=one)] * 3
            + [pl.BlockSpec((8, d), const)],
            out_specs=[
                pl.BlockSpec((1, own, d), by_page),
                pl.BlockSpec((1, rows, d), by_page),
                pl.BlockSpec((1, rows, d), by_page),
                pl.BlockSpec((1, HEADS, rows, own), lambda p, t: (p, 0, 0, 0)),
                pl.BlockSpec((1, own, d), by_page),
            ],
            scratch_shapes=[pltpu.VMEM((rows, own), F32)],
        ),
        out_shape=[
            jax.ShapeDtypeStruct((pages, own, d), BF),
            jax.ShapeDtypeStruct((pages, rows, d), BF),
            jax.ShapeDtypeStruct((pages, rows, d), BF),
            jax.ShapeDtypeStruct((pages, HEADS, rows, own), BF),
            jax.ShapeDtypeStruct((pages, own, d), BF),
        ],
        name="attn_fwd",
    )(thr, xall, wq, wk, wv, vec)


def attn_bwd_body(q, k, v, p, ctx, dctx, dq_o, dk_own, dk_oth, dv_own, dv_oth):
    own = q.shape[1]
    low_lane = lax.broadcasted_iota(jnp.int32, (own, PAIR), 1) < HEAD_DIM
    scale = 1.0 / math.sqrt(HEAD_DIM)

    def pair(i, carry):
        cols = pl.ds(pl.multiple_of(i * PAIR, PAIR), PAIR)
        qp = q[0, :, cols] * jnp.array(scale, BF)
        kp = k[0, :, cols]
        kt = kp.T
        vp = v[0, :, cols]
        dc = dctx[0, :, cols]
        prod = (dc.astype(F32) * ctx[0, :, cols].astype(F32)).T
        dk = None
        dv = None
        dqs = []
        for h in range(2):
            keep = low_lane if h == 0 else jnp.logical_not(low_lane)
            feats = slice(h * HEAD_DIM, (h + 1) * HEAD_DIM)
            dch = jnp.where(keep, dc, jnp.zeros_like(dc))
            qh = jnp.where(keep, qp, jnp.zeros_like(qp))
            pt = p[0, 2 * i + h]
            delta = jnp.sum(prod[feats], axis=0, keepdims=True)
            dpt = dot(vp, dch, NT)
            dst = (pt.astype(F32) * (dpt - delta)).astype(BF)
            dvh = dot(pt, dch)
            dkh = dot(dst, qh)
            dk = dkh if dk is None else dk + dkh
            dv = dvh if dv is None else dv + dvh
            dqs.append(dot(kt[feats], dst))
        dq_o[0, :, cols] = (jnp.concatenate(dqs, axis=0) * scale).T.astype(BF)
        dk_own[0, :, cols] = dk[:own].astype(BF)
        dk_oth[0, :, cols] = dk[own:].astype(BF)
        dv_own[0, :, cols] = dv[:own].astype(BF)
        dv_oth[0, :, cols] = dv[own:].astype(BF)
        return carry

    lax.fori_loop(0, HEADS // 2, pair, 0)


def attn_bwd(q, k, v, p, ctx, dctx):
    pages, own, d = q.shape
    rows = k.shape[1]
    by_page = lambda i: (i, 0, 0)
    o = pl.BlockSpec((1, own, d), by_page)
    r = pl.BlockSpec((1, rows, d), by_page)
    return call(
        attn_bwd_body,
        (pages * 10 * own * rows * d, pages * (own * rows * HEADS * 2 + 10 * own * d * 2), 0),
        grid=(pages,),
        in_specs=[o, r, r, pl.BlockSpec((1, HEADS, rows, own), lambda i: (i, 0, 0, 0)), o, o],
        out_specs=[o] * 5,
        out_shape=[jax.ShapeDtypeStruct((pages, own, d), BF)] * 5,
        name="attn_bwd",
    )(q, k, v, p, ctx, dctx)


def normal_parts(v):
    bell = jnp.exp(v * v * -0.5)
    t = 1.0 / (1.0 + jnp.abs(v) * (0.3275911 / math.sqrt(2.0)))
    tail = t * (
        0.127414796 + t * (-0.142248368 + t * (0.7107068705 + t * (-0.7265760135 + t * 0.5307027145)))
    )
    tail = tail * bell
    return jnp.where(v >= 0.0, 1.0 - tail, tail), bell * (1.0 / math.sqrt(2.0 * math.pi))


def row_norm(v):
    centered = v - jnp.mean(v, -1, keepdims=True)
    inv = lax.rsqrt(jnp.mean(centered * centered, -1, keepdims=True) + EPS)
    return centered * inv, inv


def norm_back(e, n, inv):
    return inv * (e - jnp.mean(e, -1, keepdims=True) - n * jnp.mean(e * n, -1, keepdims=True))


def ffn_body(
    ctx, xall, cown, wo, wi_h, w2_h, vec, b_in,
    out, gm1_o, dctx_o, dwo_o, dwi_h, dw2_h, gvec, gbin,
    wi, w2, act, din, dgel, hid, gout, gatt, n1s, h1s, accs, r1s, dwi, dw2, lsem, osem,
):
    n, ff = act.shape
    pages, own, d = ctx.shape

    def cols_of(j):
        return pl.ds(pl.multiple_of(j * CHUNK, CHUNK), CHUNK)

    def loads(j):
        cols = cols_of(j)
        return (
            pltpu.make_async_copy(wi_h.at[:, cols], wi.at[:, cols], lsem.at[0, j]),
            pltpu.make_async_copy(w2_h.at[cols, :], w2.at[cols, :], lsem.at[1, j]),
        )

    def store_w2(j):
        return pltpu.make_async_copy(dw2.at[cols_of(j), :], dw2_h.at[cols_of(j), :], osem.at[0, j])

    def store_wi(j):
        return pltpu.make_async_copy(dwi.at[:, cols_of(j)], dwi_h.at[:, cols_of(j)], osem.at[1, j])

    n_chunks = ff // CHUNK
    for j in range(n_chunks):
        for copy in loads(j):
            copy.start()
    gvec[...] = jnp.zeros_like(gvec)

    def add(row, value):
        gvec[row : row + 1, :] += jnp.sum(value, 0, keepdims=True)

    for p in range(pages):
        r = slice(p * own, (p + 1) * own)
        mid = xall[p].astype(F32) + (dot(ctx[p], wo[...]) + vec[2:3, :])
        n1, r1 = row_norm(mid)
        n1s[r, :] = n1
        r1s[r, :] = jnp.broadcast_to(r1, (own, 128))
        h1 = n1 * vec[3:4, :] + vec[4:5, :]
        h1s[r, :] = h1
        hid[r, :] = h1.astype(BF)
    accs[...] = jnp.zeros_like(accs)

    def up(j, carry):
        cols = cols_of(j)
        for copy in loads(j):
            copy.wait()
        pre = dot(hid[...], wi[:, cols]) + b_in[:, cols]
        big, bell = normal_parts(pre)
        a = (pre * big).astype(BF)
        dgel[:, cols] = (big + pre * bell).astype(BF)
        act[:, cols] = a
        accs[...] += dot(a, w2[cols, :])
        return carry

    lax.fori_loop(0, n_chunks, up, 0)
    for p in range(pages):
        r = slice(p * own, (p + 1) * own)
        mid = h1s[r, :] + (accs[r, :] + vec[5:6, :])
        n2, r2 = row_norm(mid)
        out[p] = (n2 * vec[6:7, :] + vec[7:8, :]).astype(BF)
        cot = cown[p].astype(F32)
        gm2 = norm_back(cot * vec[6:7, :], n2, r2)
        go = gm2.astype(BF)
        gout[r, :] = go
        accs[r, :] = gm2
        add(5, go.astype(F32))
        add(6, cot * n2)
        add(7, cot)

    def down(j, carry):
        cols = cols_of(j)
        di = (dot(gout[...], w2[cols, :], NT) * dgel[:, cols].astype(F32)).astype(BF)
        din[:, cols] = di
        accs[...] += dot(di, wi[:, cols], NT)
        gbin[:, cols] = jnp.sum(di.astype(F32), 0, keepdims=True)
        dw2[cols, :] = dot(act[:, cols], gout[...], TN).astype(BF)
        store_w2(j).start()
        return carry

    lax.fori_loop(0, n_chunks, down, 0)
    for p in range(pages):
        r = slice(p * own, (p + 1) * own)
        gh = accs[r, :]
        n1 = n1s[r, :]
        gm1 = norm_back(gh * vec[3:4, :], n1, r1s[r, 0:1])
        gm1_o[p] = gm1
        ga = gm1.astype(BF)
        gatt[r, :] = ga
        dctx_o[p] = dot(ga, wo[...], NT).astype(BF)
        add(2, ga.astype(F32))
        add(3, gh * n1)
        add(4, gh)
    hid_t = hid[...].T

    def grads(j, carry):
        cols = cols_of(j)
        dwi[:, cols] = dot(hid_t, din[:, cols]).astype(BF)
        store_wi(j).start()
        return carry

    lax.fori_loop(0, n_chunks, grads, 0)
    dwo_o[...] = dot(ctx[...].reshape(n, d), gatt[...], TN).astype(BF)
    for j in range(n_chunks):
        store_w2(j).wait()
        store_wi(j).wait()


def ffn(ctx, xall, cown, wo, wi, w2, vec, b_in):
    pages, own, d = ctx.shape
    ff = wi.shape[1]
    n = pages * own
    sds = jax.ShapeDtypeStruct
    vm = pltpu.VMEM
    dma = pltpu.SemaphoreType.DMA
    return call(
        ffn_body,
        (n * d * (12 * ff + 6 * d), 4 * d * ff * 2 + 12 * n * d * 2, n * ff),
        grid=(1,),
        in_specs=[
            pl.BlockSpec((pages, own, d), lambda i: (0, 0, 0)),
            pl.BlockSpec((pages, own, d), lambda i: (0, 0, 0)),
            VM, VM, ANY, ANY, VM, VM,
        ],
        out_specs=[VM] * 4 + [ANY, ANY, VM, VM],
        out_shape=[
            sds((pages, own, d), BF), sds((pages, own, d), F32), sds((pages, own, d), BF),
            sds((d, d), BF), sds((d, ff), BF), sds((ff, d), BF), sds((8, d), F32), sds((1, ff), F32),
        ],
        scratch_shapes=[
            vm((d, ff), BF), vm((ff, d), BF), vm((n, ff), BF), vm((n, ff), BF), vm((n, ff), BF),
            vm((n, d), BF), vm((n, d), BF), vm((n, d), BF), vm((n, d), F32), vm((n, d), F32),
            vm((n, d), F32), vm((n, 128), F32), vm((d, ff), BF), vm((ff, d), BF),
            dma((2, ff // CHUNK)), dma((2, ff // CHUNK)),
        ],
        params=dict(vmem_limit_bytes=63 << 20),
        name="ffn",
    )(ctx, xall, cown, wo, wi, w2, vec, b_in)


def proj_body(
    xall, dq, dk, dkr, dv, dvr, gm1, wq, wk, wv,
    ga_o, gb_o, dwq_o, dwk_o, dwv_o, gvec, x_all, dq_all, dk_all, dv_all,
):
    page = pl.program_id(0)
    own = xall.shape[1]
    blk = own // 2
    here = pl.ds(pl.multiple_of(page * own, own), own)
    x_all[here, :] = xall[0]
    dq_v = dq[0]
    dk_v = (dk[0].astype(F32) + dkr[0].astype(F32)).astype(BF)
    dv_v = (dv[0].astype(F32) + dvr[0].astype(F32)).astype(BF)
    dq_all[here, :] = dq_v
    dk_all[here, :] = dk_v
    dv_all[here, :] = dv_v
    gx = gm1[0] + dot(dq_v, wq[...], NT) + dot(dk_v, wk[...], NT) + dot(dv_v, wv[...], NT)
    ga_o[0] = gx[:blk]
    gb_o[0] = gx[blk:].astype(BF)

    @pl.when(page == 0)
    def _():
        gvec[...] = jnp.zeros_like(gvec)

    gvec[0:1, :] += jnp.sum(dq_v.astype(F32), 0, keepdims=True)
    gvec[1:2, :] += jnp.sum(dv_v.astype(F32), 0, keepdims=True)

    @pl.when(page == pl.num_programs(0) - 1)
    def _():
        x_t = x_all[...].T
        dwq_o[...] = dot(x_t, dq_all[...]).astype(BF)
        dwk_o[...] = dot(x_t, dk_all[...]).astype(BF)
        dwv_o[...] = dot(x_t, dv_all[...]).astype(BF)


def proj(xall, dq, dk, dkr, dv, dvr, gm1, wq, wk, wv):
    pages, own, d = dq.shape
    blk = own // 2
    n = pages * own
    by_page = lambda p: (p, 0, 0)
    const = lambda p: (0, 0)
    one = pl.Buffered(1)
    half = pl.BlockSpec((1, blk, d), by_page)
    whole = pl.BlockSpec((1, own, d), by_page)
    square = pl.BlockSpec((d, d), const, pipeline_mode=one)
    return call(
        proj_body,
        (12 * n * d * d, 12 * d * d + 16 * n * d, 0),
        grid=(pages,),
        in_specs=[whole] * 7 + [square] * 3,
        out_specs=[half, half] + [square] * 3 + [pl.BlockSpec((8, d), const)],
        out_shape=[
            jax.ShapeDtypeStruct((pages, blk, d), F32),
            jax.ShapeDtypeStruct((pages, blk, d), BF),
        ]
        + [jax.ShapeDtypeStruct((d, d), BF)] * 3
        + [jax.ShapeDtypeStruct((8, d), F32)],
        scratch_shapes=[pltpu.VMEM((n, d), BF)] * 4,
        name="proj_bwd",
    )(xall, dq, dk, dkr, dv, dvr, gm1, wq, wk, wv)


def place():
    f, s = lax.axis_index("fsdp"), lax.axis_index("seq")
    return lax.div(f, 2), lax.rem(f, 2), lax.div(s, 2), lax.rem(s, 2)


def at(z, y, x, c):
    return {"fsdp": 2 * z + y, "seq": 2 * x + c}


def meet(others):
    barrier = pltpu.get_barrier_semaphore()
    for other in others:
        pl.semaphore_signal(barrier, inc=1, device_id=other, device_id_type=MESH)
    pl.semaphore_wait(barrier, len(others))


def remote(src, dst, send, recv, other):
    return pltpu.make_async_remote_copy(
        src_ref=src, dst_ref=dst, send_sem=send, recv_sem=recv,
        device_id=other, device_id_type=MESH,
    )


def begin(copy):
    copy.start()
    return copy


class Spread:
    def __init__(self, where, src, dst, row0, col0, width, sems, key, from0=None):
        self.z, self.y, self.x, self.c = where
        z, y, x, c = where
        zs, zr, fs, ys, yr, xs, xr, cs, cr, lo = sems
        k = key
        cols = pl.ds(pl.multiple_of(col0 + width * c, 128), width)
        origin = pl.ds(pl.multiple_of((col0 if from0 is None else from0) + width * c, 128), width)
        full = pl.ds(row0, ROW)
        mine = pl.ds(pl.multiple_of(row0 + (ROW - YROWS) * x, 16), YROWS)
        lacks = pl.ds(pl.multiple_of(row0 + YROWS * x, 16), ROW - YROWS)
        near, far, across = z + 1 - 2 * lax.rem(z, 2), lax.rem(z + 2, 4), 3 - z
        self.inner = jnp.logical_or(z == 1, z == 2)
        self.local = lambda: pltpu.make_async_copy(src.at[full, origin], dst.at[z, y, full, cols], lo.at[k])

        def send(block, n, target, sem):
            from_ref = src.at[full, origin] if block is None else dst.at[block, y, full, cols]
            b = z if block is None else block
            return remote(from_ref, dst.at[b, y, full, cols], sem, zr.at[k + (n,)], at(target, y, x, c))

        self.a = lambda: send(None, 0, near, zs.at[k + (0,)])
        self.b = lambda: send(None, 1, far, zs.at[k + (1,)])
        self.d = lambda: send(None, 2, across, zs.at[k + (2,)])
        self.fwd = lambda: send(far, 2, near, fs.at[k])
        yv = lambda: dst.at[:, y, mine, cols]
        self.ycopy = lambda: remote(yv(), yv(), ys.at[k], yr.at[k], at(z, 1 - y, x, c))
        xv = lambda: dst.at[:, 1 - y, lacks, cols]
        self.xcopy = lambda: remote(xv(), xv(), xs.at[k], xr.at[k], at(z, y, 1 - x, c))
        cv = lambda: dst.at[:, :, full, cols]
        self.ccopy = lambda: remote(cv(), cv(), cs.at[k], cr.at[k], at(z, y, x, 1 - c))

    def along_z(self):
        self.local().start()
        self.b().start()
        self.a().start()

        @pl.when(self.inner)
        def _():
            self.d().start()

    def forward(self):
        self.b().wait_recv()

        @pl.when(self.inner)
        def _():
            self.fwd().start()

    def along_y(self):
        self.a().wait_recv()
        self.d().wait_recv()
        self.local().wait()
        self.ycopy().start()

    def along_x(self):
        self.ycopy().wait_recv()
        self.xcopy().start()

    def to_core(self):
        self.xcopy().wait_recv()
        self.ccopy().start()

    def arrive(self):
        self.ccopy().wait_recv()

    def drain(self):
        self.a().wait_send()
        self.b().wait_send()

        @pl.when(self.inner)
        def _():
            self.d().wait_send()
            self.fwd().wait_send()

        self.ycopy().wait_send()
        self.xcopy().wait_send()
        self.ccopy().wait_send()


def spread_sems(*lead):
    dma = pltpu.SemaphoreType.DMA
    return [dma(lead + (3,)), dma(lead + (3,))] + [dma(lead)] * 8


GROUPS = 3
GCOLS = 256
REST = 9
EARLY = 3
YROWS = 64


def fwd_body(
    lens, x_in, cot, wq, wk, wv, wo, wi, w2, *refs,
):
    smalls = refs[:9]
    (
        gq_h, gk_h, gv_h, xall_h, q_h, k_h, v_h, c_h, p_o,
        go_h, gi_h, g2_h, act_h, dd_h, hid_h, gout_h, n1_h, gm2_h, r1_h, out_h, gvs, vec,
    ) = refs[9:31]
    (
        gq, gk, gv, go, gi, g2, xall, q_o, k_o, v_o, c_o, cown, bias, pbuf, vpk, gvec, b_in,
        act, dd, hid, gout, n1b, n1s, accs, r1s,
    ) = refs[31:56]
    qs, rs = refs[56:66], refs[66:76]
    asend, arecv, aloc, vs, vr, ps, outs_sem, chunk_sem = refs[76:]
    z, y, x, c = where = place()
    f = 2 * z + y
    pages, rows = xall.shape[0], xall.shape[1]
    own, blk = rows // 2, rows // 4
    width = smalls[0].shape[-1]
    for i in range(8):
        vpk[i : i + 1, :width] = smalls[i][...].astype(F32).reshape(1, width)
    for i in range(3):
        vpk[8 + i : 9 + i, :] = smalls[8][128 * i : 128 * (i + 1)].astype(F32).reshape(1, 128)
    gvec[f] = vpk[...]
    x_peer, c_peer = at(z, y, 1 - x, c), at(z, y, x, 1 - c)
    meet([{"fsdp": lax.rem(f + k + 1, 8)} for k in range(7)] + [x_peer, c_peer])

    groups = [
        [Spread(where, src, dst, 0, GCOLS * g, GCOLS // 2, qs, (g, w)) for w, (src, dst) in enumerate(((wq, gq), (wk, gk), (wv, gv)))]
        for g in range(GROUPS)
    ]

    def each(g, step):
        for part in groups[g]:
            getattr(part, step)()

    mine, sent = pl.ds(pages * x, pages), pl.ds(pages * (1 - x), pages)

    def band(b):
        return xall.at[:, pl.ds(blk * b, blk), :]

    to_b = remote(x_in.at[sent], band(1), asend.at[0], arecv.at[0], x_peer)
    to_c = remote(x_in.at[mine], band(2), asend.at[1], arecv.at[1], c_peer)
    to_d = remote(band(1), band(3), asend.at[2], arecv.at[2], c_peer)
    cot_b = remote(cot.at[sent], cown.at[:, pl.ds(blk, blk), :], asend.at[3], arecv.at[3], x_peer)
    keep_x = pltpu.make_async_copy(x_in.at[mine], band(0), aloc.at[0])
    keep_c = pltpu.make_async_copy(cot.at[mine], cown.at[:, pl.ds(0, blk), :], aloc.at[1])
    vecs = [
        remote(vpk, gvec.at[f], vs.at[k], vr.at[k], {"fsdp": lax.rem(f + k + 1, 8)}) for k in range(7)
    ]
    def rest(p, step):
        def run(src, dst, row0, col0, from0=None):
            getattr(Spread(where, src, dst, row0, col0, 384, rs, (p,), from0), step)()

        @pl.when(p == 0)
        def _():
            run(wo, go, 0, 0)

        @pl.when(jnp.logical_and(p >= 1, p < 5))
        def _():
            run(wi, gi.at[p - 1], 0, 0, 768 * (p - 1))

        @pl.when(jnp.logical_and(p >= 5, p < REST))
        def _():
            run(w2, g2, ROW * (p - 5), 0)

    to_b.start()
    each(0, "along_z")
    keep_x.start()
    to_c.start()
    for copy in vecs:
        copy.start()
    place_row = lax.broadcasted_iota(jnp.int32, (blk, own), 0)
    for page in range(pages):
        for b in range(4):
            side = x if b % 2 == 0 else 1 - x
            core = c if b < 2 else 1 - c
            limit = lens[pages * x + page] - (2 * side + core) * blk
            bias[page, b * blk : (b + 1) * blk, :] = jnp.where(place_row < limit, 0.0, NEG)
    each(0, "forward")
    each(1, "along_z")
    each(0, "along_y")
    each(1, "forward")
    each(2, "along_z")
    each(1, "along_y")
    each(0, "along_x")
    each(2, "forward")
    for p in range(EARLY):
        rest(p, "along_z")
    each(2, "along_y")
    to_b.wait_recv()
    to_d.start()
    each(0, "to_core")
    each(1, "along_x")
    for copy in vecs:
        copy.wait_recv()
    for i in range(8):
        vec[i : i + 1, :] = jnp.concatenate([gvec[j, i : i + 1, :width] for j in range(8)], axis=1)
    for j in range(8):
        for i in range(3):
            b_in[:, (3 * j + i) * 128 : (3 * j + i + 1) * 128] = gvec[j, 8 + i : 9 + i, :]
    keep_c.start()
    keep_x.wait()
    to_c.wait_recv()
    to_d.wait_recv()
    each(0, "arrive")

    low_lane = lax.broadcasted_iota(jnp.int32, (own, PAIR), 1) < HEAD_DIM
    stages = (("along_z", 1 - 8 * EARLY // 3), ("forward", 0), ("along_y", 3), ("along_x", 8), ("to_core", 13))

    def tick(t):
        for step, late in stages:
            n = t - late
            p = lax.div(3 * n + 7, 8)

            @pl.when(jnp.logical_and(n >= 0, lax.div(8 * p, 3) == n))
            def _():
                if step == "along_z":
                    pl.when(p >= EARLY)(lambda: rest(p, step))
                else:
                    rest(p, step)

    def p_copy(page, pair, slot):
        return pltpu.make_async_copy(pbuf.at[slot], p_o.at[page, pl.ds(2 * pair, 2)], ps.at[slot])

    def unit(it, carry):
        g, page = lax.div(it, pages), lax.rem(it, pages)

        @pl.when(it == 0)
        def _():
            each(2, "along_x")
            each(1, "to_core")

        @pl.when(it == 1)
        def _():
            each(2, "to_core")
            cot_b.start()

        @pl.when(it == pages)
        def _():
            each(1, "arrive")

        @pl.when(it == 2 * pages)
        def _():
            each(2, "arrive")

        gcols = pl.ds(pl.multiple_of(g * GCOLS, GCOLS), GCOLS)
        x_all = xall[page]
        d = x_all.shape[1]
        query = (dot(x_all[:own], gq[:, :, :, gcols].reshape(d, GCOLS)) + vec[0:1, gcols]).astype(BF)
        keys = dot(x_all, gk[:, :, :, gcols].reshape(d, GCOLS)).astype(BF)
        vals = (dot(x_all, gv[:, :, :, gcols].reshape(d, GCOLS)) + vec[1:2, gcols]).astype(BF)
        q_o[page, :, gcols] = query
        k_o[page, :, gcols] = keys
        v_o[page, :, gcols] = vals
        for half in range(2):
            lanes = slice(half * PAIR, (half + 1) * PAIR)
            pair = 2 * g + half

            @pl.when(it > 0)
            def _():
                p_copy(page, pair, half).wait()

            qp = query[:, lanes] * jnp.array(1.0 / math.sqrt(HEAD_DIM), BF)
            kp = keys[:, lanes]
            vt = vals[:, lanes].T
            outs = []
            for h in range(2):
                keep = low_lane if h == 0 else jnp.logical_not(low_lane)
                qh = jnp.where(keep, qp, jnp.zeros_like(qp))
                st = dot(kp, qh, NT) + bias[page]
                top = jnp.max(st, axis=0, keepdims=True)
                ex = jnp.exp(st - top)
                tot = jnp.sum(ex, axis=0, keepdims=True)
                pt = (ex * (1.0 / tot)).astype(BF)
                pbuf[half, h] = pt
                outs.append(dot(vt[h * HEAD_DIM : (h + 1) * HEAD_DIM], pt))
            p_copy(page, pair, half).start()
            cols = pl.ds(pl.multiple_of(pair * PAIR, PAIR), PAIR)
            c_o[page, :, cols] = jnp.concatenate(outs, axis=0).T.astype(BF)
            tick(2 * it + half)
        return carry

    lax.fori_loop(0, GROUPS * pages, unit, 0)
    n_ticks = 2 * GROUPS * pages
    stores = [
        pltpu.make_async_copy(src, dst, outs_sem.at[i])
        for i, (src, dst) in enumerate(
            ((q_o, q_h), (k_o, k_h), (v_o, v_h), (c_o, c_h), (xall, xall_h), (gq, gq_h), (gk, gk_h), (gv, gv_h))
        )
    ]
    for copy in stores:
        copy.start()
    for half in range(2):
        p_copy(0, 0, half).wait()

    d = xall.shape[2]
    n_chunks = gi.shape[0]
    last = 8 * (REST - 1) // 3 + stages[-1][1] + 1
    gvs[...] = jnp.zeros_like(gvs)

    def add(row, value):
        gvs[row : row + 1, :] += jnp.sum(value, 0, keepdims=True)

    def square(ref):
        return ref[...].reshape(d, d)

    rest(0, "arrive")
    later = [pltpu.make_async_copy(go, go_h, outs_sem.at[8])]
    later[0].start()
    for page in range(pages):
        r = slice(page * own, (page + 1) * own)
        mid = xall[page, :own].astype(F32) + (dot(c_o[page], square(go)) + vec[2:3, :])
        n1, r1 = row_norm(mid)
        n1s[r, :] = n1
        n1b[r, :] = n1.astype(BF)
        r1s[r, :] = jnp.broadcast_to(r1, (own, 128))
        hid[r, :] = (n1 * vec[3:4, :] + vec[4:5, :]).astype(BF)

    def ticks(lo, hi):
        lax.fori_loop(lo, hi, lambda t, carry: (tick(t), carry)[1], 0)

    def chunk_stores(j):
        cols = pl.ds(pl.multiple_of(j * d, d), d)
        return [
            pltpu.make_async_copy(src, dst.at[j], chunk_sem.at[i, j])
            for i, (src, dst) in enumerate(((gi.at[j], gi_h), (act.at[:, cols], act_h), (dd.at[:, cols], dd_h)))
        ]

    def up(j, carry):
        ticks(n_ticks + 3 * j, jnp.minimum(n_ticks + 3 * j + 3, last))
        rest(j + 1, "arrive")
        cols = pl.ds(pl.multiple_of(j * d, d), d)
        pre = dot(hid[...], gi[j].reshape(d, d)) + b_in[:, cols]
        big, bell = normal_parts(pre)
        act[:, cols] = (pre * big).astype(BF)
        dd[:, cols] = (big + pre * bell).astype(BF)
        for copy in chunk_stores(j):
            copy.start()
        return carry

    lax.fori_loop(0, n_chunks, up, 0)
    ticks(n_ticks + 3 * n_chunks, last)
    for p in range(5, REST):
        rest(p, "arrive")
    keep_c.wait()
    cot_b.wait_recv()
    stores[0].wait()
    later.append(pltpu.make_async_copy(g2, g2_h, outs_sem.at[9]))
    later[1].start()

    def w2_rows(j):
        return g2[j].reshape(d, d)

    accs[...] = jnp.zeros_like(accs)

    def outer(j, carry):
        cols = pl.ds(pl.multiple_of(j * d, d), d)
        accs[...] += dot(act[:, cols], w2_rows(j))
        return carry

    lax.fori_loop(0, n_chunks, outer, 0)
    for page in range(pages):
        r = slice(page * own, (page + 1) * own)
        h1 = n1s[r, :] * vec[3:4, :] + vec[4:5, :]
        mid = h1 + (accs[r, :] + vec[5:6, :])
        n2, r2 = row_norm(mid)
        q_o[page] = (n2 * vec[6:7, :] + vec[7:8, :]).astype(BF)
        ct = cown[page].astype(F32)
        gm2 = norm_back(ct * vec[6:7, :], n2, r2)
        gob = gm2.astype(BF)
        gout[r, :] = gob
        accs[r, :] = gm2
        add(5, gob.astype(F32))
        add(6, ct * n2)
        add(7, ct)
    for i, (src, dst) in enumerate(((accs, gm2_h), (gout, gout_h), (hid, hid_h), (n1b, n1_h), (r1s, r1_h), (q_o, out_h))):
        later.append(pltpu.make_async_copy(src, dst, outs_sem.at[10 + i]))
        later[-1].start()

    def finish(p, carry):
        rest(p, "drain")
        return carry

    lax.fori_loop(0, REST, finish, 0)
    for g in range(GROUPS):
        each(g, "drain")
    for copy in vecs + [to_b, to_c, to_d, cot_b]:
        copy.wait_send()
    for j in range(n_chunks):
        later += chunk_stores(j)
    for copy in stores[1:] + later:
        copy.wait()


def fwd(lens, x_in, cot, ws, smalls):
    pages_all, blk, d = x_in.shape
    pages, own, rows = pages_all // 2, 2 * blk, 4 * blk
    n = pages * own
    dma = pltpu.SemaphoreType.DMA
    sds = jax.ShapeDtypeStruct
    vm = pltpu.VMEM
    ff = ws[4].shape[1]
    quarter = (4, 2, ROW, d)
    res = call(
        fwd_body,
        (n * d * (12 * ff + 12 * d), sum(16 * w.size for w in ws), pages * HEADS * own * rows),
        in_specs=[pl.BlockSpec(memory_space=pltpu.SMEM)] + [ANY] * 5 + [VM] * 12,
        out_specs=[ANY] * 20 + [VM, VM],
        out_shape=[sds(quarter, BF)] * 3
        + [
            sds((pages, rows, d), BF),
            sds((pages, own, d), BF), sds((pages, rows, d), BF), sds((pages, rows, d), BF), sds((pages, own, d), BF),
            sds((pages, HEADS, rows, own), BF),
            sds(quarter, BF), sds((ff // d,) + quarter, BF), sds((4, 2, ff // 8, d), BF),
            sds((ff // d, n, d), BF), sds((ff // d, n, d), BF), sds((n, d), BF), sds((n, d), BF), sds((n, d), BF),
            sds((n, d), F32), sds((n, 128), F32), sds((pages, own, d), BF),
            sds((8, d), F32), sds((8, d), F32),
        ],
        scratch_shapes=[
            vm(quarter, BF), vm(quarter, BF), vm(quarter, BF), vm(quarter, BF),
            vm((ff // d,) + quarter, BF), vm((4, 2, ff // 8, d), BF),
            vm((pages, rows, d), BF), vm((pages, own, d), BF), vm((pages, rows, d), BF), vm((pages, rows, d), BF),
            vm((pages, own, d), BF), vm((pages, own, d), BF), vm((pages, rows, own), F32), vm((2, 2, rows, own), BF),
            vm((16, 128), F32), vm((8, 16, 128), F32), vm((1, ff), F32),
            vm((n, ff), BF), vm((n, ff), BF), vm((n, d), BF), vm((n, d), BF), vm((n, d), BF),
            vm((n, d), F32), vm((n, d), F32), vm((n, 128), F32),
        ]
        + spread_sems(GROUPS, 3)
        + spread_sems(REST)
        + [dma((5,)), dma((5,)), dma((3,)), dma((7,)), dma((7,)), dma((2,)), dma((16,)), dma((3, ff // d))],
        params=dict(collective_id=0, has_side_effects=True, vmem_limit_bytes=64 << 20),
        name="gather_forward",
    )(lens, x_in, cot, *ws, *smalls)
    return res


class Fold:
    def __init__(self, where, acc, bufs, sems, key, keep):
        self.z, self.y, self.x, self.c = where
        self.acc, self.key = acc, key
        give = ROW - keep
        self.rc, self.rx, self.ry, self.rz, self.fin, self.rf = [b.at[key] for b in bufs]
        self.cs, self.cr, self.xs, self.xr, self.ys, self.yr, self.zs, self.zr, self.fs, self.fr, self.es, self.er = sems
        z = self.z
        self.near, self.far, self.across = z + 1 - 2 * lax.rem(z, 2), lax.rem(z + 2, 4), 3 - z
        self.inner = jnp.logical_or(z == 1, z == 2)
        self.outer = jnp.logical_not(self.inner)
        self.keep = pl.ds(pl.multiple_of(give * self.x, 16), keep)
        self.give = pl.ds(pl.multiple_of(keep * (1 - self.x), 16), give)
        self.gain = pl.ds(pl.multiple_of(keep * self.x, 16), give)

    def part(self, *sel):
        return self.acc(sel)

    def xcopy(self):
        return remote(
            self.part(ALL, 1 - self.y, self.give), self.rx, self.xs.at[self.key], self.xr.at[self.key],
            at(self.z, self.y, 1 - self.x, self.c),
        )

    def ycopy(self):
        return remote(
            self.part(ALL, 1 - self.y, self.keep), self.ry, self.ys.at[self.key], self.yr.at[self.key],
            at(self.z, 1 - self.y, self.x, self.c),
        )

    def zcopy(self, block, target, slot):
        return remote(
            self.part(block, self.y, ALL), self.rz.at[slot], self.zs.at[self.key + (slot,)],
            self.zr.at[self.key + (slot,)], at(target, self.y, self.x, self.c),
        )

    def a(self):
        return self.zcopy(self.near, self.near, 0)

    def b(self):
        return self.zcopy(self.far, self.far, 1)

    def d(self):
        return self.zcopy(self.across, self.across, 2)

    def f(self):
        return self.zcopy(self.across, self.near, 3)

    def fcopy(self):
        return remote(
            self.fin, self.rf, self.fs.at[self.key], self.fr.at[self.key],
            at(self.z, self.y, 1 - self.x, self.c),
        )

    def over_x(self, first):
        first.wait_recv()
        whole = self.part(ALL, ALL, ALL)
        whole[...] = whole[...] + self.rc[...]
        self.xcopy().start()

    def over_y(self):
        self.xcopy().wait_recv()
        rows = self.part(ALL, 1 - self.y, self.gain)
        rows[...] = rows[...] + self.rx[...]
        self.ycopy().start()

    def over_z(self):
        self.ycopy().wait_recv()
        rows = self.part(ALL, self.y, self.keep)
        rows[...] = rows[...] + self.ry[...]
        self.a().start()

        @pl.when(self.outer)
        def _():
            self.f().start()
            self.b().start()

        @pl.when(self.inner)
        def _():
            self.d().start()

    def inside(self):
        @pl.when(self.inner)
        def _():
            self.f().wait_recv()
            rows = self.part(self.far, self.y, ALL)
            rows[...] = rows[...] + self.rz[3]
            self.b().start()

    def total(self):
        self.a().wait_recv()
        self.b().wait_recv()
        own = self.part(self.z, self.y, ALL)

        @pl.when(self.outer)
        def _():
            self.fin[...] = (own[...].astype(F32) + self.rz[0].astype(F32) + self.rz[1].astype(F32)).astype(BF)

        @pl.when(self.inner)
        def _():
            self.d().wait_recv()
            self.fin[...] = (
                own[...].astype(F32) + self.rz[0].astype(F32) + self.rz[1].astype(F32) + self.rz[2].astype(F32)
            ).astype(BF)

        self.fcopy().start()

    def ecopy(self, view):
        return remote(view, view, self.es.at[self.key], self.er.at[self.key], at(self.z, self.y, self.x, 1 - self.c))

    def write(self, view):
        self.fcopy().wait_recv()
        view[...] = self.fin[...].astype(F32) + self.rf[...].astype(F32)
        self.ecopy(view).start()

    def drain(self, view):
        self.ecopy(view).wait_recv()
        self.xcopy().wait_send()
        self.ycopy().wait_send()
        self.a().wait_send()
        self.b().wait_send()

        @pl.when(self.outer)
        def _():
            self.f().wait_send()

        @pl.when(self.inner)
        def _():
            self.d().wait_send()

        self.fcopy().wait_send()
        self.ecopy(view).wait_send()


ALL = slice(None)
KEEP_REST = 64
KEEP_GROUP = 80


def fold_sems(*lead):
    dma = pltpu.SemaphoreType.DMA
    return [dma(lead)] * 6 + [dma(lead + (4,))] * 2 + [dma(lead)] * 4


def fold_bufs(width, keep, *lead):
    return [
        pltpu.VMEM(lead + shape, BF)
        for shape in (
            (4, 2, ROW, width), (4, ROW - keep, width), (4, keep, width), (4, ROW, width), (ROW, width), (ROW, width),
        )
    ]


def bwd_body(
    gq_h, gk_h, gv_h, x_h, q_h, k_h, v_h, c_h, p_h, go_h, gi_h, g2_h, act_h, dd_h, hid_h, gout_h, n1_h, gm2_h, r1_h, out_h,
    gvf, vec,
    oq, ok, ov, oo, oi, o2, gx, fin_out, ovec,
    *refs,
):
    (
        pool, hid, gout, go, n1b, accs, r1s, c_v, dc_v, acc, dwg, st, dq_all, dk_all, dv_all, rk, rv, sk, sv, pbuf,
        rgx, pack, vecin, vtot, vx, brow, gvs, gbin, stay,
    ) = refs[:29]
    fb, gb = refs[29:35], refs[35:41]
    fsem, gsem = refs[41:53], refs[53:65]
    lsem, msem, ssem, ps, ks, kr, gs, gr, os, vs, vr, us, ur, bs, br, bl = refs[65:]
    z, y, x, c = where = place()
    f = 2 * z + y
    pages, own, d = c_h.shape
    n = pages * own
    blk = own // 2
    rows = 2 * own
    at_k, at_v, at_q, at_gq, at_gk, at_gv = 0, 2 * n, 4 * n, 5 * n, 6 * n, 7 * n
    x_peer, c_peer = at(z, y, 1 - x, c), at(z, y, x, 1 - c)
    meet([{"fsdp": lax.rem(f + k + 1, 8)} for k in range(7)] + [x_peer, c_peer])

    def other_half(p, run):
        @pl.when(p < 6)
        def _():
            run(dwg.at[lax.div(p, 2), :, :, :, pl.ds(pl.multiple_of(384 * lax.rem(p, 2), 128), 384)])

        @pl.when(p >= 6)
        def _():
            run(st.at[p - 6])

    def launch(p):
        other_half(p, lambda ref: remote(ref, fb[0].at[p], fsem[0].at[p], fsem[1].at[p], c_peer).start())

    def rest_out(p, run):
        @pl.when(p < 4)
        def _():
            run(oi.at[:, pl.ds(pl.multiple_of(768 * p + 384 * c, 128), 384)])

        @pl.when(jnp.logical_and(p >= 4, p < 8))
        def _():
            run(o2.at[pl.ds(pl.multiple_of(ROW * (p - 4), 32), ROW), pl.ds(pl.multiple_of(384 * c, 128), 384)])

        @pl.when(p == 8)
        def _():
            run(oo.at[:, pl.ds(pl.multiple_of(384 * c, 128), 384)])

    def fold(p):
        return Fold(where, lambda sel: acc.at[(p,) + sel], fb, fsem, (p,), KEEP_REST)

    def any_first(p):
        return remote(fb[0].at[p], fb[0].at[p], fsem[0].at[p], fsem[1].at[p], c_peer)

    def step(p, name):
        ok_p = jnp.logical_and(p >= 0, p < REST)

        @pl.when(ok_p)
        def _():
            if name == "over_x":
                fold(p).over_x(any_first(p))
            elif name == "write":
                rest_out(p, lambda view: fold(p).write(view))
            elif name == "drain":
                rest_out(p, lambda view: fold(p).drain(view))
            else:
                getattr(fold(p), name)()

    def gfold(g, w):
        cols = pl.ds(pl.multiple_of(GCOLS * w + 128 * c, 128), 128)
        return Fold(where, lambda sel: dwg.at[(g,) + sel + (cols,)], gb, gsem, (g, w), KEEP_GROUP)

    def gfirst(g, w):
        cols = pl.ds(pl.multiple_of(GCOLS * w + 128 * (1 - c), 128), 128)
        return remote(dwg.at[g, :, :, :, cols], gb[0].at[g, w], gsem[0].at[g, w], gsem[1].at[g, w], c_peer)

    def gstep(g, name):
        for w, o in enumerate((oq, ok, ov)):
            view = o.at[:, pl.ds(pl.multiple_of(GCOLS * g + 128 * c, 128), 128)]
            if name == "start":
                gfirst(g, w).start()
            elif name == "over_x":
                gfold(g, w).over_x(gfirst(g, w))
            elif name == "write":
                gfold(g, w).write(view)
            elif name == "drain":
                gfold(g, w).drain(view)
                gfirst(g, w).wait_send()
            else:
                getattr(gfold(g, w), name)()

    stages = (("over_x", 0), ("over_y", 4), ("over_z", 10), ("inside", 15), ("total", 19), ("write", 24))
    pace = 3
    last = pace * (REST + GROUPS - 1) + stages[-1][1] + 1

    def tick(t):
        for name, late in stages:
            n = t - late
            p = lax.div(n, pace)

            @pl.when(jnp.logical_and(n >= 0, jnp.logical_and(lax.rem(n, pace) == 0, p < REST + GROUPS)))
            def _():
                step(p, name)

                @pl.when(p >= REST)
                def _():
                    gstep(p - REST, name)

    firsts = [
        pltpu.make_async_copy(src, dst, lsem.at[i])
        for i, (src, dst) in enumerate(
            ((gout_h, gout), (hid_h, hid), (gm2_h, accs), (n1_h, n1b), (r1_h, r1s), (go_h, go), (c_h, c_v))
        )
    ]

    def row_block(start, size):
        return pl.ds(pl.multiple_of(start, 256), size)

    def slot(kind, j):
        return pool.at[row_block((2 * kind + lax.rem(j, 2)) * n, n), :]

    def chunk_loads(j):
        return [
            pltpu.make_async_copy(src.at[j], slot(kind, j), msem.at[kind, lax.rem(j, 2)])
            for kind, src in enumerate((gi_h, g2_h, act_h, dd_h))
        ]

    seconds = [
        pltpu.make_async_copy(src, pool.at[pl.ds(start, src.shape[0]), :], ssem.at[i])
        for i, (src, start) in enumerate(
            ((q_h, at_q), (k_h, at_k), (v_h, at_v), (gq_h, at_gq), (gk_h, at_gk), (gv_h, at_gv))
        )
    ] + [
        pltpu.make_async_copy(x_h.at[page, pl.ds(0, own), :], hid.at[pl.ds(page * own, own), :], ssem.at[6 + page])
        for page in range(pages)
    ]

    def p_copy(it, half):
        g, page = lax.div(it, pages), lax.rem(it, pages)
        return pltpu.make_async_copy(p_h.at[page, pl.ds(4 * g + 2 * half, 2)], pbuf.at[half], ps.at[half])

    pages_mine = pl.ds(pages * x, pages)
    back_out = remote(out_h.at[:, pl.ds(blk, blk), :], fin_out.at[pages_mine], bs.at[0], br.at[0], x_peer)
    stay_in = pltpu.make_async_copy(out_h.at[:, pl.ds(0, blk), :], stay, bl.at[0])
    stay_out = pltpu.make_async_copy(stay, fin_out.at[pages_mine], bl.at[1])
    back_out.start()
    for copy in firsts[:1]:
        copy.start()
    for copy in chunk_loads(0):
        copy.start()
    for copy in firsts[1:]:
        copy.start()
    for copy in chunk_loads(1):
        copy.start()
    for half in range(2):
        p_copy(0, half).start()
    stay_in.start()
    gvs[...] = gvf[...]

    def halves(value):
        low, high = value[..., :384], value[..., 384:]
        return jnp.where(c == 0, low, high), jnp.where(c == 0, high, low)

    n_chunks = gi_h.shape[0]
    firsts[0].wait()
    firsts[1].wait()
    firsts[2].wait()

    def down(j, carry):
        for copy in chunk_loads(j):
            copy.wait()
        cols = pl.ds(pl.multiple_of(j * d, d), d)
        di = (dot(gout[...], slot(1, j)[...], NT) * slot(3, j)[...].astype(F32)).astype(BF)
        accs[...] += dot(di, slot(0, j)[...], NT)
        gbin[:, cols] = jnp.sum(di.astype(F32), 0, keepdims=True)
        keep, pass_on = halves(dot(hid[...], di, TN).astype(BF))
        acc[j] = keep.reshape(4, 2, ROW, 384)
        other_half(j, lambda ref: ref.__setitem__(Ellipsis, pass_on.reshape(4, 2, ROW, 384)))
        launch(j)
        keep, pass_on = halves(dot(slot(2, j)[...], gout[...], TN).astype(BF))
        keep, pass_on = keep.reshape(2, 4, ROW, 384), pass_on.reshape(2, 4, ROW, 384)
        for p in range(4):
            acc[4 + p, j] = keep[:, p]
            if p < 2:
                dwg[2, j, :, :, 384 * p : 384 * p + 384] = pass_on[:, p]
            else:
                st[p - 2, j] = pass_on[:, p]

        @pl.when(j + 2 < n_chunks)
        def _():
            for copy in chunk_loads(j + 2):
                copy.start()

        @pl.when(j > 0)
        def _():
            lax.fori_loop(pace * (j - 1), pace * j, lambda t, carry: (tick(t), carry)[1], 0)

        return carry

    lax.fori_loop(0, n_chunks, down, 0)
    for p in range(4):
        launch(4 + p)
    stay_in.wait()
    stay_out.start()
    for copy in seconds:
        copy.start()
    for copy in firsts[3:]:
        copy.wait()

    def add(row, value):
        gvs[row : row + 1, :] += jnp.sum(value, 0, keepdims=True)

    before = pace * (n_chunks - 1)
    for page in range(pages):
        r = slice(page * own, (page + 1) * own)
        gh = accs[r, :]
        n1 = n1b[r, :].astype(F32)
        gm1 = norm_back(gh * vec[3:4, :], n1, r1s[r, 0:1])
        accs[r, :] = gm1
        ga = gm1.astype(BF)
        gout[r, :] = ga
        dc_v[page] = dot(ga, go[...], NT).astype(BF)
        add(2, ga.astype(F32))
        add(3, gh * n1)
        add(4, gh)
        tick(before + page)
    before += pages
    keep, pass_on = halves(dot(c_v[...].reshape(n, d), gout[...], TN).astype(BF))
    acc[8] = keep.reshape(4, 2, ROW, 384)
    st[2] = pass_on.reshape(4, 2, ROW, 384)
    launch(8)
    for copy in seconds:
        copy.wait()

    low_lane = lax.broadcasted_iota(jnp.int32, (own, PAIR), 1) < HEAD_DIM
    scale = 1.0 / math.sqrt(HEAD_DIM)

    def kv_send(it):
        g, page = lax.div(it, pages), lax.rem(it, pages)
        gcols = pl.ds(pl.multiple_of(g * GCOLS, GCOLS), GCOLS)
        return [
            remote(s_ref.at[page], r_ref.at[page, :, gcols], ks.at[g, page, i], kr.at[g, page, i], c_peer)
            for i, (s_ref, r_ref) in enumerate(((sk, rk), (sv, rv)))
        ]

    def attend(it, half):
        g, page = lax.div(it, pages), lax.rem(it, pages)
        here = pl.ds(pl.multiple_of(page * own, own), own)
        p_copy(it, half).wait()
        local = slice(half * PAIR, (half + 1) * PAIR)
        cols = pl.ds(pl.multiple_of(g * GCOLS + half * PAIR, PAIR), PAIR)
        qp = pool[row_block(at_q + page * own, own), cols] * jnp.array(scale, BF)
        kp = pool[row_block(at_k + page * rows, rows), cols]
        kt = kp.T
        vp = pool[row_block(at_v + page * rows, rows), cols]
        dc = dc_v[page, :, cols]
        prod = (dc.astype(F32) * c_v[page, :, cols].astype(F32)).T
        dk = None
        dv = None
        dqs = []
        for h in range(2):
            keep = low_lane if h == 0 else jnp.logical_not(low_lane)
            feats = slice(h * HEAD_DIM, (h + 1) * HEAD_DIM)
            dch = jnp.where(keep, dc, jnp.zeros_like(dc))
            qh = jnp.where(keep, qp, jnp.zeros_like(qp))
            pt = pbuf[half, h]
            delta = jnp.sum(prod[feats], axis=0, keepdims=True)
            dpt = dot(vp, dch, NT)
            dst = (pt.astype(F32) * (dpt - delta)).astype(BF)
            dvh = dot(pt, dch)
            dkh = dot(dst, qh)
            dk = dkh if dk is None else dk + dkh
            dv = dvh if dv is None else dv + dvh
            dqs.append(dot(kt[feats], dst))
        dq_all[here, cols] = (jnp.concatenate(dqs, axis=0) * scale).T.astype(BF)
        dk_all[here, cols] = dk[:own].astype(BF)
        sk[page, :, local] = dk[own:].astype(BF)
        dv_all[here, cols] = dv[:own].astype(BF)
        sv[page, :, local] = dv[own:].astype(BF)

        @pl.when(it + 1 < GROUPS * pages)
        def _():
            p_copy(it + 1, half).start()

    def group_grads(g):
        for i in range(2):
            any_first(2 * g + i).wait_send()
        gcols = pl.ds(pl.multiple_of(g * GCOLS, GCOLS), GCOLS)
        for page in range(pages):
            here = pl.ds(page * own, own)
            for copy in kv_send(g * pages + page):
                copy.wait_recv()
            dk_all[here, gcols] = dk_all[here, gcols] + rk[page, :, gcols]
            dv_all[here, gcols] = dv_all[here, gcols] + rv[page, :, gcols]
        for w, grad in enumerate((dq_all, dk_all, dv_all)):
            value = grad[:, gcols]
            dwg[g, :, :, :, w * GCOLS : (w + 1) * GCOLS] = (
                dot(hid[...], value, TN).astype(BF).reshape(4, 2, ROW, GCOLS)
            )
            if w != 1:
                brow[w : w + 1, gcols] = jnp.sum(value.astype(F32), 0, keepdims=True)
        gstep(g, "start")

    def gx_send(page):
        return remote(go.at[pl.ds(pl.multiple_of(page * blk, 128), blk), :], rgx.at[page], gs.at[page], gr.at[page], x_peer)

    def input_grads(page):
        here = pl.ds(pl.multiple_of(page * own, own), own)
        total = accs[here, :]
        for grad, start in ((dq_all, at_gq), (dk_all, at_gk), (dv_all, at_gv)):
            total = total + dot(grad[here, :], pool[pl.ds(start, d), :], NT)
        accs[here, :] = total
        go[pl.ds(pl.multiple_of(page * blk, 128), blk), :] = total[blk:].astype(BF)
        gx_send(page).start()
        gx_store(page, 0).start()

    def gx_store(page, side):
        src = accs.at[pl.ds(pl.multiple_of(page * own + side * blk, 128), blk), :]
        return pltpu.make_async_copy(src, gx.at[pages * (x if side == 0 else 1 - x) + page], os.at[page, side])

    n_it = GROUPS * pages

    def unit(it, carry):
        for half in range(2):

            if half == 0:

                @pl.when(jnp.logical_and(it >= pages, it < n_it))
                def _():
                    for copy in kv_send(it - pages):
                        copy.wait_send()

            @pl.when(it < n_it)
            def _():
                attend(it, half)

            if half == 1:

                @pl.when(it < n_it)
                def _():
                    for copy in kv_send(it):
                        copy.start()

            tick(before + 2 * it + half)

        @pl.when(jnp.logical_and(it > 0, jnp.logical_and(lax.rem(it, pages) == 0, it <= n_it)))
        def _():
            group_grads(lax.div(it, pages) - 1)

        page = it - n_it

        @pl.when(jnp.logical_and(page >= 0, page < pages))
        def _():
            input_grads(page)

        return carry

    def vec_send(k):
        to = lax.rem(f + k + 1, 8)
        return remote(pack.at[to], vecin.at[k], vs.at[k], vr.at[k], {"fsdp": to})

    vec_x = lambda: remote(vtot, vx.at[0], us.at[0], ur.at[0], x_peer)
    vec_c = lambda: remote(vx.at[1], vx.at[2], us.at[1], ur.at[1], c_peer)

    def small_pack():
        for i in range(8):
            row = brow[0:1, :] if i == 0 else brow[2:3, :] if i == 1 else gvs[i : i + 1, :]
            for j in range(8):
                pack[j, i : i + 1, :ROW] = row[:, ROW * j : ROW * (j + 1)]
        for j in range(8):
            for i in range(3):
                pack[j, 8 + i : 9 + i, :] = gbin[:, (3 * j + i) * 128 : (3 * j + i + 1) * 128]
        for k in range(7):
            vec_send(k).start()

    def small_sum():
        total = pack[f]
        for k in range(7):
            vec_send(k).wait_recv()
            total = total + vecin[k]
        vtot[...] = total
        vec_x().start()

    def small_pair():
        vec_x().wait_recv()
        vx[1] = vtot[...] + vx[0]
        vec_c().start()

    def all_steps(it, carry):
        unit(it, carry)
        for when, run in ((n_it, small_pack), (n_it + 3, small_sum), (n_it + 6, small_pair)):
            pl.when(it == when)(run)
        return carry

    lax.fori_loop(0, (last - before + 2) // 2, all_steps, 0)
    for page in range(pages):
        gx_send(page).wait_recv()
        accs[page * own + blk : (page + 1) * own, :] = rgx[page].astype(F32)
        gx_store(page, 1).start()
    vec_c().wait_recv()
    ovec[...] = vx[1] + vx[2]

    def finish(p, carry):
        step(p, "drain")
        return carry

    lax.fori_loop(0, REST, finish, 0)
    for g in range(GROUPS):
        gstep(g, "drain")
    for p in range(6, REST):
        any_first(p).wait_send()
    for it in range(n_it - pages, n_it):
        for copy in kv_send(it):
            copy.wait_send()
    for page in range(pages):
        gx_send(page).wait_send()
        gx_store(page, 0).wait()
        gx_store(page, 1).wait()
    for k in range(7):
        vec_send(k).wait_send()
    back_out.wait()
    stay_out.wait()
    vec_x().wait_send()
    vec_c().wait_send()


def bwd(kept, shards):
    (gq, gk, gv, xall, q, k, v, ctx, p, go, gi, g2, act, dd, hid, gout, n1, gm2, r1, out, gvs, vec) = kept
    pages, own, d = ctx.shape
    rows, blk = 2 * own, own // 2
    n = pages * own
    dma = pltpu.SemaphoreType.DMA
    vm = pltpu.VMEM
    sds = jax.ShapeDtypeStruct
    n_chunks = act.shape[0]
    flat = lambda a: a.reshape(-1, d)
    args = (
        flat(gq), flat(gk), flat(gv), xall, flat(q), flat(k), flat(v), ctx, p, flat(go),
        gi.reshape(n_chunks, d, d), g2.reshape(n_chunks, d, d), act, dd, hid, gout, n1, gm2, r1, out, gvs, vec,
    )
    res = call(
        bwd_body,
        (24 * n * d * d + pages * 10 * own * rows * d, 60 << 20, 0),
        in_specs=[ANY] * 20 + [VM, VM],
        out_specs=[VM] * 6 + [ANY, ANY, VM],
        out_shape=[sds(shape, F32) for shape in shards]
        + [sds((2 * pages, blk, d), F32), sds((2 * pages, blk, d), BF), sds((16, 128), F32)],
        scratch_shapes=[
            vm((8 * n, d), BF), vm((n, d), BF), vm((n, d), BF), vm((d, d), BF), vm((n, d), BF), vm((n, d), F32),
            vm((n, 128), F32), vm((pages, own, d), BF), vm((pages, own, d), BF),
            vm((REST, 4, 2, ROW, 384), BF), vm((GROUPS, 4, 2, ROW, 3 * GCOLS), BF), vm((3, 4, 2, ROW, 384), BF),
            vm((n, d), BF), vm((n, d), BF), vm((n, d), BF),
            vm((pages, own, d), BF), vm((pages, own, d), BF), vm((pages, own, GCOLS), BF), vm((pages, own, GCOLS), BF),
            vm((2, 2, rows, own), BF), vm((pages, blk, d), BF),
            vm((8, 16, 128), F32), vm((7, 16, 128), F32), vm((16, 128), F32), vm((3, 16, 128), F32), vm((8, d), F32),
            vm((8, d), F32), vm((1, n_chunks * d), F32), vm((pages, blk, d), BF),
        ]
        + fold_bufs(384, KEEP_REST, REST)
        + fold_bufs(128, KEEP_GROUP, GROUPS, 3)
        + fold_sems(REST)
        + fold_sems(GROUPS, 3)
        + [
            dma((7,)), dma((4, 2)), dma((6 + pages,)), dma((2,)), dma((GROUPS, pages, 2)), dma((GROUPS, pages, 2)),
            dma((pages,)), dma((pages,)), dma((pages, 2)), dma((7,)), dma((7,)), dma((2,)), dma((2,)),
            dma((1,)), dma((1,)), dma((2,)),
        ],
        params=dict(collective_id=1, has_side_effects=True, vmem_limit_bytes=64 << 20),
        name="backward_reduce",
    )(*args)
    return res[:6], res[6], res[7], res[8]


def finish_body(*refs):
    n = 8
    src, small, dst, lows = refs[:n], refs[n], refs[n + 1 : 2 * n + 1], refs[2 * n + 1 : 2 * n + 10]
    held, sem_in, sem_out = refs[2 * n + 10 : 3 * n + 10], refs[-2], refs[-1]
    loads = [pltpu.make_async_copy(src[i], held[i], sem_in.at[i]) for i in range(n)]
    stores = [pltpu.make_async_copy(held[i], dst[i], sem_out.at[i]) for i in range(n)]
    for copy in loads:
        copy.start()
    width = lows[0].shape[0]
    for i in range(8):
        lows[i][...] = small[i, :width]
    for i in range(3):
        lows[8][128 * i : 128 * (i + 1)] = small[8 + i, :]
    for load, store in zip(loads, stores):
        load.wait()
        store.start()
    for copy in stores:
        copy.wait()


def finish(arrays, small, width, wide):
    sds = jax.ShapeDtypeStruct
    dma = pltpu.SemaphoreType.DMA
    n = len(arrays)
    return call(
        finish_body,
        (0, 2 * sum(a.size * a.dtype.itemsize for a in arrays), 0),
        in_specs=[ANY] * n + [VM],
        out_specs=[ANY] * n + [VM] * 9,
        out_shape=[sds(a.shape, a.dtype) for a in arrays] + [sds((width,), F32)] * 8 + [sds((wide,), F32)],
        scratch_shapes=[pltpu.VMEM(a.shape, a.dtype) for a in arrays] + [dma((n,)), dma((n,))],
        name="finish",
    )(*arrays, small)


SWAP_X = [(0, 2), (2, 0), (1, 3), (3, 1)]
SWAP_C = [(0, 1), (1, 0), (2, 3), (3, 2)]


def swap(value, pairs):
    return lax.ppermute(value, "seq", pairs)


def per_device(
    fsdp, inputs, lengths, w_query, b_query, w_key, w_value, b_value, w_out, b_out,
    gain_one, shift_one, w_inner, b_inner, w_outer, b_outer, gain_two, shift_two, cotangent,
):
    pages_all, blk, d = inputs.shape
    pages = pages_all // 2
    s = lax.axis_index("seq")
    x_at = lax.div(s, 2)
    direct = fsdp == 8
    ws = (w_query, w_key, w_value, w_out, w_inner, w_outer)
    shards = [w.shape for w in ws]
    width = b_query.shape[0]
    names = (b_query, b_value, b_out, gain_one, shift_one, b_outer, gain_two, shift_two)

    def pages_of(array, side):
        return lax.dynamic_slice_in_dim(array, side * pages, pages, 0)

    order = jnp.stack([s, s ^ 2, s ^ 1, s ^ 3]).astype(jnp.int32)
    thr = pages_of(lengths, x_at).astype(jnp.int32)[:, None] - order[None, :] * blk
    if direct:
        kept = fwd(lengths.astype(jnp.int32), inputs, cotangent, ws, names + (b_inner,))
    else:
        wq, wk, wv, wo, wi, w2 = [lax.all_gather(w, "fsdp", axis=0, tiled=True) for w in ws]
        vec = jnp.concatenate(names + (b_inner,)).reshape(12, width)
        gvec = lax.all_gather(vec, "fsdp", axis=0)
        vec_full = jnp.swapaxes(gvec[:, :8], 0, 1).reshape(8, d).astype(F32)
        bin_full = gvec[:, 8:].reshape(1, -1).astype(F32)

        def own_rows(array):
            other = swap(pages_of(array, 1 - x_at), SWAP_X)
            return jnp.concatenate([pages_of(array, x_at), other], axis=1)

        xown, cown = own_rows(inputs), own_rows(cotangent)
        xall = jnp.concatenate([xown, swap(xown, SWAP_C)], axis=1)
        q, k, v, p, ctx = attn_fwd(thr, xall, wq, wk, wv, vec_full)
    if direct:
        tot, grad_inputs, output, tvec = bwd(kept, shards)
        res = finish((output, grad_inputs) + tuple(tot), tvec, width, b_inner.shape[0])
        output, grad_inputs, tot, small, g_bi = res[0], res[1], res[2:8], res[8:16], res[16]
    else:
        out, gm1, dctx, dwo, dwi, dw2, gv_ffn, gbin = ffn(ctx, xall, cown, wo, wi, w2, vec_full, bin_full)
        dq, dk, dk_send, dv, dv_send = attn_bwd(q, k, v, p, ctx, dctx)
        dkr, dvr = swap(dk_send, SWAP_C), swap(dv_send, SWAP_C)
        gx_a, gx_b, dwq, dwk, dwv, gv_proj = proj(xall, dq, dk, dkr, dv, dvr, gm1, wq, wk, wv)
        gv = jnp.concatenate([gv_proj[:2], gv_ffn[2:]], axis=0)
        by_owner = jnp.concatenate(
            [jnp.swapaxes(gv.reshape(8, fsdp, width), 0, 1), gbin.reshape(fsdp, 4, width)], axis=1
        )
        tot = [
            lax.psum(lax.psum_scatter(g, "fsdp", scatter_dimension=0, tiled=True), "seq").astype(F32)
            for g in (dwq, dwk, dwv, dwo, dwi, dw2)
        ]
        tvec = lax.psum(lax.psum_scatter(by_owner, "fsdp", scatter_dimension=0, tiled=True)[0], "seq")

        def joined(mine, other):
            here = lax.dynamic_update_slice_in_dim(
                jnp.zeros((pages_all, blk, d), mine.dtype), mine, x_at * pages, 0
            )
            return lax.dynamic_update_slice_in_dim(here, other, (1 - x_at) * pages, 0)

        output = joined(out[:, :blk], swap(out[:, blk:], SWAP_X))
        grad_inputs = joined(gx_a, swap(gx_b, SWAP_X).astype(F32))
        small = [tvec[i] for i in range(8)]
        g_bi = tvec[8:].reshape(-1)
    g_bq, g_bv, g_bo, g_g1, g_s1, g_bo2, g_g2, g_s2 = small
    t_q, t_k, t_v, t_o, t_i, t_2 = tot
    return (
        output, grad_inputs, t_q, g_bq, t_k, t_v, g_bv, t_o, g_bo, g_g1, g_s1,
        t_i, g_bi, t_2, g_bo2, g_g2, g_s2,
    )


def solution(mesh):
    vec, mat, act = P("fsdp"), P("fsdp", None), P("fsdp", "seq", None)
    return jax.shard_map(
        functools.partial(per_device, mesh.shape["fsdp"]),
        mesh=mesh,
        in_specs=(act, vec, mat, vec, mat, mat, vec, mat, vec, vec, vec, mat, vec, mat, vec, vec, vec, act),
        out_specs=(act, act, mat, vec, mat, mat, vec, mat, vec, vec, vec, mat, vec, mat, vec, vec, vec),
        check_vma=False,
    )
```

```python
import functools
import math

import jax
import jax.numpy as jnp
from jax import lax
from jax.experimental import pallas as pl
from jax.experimental.pallas import tpu as pltpu
from jax.sharding import PartitionSpec as P

HEADS = 12
HEAD_DIM = 64
PAIR = 2 * HEAD_DIM
NEG = -1e30
EPS = 1e-12
BF = jnp.bfloat16
F32 = jnp.float32
MESH = pl.DeviceIdType.MESH
ANY = pl.BlockSpec(memory_space=pl.ANY)
VM = pl.BlockSpec(memory_space=pltpu.VMEM)
CHUNK = 1024
ROW = 96
VMEM_CAP = 60 << 20

NN = (((1,), (0,)), ((), ()))
NT = (((1,), (1,)), ((), ()))
TN = (((0,), (0,)), ((), ()))


def dot(a, b, dims=NN):
    return lax.dot_general(a, b, dims, preferred_element_type=F32)


def call(body, cost, **kw):
    flops, byts, trans = cost
    params = dict(vmem_limit_bytes=VMEM_CAP)
    params.update(kw.pop("params", {}))
    return pl.pallas_call(
        body,
        compiler_params=pltpu.CompilerParams(**params),
        cost_estimate=pl.CostEstimate(
            flops=int(flops), bytes_accessed=int(byts), transcendentals=int(trans)
        ),
        **kw,
    )


def attn_fwd_body(thr, xall, wq, wk, wv, vec, q_o, k_o, v_o, p_o, c_o, bias):
    page = pl.program_id(0)
    x_all = xall[0]
    own = x_all.shape[0] // 2
    query = (dot(x_all[:own], wq[...]) + vec[0:1, :]).astype(BF)
    q_o[0] = query
    k_o[0] = dot(x_all, wk[...]).astype(BF)
    v_o[0] = (dot(x_all, wv[...]) + vec[1:2, :]).astype(BF)
    blk = x_all.shape[0] // 4
    place = lax.broadcasted_iota(jnp.int32, (blk, own), 0)
    for b in range(4):
        bias[b * blk : (b + 1) * blk, :] = jnp.where(place < thr[page, b], 0.0, NEG)
    low_lane = lax.broadcasted_iota(jnp.int32, (own, PAIR), 1) < HEAD_DIM

    def pair(i, carry):
        cols = pl.ds(pl.multiple_of(i * PAIR, PAIR), PAIR)
        qp = q_o[0, :, cols] * jnp.array(1.0 / math.sqrt(HEAD_DIM), BF)
        kp = k_o[0, :, cols]
        vt = v_o[0, :, cols].T
        outs = []
        for h in range(2):
            keep = low_lane if h == 0 else jnp.logical_not(low_lane)
            qh = jnp.where(keep, qp, jnp.zeros_like(qp))
            st = dot(kp, qh, NT) + bias[...]
            top = jnp.max(st, axis=0, keepdims=True)
            ex = jnp.exp(st - top)
            tot = jnp.sum(ex, axis=0, keepdims=True)
            pt = (ex * (1.0 / tot)).astype(BF)
            p_o[0, 2 * i + h] = pt
            outs.append(dot(vt[h * HEAD_DIM : (h + 1) * HEAD_DIM], pt))
        c_o[0, :, cols] = jnp.concatenate(outs, axis=0).T.astype(BF)
        return carry

    lax.fori_loop(0, HEADS // 2, pair, 0)


def attn_fwd(thr, xall, wq, wk, wv, vec):
    pages, rows, d = xall.shape
    own = rows // 2
    const = lambda p, t: (0, 0)
    by_page = lambda p, t: (p, 0, 0)
    one = pl.Buffered(1)
    return call(
        attn_fwd_body,
        (
            pages * (2 * d * d * (own + 2 * rows) + 4 * own * rows * d),
            pages * rows * d * 2 * 4 + 6 * d * d + pages * HEADS * own * rows * 2,
            pages * HEADS * own * rows,
        ),
        grid_spec=pltpu.PrefetchScalarGridSpec(
            num_scalar_prefetch=1,
            grid=(pages,),
            in_specs=[pl.BlockSpec((1, rows, d), by_page)]
            + [pl.BlockSpec((d, d), const, pipeline_mode=one)] * 3
            + [pl.BlockSpec((8, d), const)],
            out_specs=[
                pl.BlockSpec((1, own, d), by_page),
                pl.BlockSpec((1, rows, d), by_page),
                pl.BlockSpec((1, rows, d), by_page),
                pl.BlockSpec((1, HEADS, rows, own), lambda p, t: (p, 0, 0, 0)),
                pl.BlockSpec((1, own, d), by_page),
            ],
            scratch_shapes=[pltpu.VMEM((rows, own), F32)],
        ),
        out_shape=[
            jax.ShapeDtypeStruct((pages, own, d), BF),
            jax.ShapeDtypeStruct((pages, rows, d), BF),
            jax.ShapeDtypeStruct((pages, rows, d), BF),
            jax.ShapeDtypeStruct((pages, HEADS, rows, own), BF),
            jax.ShapeDtypeStruct((pages, own, d), BF),
        ],
        name="attn_fwd",
    )(thr, xall, wq, wk, wv, vec)


def attn_bwd_body(q, k, v, p, ctx, dctx, dq_o, dk_own, dk_oth, dv_own, dv_oth):
    own = q.shape[1]
    low_lane = lax.broadcasted_iota(jnp.int32, (own, PAIR), 1) < HEAD_DIM
    scale = 1.0 / math.sqrt(HEAD_DIM)

    def pair(i, carry):
        cols = pl.ds(pl.multiple_of(i * PAIR, PAIR), PAIR)
        qp = q[0, :, cols] * jnp.array(scale, BF)
        kp = k[0, :, cols]
        kt = kp.T
        vp = v[0, :, cols]
        dc = dctx[0, :, cols]
        prod = (dc.astype(F32) * ctx[0, :, cols].astype(F32)).T
        dk = None
        dv = None
        dqs = []
        for h in range(2):
            keep = low_lane if h == 0 else jnp.logical_not(low_lane)
            feats = slice(h * HEAD_DIM, (h + 1) * HEAD_DIM)
            dch = jnp.where(keep, dc, jnp.zeros_like(dc))
            qh = jnp.where(keep, qp, jnp.zeros_like(qp))
            pt = p[0, 2 * i + h]
            delta = jnp.sum(prod[feats], axis=0, keepdims=True)
            dpt = dot(vp, dch, NT)
            dst = (pt.astype(F32) * (dpt - delta)).astype(BF)
            dvh = dot(pt, dch)
            dkh = dot(dst, qh)
            dk = dkh if dk is None else dk + dkh
            dv = dvh if dv is None else dv + dvh
            dqs.append(dot(kt[feats], dst))
        dq_o[0, :, cols] = (jnp.concatenate(dqs, axis=0) * scale).T.astype(BF)
        dk_own[0, :, cols] = dk[:own].astype(BF)
        dk_oth[0, :, cols] = dk[own:].astype(BF)
        dv_own[0, :, cols] = dv[:own].astype(BF)
        dv_oth[0, :, cols] = dv[own:].astype(BF)
        return carry

    lax.fori_loop(0, HEADS // 2, pair, 0)


def attn_bwd(q, k, v, p, ctx, dctx):
    pages, own, d = q.shape
    rows = k.shape[1]
    by_page = lambda i: (i, 0, 0)
    o = pl.BlockSpec((1, own, d), by_page)
    r = pl.BlockSpec((1, rows, d), by_page)
    return call(
        attn_bwd_body,
        (pages * 10 * own * rows * d, pages * (own * rows * HEADS * 2 + 10 * own * d * 2), 0),
        grid=(pages,),
        in_specs=[o, r, r, pl.BlockSpec((1, HEADS, rows, own), lambda i: (i, 0, 0, 0)), o, o],
        out_specs=[o] * 5,
        out_shape=[jax.ShapeDtypeStruct((pages, own, d), BF)] * 5,
        name="attn_bwd",
    )(q, k, v, p, ctx, dctx)


def normal_parts(v):
    bell = jnp.exp(v * v * -0.5)
    t = 1.0 / (1.0 + jnp.abs(v) * (0.3275911 / math.sqrt(2.0)))
    tail = t * (
        0.127414796 + t * (-0.142248368 + t * (0.7107068705 + t * (-0.7265760135 + t * 0.5307027145)))
    )
    tail = tail * bell
    return jnp.where(v >= 0.0, 1.0 - tail, tail), bell * (1.0 / math.sqrt(2.0 * math.pi))


def row_norm(v):
    centered = v - jnp.mean(v, -1, keepdims=True)
    inv = lax.rsqrt(jnp.mean(centered * centered, -1, keepdims=True) + EPS)
    return centered * inv, inv


def norm_back(e, n, inv):
    return inv * (e - jnp.mean(e, -1, keepdims=True) - n * jnp.mean(e * n, -1, keepdims=True))


def ffn_body(
    ctx, xall, cown, wo, wi_h, w2_h, vec, b_in,
    out, gm1_o, dctx_o, dwo_o, dwi_h, dw2_h, gvec, gbin,
    wi, w2, act, din, dgel, hid, gout, gatt, n1s, h1s, accs, r1s, dwi, dw2, lsem, osem,
):
    n, ff = act.shape
    pages, own, d = ctx.shape

    def cols_of(j):
        return pl.ds(pl.multiple_of(j * CHUNK, CHUNK), CHUNK)

    def loads(j):
        cols = cols_of(j)
        return (
            pltpu.make_async_copy(wi_h.at[:, cols], wi.at[:, cols], lsem.at[0, j]),
            pltpu.make_async_copy(w2_h.at[cols, :], w2.at[cols, :], lsem.at[1, j]),
        )

    def store_w2(j):
        return pltpu.make_async_copy(dw2.at[cols_of(j), :], dw2_h.at[cols_of(j), :], osem.at[0, j])

    def store_wi(j):
        return pltpu.make_async_copy(dwi.at[:, cols_of(j)], dwi_h.at[:, cols_of(j)], osem.at[1, j])

    n_chunks = ff // CHUNK
    for j in range(n_chunks):
        for copy in loads(j):
            copy.start()
    gvec[...] = jnp.zeros_like(gvec)

    def add(row, value):
        gvec[row : row + 1, :] += jnp.sum(value, 0, keepdims=True)

    for p in range(pages):
        r = slice(p * own, (p + 1) * own)
        mid = xall[p].astype(F32) + (dot(ctx[p], wo[...]) + vec[2:3, :])
        n1, r1 = row_norm(mid)
        n1s[r, :] = n1
        r1s[r, :] = jnp.broadcast_to(r1, (own, 128))
        h1 = n1 * vec[3:4, :] + vec[4:5, :]
        h1s[r, :] = h1
        hid[r, :] = h1.astype(BF)
    accs[...] = jnp.zeros_like(accs)

    def up(j, carry):
        cols = cols_of(j)
        for copy in loads(j):
            copy.wait()
        pre = dot(hid[...], wi[:, cols]) + b_in[:, cols]
        big, bell = normal_parts(pre)
        a = (pre * big).astype(BF)
        dgel[:, cols] = (big + pre * bell).astype(BF)
        act[:, cols] = a
        accs[...] += dot(a, w2[cols, :])
        return carry

    lax.fori_loop(0, n_chunks, up, 0)
    for p in range(pages):
        r = slice(p * own, (p + 1) * own)
        mid = h1s[r, :] + (accs[r, :] + vec[5:6, :])
        n2, r2 = row_norm(mid)
        out[p] = (n2 * vec[6:7, :] + vec[7:8, :]).astype(BF)
        cot = cown[p].astype(F32)
        gm2 = norm_back(cot * vec[6:7, :], n2, r2)
        go = gm2.astype(BF)
        gout[r, :] = go
        accs[r, :] = gm2
        add(5, go.astype(F32))
        add(6, cot * n2)
        add(7, cot)

    def down(j, carry):
        cols = cols_of(j)
        di = (dot(gout[...], w2[cols, :], NT) * dgel[:, cols].astype(F32)).astype(BF)
        din[:, cols] = di
        accs[...] += dot(di, wi[:, cols], NT)
        gbin[:, cols] = jnp.sum(di.astype(F32), 0, keepdims=True)
        dw2[cols, :] = dot(act[:, cols], gout[...], TN).astype(BF)
        store_w2(j).start()
        return carry

    lax.fori_loop(0, n_chunks, down, 0)
    for p in range(pages):
        r = slice(p * own, (p + 1) * own)
        gh = accs[r, :]
        n1 = n1s[r, :]
        gm1 = norm_back(gh * vec[3:4, :], n1, r1s[r, 0:1])
        gm1_o[p] = gm1
        ga = gm1.astype(BF)
        gatt[r, :] = ga
        dctx_o[p] = dot(ga, wo[...], NT).astype(BF)
        add(2, ga.astype(F32))
        add(3, gh * n1)
        add(4, gh)
    hid_t = hid[...].T

    def grads(j, carry):
        cols = cols_of(j)
        dwi[:, cols] = dot(hid_t, din[:, cols]).astype(BF)
        store_wi(j).start()
        return carry

    lax.fori_loop(0, n_chunks, grads, 0)
    dwo_o[...] = dot(ctx[...].reshape(n, d), gatt[...], TN).astype(BF)
    for j in range(n_chunks):
        store_w2(j).wait()
        store_wi(j).wait()


def ffn(ctx, xall, cown, wo, wi, w2, vec, b_in):
    pages, own, d = ctx.shape
    ff = wi.shape[1]
    n = pages * own
    sds = jax.ShapeDtypeStruct
    vm = pltpu.VMEM
    dma = pltpu.SemaphoreType.DMA
    return call(
        ffn_body,
        (n * d * (12 * ff + 6 * d), 4 * d * ff * 2 + 12 * n * d * 2, n * ff),
        grid=(1,),
        in_specs=[
            pl.BlockSpec((pages, own, d), lambda i: (0, 0, 0)),
            pl.BlockSpec((pages, own, d), lambda i: (0, 0, 0)),
            VM, VM, ANY, ANY, VM, VM,
        ],
        out_specs=[VM] * 4 + [ANY, ANY, VM, VM],
        out_shape=[
            sds((pages, own, d), BF), sds((pages, own, d), F32), sds((pages, own, d), BF),
            sds((d, d), BF), sds((d, ff), BF), sds((ff, d), BF), sds((8, d), F32), sds((1, ff), F32),
        ],
        scratch_shapes=[
            vm((d, ff), BF), vm((ff, d), BF), vm((n, ff), BF), vm((n, ff), BF), vm((n, ff), BF),
            vm((n, d), BF), vm((n, d), BF), vm((n, d), BF), vm((n, d), F32), vm((n, d), F32),
            vm((n, d), F32), vm((n, 128), F32), vm((d, ff), BF), vm((ff, d), BF),
            dma((2, ff // CHUNK)), dma((2, ff // CHUNK)),
        ],
        params=dict(vmem_limit_bytes=63 << 20),
        name="ffn",
    )(ctx, xall, cown, wo, wi, w2, vec, b_in)


def proj_body(
    xall, dq, dk, dkr, dv, dvr, gm1, wq, wk, wv,
    ga_o, gb_o, dwq_o, dwk_o, dwv_o, gvec, x_all, dq_all, dk_all, dv_all,
):
    page = pl.program_id(0)
    own = xall.shape[1]
    blk = own // 2
    here = pl.ds(pl.multiple_of(page * own, own), own)
    x_all[here, :] = xall[0]
    dq_v = dq[0]
    dk_v = (dk[0].astype(F32) + dkr[0].astype(F32)).astype(BF)
    dv_v = (dv[0].astype(F32) + dvr[0].astype(F32)).astype(BF)
    dq_all[here, :] = dq_v
    dk_all[here, :] = dk_v
    dv_all[here, :] = dv_v
    gx = gm1[0] + dot(dq_v, wq[...], NT) + dot(dk_v, wk[...], NT) + dot(dv_v, wv[...], NT)
    ga_o[0] = gx[:blk]
    gb_o[0] = gx[blk:].astype(BF)

    @pl.when(page == 0)
    def _():
        gvec[...] = jnp.zeros_like(gvec)

    gvec[0:1, :] += jnp.sum(dq_v.astype(F32), 0, keepdims=True)
    gvec[1:2, :] += jnp.sum(dv_v.astype(F32), 0, keepdims=True)

    @pl.when(page == pl.num_programs(0) - 1)
    def _():
        x_t = x_all[...].T
        dwq_o[...] = dot(x_t, dq_all[...]).astype(BF)
        dwk_o[...] = dot(x_t, dk_all[...]).astype(BF)
        dwv_o[...] = dot(x_t, dv_all[...]).astype(BF)


def proj(xall, dq, dk, dkr, dv, dvr, gm1, wq, wk, wv):
    pages, own, d = dq.shape
    blk = own // 2
    n = pages * own
    by_page = lambda p: (p, 0, 0)
    const = lambda p: (0, 0)
    one = pl.Buffered(1)
    half = pl.BlockSpec((1, blk, d), by_page)
    whole = pl.BlockSpec((1, own, d), by_page)
    square = pl.BlockSpec((d, d), const, pipeline_mode=one)
    return call(
        proj_body,
        (12 * n * d * d, 12 * d * d + 16 * n * d, 0),
        grid=(pages,),
        in_specs=[whole] * 7 + [square] * 3,
        out_specs=[half, half] + [square] * 3 + [pl.BlockSpec((8, d), const)],
        out_shape=[
            jax.ShapeDtypeStruct((pages, blk, d), F32),
            jax.ShapeDtypeStruct((pages, blk, d), BF),
        ]
        + [jax.ShapeDtypeStruct((d, d), BF)] * 3
        + [jax.ShapeDtypeStruct((8, d), F32)],
        scratch_shapes=[pltpu.VMEM((n, d), BF)] * 4,
        name="proj_bwd",
    )(xall, dq, dk, dkr, dv, dvr, gm1, wq, wk, wv)


def place():
    f, s = lax.axis_index("fsdp"), lax.axis_index("seq")
    return lax.div(f, 2), lax.rem(f, 2), lax.div(s, 2), lax.rem(s, 2)


def at(z, y, x, c):
    return {"fsdp": 2 * z + y, "seq": 2 * x + c}


def meet(others):
    barrier = pltpu.get_barrier_semaphore()
    for other in others:
        pl.semaphore_signal(barrier, inc=1, device_id=other, device_id_type=MESH)
    pl.semaphore_wait(barrier, len(others))


def remote(src, dst, send, recv, other):
    return pltpu.make_async_remote_copy(
        src_ref=src, dst_ref=dst, send_sem=send, recv_sem=recv,
        device_id=other, device_id_type=MESH,
    )


def begin(copy):
    copy.start()
    return copy


class Spread:
    def __init__(self, where, src, dst, row0, col0, width, sems, key, from0=None):
        self.z, self.y, self.x, self.c = where
        z, y, x, c = where
        zs, zr, fs, ys, yr, xs, xr, cs, cr, lo = sems
        k = key
        cols = pl.ds(pl.multiple_of(col0 + width * c, 128), width)
        origin = pl.ds(pl.multiple_of((col0 if from0 is None else from0) + width * c, 128), width)
        full = pl.ds(row0, ROW)
        mine = pl.ds(pl.multiple_of(row0 + (ROW - YROWS) * x, 16), YROWS)
        lacks = pl.ds(pl.multiple_of(row0 + YROWS * x, 16), ROW - YROWS)
        near, far, across = z + 1 - 2 * lax.rem(z, 2), lax.rem(z + 2, 4), 3 - z
        self.inner = jnp.logical_or(z == 1, z == 2)
        self.local = lambda: pltpu.make_async_copy(src.at[full, origin], dst.at[z, y, full, cols], lo.at[k])

        def send(block, n, target, sem):
            from_ref = src.at[full, origin] if block is None else dst.at[block, y, full, cols]
            b = z if block is None else block
            return remote(from_ref, dst.at[b, y, full, cols], sem, zr.at[k + (n,)], at(target, y, x, c))

        self.a = lambda: send(None, 0, near, zs.at[k + (0,)])
        self.b = lambda: send(None, 1, far, zs.at[k + (1,)])
        self.d = lambda: send(None, 2, across, zs.at[k + (2,)])
        self.fwd = lambda: send(far, 2, near, fs.at[k])
        yv = lambda: dst.at[:, y, mine, cols]
        self.ycopy = lambda: remote(yv(), yv(), ys.at[k], yr.at[k], at(z, 1 - y, x, c))
        xv = lambda: dst.at[:, 1 - y, lacks, cols]
        self.xcopy = lambda: remote(xv(), xv(), xs.at[k], xr.at[k], at(z, y, 1 - x, c))
        cv = lambda: dst.at[:, :, full, cols]
        self.ccopy = lambda: remote(cv(), cv(), cs.at[k], cr.at[k], at(z, y, x, 1 - c))

    def along_z(self):
        self.local().start()
        self.b().start()
        self.a().start()

        @pl.when(self.inner)
        def _():
            self.d().start()

    def forward(self):
        self.b().wait_recv()

        @pl.when(self.inner)
        def _():
            self.fwd().start()

    def along_y(self):
        self.a().wait_recv()
        self.d().wait_recv()
        self.local().wait()
        self.ycopy().start()

    def along_x(self):
        self.ycopy().wait_recv()
        self.xcopy().start()

    def to_core(self):
        self.xcopy().wait_recv()
        self.ccopy().start()

    def arrive(self):
        self.ccopy().wait_recv()

    def drain(self):
        self.a().wait_send()
        self.b().wait_send()

        @pl.when(self.inner)
        def _():
            self.d().wait_send()
            self.fwd().wait_send()

        self.ycopy().wait_send()
        self.xcopy().wait_send()
        self.ccopy().wait_send()


def spread_sems(*lead):
    dma = pltpu.SemaphoreType.DMA
    return [dma(lead + (3,)), dma(lead + (3,))] + [dma(lead)] * 8


GROUPS = 3
GCOLS = 256
REST = 9
EARLY = 3
YROWS = 64


def fwd_body(
    lens, x_in, cot, wq, wk, wv, wo, wi, w2, *refs,
):
    smalls = refs[:9]
    (
        gq_h, gk_h, gv_h, xall_h, q_h, k_h, v_h, c_h, p_o,
        go_h, gi_h, g2_h, act_h, dd_h, hid_h, gout_h, n1_h, gm2_h, r1_h, out_h, gvs, vec,
    ) = refs[9:31]
    (
        gq, gk, gv, go, gi, g2, xall, q_o, k_o, v_o, c_o, cown, bias, pbuf, vpk, gvec, b_in,
        act, dd, hid, gout, n1b, n1s, accs, r1s,
    ) = refs[31:56]
    qs, rs = refs[56:66], refs[66:76]
    asend, arecv, aloc, vs, vr, ps, outs_sem, chunk_sem = refs[76:]
    z, y, x, c = where = place()
    f = 2 * z + y
    pages, rows = xall.shape[0], xall.shape[1]
    own, blk = rows // 2, rows // 4
    width = smalls[0].shape[-1]
    for i in range(8):
        vpk[i : i + 1, :width] = smalls[i][...].astype(F32).reshape(1, width)
    for i in range(3):
        vpk[8 + i : 9 + i, :] = smalls[8][128 * i : 128 * (i + 1)].astype(F32).reshape(1, 128)
    gvec[f] = vpk[...]
    x_peer, c_peer = at(z, y, 1 - x, c), at(z, y, x, 1 - c)
    meet([{"fsdp": lax.rem(f + k + 1, 8)} for k in range(7)] + [x_peer, c_peer])

    groups = [
        [Spread(where, src, dst, 0, GCOLS * g, GCOLS // 2, qs, (g, w)) for w, (src, dst) in enumerate(((wq, gq), (wk, gk), (wv, gv)))]
        for g in range(GROUPS)
    ]

    def each(g, step):
        for part in groups[g]:
            getattr(part, step)()

    mine, sent = pl.ds(pages * x, pages), pl.ds(pages * (1 - x), pages)

    def band(b):
        return xall.at[:, pl.ds(blk * b, blk), :]

    to_b = remote(x_in.at[sent], band(1), asend.at[0], arecv.at[0], x_peer)
    to_c = remote(x_in.at[mine], band(2), asend.at[1], arecv.at[1], c_peer)
    to_d = remote(band(1), band(3), asend.at[2], arecv.at[2], c_peer)
    cot_b = remote(cot.at[sent], cown.at[:, pl.ds(blk, blk), :], asend.at[3], arecv.at[3], x_peer)
    keep_x = pltpu.make_async_copy(x_in.at[mine], band(0), aloc.at[0])
    keep_c = pltpu.make_async_copy(cot.at[mine], cown.at[:, pl.ds(0, blk), :], aloc.at[1])
    vecs = [
        remote(vpk, gvec.at[f], vs.at[k], vr.at[k], {"fsdp": lax.rem(f + k + 1, 8)}) for k in range(7)
    ]
    def rest(p, step):
        def run(src, dst, row0, col0, from0=None):
            getattr(Spread(where, src, dst, row0, col0, 384, rs, (p,), from0), step)()

        @pl.when(p == 0)
        def _():
            run(wo, go, 0, 0)

        @pl.when(jnp.logical_and(p >= 1, p < 5))
        def _():
            run(wi, gi.at[p - 1], 0, 0, 768 * (p - 1))

        @pl.when(jnp.logical_and(p >= 5, p < REST))
        def _():
            run(w2, g2, ROW * (p - 5), 0)

    to_b.start()
    each(0, "along_z")
    keep_x.start()
    to_c.start()
    for copy in vecs:
        copy.start()
    place_row = lax.broadcasted_iota(jnp.int32, (blk, own), 0)
    for page in range(pages):
        for b in range(4):
            side = x if b % 2 == 0 else 1 - x
            core = c if b < 2 else 1 - c
            limit = lens[pages * x + page] - (2 * side + core) * blk
            bias[page, b * blk : (b + 1) * blk, :] = jnp.where(place_row < limit, 0.0, NEG)
    each(0, "forward")
    each(1, "along_z")
    each(0, "along_y")
    each(1, "forward")
    each(2, "along_z")
    each(1, "along_y")
    each(0, "along_x")
    each(2, "forward")
    for p in range(EARLY):
        rest(p, "along_z")
    each(2, "along_y")
    to_b.wait_recv()
    to_d.start()
    each(0, "to_core")
    each(1, "along_x")
    for copy in vecs:
        copy.wait_recv()
    for i in range(8):
        vec[i : i + 1, :] = jnp.concatenate([gvec[j, i : i + 1, :width] for j in range(8)], axis=1)
    for j in range(8):
        for i in range(3):
            b_in[:, (3 * j + i) * 128 : (3 * j + i + 1) * 128] = gvec[j, 8 + i : 9 + i, :]
    keep_c.start()
    keep_x.wait()
    to_c.wait_recv()
    to_d.wait_recv()
    each(0, "arrive")

    low_lane = lax.broadcasted_iota(jnp.int32, (own, PAIR), 1) < HEAD_DIM
    stages = (("along_z", 1 - 8 * EARLY // 3), ("forward", 0), ("along_y", 3), ("along_x", 8), ("to_core", 13))

    def tick(t):
        for step, late in stages:
            n = t - late
            p = lax.div(3 * n + 7, 8)

            @pl.when(jnp.logical_and(n >= 0, lax.div(8 * p, 3) == n))
            def _():
                if step == "along_z":
                    pl.when(p >= EARLY)(lambda: rest(p, step))
                else:
                    rest(p, step)

    def p_copy(page, pair, slot):
        return pltpu.make_async_copy(pbuf.at[slot], p_o.at[page, pl.ds(2 * pair, 2)], ps.at[slot])

    def unit(it, carry):
        g, page = lax.div(it, pages), lax.rem(it, pages)

        @pl.when(it == 0)
        def _():
            each(2, "along_x")
            each(1, "to_core")

        @pl.when(it == 1)
        def _():
            each(2, "to_core")
            cot_b.start()

        @pl.when(it == pages)
        def _():
            each(1, "arrive")

        @pl.when(it == 2 * pages)
        def _():
            each(2, "arrive")

        gcols = pl.ds(pl.multiple_of(g * GCOLS, GCOLS), GCOLS)
        x_all = xall[page]
        d = x_all.shape[1]
        query = (dot(x_all[:own], gq[:, :, :, gcols].reshape(d, GCOLS)) + vec[0:1, gcols]).astype(BF)
        keys = dot(x_all, gk[:, :, :, gcols].reshape(d, GCOLS)).astype(BF)
        vals = (dot(x_all, gv[:, :, :, gcols].reshape(d, GCOLS)) + vec[1:2, gcols]).astype(BF)
        q_o[page, :, gcols] = query
        k_o[page, :, gcols] = keys
        v_o[page, :, gcols] = vals
        for half in range(2):
            lanes = slice(half * PAIR, (half + 1) * PAIR)
            pair = 2 * g + half

            @pl.when(it > 0)
            def _():
                p_copy(page, pair, half).wait()

            qp = query[:, lanes] * jnp.array(1.0 / math.sqrt(HEAD_DIM), BF)
            kp = keys[:, lanes]
            vt = vals[:, lanes].T
            outs = []
            for h in range(2):
                keep = low_lane if h == 0 else jnp.logical_not(low_lane)
                qh = jnp.where(keep, qp, jnp.zeros_like(qp))
                st = dot(kp, qh, NT) + bias[page]
                top = jnp.max(st, axis=0, keepdims=True)
                ex = jnp.exp(st - top)
                tot = jnp.sum(ex, axis=0, keepdims=True)
                pt = (ex * (1.0 / tot)).astype(BF)
                pbuf[half, h] = pt
                outs.append(dot(vt[h * HEAD_DIM : (h + 1) * HEAD_DIM], pt))
            p_copy(page, pair, half).start()
            cols = pl.ds(pl.multiple_of(pair * PAIR, PAIR), PAIR)
            c_o[page, :, cols] = jnp.concatenate(outs, axis=0).T.astype(BF)
            tick(2 * it + half)
        return carry

    lax.fori_loop(0, GROUPS * pages, unit, 0)
    n_ticks = 2 * GROUPS * pages
    stores = [
        pltpu.make_async_copy(src, dst, outs_sem.at[i])
        for i, (src, dst) in enumerate(
            ((q_o, q_h), (k_o, k_h), (v_o, v_h), (c_o, c_h), (xall, xall_h), (gq, gq_h), (gk, gk_h), (gv, gv_h))
        )
    ]
    for copy in stores:
        copy.start()
    for half in range(2):
        p_copy(0, 0, half).wait()

    d = xall.shape[2]
    n_chunks = gi.shape[0]
    last = 8 * (REST - 1) // 3 + stages[-1][1] + 1
    gvs[...] = jnp.zeros_like(gvs)

    def add(row, value):
        gvs[row : row + 1, :] += jnp.sum(value, 0, keepdims=True)

    def square(ref):
        return ref[...].reshape(d, d)

    rest(0, "arrive")
    later = [pltpu.make_async_copy(go, go_h, outs_sem.at[8])]
    later[0].start()
    for page in range(pages):
        r = slice(page * own, (page + 1) * own)
        mid = xall[page, :own].astype(F32) + (dot(c_o[page], square(go)) + vec[2:3, :])
        n1, r1 = row_norm(mid)
        n1s[r, :] = n1
        n1b[r, :] = n1.astype(BF)
        r1s[r, :] = jnp.broadcast_to(r1, (own, 128))
        hid[r, :] = (n1 * vec[3:4, :] + vec[4:5, :]).astype(BF)

    def ticks(lo, hi):
        lax.fori_loop(lo, hi, lambda t, carry: (tick(t), carry)[1], 0)

    def chunk_stores(j):
        cols = pl.ds(pl.multiple_of(j * d, d), d)
        return [
            pltpu.make_async_copy(src, dst.at[j], chunk_sem.at[i, j])
            for i, (src, dst) in enumerate(((gi.at[j], gi_h), (act.at[:, cols], act_h), (dd.at[:, cols], dd_h)))
        ]

    def up(j, carry):
        ticks(n_ticks + 3 * j, jnp.minimum(n_ticks + 3 * j + 3, last))
        rest(j + 1, "arrive")
        cols = pl.ds(pl.multiple_of(j * d, d), d)
        pre = dot(hid[...], gi[j].reshape(d, d)) + b_in[:, cols]
        big, bell = normal_parts(pre)
        act[:, cols] = (pre * big).astype(BF)
        dd[:, cols] = (big + pre * bell).astype(BF)
        for copy in chunk_stores(j):
            copy.start()
        return carry

    lax.fori_loop(0, n_chunks, up, 0)
    ticks(n_ticks + 3 * n_chunks, last)
    for p in range(5, REST):
        rest(p, "arrive")
    keep_c.wait()
    cot_b.wait_recv()
    stores[0].wait()
    later.append(pltpu.make_async_copy(g2, g2_h, outs_sem.at[9]))
    later[1].start()

    def w2_rows(j):
        return g2[j].reshape(d, d)

    accs[...] = jnp.zeros_like(accs)

    def outer(j, carry):
        cols = pl.ds(pl.multiple_of(j * d, d), d)
        accs[...] += dot(act[:, cols], w2_rows(j))
        return carry

    lax.fori_loop(0, n_chunks, outer, 0)
    for page in range(pages):
        r = slice(page * own, (page + 1) * own)
        h1 = n1s[r, :] * vec[3:4, :] + vec[4:5, :]
        mid = h1 + (accs[r, :] + vec[5:6, :])
        n2, r2 = row_norm(mid)
        q_o[page] = (n2 * vec[6:7, :] + vec[7:8, :]).astype(BF)
        ct = cown[page].astype(F32)
        gm2 = norm_back(ct * vec[6:7, :], n2, r2)
        gob = gm2.astype(BF)
        gout[r, :] = gob
        accs[r, :] = gm2
        add(5, gob.astype(F32))
        add(6, ct * n2)
        add(7, ct)
    for i, (src, dst) in enumerate(((accs, gm2_h), (gout, gout_h), (hid, hid_h), (n1b, n1_h), (r1s, r1_h), (q_o, out_h))):
        later.append(pltpu.make_async_copy(src, dst, outs_sem.at[10 + i]))
        later[-1].start()

    def finish(p, carry):
        rest(p, "drain")
        return carry

    lax.fori_loop(0, REST, finish, 0)
    for g in range(GROUPS):
        each(g, "drain")
    for copy in vecs + [to_b, to_c, to_d, cot_b]:
        copy.wait_send()
    for j in range(n_chunks):
        later += chunk_stores(j)
    for copy in stores[1:] + later:
        copy.wait()


def fwd(lens, x_in, cot, ws, smalls):
    pages_all, blk, d = x_in.shape
    pages, own, rows = pages_all // 2, 2 * blk, 4 * blk
    n = pages * own
    dma = pltpu.SemaphoreType.DMA
    sds = jax.ShapeDtypeStruct
    vm = pltpu.VMEM
    ff = ws[4].shape[1]
    quarter = (4, 2, ROW, d)
    res = call(
        fwd_body,
        (n * d * (12 * ff + 12 * d), sum(16 * w.size for w in ws), pages * HEADS * own * rows),
        in_specs=[pl.BlockSpec(memory_space=pltpu.SMEM)] + [ANY] * 5 + [VM] * 12,
        out_specs=[ANY] * 20 + [VM, VM],
        out_shape=[sds(quarter, BF)] * 3
        + [
            sds((pages, rows, d), BF),
            sds((pages, own, d), BF), sds((pages, rows, d), BF), sds((pages, rows, d), BF), sds((pages, own, d), BF),
            sds((pages, HEADS, rows, own), BF),
            sds(quarter, BF), sds((ff // d,) + quarter, BF), sds((4, 2, ff // 8, d), BF),
            sds((ff // d, n, d), BF), sds((ff // d, n, d), BF), sds((n, d), BF), sds((n, d), BF), sds((n, d), BF),
            sds((n, d), F32), sds((n, 128), F32), sds((pages, own, d), BF),
            sds((8, d), F32), sds((8, d), F32),
        ],
        scratch_shapes=[
            vm(quarter, BF), vm(quarter, BF), vm(quarter, BF), vm(quarter, BF),
            vm((ff // d,) + quarter, BF), vm((4, 2, ff // 8, d), BF),
            vm((pages, rows, d), BF), vm((pages, own, d), BF), vm((pages, rows, d), BF), vm((pages, rows, d), BF),
            vm((pages, own, d), BF), vm((pages, own, d), BF), vm((pages, rows, own), F32), vm((2, 2, rows, own), BF),
            vm((16, 128), F32), vm((8, 16, 128), F32), vm((1, ff), F32),
            vm((n, ff), BF), vm((n, ff), BF), vm((n, d), BF), vm((n, d), BF), vm((n, d), BF),
            vm((n, d), F32), vm((n, d), F32), vm((n, 128), F32),
        ]
        + spread_sems(GROUPS, 3)
        + spread_sems(REST)
        + [dma((5,)), dma((5,)), dma((3,)), dma((7,)), dma((7,)), dma((2,)), dma((16,)), dma((3, ff // d))],
        params=dict(collective_id=0, has_side_effects=True, vmem_limit_bytes=64 << 20),
        name="gather_forward",
    )(lens, x_in, cot, *ws, *smalls)
    return res


class Fold:
    def __init__(self, where, acc, bufs, sems, key, keep):
        self.z, self.y, self.x, self.c = where
        self.acc, self.key = acc, key
        give = ROW - keep
        self.split = give > 0
        self.rc, self.rx, self.ry, self.rz, self.fin, self.rf = [b.at[key] for b in bufs]
        self.cs, self.cr, self.xs, self.xr, self.ys, self.yr, self.zs, self.zr, self.fs, self.fr, self.es, self.er = sems
        z = self.z
        self.near, self.far, self.across = z + 1 - 2 * lax.rem(z, 2), lax.rem(z + 2, 4), 3 - z
        self.inner = jnp.logical_or(z == 1, z == 2)
        self.outer = jnp.logical_not(self.inner)
        self.keep = pl.ds(pl.multiple_of(give * self.x, 16), keep)
        self.give = pl.ds(pl.multiple_of(keep * (1 - self.x), 16), give)
        self.gain = pl.ds(pl.multiple_of(keep * self.x, 16), give)

    def part(self, *sel):
        return self.acc(sel)

    def xcopy(self):
        return remote(
            self.part(ALL, 1 - self.y, self.give), self.rx, self.xs.at[self.key], self.xr.at[self.key],
            at(self.z, self.y, 1 - self.x, self.c),
        )

    def ycopy(self):
        return remote(
            self.part(ALL, 1 - self.y, self.keep), self.ry, self.ys.at[self.key], self.yr.at[self.key],
            at(self.z, 1 - self.y, self.x, self.c),
        )

    def zcopy(self, block, target, slot):
        return remote(
            self.part(block, self.y, ALL), self.rz.at[slot], self.zs.at[self.key + (slot,)],
            self.zr.at[self.key + (slot,)], at(target, self.y, self.x, self.c),
        )

    def a(self):
        return self.zcopy(self.near, self.near, 0)

    def b(self):
        return self.zcopy(self.far, self.far, 1)

    def d(self):
        return self.zcopy(self.across, self.across, 2)

    def f(self):
        return self.zcopy(self.across, self.near, 3)

    def fcopy(self):
        return remote(
            self.fin, self.rf, self.fs.at[self.key], self.fr.at[self.key],
            at(self.z, self.y, 1 - self.x, self.c),
        )

    def over_x(self, first):
        first.wait_recv()
        whole = self.part(ALL, ALL, ALL)
        whole[...] = whole[...] + self.rc[...]
        if self.split:
            self.xcopy().start()
        else:
            self.ycopy().start()

    def over_y(self):
        if not self.split:
            return
        self.xcopy().wait_recv()
        rows = self.part(ALL, 1 - self.y, self.gain)
        rows[...] = rows[...] + self.rx[...]
        self.ycopy().start()

    def over_z(self):
        self.ycopy().wait_recv()
        rows = self.part(ALL, self.y, self.keep)
        rows[...] = rows[...] + self.ry[...]
        self.a().start()

        @pl.when(self.outer)
        def _():
            self.f().start()
            self.b().start()

        @pl.when(self.inner)
        def _():
            self.d().start()

    def inside(self):
        @pl.when(self.inner)
        def _():
            self.f().wait_recv()
            rows = self.part(self.far, self.y, ALL)
            rows[...] = rows[...] + self.rz[3]
            self.b().start()

    def total(self):
        self.a().wait_recv()
        self.b().wait_recv()
        own = self.part(self.z, self.y, ALL)

        @pl.when(self.outer)
        def _():
            self.fin[...] = (own[...].astype(F32) + self.rz[0].astype(F32) + self.rz[1].astype(F32)).astype(BF)

        @pl.when(self.inner)
        def _():
            self.d().wait_recv()
            self.fin[...] = (
                own[...].astype(F32) + self.rz[0].astype(F32) + self.rz[1].astype(F32) + self.rz[2].astype(F32)
            ).astype(BF)

        self.fcopy().start()

    def ecopy(self, view):
        return remote(view, view, self.es.at[self.key], self.er.at[self.key], at(self.z, self.y, self.x, 1 - self.c))

    def write(self, view):
        self.fcopy().wait_recv()
        view[...] = self.fin[...].astype(F32) + self.rf[...].astype(F32)
        self.ecopy(view).start()

    def drain(self, view):
        self.ecopy(view).wait_recv()
        if self.split:
            self.xcopy().wait_send()
        self.ycopy().wait_send()
        self.a().wait_send()
        self.b().wait_send()

        @pl.when(self.outer)
        def _():
            self.f().wait_send()

        @pl.when(self.inner)
        def _():
            self.d().wait_send()

        self.fcopy().wait_send()
        self.ecopy(view).wait_send()


ALL = slice(None)
KEEP_REST = 64
KEEP_GROUP = 96


def fold_sems(*lead):
    dma = pltpu.SemaphoreType.DMA
    return [dma(lead)] * 6 + [dma(lead + (4,))] * 2 + [dma(lead)] * 4


def fold_bufs(width, keep, *lead):
    return [
        pltpu.VMEM(lead + shape, BF)
        for shape in (
            (4, 2, ROW, width), (4, max(ROW - keep, 16), width), (4, keep, width), (4, ROW, width), (ROW, width), (ROW, width),
        )
    ]


def bwd_body(
    gq_h, gk_h, gv_h, x_h, q_h, k_h, v_h, c_h, p_h, go_h, gi_h, g2_h, act_h, dd_h, hid_h, gout_h, n1_h, gm2_h, r1_h, out_h,
    gvf, vec,
    oq, ok, ov, oo, oi, o2, gx, fin_out, ovec,
    *refs,
):
    (
        pool, hid, gout, go, n1b, accs, r1s, c_v, dc_v, acc, dwg, st, dq_all, dk_all, dv_all, rk, rv, sk, sv, pbuf,
        rgx, pack, vecin, vtot, vx, brow, gvs, gbin, stay,
    ) = refs[:29]
    fb, gb = refs[29:35], refs[35:41]
    fsem, gsem = refs[41:53], refs[53:65]
    lsem, msem, ssem, ps, ks, kr, gs, gr, os, vs, vr, us, ur, bs, br, bl = refs[65:]
    z, y, x, c = where = place()
    f = 2 * z + y
    pages, own, d = c_h.shape
    n = pages * own
    blk = own // 2
    rows = 2 * own
    at_k, at_v, at_q, at_gq, at_gk, at_gv = 0, 2 * n, 4 * n, 5 * n, 6 * n, 7 * n
    x_peer, c_peer = at(z, y, 1 - x, c), at(z, y, x, 1 - c)
    meet([{"fsdp": lax.rem(f + k + 1, 8)} for k in range(7)] + [x_peer, c_peer])

    def other_half(p, run):
        @pl.when(p < 6)
        def _():
            run(dwg.at[lax.div(p, 2), :, :, :, pl.ds(pl.multiple_of(384 * lax.rem(p, 2), 128), 384)])

        @pl.when(p >= 6)
        def _():
            run(st.at[p - 6])

    def launch(p):
        other_half(p, lambda ref: remote(ref, fb[0].at[p], fsem[0].at[p], fsem[1].at[p], c_peer).start())

    def rest_out(p, run):
        @pl.when(p < 4)
        def _():
            run(oi.at[:, pl.ds(pl.multiple_of(768 * p + 384 * c, 128), 384)])

        @pl.when(jnp.logical_and(p >= 4, p < 8))
        def _():
            run(o2.at[pl.ds(pl.multiple_of(ROW * (p - 4), 32), ROW), pl.ds(pl.multiple_of(384 * c, 128), 384)])

        @pl.when(p == 8)
        def _():
            run(oo.at[:, pl.ds(pl.multiple_of(384 * c, 128), 384)])

    def fold(p):
        return Fold(where, lambda sel: acc.at[(p,) + sel], fb, fsem, (p,), KEEP_REST)

    def any_first(p):
        return remote(fb[0].at[p], fb[0].at[p], fsem[0].at[p], fsem[1].at[p], c_peer)

    def step(p, name):
        ok_p = jnp.logical_and(p >= 0, p < REST)

        @pl.when(ok_p)
        def _():
            if name == "over_x":
                fold(p).over_x(any_first(p))
            elif name == "write":
                rest_out(p, lambda view: fold(p).write(view))
            elif name == "drain":
                rest_out(p, lambda view: fold(p).drain(view))
            else:
                getattr(fold(p), name)()

    def gfold(g, w):
        cols = pl.ds(pl.multiple_of(GCOLS * w + 128 * c, 128), 128)
        return Fold(where, lambda sel: dwg.at[(g,) + sel + (cols,)], gb, gsem, (g, w), KEEP_GROUP)

    def gfirst(g, w):
        cols = pl.ds(pl.multiple_of(GCOLS * w + 128 * (1 - c), 128), 128)
        return remote(dwg.at[g, :, :, :, cols], gb[0].at[g, w], gsem[0].at[g, w], gsem[1].at[g, w], c_peer)

    def gstep(g, name):
        for w, o in enumerate((oq, ok, ov)):
            view = o.at[:, pl.ds(pl.multiple_of(GCOLS * g + 128 * c, 128), 128)]
            if name == "start":
                gfirst(g, w).start()
            elif name == "over_x":
                gfold(g, w).over_x(gfirst(g, w))
            elif name == "write":
                gfold(g, w).write(view)
            elif name == "drain":
                gfold(g, w).drain(view)
                gfirst(g, w).wait_send()
            else:
                getattr(gfold(g, w), name)()

    stages = (("over_x", 0), ("over_y", 4), ("over_z", 9), ("inside", 14), ("total", 18), ("write", 22))
    pace = 3
    last = pace * (REST + GROUPS - 1) + stages[-1][1] + 1

    def tick(t):
        for name, late in stages:
            n = t - late
            p = lax.div(n, pace)

            @pl.when(jnp.logical_and(n >= 0, jnp.logical_and(lax.rem(n, pace) == 0, p < REST + GROUPS)))
            def _():
                step(p, name)

                @pl.when(p >= REST)
                def _():
                    gstep(p - REST, name)

    firsts = [
        pltpu.make_async_copy(src, dst, lsem.at[i])
        for i, (src, dst) in enumerate(
            ((gout_h, gout), (hid_h, hid), (gm2_h, accs), (n1_h, n1b), (r1_h, r1s), (go_h, go), (c_h, c_v))
        )
    ]

    def row_block(start, size):
        return pl.ds(pl.multiple_of(start, 256), size)

    def slot(kind, j):
        return pool.at[row_block((2 * kind + lax.rem(j, 2)) * n, n), :]

    def chunk_loads(j):
        return [
            pltpu.make_async_copy(src.at[j], slot(kind, j), msem.at[kind, lax.rem(j, 2)])
            for kind, src in enumerate((gi_h, g2_h, act_h, dd_h))
        ]

    seconds = [
        pltpu.make_async_copy(src, pool.at[pl.ds(start, src.shape[0]), :], ssem.at[i])
        for i, (src, start) in enumerate(
            ((q_h, at_q), (k_h, at_k), (v_h, at_v), (gq_h, at_gq), (gk_h, at_gk), (gv_h, at_gv))
        )
    ] + [
        pltpu.make_async_copy(x_h.at[page, pl.ds(0, own), :], hid.at[pl.ds(page * own, own), :], ssem.at[6 + page])
        for page in range(pages)
    ]

    def p_copy(it, half):
        g, page = lax.div(it, pages), lax.rem(it, pages)
        return pltpu.make_async_copy(p_h.at[page, pl.ds(4 * g + 2 * half, 2)], pbuf.at[half], ps.at[half])

    pages_mine = pl.ds(pages * x, pages)
    back_out = remote(out_h.at[:, pl.ds(blk, blk), :], fin_out.at[pages_mine], bs.at[0], br.at[0], x_peer)
    stay_in = pltpu.make_async_copy(out_h.at[:, pl.ds(0, blk), :], stay, bl.at[0])
    stay_out = pltpu.make_async_copy(stay, fin_out.at[pages_mine], bl.at[1])
    back_out.start()
    begin_with = chunk_loads(0)
    for copy in firsts[:1] + [begin_with[1], begin_with[3]] + firsts[1:2] + [begin_with[0]] + firsts[2:3] + [begin_with[2]]:
        copy.start()
    for copy in firsts[3:]:
        copy.start()
    for copy in chunk_loads(1):
        copy.start()
    for half in range(2):
        p_copy(0, half).start()
    stay_in.start()
    gvs[...] = gvf[...]

    def halves(value):
        low, high = value[..., :384], value[..., 384:]
        return jnp.where(c == 0, low, high), jnp.where(c == 0, high, low)

    n_chunks = gi_h.shape[0]
    firsts[0].wait()

    def down(j, carry):
        wi_in, w2_in, act_in, dd_in = chunk_loads(j)
        w2_in.wait()
        dd_in.wait()
        cols = pl.ds(pl.multiple_of(j * d, d), d)
        di = (dot(gout[...], slot(1, j)[...], NT) * slot(3, j)[...].astype(F32)).astype(BF)

        @pl.when(j == 0)
        def _():
            firsts[1].wait()

        keep, pass_on = halves(dot(hid[...], di, TN).astype(BF))
        acc[j] = keep.reshape(4, 2, ROW, 384)
        other_half(j, lambda ref: ref.__setitem__(Ellipsis, pass_on.reshape(4, 2, ROW, 384)))
        launch(j)

        @pl.when(j == 0)
        def _():
            firsts[2].wait()

        @pl.when(j > 0)
        def _():
            tick(pace * j - 2)
            tick(pace * j - 1)

        wi_in.wait()
        accs[...] += dot(di, slot(0, j)[...], NT)
        gbin[:, cols] = jnp.sum(di.astype(F32), 0, keepdims=True)
        act_in.wait()
        keep, pass_on = halves(dot(slot(2, j)[...], gout[...], TN).astype(BF))
        keep, pass_on = keep.reshape(2, 4, ROW, 384), pass_on.reshape(2, 4, ROW, 384)
        for p in range(4):
            acc[4 + p, j] = keep[:, p]
            if p < 2:
                dwg[2, j, :, :, 384 * p : 384 * p + 384] = pass_on[:, p]
            else:
                st[p - 2, j] = pass_on[:, p]

        @pl.when(j + 2 < n_chunks)
        def _():
            for copy in chunk_loads(j + 2):
                copy.start()

        tick(pace * j)
        return carry

    lax.fori_loop(0, n_chunks, down, 0)
    for p in range(4):
        launch(4 + p)
    stay_in.wait()
    stay_out.start()
    for copy in seconds:
        copy.start()
    for copy in firsts[3:]:
        copy.wait()

    def add(row, value):
        gvs[row : row + 1, :] += jnp.sum(value, 0, keepdims=True)

    before = pace * (n_chunks - 1) + 1
    for page in range(pages):
        r = slice(page * own, (page + 1) * own)
        gh = accs[r, :]
        n1 = n1b[r, :].astype(F32)
        gm1 = norm_back(gh * vec[3:4, :], n1, r1s[r, 0:1])
        accs[r, :] = gm1
        ga = gm1.astype(BF)
        gout[r, :] = ga
        dc_v[page] = dot(ga, go[...], NT).astype(BF)
        add(2, ga.astype(F32))
        add(3, gh * n1)
        add(4, gh)
        tick(before + page)
    before += pages
    keep, pass_on = halves(dot(c_v[...].reshape(n, d), gout[...], TN).astype(BF))
    acc[8] = keep.reshape(4, 2, ROW, 384)
    st[2] = pass_on.reshape(4, 2, ROW, 384)
    launch(8)
    for copy in seconds:
        copy.wait()

    low_lane = lax.broadcasted_iota(jnp.int32, (own, PAIR), 1) < HEAD_DIM
    scale = 1.0 / math.sqrt(HEAD_DIM)

    def kv_send(it):
        g, page = lax.div(it, pages), lax.rem(it, pages)
        gcols = pl.ds(pl.multiple_of(g * GCOLS, GCOLS), GCOLS)
        return [
            remote(s_ref.at[page], r_ref.at[page, :, gcols], ks.at[g, page, i], kr.at[g, page, i], c_peer)
            for i, (s_ref, r_ref) in enumerate(((sk, rk), (sv, rv)))
        ]

    def attend(it, half):
        g, page = lax.div(it, pages), lax.rem(it, pages)
        here = pl.ds(pl.multiple_of(page * own, own), own)
        p_copy(it, half).wait()
        local = slice(half * PAIR, (half + 1) * PAIR)
        cols = pl.ds(pl.multiple_of(g * GCOLS + half * PAIR, PAIR), PAIR)
        qp = pool[row_block(at_q + page * own, own), cols] * jnp.array(scale, BF)
        kp = pool[row_block(at_k + page * rows, rows), cols]
        kt = kp.T
        vp = pool[row_block(at_v + page * rows, rows), cols]
        dc = dc_v[page, :, cols]
        prod = (dc.astype(F32) * c_v[page, :, cols].astype(F32)).T
        dk = None
        dv = None
        dqs = []
        for h in range(2):
            keep = low_lane if h == 0 else jnp.logical_not(low_lane)
            feats = slice(h * HEAD_DIM, (h + 1) * HEAD_DIM)
            dch = jnp.where(keep, dc, jnp.zeros_like(dc))
            qh = jnp.where(keep, qp, jnp.zeros_like(qp))
            pt = pbuf[half, h]
            delta = jnp.sum(prod[feats], axis=0, keepdims=True)
            dpt = dot(vp, dch, NT)
            dst = (pt.astype(F32) * (dpt - delta)).astype(BF)
            dvh = dot(pt, dch)
            dkh = dot(dst, qh)
            dk = dkh if dk is None else dk + dkh
            dv = dvh if dv is None else dv + dvh
            dqs.append(dot(kt[feats], dst))
        dq_all[here, cols] = (jnp.concatenate(dqs, axis=0) * scale).T.astype(BF)
        dk_all[here, cols] = dk[:own].astype(BF)
        sk[page, :, local] = dk[own:].astype(BF)
        dv_all[here, cols] = dv[:own].astype(BF)
        sv[page, :, local] = dv[own:].astype(BF)

        @pl.when(it + 1 < GROUPS * pages)
        def _():
            p_copy(it + 1, half).start()

    def group_grads(g):
        for i in range(2):
            any_first(2 * g + i).wait_send()
        gcols = pl.ds(pl.multiple_of(g * GCOLS, GCOLS), GCOLS)
        for page in range(pages):
            here = pl.ds(page * own, own)
            for copy in kv_send(g * pages + page):
                copy.wait_recv()
            dk_all[here, gcols] = dk_all[here, gcols] + rk[page, :, gcols]
            dv_all[here, gcols] = dv_all[here, gcols] + rv[page, :, gcols]
        for w, grad in enumerate((dq_all, dk_all, dv_all)):
            value = grad[:, gcols]
            dwg[g, :, :, :, w * GCOLS : (w + 1) * GCOLS] = (
                dot(hid[...], value, TN).astype(BF).reshape(4, 2, ROW, GCOLS)
            )
            if w != 1:
                brow[w : w + 1, gcols] = jnp.sum(value.astype(F32), 0, keepdims=True)
        gstep(g, "start")

    def gx_send(page):
        return remote(go.at[pl.ds(pl.multiple_of(page * blk, 128), blk), :], rgx.at[page], gs.at[page], gr.at[page], x_peer)

    def input_grads(page):
        here = pl.ds(pl.multiple_of(page * own, own), own)
        total = accs[here, :]
        for grad, start in ((dq_all, at_gq), (dk_all, at_gk), (dv_all, at_gv)):
            total = total + dot(grad[here, :], pool[pl.ds(start, d), :], NT)
        accs[here, :] = total
        go[pl.ds(pl.multiple_of(page * blk, 128), blk), :] = total[blk:].astype(BF)
        gx_send(page).start()
        gx_store(page, 0).start()

    def gx_store(page, side):
        src = accs.at[pl.ds(pl.multiple_of(page * own + side * blk, 128), blk), :]
        return pltpu.make_async_copy(src, gx.at[pages * (x if side == 0 else 1 - x) + page], os.at[page, side])

    n_it = GROUPS * pages

    def unit(it, carry):
        @pl.when(it == n_it)
        def _():
            group_grads(GROUPS - 1)

        for half in range(2):

            if half == 0:

                @pl.when(jnp.logical_and(it >= pages, it < n_it))
                def _():
                    for copy in kv_send(it - pages):
                        copy.wait_send()

            @pl.when(it < n_it)
            def _():
                attend(it, half)

            if half == 1:

                @pl.when(it < n_it)
                def _():
                    for copy in kv_send(it):
                        copy.start()

            tick(before + 2 * it + half)

        @pl.when(jnp.logical_and(it > 0, jnp.logical_and(lax.rem(it, pages) == 0, it < n_it)))
        def _():
            group_grads(lax.div(it, pages) - 1)

        page = it - n_it

        @pl.when(jnp.logical_and(page >= 0, page < pages))
        def _():
            input_grads(page)

        return carry

    def vec_send(k):
        to = lax.rem(f + k + 1, 8)
        return remote(pack.at[to], vecin.at[k], vs.at[k], vr.at[k], {"fsdp": to})

    vec_x = lambda: remote(vtot, vx.at[0], us.at[0], ur.at[0], x_peer)
    vec_c = lambda: remote(vx.at[1], vx.at[2], us.at[1], ur.at[1], c_peer)

    def small_pack():
        for i in range(8):
            row = brow[0:1, :] if i == 0 else brow[2:3, :] if i == 1 else gvs[i : i + 1, :]
            for j in range(8):
                pack[j, i : i + 1, :ROW] = row[:, ROW * j : ROW * (j + 1)]
        for j in range(8):
            for i in range(3):
                pack[j, 8 + i : 9 + i, :] = gbin[:, (3 * j + i) * 128 : (3 * j + i + 1) * 128]
        for k in range(7):
            vec_send(k).start()

    def small_sum():
        total = pack[f]
        for k in range(7):
            vec_send(k).wait_recv()
            total = total + vecin[k]
        vtot[...] = total
        vec_x().start()

    def small_pair():
        vec_x().wait_recv()
        vx[1] = vtot[...] + vx[0]
        vec_c().start()

    def all_steps(it, carry):
        unit(it, carry)
        for when, run in ((n_it, small_pack), (n_it + 3, small_sum), (n_it + 6, small_pair)):
            pl.when(it == when)(run)
        return carry

    lax.fori_loop(0, (last - before + 2) // 2, all_steps, 0)
    for page in range(pages):
        gx_send(page).wait_recv()
        accs[page * own + blk : (page + 1) * own, :] = rgx[page].astype(F32)
        gx_store(page, 1).start()
    vec_c().wait_recv()
    ovec[...] = vx[1] + vx[2]

    def finish(p, carry):
        step(p, "drain")
        return carry

    lax.fori_loop(0, REST, finish, 0)
    for g in range(GROUPS):
        gstep(g, "drain")
    for p in range(6, REST):
        any_first(p).wait_send()
    for it in range(n_it - pages, n_it):
        for copy in kv_send(it):
            copy.wait_send()
    for page in range(pages):
        gx_send(page).wait_send()
        gx_store(page, 0).wait()
        gx_store(page, 1).wait()
    for k in range(7):
        vec_send(k).wait_send()
    back_out.wait()
    stay_out.wait()
    vec_x().wait_send()
    vec_c().wait_send()


def bwd(kept, shards):
    (gq, gk, gv, xall, q, k, v, ctx, p, go, gi, g2, act, dd, hid, gout, n1, gm2, r1, out, gvs, vec) = kept
    pages, own, d = ctx.shape
    rows, blk = 2 * own, own // 2
    n = pages * own
    dma = pltpu.SemaphoreType.DMA
    vm = pltpu.VMEM
    sds = jax.ShapeDtypeStruct
    n_chunks = act.shape[0]
    flat = lambda a: a.reshape(-1, d)
    args = (
        flat(gq), flat(gk), flat(gv), xall, flat(q), flat(k), flat(v), ctx, p, flat(go),
        gi.reshape(n_chunks, d, d), g2.reshape(n_chunks, d, d), act, dd, hid, gout, n1, gm2, r1, out, gvs, vec,
    )
    res = call(
        bwd_body,
        (24 * n * d * d + pages * 10 * own * rows * d, 60 << 20, 0),
        in_specs=[ANY] * 20 + [VM, VM],
        out_specs=[VM] * 6 + [ANY, ANY, VM],
        out_shape=[sds(shape, F32) for shape in shards]
        + [sds((2 * pages, blk, d), F32), sds((2 * pages, blk, d), BF), sds((16, 128), F32)],
        scratch_shapes=[
            vm((8 * n, d), BF), vm((n, d), BF), vm((n, d), BF), vm((d, d), BF), vm((n, d), BF), vm((n, d), F32),
            vm((n, 128), F32), vm((pages, own, d), BF), vm((pages, own, d), BF),
            vm((REST, 4, 2, ROW, 384), BF), vm((GROUPS, 4, 2, ROW, 3 * GCOLS), BF), vm((3, 4, 2, ROW, 384), BF),
            vm((n, d), BF), vm((n, d), BF), vm((n, d), BF),
            vm((pages, own, d), BF), vm((pages, own, d), BF), vm((pages, own, GCOLS), BF), vm((pages, own, GCOLS), BF),
            vm((2, 2, rows, own), BF), vm((pages, blk, d), BF),
            vm((8, 16, 128), F32), vm((7, 16, 128), F32), vm((16, 128), F32), vm((3, 16, 128), F32), vm((8, d), F32),
            vm((8, d), F32), vm((1, n_chunks * d), F32), vm((pages, blk, d), BF),
        ]
        + fold_bufs(384, KEEP_REST, REST)
        + fold_bufs(128, KEEP_GROUP, GROUPS, 3)
        + fold_sems(REST)
        + fold_sems(GROUPS, 3)
        + [
            dma((7,)), dma((4, 2)), dma((6 + pages,)), dma((2,)), dma((GROUPS, pages, 2)), dma((GROUPS, pages, 2)),
            dma((pages,)), dma((pages,)), dma((pages, 2)), dma((7,)), dma((7,)), dma((2,)), dma((2,)),
            dma((1,)), dma((1,)), dma((2,)),
        ],
        params=dict(collective_id=1, has_side_effects=True, vmem_limit_bytes=64 << 20),
        name="backward_reduce",
    )(*args)
    return res[:6], res[6], res[7], res[8]


def finish_body(*refs):
    n = 8
    src, small, dst, lows = refs[:n], refs[n], refs[n + 1 : 2 * n + 1], refs[2 * n + 1 : 2 * n + 10]
    held, sem_in, sem_out = refs[2 * n + 10 : 3 * n + 10], refs[-2], refs[-1]
    loads = [pltpu.make_async_copy(src[i], held[i], sem_in.at[i]) for i in range(n)]
    stores = [pltpu.make_async_copy(held[i], dst[i], sem_out.at[i]) for i in range(n)]
    for copy in loads:
        copy.start()
    width = lows[0].shape[0]
    for i in range(8):
        lows[i][...] = small[i, :width]
    for i in range(3):
        lows[8][128 * i : 128 * (i + 1)] = small[8 + i, :]
    for load, store in zip(loads, stores):
        load.wait()
        store.start()
    for copy in stores:
        copy.wait()


def finish(arrays, small, width, wide):
    sds = jax.ShapeDtypeStruct
    dma = pltpu.SemaphoreType.DMA
    n = len(arrays)
    return call(
        finish_body,
        (0, 2 * sum(a.size * a.dtype.itemsize for a in arrays), 0),
        in_specs=[ANY] * n + [VM],
        out_specs=[ANY] * n + [VM] * 9,
        out_shape=[sds(a.shape, a.dtype) for a in arrays] + [sds((width,), F32)] * 8 + [sds((wide,), F32)],
        scratch_shapes=[pltpu.VMEM(a.shape, a.dtype) for a in arrays] + [dma((n,)), dma((n,))],
        name="finish",
    )(*arrays, small)


SWAP_X = [(0, 2), (2, 0), (1, 3), (3, 1)]
SWAP_C = [(0, 1), (1, 0), (2, 3), (3, 2)]


def swap(value, pairs):
    return lax.ppermute(value, "seq", pairs)


def per_device(
    fsdp, inputs, lengths, w_query, b_query, w_key, w_value, b_value, w_out, b_out,
    gain_one, shift_one, w_inner, b_inner, w_outer, b_outer, gain_two, shift_two, cotangent,
):
    pages_all, blk, d = inputs.shape
    pages = pages_all // 2
    s = lax.axis_index("seq")
    x_at = lax.div(s, 2)
    direct = fsdp == 8
    ws = (w_query, w_key, w_value, w_out, w_inner, w_outer)
    shards = [w.shape for w in ws]
    width = b_query.shape[0]
    names = (b_query, b_value, b_out, gain_one, shift_one, b_outer, gain_two, shift_two)

    def pages_of(array, side):
        return lax.dynamic_slice_in_dim(array, side * pages, pages, 0)

    order = jnp.stack([s, s ^ 2, s ^ 1, s ^ 3]).astype(jnp.int32)
    thr = pages_of(lengths, x_at).astype(jnp.int32)[:, None] - order[None, :] * blk
    if direct:
        kept = fwd(lengths.astype(jnp.int32), inputs, cotangent, ws, names + (b_inner,))
    else:
        wq, wk, wv, wo, wi, w2 = [lax.all_gather(w, "fsdp", axis=0, tiled=True) for w in ws]
        vec = jnp.concatenate(names + (b_inner,)).reshape(12, width)
        gvec = lax.all_gather(vec, "fsdp", axis=0)
        vec_full = jnp.swapaxes(gvec[:, :8], 0, 1).reshape(8, d).astype(F32)
        bin_full = gvec[:, 8:].reshape(1, -1).astype(F32)

        def own_rows(array):
            other = swap(pages_of(array, 1 - x_at), SWAP_X)
            return jnp.concatenate([pages_of(array, x_at), other], axis=1)

        xown, cown = own_rows(inputs), own_rows(cotangent)
        xall = jnp.concatenate([xown, swap(xown, SWAP_C)], axis=1)
        q, k, v, p, ctx = attn_fwd(thr, xall, wq, wk, wv, vec_full)
    if direct:
        tot, grad_inputs, output, tvec = bwd(kept, shards)
        res = finish((output, grad_inputs) + tuple(tot), tvec, width, b_inner.shape[0])
        output, grad_inputs, tot, small, g_bi = res[0], res[1], res[2:8], res[8:16], res[16]
    else:
        out, gm1, dctx, dwo, dwi, dw2, gv_ffn, gbin = ffn(ctx, xall, cown, wo, wi, w2, vec_full, bin_full)
        dq, dk, dk_send, dv, dv_send = attn_bwd(q, k, v, p, ctx, dctx)
        dkr, dvr = swap(dk_send, SWAP_C), swap(dv_send, SWAP_C)
        gx_a, gx_b, dwq, dwk, dwv, gv_proj = proj(xall, dq, dk, dkr, dv, dvr, gm1, wq, wk, wv)
        gv = jnp.concatenate([gv_proj[:2], gv_ffn[2:]], axis=0)
        by_owner = jnp.concatenate(
            [jnp.swapaxes(gv.reshape(8, fsdp, width), 0, 1), gbin.reshape(fsdp, 4, width)], axis=1
        )
        tot = [
            lax.psum(lax.psum_scatter(g, "fsdp", scatter_dimension=0, tiled=True), "seq").astype(F32)
            for g in (dwq, dwk, dwv, dwo, dwi, dw2)
        ]
        tvec = lax.psum(lax.psum_scatter(by_owner, "fsdp", scatter_dimension=0, tiled=True)[0], "seq")

        def joined(mine, other):
            here = lax.dynamic_update_slice_in_dim(
                jnp.zeros((pages_all, blk, d), mine.dtype), mine, x_at * pages, 0
            )
            return lax.dynamic_update_slice_in_dim(here, other, (1 - x_at) * pages, 0)

        output = joined(out[:, :blk], swap(out[:, blk:], SWAP_X))
        grad_inputs = joined(gx_a, swap(gx_b, SWAP_X).astype(F32))
        small = [tvec[i] for i in range(8)]
        g_bi = tvec[8:].reshape(-1)
    g_bq, g_bv, g_bo, g_g1, g_s1, g_bo2, g_g2, g_s2 = small
    t_q, t_k, t_v, t_o, t_i, t_2 = tot
    return (
        output, grad_inputs, t_q, g_bq, t_k, t_v, g_bv, t_o, g_bo, g_g1, g_s1,
        t_i, g_bi, t_2, g_bo2, g_g2, g_s2,
    )


def solution(mesh):
    vec, mat, act = P("fsdp"), P("fsdp", None), P("fsdp", "seq", None)
    return jax.shard_map(
        functools.partial(per_device, mesh.shape["fsdp"]),
        mesh=mesh,
        in_specs=(act, vec, mat, vec, mat, mat, vec, mat, vec, vec, vec, mat, vec, mat, vec, vec, vec, act),
        out_specs=(act, act, mat, vec, mat, mat, vec, mat, vec, vec, vec, mat, vec, mat, vec, vec, vec),
        check_vma=False,
    )
```

```python
import functools
import math

import jax
import jax.numpy as jnp
from jax import lax
from jax.experimental import pallas as pl
from jax.experimental.pallas import tpu as pltpu
from jax.sharding import PartitionSpec as P

HEADS = 12
HEAD_DIM = 64
PAIR = 2 * HEAD_DIM
NEG = -1e30
EPS = 1e-12
BF = jnp.bfloat16
F32 = jnp.float32
MESH = pl.DeviceIdType.MESH
ANY = pl.BlockSpec(memory_space=pl.ANY)
VM = pl.BlockSpec(memory_space=pltpu.VMEM)
CHUNK = 1024
ROW = 96
VMEM_CAP = 60 << 20

NN = (((1,), (0,)), ((), ()))
NT = (((1,), (1,)), ((), ()))
TN = (((0,), (0,)), ((), ()))


def dot(a, b, dims=NN):
    return lax.dot_general(a, b, dims, preferred_element_type=F32)


def call(body, cost, **kw):
    flops, byts, trans = cost
    params = dict(vmem_limit_bytes=VMEM_CAP)
    params.update(kw.pop("params", {}))
    return pl.pallas_call(
        body,
        compiler_params=pltpu.CompilerParams(**params),
        cost_estimate=pl.CostEstimate(
            flops=int(flops), bytes_accessed=int(byts), transcendentals=int(trans)
        ),
        **kw,
    )


def attn_fwd_body(thr, xall, wq, wk, wv, vec, q_o, k_o, v_o, p_o, c_o, bias):
    page = pl.program_id(0)
    x_all = xall[0]
    own = x_all.shape[0] // 2
    query = (dot(x_all[:own], wq[...]) + vec[0:1, :]).astype(BF)
    q_o[0] = query
    k_o[0] = dot(x_all, wk[...]).astype(BF)
    v_o[0] = (dot(x_all, wv[...]) + vec[1:2, :]).astype(BF)
    blk = x_all.shape[0] // 4
    place = lax.broadcasted_iota(jnp.int32, (blk, own), 0)
    for b in range(4):
        bias[b * blk : (b + 1) * blk, :] = jnp.where(place < thr[page, b], 0.0, NEG)
    low_lane = lax.broadcasted_iota(jnp.int32, (own, PAIR), 1) < HEAD_DIM

    def pair(i, carry):
        cols = pl.ds(pl.multiple_of(i * PAIR, PAIR), PAIR)
        qp = q_o[0, :, cols] * jnp.array(1.0 / math.sqrt(HEAD_DIM), BF)
        kp = k_o[0, :, cols]
        vt = v_o[0, :, cols].T
        outs = []
        for h in range(2):
            keep = low_lane if h == 0 else jnp.logical_not(low_lane)
            qh = jnp.where(keep, qp, jnp.zeros_like(qp))
            st = dot(kp, qh, NT) + bias[...]
            top = jnp.max(st, axis=0, keepdims=True)
            ex = jnp.exp(st - top)
            tot = jnp.sum(ex, axis=0, keepdims=True)
            pt = (ex * (1.0 / tot)).astype(BF)
            p_o[0, 2 * i + h] = pt
            outs.append(dot(vt[h * HEAD_DIM : (h + 1) * HEAD_DIM], pt))
        c_o[0, :, cols] = jnp.concatenate(outs, axis=0).T.astype(BF)
        return carry

    lax.fori_loop(0, HEADS // 2, pair, 0)


def attn_fwd(thr, xall, wq, wk, wv, vec):
    pages, rows, d = xall.shape
    own = rows // 2
    const = lambda p, t: (0, 0)
    by_page = lambda p, t: (p, 0, 0)
    one = pl.Buffered(1)
    return call(
        attn_fwd_body,
        (
            pages * (2 * d * d * (own + 2 * rows) + 4 * own * rows * d),
            pages * rows * d * 2 * 4 + 6 * d * d + pages * HEADS * own * rows * 2,
            pages * HEADS * own * rows,
        ),
        grid_spec=pltpu.PrefetchScalarGridSpec(
            num_scalar_prefetch=1,
            grid=(pages,),
            in_specs=[pl.BlockSpec((1, rows, d), by_page)]
            + [pl.BlockSpec((d, d), const, pipeline_mode=one)] * 3
            + [pl.BlockSpec((8, d), const)],
            out_specs=[
                pl.BlockSpec((1, own, d), by_page),
                pl.BlockSpec((1, rows, d), by_page),
                pl.BlockSpec((1, rows, d), by_page),
                pl.BlockSpec((1, HEADS, rows, own), lambda p, t: (p, 0, 0, 0)),
                pl.BlockSpec((1, own, d), by_page),
            ],
            scratch_shapes=[pltpu.VMEM((rows, own), F32)],
        ),
        out_shape=[
            jax.ShapeDtypeStruct((pages, own, d), BF),
            jax.ShapeDtypeStruct((pages, rows, d), BF),
            jax.ShapeDtypeStruct((pages, rows, d), BF),
            jax.ShapeDtypeStruct((pages, HEADS, rows, own), BF),
            jax.ShapeDtypeStruct((pages, own, d), BF),
        ],
        name="attn_fwd",
    )(thr, xall, wq, wk, wv, vec)


def attn_bwd_body(q, k, v, p, ctx, dctx, dq_o, dk_own, dk_oth, dv_own, dv_oth):
    own = q.shape[1]
    low_lane = lax.broadcasted_iota(jnp.int32, (own, PAIR), 1) < HEAD_DIM
    scale = 1.0 / math.sqrt(HEAD_DIM)

    def pair(i, carry):
        cols = pl.ds(pl.multiple_of(i * PAIR, PAIR), PAIR)
        qp = q[0, :, cols] * jnp.array(scale, BF)
        kp = k[0, :, cols]
        kt = kp.T
        vp = v[0, :, cols]
        dc = dctx[0, :, cols]
        prod = (dc.astype(F32) * ctx[0, :, cols].astype(F32)).T
        dk = None
        dv = None
        dqs = []
        for h in range(2):
            keep = low_lane if h == 0 else jnp.logical_not(low_lane)
            feats = slice(h * HEAD_DIM, (h + 1) * HEAD_DIM)
            dch = jnp.where(keep, dc, jnp.zeros_like(dc))
            qh = jnp.where(keep, qp, jnp.zeros_like(qp))
            pt = p[0, 2 * i + h]
            delta = jnp.sum(prod[feats], axis=0, keepdims=True)
            dpt = dot(vp, dch, NT)
            dst = (pt.astype(F32) * (dpt - delta)).astype(BF)
            dvh = dot(pt, dch)
            dkh = dot(dst, qh)
            dk = dkh if dk is None else dk + dkh
            dv = dvh if dv is None else dv + dvh
            dqs.append(dot(kt[feats], dst))
        dq_o[0, :, cols] = (jnp.concatenate(dqs, axis=0) * scale).T.astype(BF)
        dk_own[0, :, cols] = dk[:own].astype(BF)
        dk_oth[0, :, cols] = dk[own:].astype(BF)
        dv_own[0, :, cols] = dv[:own].astype(BF)
        dv_oth[0, :, cols] = dv[own:].astype(BF)
        return carry

    lax.fori_loop(0, HEADS // 2, pair, 0)


def attn_bwd(q, k, v, p, ctx, dctx):
    pages, own, d = q.shape
    rows = k.shape[1]
    by_page = lambda i: (i, 0, 0)
    o = pl.BlockSpec((1, own, d), by_page)
    r = pl.BlockSpec((1, rows, d), by_page)
    return call(
        attn_bwd_body,
        (pages * 10 * own * rows * d, pages * (own * rows * HEADS * 2 + 10 * own * d * 2), 0),
        grid=(pages,),
        in_specs=[o, r, r, pl.BlockSpec((1, HEADS, rows, own), lambda i: (i, 0, 0, 0)), o, o],
        out_specs=[o] * 5,
        out_shape=[jax.ShapeDtypeStruct((pages, own, d), BF)] * 5,
        name="attn_bwd",
    )(q, k, v, p, ctx, dctx)


def normal_parts(v):
    bell = jnp.exp(v * v * -0.5)
    t = 1.0 / (1.0 + jnp.abs(v) * (0.3275911 / math.sqrt(2.0)))
    tail = t * (
        0.127414796 + t * (-0.142248368 + t * (0.7107068705 + t * (-0.7265760135 + t * 0.5307027145)))
    )
    tail = tail * bell
    return jnp.where(v >= 0.0, 1.0 - tail, tail), bell * (1.0 / math.sqrt(2.0 * math.pi))


def row_norm(v):
    centered = v - jnp.mean(v, -1, keepdims=True)
    inv = lax.rsqrt(jnp.mean(centered * centered, -1, keepdims=True) + EPS)
    return centered * inv, inv


def norm_back(e, n, inv):
    return inv * (e - jnp.mean(e, -1, keepdims=True) - n * jnp.mean(e * n, -1, keepdims=True))


def ffn_body(
    ctx, xall, cown, wo, wi_h, w2_h, vec, b_in,
    out, gm1_o, dctx_o, dwo_o, dwi_h, dw2_h, gvec, gbin,
    wi, w2, act, din, dgel, hid, gout, gatt, n1s, h1s, accs, r1s, dwi, dw2, lsem, osem,
):
    n, ff = act.shape
    pages, own, d = ctx.shape

    def cols_of(j):
        return pl.ds(pl.multiple_of(j * CHUNK, CHUNK), CHUNK)

    def loads(j):
        cols = cols_of(j)
        return (
            pltpu.make_async_copy(wi_h.at[:, cols], wi.at[:, cols], lsem.at[0, j]),
            pltpu.make_async_copy(w2_h.at[cols, :], w2.at[cols, :], lsem.at[1, j]),
        )

    def store_w2(j):
        return pltpu.make_async_copy(dw2.at[cols_of(j), :], dw2_h.at[cols_of(j), :], osem.at[0, j])

    def store_wi(j):
        return pltpu.make_async_copy(dwi.at[:, cols_of(j)], dwi_h.at[:, cols_of(j)], osem.at[1, j])

    n_chunks = ff // CHUNK
    for j in range(n_chunks):
        for copy in loads(j):
            copy.start()
    gvec[...] = jnp.zeros_like(gvec)

    def add(row, value):
        gvec[row : row + 1, :] += jnp.sum(value, 0, keepdims=True)

    for p in range(pages):
        r = slice(p * own, (p + 1) * own)
        mid = xall[p].astype(F32) + (dot(ctx[p], wo[...]) + vec[2:3, :])
        n1, r1 = row_norm(mid)
        n1s[r, :] = n1
        r1s[r, :] = jnp.broadcast_to(r1, (own, 128))
        h1 = n1 * vec[3:4, :] + vec[4:5, :]
        h1s[r, :] = h1
        hid[r, :] = h1.astype(BF)
    accs[...] = jnp.zeros_like(accs)

    def up(j, carry):
        cols = cols_of(j)
        for copy in loads(j):
            copy.wait()
        pre = dot(hid[...], wi[:, cols]) + b_in[:, cols]
        big, bell = normal_parts(pre)
        a = (pre * big).astype(BF)
        dgel[:, cols] = (big + pre * bell).astype(BF)
        act[:, cols] = a
        accs[...] += dot(a, w2[cols, :])
        return carry

    lax.fori_loop(0, n_chunks, up, 0)
    for p in range(pages):
        r = slice(p * own, (p + 1) * own)
        mid = h1s[r, :] + (accs[r, :] + vec[5:6, :])
        n2, r2 = row_norm(mid)
        out[p] = (n2 * vec[6:7, :] + vec[7:8, :]).astype(BF)
        cot = cown[p].astype(F32)
        gm2 = norm_back(cot * vec[6:7, :], n2, r2)
        go = gm2.astype(BF)
        gout[r, :] = go
        accs[r, :] = gm2
        add(5, go.astype(F32))
        add(6, cot * n2)
        add(7, cot)

    def down(j, carry):
        cols = cols_of(j)
        di = (dot(gout[...], w2[cols, :], NT) * dgel[:, cols].astype(F32)).astype(BF)
        din[:, cols] = di
        accs[...] += dot(di, wi[:, cols], NT)
        gbin[:, cols] = jnp.sum(di.astype(F32), 0, keepdims=True)
        dw2[cols, :] = dot(act[:, cols], gout[...], TN).astype(BF)
        store_w2(j).start()
        return carry

    lax.fori_loop(0, n_chunks, down, 0)
    for p in range(pages):
        r = slice(p * own, (p + 1) * own)
        gh = accs[r, :]
        n1 = n1s[r, :]
        gm1 = norm_back(gh * vec[3:4, :], n1, r1s[r, 0:1])
        gm1_o[p] = gm1
        ga = gm1.astype(BF)
        gatt[r, :] = ga
        dctx_o[p] = dot(ga, wo[...], NT).astype(BF)
        add(2, ga.astype(F32))
        add(3, gh * n1)
        add(4, gh)
    hid_t = hid[...].T

    def grads(j, carry):
        cols = cols_of(j)
        dwi[:, cols] = dot(hid_t, din[:, cols]).astype(BF)
        store_wi(j).start()
        return carry

    lax.fori_loop(0, n_chunks, grads, 0)
    dwo_o[...] = dot(ctx[...].reshape(n, d), gatt[...], TN).astype(BF)
    for j in range(n_chunks):
        store_w2(j).wait()
        store_wi(j).wait()


def ffn(ctx, xall, cown, wo, wi, w2, vec, b_in):
    pages, own, d = ctx.shape
    ff = wi.shape[1]
    n = pages * own
    sds = jax.ShapeDtypeStruct
    vm = pltpu.VMEM
    dma = pltpu.SemaphoreType.DMA
    return call(
        ffn_body,
        (n * d * (12 * ff + 6 * d), 4 * d * ff * 2 + 12 * n * d * 2, n * ff),
        grid=(1,),
        in_specs=[
            pl.BlockSpec((pages, own, d), lambda i: (0, 0, 0)),
            pl.BlockSpec((pages, own, d), lambda i: (0, 0, 0)),
            VM, VM, ANY, ANY, VM, VM,
        ],
        out_specs=[VM] * 4 + [ANY, ANY, VM, VM],
        out_shape=[
            sds((pages, own, d), BF), sds((pages, own, d), F32), sds((pages, own, d), BF),
            sds((d, d), BF), sds((d, ff), BF), sds((ff, d), BF), sds((8, d), F32), sds((1, ff), F32),
        ],
        scratch_shapes=[
            vm((d, ff), BF), vm((ff, d), BF), vm((n, ff), BF), vm((n, ff), BF), vm((n, ff), BF),
            vm((n, d), BF), vm((n, d), BF), vm((n, d), BF), vm((n, d), F32), vm((n, d), F32),
            vm((n, d), F32), vm((n, 128), F32), vm((d, ff), BF), vm((ff, d), BF),
            dma((2, ff // CHUNK)), dma((2, ff // CHUNK)),
        ],
        params=dict(vmem_limit_bytes=63 << 20),
        name="ffn",
    )(ctx, xall, cown, wo, wi, w2, vec, b_in)


def proj_body(
    xall, dq, dk, dkr, dv, dvr, gm1, wq, wk, wv,
    ga_o, gb_o, dwq_o, dwk_o, dwv_o, gvec, x_all, dq_all, dk_all, dv_all,
):
    page = pl.program_id(0)
    own = xall.shape[1]
    blk = own // 2
    here = pl.ds(pl.multiple_of(page * own, own), own)
    x_all[here, :] = xall[0]
    dq_v = dq[0]
    dk_v = (dk[0].astype(F32) + dkr[0].astype(F32)).astype(BF)
    dv_v = (dv[0].astype(F32) + dvr[0].astype(F32)).astype(BF)
    dq_all[here, :] = dq_v
    dk_all[here, :] = dk_v
    dv_all[here, :] = dv_v
    gx = gm1[0] + dot(dq_v, wq[...], NT) + dot(dk_v, wk[...], NT) + dot(dv_v, wv[...], NT)
    ga_o[0] = gx[:blk]
    gb_o[0] = gx[blk:].astype(BF)

    @pl.when(page == 0)
    def _():
        gvec[...] = jnp.zeros_like(gvec)

    gvec[0:1, :] += jnp.sum(dq_v.astype(F32), 0, keepdims=True)
    gvec[1:2, :] += jnp.sum(dv_v.astype(F32), 0, keepdims=True)

    @pl.when(page == pl.num_programs(0) - 1)
    def _():
        x_t = x_all[...].T
        dwq_o[...] = dot(x_t, dq_all[...]).astype(BF)
        dwk_o[...] = dot(x_t, dk_all[...]).astype(BF)
        dwv_o[...] = dot(x_t, dv_all[...]).astype(BF)


def proj(xall, dq, dk, dkr, dv, dvr, gm1, wq, wk, wv):
    pages, own, d = dq.shape
    blk = own // 2
    n = pages * own
    by_page = lambda p: (p, 0, 0)
    const = lambda p: (0, 0)
    one = pl.Buffered(1)
    half = pl.BlockSpec((1, blk, d), by_page)
    whole = pl.BlockSpec((1, own, d), by_page)
    square = pl.BlockSpec((d, d), const, pipeline_mode=one)
    return call(
        proj_body,
        (12 * n * d * d, 12 * d * d + 16 * n * d, 0),
        grid=(pages,),
        in_specs=[whole] * 7 + [square] * 3,
        out_specs=[half, half] + [square] * 3 + [pl.BlockSpec((8, d), const)],
        out_shape=[
            jax.ShapeDtypeStruct((pages, blk, d), F32),
            jax.ShapeDtypeStruct((pages, blk, d), BF),
        ]
        + [jax.ShapeDtypeStruct((d, d), BF)] * 3
        + [jax.ShapeDtypeStruct((8, d), F32)],
        scratch_shapes=[pltpu.VMEM((n, d), BF)] * 4,
        name="proj_bwd",
    )(xall, dq, dk, dkr, dv, dvr, gm1, wq, wk, wv)


def place():
    f, s = lax.axis_index("fsdp"), lax.axis_index("seq")
    return lax.div(f, 2), lax.rem(f, 2), lax.div(s, 2), lax.rem(s, 2)


def at(z, y, x, c):
    return {"fsdp": 2 * z + y, "seq": 2 * x + c}


def meet(others):
    barrier = pltpu.get_barrier_semaphore()
    for other in others:
        pl.semaphore_signal(barrier, inc=1, device_id=other, device_id_type=MESH)
    pl.semaphore_wait(barrier, len(others))


def remote(src, dst, send, recv, other):
    return pltpu.make_async_remote_copy(
        src_ref=src, dst_ref=dst, send_sem=send, recv_sem=recv,
        device_id=other, device_id_type=MESH,
    )


def begin(copy):
    copy.start()
    return copy


class Spread:
    def __init__(self, where, src, dst, row0, col0, width, sems, key, from0=None):
        self.z, self.y, self.x, self.c = where
        z, y, x, c = where
        zs, zr, fs, ys, yr, xs, xr, cs, cr, lo = sems
        k = key
        cols = pl.ds(pl.multiple_of(col0 + width * c, 128), width)
        origin = pl.ds(pl.multiple_of((col0 if from0 is None else from0) + width * c, 128), width)
        full = pl.ds(row0, ROW)
        mine = pl.ds(pl.multiple_of(row0 + (ROW - YROWS) * x, 16), YROWS)
        lacks = pl.ds(pl.multiple_of(row0 + YROWS * x, 16), ROW - YROWS)
        near, far, across = z + 1 - 2 * lax.rem(z, 2), lax.rem(z + 2, 4), 3 - z
        self.inner = jnp.logical_or(z == 1, z == 2)
        self.local = lambda: pltpu.make_async_copy(src.at[full, origin], dst.at[z, y, full, cols], lo.at[k])

        def send(block, n, target, sem):
            from_ref = src.at[full, origin] if block is None else dst.at[block, y, full, cols]
            b = z if block is None else block
            return remote(from_ref, dst.at[b, y, full, cols], sem, zr.at[k + (n,)], at(target, y, x, c))

        self.a = lambda: send(None, 0, near, zs.at[k + (0,)])
        self.b = lambda: send(None, 1, far, zs.at[k + (1,)])
        self.d = lambda: send(None, 2, across, zs.at[k + (2,)])
        self.fwd = lambda: send(far, 2, near, fs.at[k])
        yv = lambda: dst.at[:, y, mine, cols]
        self.ycopy = lambda: remote(yv(), yv(), ys.at[k], yr.at[k], at(z, 1 - y, x, c))
        xv = lambda: dst.at[:, 1 - y, lacks, cols]
        self.xcopy = lambda: remote(xv(), xv(), xs.at[k], xr.at[k], at(z, y, 1 - x, c))
        cv = lambda: dst.at[:, :, full, cols]
        self.ccopy = lambda: remote(cv(), cv(), cs.at[k], cr.at[k], at(z, y, x, 1 - c))

    def along_z(self):
        self.local().start()
        self.b().start()
        self.a().start()

        @pl.when(self.inner)
        def _():
            self.d().start()

    def forward(self):
        self.b().wait_recv()

        @pl.when(self.inner)
        def _():
            self.fwd().start()

    def along_y(self):
        self.a().wait_recv()
        self.d().wait_recv()
        self.local().wait()
        self.ycopy().start()

    def along_x(self):
        self.ycopy().wait_recv()
        self.xcopy().start()

    def to_core(self):
        self.xcopy().wait_recv()
        self.ccopy().start()

    def arrive(self):
        self.ccopy().wait_recv()

    def drain(self):
        self.a().wait_send()
        self.b().wait_send()

        @pl.when(self.inner)
        def _():
            self.d().wait_send()
            self.fwd().wait_send()

        self.ycopy().wait_send()
        self.xcopy().wait_send()
        self.ccopy().wait_send()


def spread_sems(*lead):
    dma = pltpu.SemaphoreType.DMA
    return [dma(lead + (3,)), dma(lead + (3,))] + [dma(lead)] * 8


GROUPS = 3
GCOLS = 256
REST = 9
EARLY = 2
YROWS = 64


def fwd_body(
    lens, x_in, cot, wq, wk, wv, wo, wi, w2, *refs,
):
    smalls = refs[:9]
    (
        gq_h, gk_h, gv_h, xall_h, q_h, k_h, v_h, c_h, p_o,
        go_h, gi_h, g2_h, act_h, dd_h, hid_h, gout_h, n1_h, gm2_h, r1_h, out_h, gvs, vec,
    ) = refs[9:31]
    (
        gq, gk, gv, go, gi, g2, xall, q_o, k_o, v_o, c_o, cown, bias, pbuf, vpk, gvec, b_in,
        act, dd, hid, gout, n1b, n1s, accs, r1s,
    ) = refs[31:56]
    qs, rs = refs[56:66], refs[66:76]
    asend, arecv, aloc, vs, vr, ps, outs_sem, chunk_sem = refs[76:]
    z, y, x, c = where = place()
    f = 2 * z + y
    pages, rows = xall.shape[0], xall.shape[1]
    own, blk = rows // 2, rows // 4
    width = smalls[0].shape[-1]
    for i in range(8):
        vpk[i : i + 1, :width] = smalls[i][...].astype(F32).reshape(1, width)
    for i in range(3):
        vpk[8 + i : 9 + i, :] = smalls[8][128 * i : 128 * (i + 1)].astype(F32).reshape(1, 128)
    gvec[f] = vpk[...]
    x_peer, c_peer = at(z, y, 1 - x, c), at(z, y, x, 1 - c)
    meet([{"fsdp": lax.rem(f + k + 1, 8)} for k in range(7)] + [x_peer, c_peer])

    groups = [
        [Spread(where, src, dst, 0, GCOLS * g, GCOLS // 2, qs, (g, w)) for w, (src, dst) in enumerate(((wq, gq), (wk, gk), (wv, gv)))]
        for g in range(GROUPS)
    ]

    def each(g, step):
        for part in groups[g]:
            getattr(part, step)()

    mine, sent = pl.ds(pages * x, pages), pl.ds(pages * (1 - x), pages)

    def band(b):
        return xall.at[:, pl.ds(blk * b, blk), :]

    to_b = remote(x_in.at[sent], band(1), asend.at[0], arecv.at[0], x_peer)
    to_c = remote(x_in.at[mine], band(2), asend.at[1], arecv.at[1], c_peer)
    to_d = remote(band(1), band(3), asend.at[2], arecv.at[2], c_peer)
    cot_b = remote(cot.at[sent], cown.at[:, pl.ds(blk, blk), :], asend.at[3], arecv.at[3], x_peer)
    keep_x = pltpu.make_async_copy(x_in.at[mine], band(0), aloc.at[0])
    keep_c = pltpu.make_async_copy(cot.at[mine], cown.at[:, pl.ds(0, blk), :], aloc.at[1])
    vecs = [
        remote(vpk, gvec.at[f], vs.at[k], vr.at[k], {"fsdp": lax.rem(f + k + 1, 8)}) for k in range(7)
    ]
    def rest(p, step):
        def run(src, dst, row0, col0, from0=None):
            getattr(Spread(where, src, dst, row0, col0, 384, rs, (p,), from0), step)()

        @pl.when(p == 0)
        def _():
            run(wo, go, 0, 0)

        @pl.when(jnp.logical_and(p >= 1, p < 5))
        def _():
            run(wi, gi.at[p - 1], 0, 0, 768 * (p - 1))

        @pl.when(jnp.logical_and(p >= 5, p < REST))
        def _():
            run(w2, g2, ROW * (p - 5), 0)

    to_b.start()
    each(0, "along_z")
    keep_x.start()
    to_c.start()
    for copy in vecs:
        copy.start()
    place_row = lax.broadcasted_iota(jnp.int32, (blk, own), 0)
    for page in range(pages):
        for b in range(4):
            side = x if b % 2 == 0 else 1 - x
            core = c if b < 2 else 1 - c
            limit = lens[pages * x + page] - (2 * side + core) * blk
            bias[page, b * blk : (b + 1) * blk, :] = jnp.where(place_row < limit, 0.0, NEG)
    each(0, "forward")
    each(1, "along_z")
    each(0, "along_y")
    each(1, "forward")
    each(2, "along_z")
    each(1, "along_y")
    each(0, "along_x")
    each(2, "forward")
    for p in range(EARLY):
        rest(p, "along_z")
    each(2, "along_y")
    to_b.wait_recv()
    to_d.start()
    each(0, "to_core")
    each(1, "along_x")
    for copy in vecs:
        copy.wait_recv()
    for i in range(8):
        vec[i : i + 1, :] = jnp.concatenate([gvec[j, i : i + 1, :width] for j in range(8)], axis=1)
    for j in range(8):
        for i in range(3):
            b_in[:, (3 * j + i) * 128 : (3 * j + i + 1) * 128] = gvec[j, 8 + i : 9 + i, :]
    keep_c.start()
    keep_x.wait()
    to_c.wait_recv()
    to_d.wait_recv()
    each(0, "arrive")

    low_lane = lax.broadcasted_iota(jnp.int32, (own, PAIR), 1) < HEAD_DIM
    stages = (("along_z", 1 - 8 * EARLY // 3), ("forward", 0), ("along_y", 3), ("along_x", 8), ("to_core", 13))

    def tick(t):
        for step, late in stages:
            n = t - late
            p = lax.div(3 * n + 7, 8)

            @pl.when(jnp.logical_and(n >= 0, lax.div(8 * p, 3) == n))
            def _():
                if step == "along_z":
                    pl.when(p >= EARLY)(lambda: rest(p, step))
                else:
                    rest(p, step)

    def p_copy(page, pair, slot):
        return pltpu.make_async_copy(pbuf.at[slot], p_o.at[page, pl.ds(2 * pair, 2)], ps.at[slot])

    def unit(it, carry):
        g, page = lax.div(it, pages), lax.rem(it, pages)

        @pl.when(it == 0)
        def _():
            each(2, "along_x")
            each(1, "to_core")

        @pl.when(it == 1)
        def _():
            each(2, "to_core")
            cot_b.start()

        @pl.when(it == pages)
        def _():
            each(1, "arrive")

        @pl.when(it == 2 * pages)
        def _():
            each(2, "arrive")

        gcols = pl.ds(pl.multiple_of(g * GCOLS, GCOLS), GCOLS)
        x_all = xall[page]
        d = x_all.shape[1]
        query = (dot(x_all[:own], gq[:, :, :, gcols].reshape(d, GCOLS)) + vec[0:1, gcols]).astype(BF)
        keys = dot(x_all, gk[:, :, :, gcols].reshape(d, GCOLS)).astype(BF)
        vals = (dot(x_all, gv[:, :, :, gcols].reshape(d, GCOLS)) + vec[1:2, gcols]).astype(BF)
        q_o[page, :, gcols] = query
        k_o[page, :, gcols] = keys
        v_o[page, :, gcols] = vals
        for half in range(2):
            lanes = slice(half * PAIR, (half + 1) * PAIR)
            pair = 2 * g + half

            @pl.when(it > 0)
            def _():
                p_copy(page, pair, half).wait()

            qp = query[:, lanes] * jnp.array(1.0 / math.sqrt(HEAD_DIM), BF)
            kp = keys[:, lanes]
            vt = vals[:, lanes].T
            outs = []
            for h in range(2):
                keep = low_lane if h == 0 else jnp.logical_not(low_lane)
                qh = jnp.where(keep, qp, jnp.zeros_like(qp))
                st = dot(kp, qh, NT) + bias[page]
                top = jnp.max(st, axis=0, keepdims=True)
                ex = jnp.exp(st - top)
                tot = jnp.sum(ex, axis=0, keepdims=True)
                pt = (ex * (1.0 / tot)).astype(BF)
                pbuf[half, h] = pt
                outs.append(dot(vt[h * HEAD_DIM : (h + 1) * HEAD_DIM], pt))
            p_copy(page, pair, half).start()
            cols = pl.ds(pl.multiple_of(pair * PAIR, PAIR), PAIR)
            c_o[page, :, cols] = jnp.concatenate(outs, axis=0).T.astype(BF)
            tick(2 * it + half)
        return carry

    lax.fori_loop(0, GROUPS * pages, unit, 0)
    n_ticks = 2 * GROUPS * pages
    stores = [
        pltpu.make_async_copy(src, dst, outs_sem.at[i])
        for i, (src, dst) in enumerate(
            ((q_o, q_h), (k_o, k_h), (v_o, v_h), (c_o, c_h), (xall, xall_h), (gq, gq_h), (gk, gk_h), (gv, gv_h))
        )
    ]
    for copy in stores:
        copy.start()
    for half in range(2):
        p_copy(0, 0, half).wait()

    d = xall.shape[2]
    n_chunks = gi.shape[0]
    last = 8 * (REST - 1) // 3 + stages[-1][1] + 1
    gvs[...] = jnp.zeros_like(gvs)

    def add(row, value):
        gvs[row : row + 1, :] += jnp.sum(value, 0, keepdims=True)

    def square(ref):
        return ref[...].reshape(d, d)

    rest(0, "arrive")
    later = [pltpu.make_async_copy(go, go_h, outs_sem.at[8])]
    later[0].start()
    for page in range(pages):
        r = slice(page * own, (page + 1) * own)
        mid = xall[page, :own].astype(F32) + (dot(c_o[page], square(go)) + vec[2:3, :])
        n1, r1 = row_norm(mid)
        n1s[r, :] = n1
        n1b[r, :] = n1.astype(BF)
        r1s[r, :] = jnp.broadcast_to(r1, (own, 128))
        hid[r, :] = (n1 * vec[3:4, :] + vec[4:5, :]).astype(BF)

    def ticks(lo, hi):
        lax.fori_loop(lo, hi, lambda t, carry: (tick(t), carry)[1], 0)

    def chunk_stores(j):
        cols = pl.ds(pl.multiple_of(j * d, d), d)
        return [
            pltpu.make_async_copy(src, dst.at[j], chunk_sem.at[i, j])
            for i, (src, dst) in enumerate(((gi.at[j], gi_h), (act.at[:, cols], act_h), (dd.at[:, cols], dd_h)))
        ]

    def up(j, carry):
        ticks(n_ticks + 3 * j, jnp.minimum(n_ticks + 3 * j + 3, last))
        rest(j + 1, "arrive")
        cols = pl.ds(pl.multiple_of(j * d, d), d)
        pre = dot(hid[...], gi[j].reshape(d, d)) + b_in[:, cols]
        big, bell = normal_parts(pre)
        act[:, cols] = (pre * big).astype(BF)
        dd[:, cols] = (big + pre * bell).astype(BF)
        for copy in chunk_stores(j):
            copy.start()
        return carry

    lax.fori_loop(0, n_chunks, up, 0)
    ticks(n_ticks + 3 * n_chunks, last)
    for p in range(5, REST):
        rest(p, "arrive")
    keep_c.wait()
    cot_b.wait_recv()
    stores[0].wait()
    later.append(pltpu.make_async_copy(g2, g2_h, outs_sem.at[9]))
    later[1].start()

    def w2_rows(j):
        return g2[j].reshape(d, d)

    accs[...] = jnp.zeros_like(accs)

    def outer(j, carry):
        cols = pl.ds(pl.multiple_of(j * d, d), d)
        accs[...] += dot(act[:, cols], w2_rows(j))
        return carry

    lax.fori_loop(0, n_chunks, outer, 0)
    for page in range(pages):
        r = slice(page * own, (page + 1) * own)
        h1 = n1s[r, :] * vec[3:4, :] + vec[4:5, :]
        mid = h1 + (accs[r, :] + vec[5:6, :])
        n2, r2 = row_norm(mid)
        q_o[page] = (n2 * vec[6:7, :] + vec[7:8, :]).astype(BF)
        ct = cown[page].astype(F32)
        gm2 = norm_back(ct * vec[6:7, :], n2, r2)
        gob = gm2.astype(BF)
        gout[r, :] = gob
        accs[r, :] = gm2
        add(5, gob.astype(F32))
        add(6, ct * n2)
        add(7, ct)
    for i, (src, dst) in enumerate(((accs, gm2_h), (gout, gout_h), (hid, hid_h), (n1b, n1_h), (r1s, r1_h), (q_o, out_h))):
        later.append(pltpu.make_async_copy(src, dst, outs_sem.at[10 + i]))
        later[-1].start()

    def finish(p, carry):
        rest(p, "drain")
        return carry

    lax.fori_loop(0, REST, finish, 0)
    for g in range(GROUPS):
        each(g, "drain")
    for copy in vecs + [to_b, to_c, to_d, cot_b]:
        copy.wait_send()
    for j in range(n_chunks):
        later += chunk_stores(j)
    for copy in stores[1:] + later:
        copy.wait()


def fwd(lens, x_in, cot, ws, smalls):
    pages_all, blk, d = x_in.shape
    pages, own, rows = pages_all // 2, 2 * blk, 4 * blk
    n = pages * own
    dma = pltpu.SemaphoreType.DMA
    sds = jax.ShapeDtypeStruct
    vm = pltpu.VMEM
    ff = ws[4].shape[1]
    quarter = (4, 2, ROW, d)
    res = call(
        fwd_body,
        (n * d * (12 * ff + 12 * d), sum(16 * w.size for w in ws), pages * HEADS * own * rows),
        in_specs=[pl.BlockSpec(memory_space=pltpu.SMEM)] + [ANY] * 5 + [VM] * 12,
        out_specs=[ANY] * 20 + [VM, VM],
        out_shape=[sds(quarter, BF)] * 3
        + [
            sds((pages, rows, d), BF),
            sds((pages, own, d), BF), sds((pages, rows, d), BF), sds((pages, rows, d), BF), sds((pages, own, d), BF),
            sds((pages, HEADS, rows, own), BF),
            sds(quarter, BF), sds((ff // d,) + quarter, BF), sds((4, 2, ff // 8, d), BF),
            sds((ff // d, n, d), BF), sds((ff // d, n, d), BF), sds((n, d), BF), sds((n, d), BF), sds((n, d), BF),
            sds((n, d), F32), sds((n, 128), F32), sds((pages, own, d), BF),
            sds((8, d), F32), sds((8, d), F32),
        ],
        scratch_shapes=[
            vm(quarter, BF), vm(quarter, BF), vm(quarter, BF), vm(quarter, BF),
            vm((ff // d,) + quarter, BF), vm((4, 2, ff // 8, d), BF),
            vm((pages, rows, d), BF), vm((pages, own, d), BF), vm((pages, rows, d), BF), vm((pages, rows, d), BF),
            vm((pages, own, d), BF), vm((pages, own, d), BF), vm((pages, rows, own), F32), vm((2, 2, rows, own), BF),
            vm((16, 128), F32), vm((8, 16, 128), F32), vm((1, ff), F32),
            vm((n, ff), BF), vm((n, ff), BF), vm((n, d), BF), vm((n, d), BF), vm((n, d), BF),
            vm((n, d), F32), vm((n, d), F32), vm((n, 128), F32),
        ]
        + spread_sems(GROUPS, 3)
        + spread_sems(REST)
        + [dma((5,)), dma((5,)), dma((3,)), dma((7,)), dma((7,)), dma((2,)), dma((16,)), dma((3, ff // d))],
        params=dict(collective_id=0, has_side_effects=True, vmem_limit_bytes=64 << 20),
        name="gather_forward",
    )(lens, x_in, cot, *ws, *smalls)
    return res


class Fold:
    def __init__(self, where, acc, bufs, sems, key, keep):
        self.z, self.y, self.x, self.c = where
        self.acc, self.key = acc, key
        give = ROW - keep
        self.split = give > 0
        self.rc, self.rx, self.ry, self.rz, self.fin, self.rf = [b.at[key] for b in bufs]
        self.cs, self.cr, self.xs, self.xr, self.ys, self.yr, self.zs, self.zr, self.fs, self.fr, self.es, self.er = sems
        z = self.z
        self.near, self.far, self.across = z + 1 - 2 * lax.rem(z, 2), lax.rem(z + 2, 4), 3 - z
        self.inner = jnp.logical_or(z == 1, z == 2)
        self.outer = jnp.logical_not(self.inner)
        self.keep = pl.ds(pl.multiple_of(give * self.x, 16), keep)
        self.give = pl.ds(pl.multiple_of(keep * (1 - self.x), 16), give)
        self.gain = pl.ds(pl.multiple_of(keep * self.x, 16), give)

    def part(self, *sel):
        return self.acc(sel)

    def xcopy(self):
        return remote(
            self.part(ALL, 1 - self.y, self.give), self.rx, self.xs.at[self.key], self.xr.at[self.key],
            at(self.z, self.y, 1 - self.x, self.c),
        )

    def ycopy(self):
        return remote(
            self.part(ALL, 1 - self.y, self.keep), self.ry, self.ys.at[self.key], self.yr.at[self.key],
            at(self.z, 1 - self.y, self.x, self.c),
        )

    def zcopy(self, block, target, slot):
        return remote(
            self.part(block, self.y, ALL), self.rz.at[slot], self.zs.at[self.key + (slot,)],
            self.zr.at[self.key + (slot,)], at(target, self.y, self.x, self.c),
        )

    def a(self):
        return self.zcopy(self.near, self.near, 0)

    def b(self):
        return self.zcopy(self.far, self.far, 1)

    def d(self):
        return self.zcopy(self.across, self.across, 2)

    def f(self):
        return self.zcopy(self.across, self.near, 3)

    def fcopy(self):
        return remote(
            self.fin, self.rf, self.fs.at[self.key], self.fr.at[self.key],
            at(self.z, self.y, 1 - self.x, self.c),
        )

    def over_x(self, first):
        first.wait_recv()
        whole = self.part(ALL, ALL, ALL)
        whole[...] = whole[...] + self.rc[...]
        if self.split:
            self.xcopy().start()
        else:
            self.ycopy().start()

    def over_y(self):
        if not self.split:
            return
        self.xcopy().wait_recv()
        rows = self.part(ALL, 1 - self.y, self.gain)
        rows[...] = rows[...] + self.rx[...]
        self.ycopy().start()

    def over_z(self):
        self.ycopy().wait_recv()
        rows = self.part(ALL, self.y, self.keep)
        rows[...] = rows[...] + self.ry[...]
        self.a().start()

        @pl.when(self.outer)
        def _():
            self.f().start()
            self.b().start()

        @pl.when(self.inner)
        def _():
            self.d().start()

    def inside(self):
        @pl.when(self.inner)
        def _():
            self.f().wait_recv()
            rows = self.part(self.far, self.y, ALL)
            rows[...] = rows[...] + self.rz[3]
            self.b().start()

    def total(self):
        self.a().wait_recv()
        self.b().wait_recv()
        own = self.part(self.z, self.y, ALL)

        @pl.when(self.outer)
        def _():
            self.fin[...] = (own[...].astype(F32) + self.rz[0].astype(F32) + self.rz[1].astype(F32)).astype(BF)

        @pl.when(self.inner)
        def _():
            self.d().wait_recv()
            self.fin[...] = (
                own[...].astype(F32) + self.rz[0].astype(F32) + self.rz[1].astype(F32) + self.rz[2].astype(F32)
            ).astype(BF)

        self.fcopy().start()

    def ecopy(self, view):
        return remote(view, view, self.es.at[self.key], self.er.at[self.key], at(self.z, self.y, self.x, 1 - self.c))

    def write(self, view):
        self.fcopy().wait_recv()
        view[...] = self.fin[...].astype(F32) + self.rf[...].astype(F32)
        self.ecopy(view).start()

    def drain(self, view):
        self.ecopy(view).wait_recv()
        if self.split:
            self.xcopy().wait_send()
        self.ycopy().wait_send()
        self.a().wait_send()
        self.b().wait_send()

        @pl.when(self.outer)
        def _():
            self.f().wait_send()

        @pl.when(self.inner)
        def _():
            self.d().wait_send()

        self.fcopy().wait_send()
        self.ecopy(view).wait_send()


ALL = slice(None)
KEEP_REST = 64
KEEP_GROUP = 96


def fold_sems(*lead):
    dma = pltpu.SemaphoreType.DMA
    return [dma(lead)] * 6 + [dma(lead + (4,))] * 2 + [dma(lead)] * 4


def fold_bufs(width, keep, *lead):
    return [
        pltpu.VMEM(lead + shape, BF)
        for shape in (
            (4, 2, ROW, width), (4, max(ROW - keep, 16), width), (4, keep, width), (4, ROW, width), (ROW, width), (ROW, width),
        )
    ]


def bwd_body(
    gq_h, gk_h, gv_h, x_h, q_h, k_h, v_h, c_h, p_h, go_h, gi_h, g2_h, act_h, dd_h, hid_h, gout_h, n1_h, gm2_h, r1_h, out_h,
    gvf, vec,
    oq, ok, ov, oo, oi, o2, gx, fin_out, ovec,
    *refs,
):
    (
        pool, hid, gout, go, n1b, accs, r1s, c_v, dc_v, acc, dwg, st, dq_all, dk_all, dv_all, rk, rv, sk, sv, pbuf,
        rgx, pack, vecin, vtot, vx, brow, gvs, gbin, stay,
    ) = refs[:29]
    fb, gb = refs[29:35], refs[35:41]
    fsem, gsem = refs[41:53], refs[53:65]
    lsem, msem, ssem, ps, ks, kr, gs, gr, os, vs, vr, us, ur, bs, br, bl = refs[65:]
    z, y, x, c = where = place()
    f = 2 * z + y
    pages, own, d = c_h.shape
    n = pages * own
    blk = own // 2
    rows = 2 * own
    at_k, at_v, at_q, at_gq, at_gk, at_gv = 0, 2 * n, 4 * n, 5 * n, 6 * n, 7 * n
    x_peer, c_peer = at(z, y, 1 - x, c), at(z, y, x, 1 - c)
    meet([{"fsdp": lax.rem(f + k + 1, 8)} for k in range(7)] + [x_peer, c_peer])

    def other_half(p, run):
        @pl.when(p < 6)
        def _():
            run(dwg.at[lax.div(p, 2), :, :, :, pl.ds(pl.multiple_of(384 * lax.rem(p, 2), 128), 384)])

        @pl.when(p >= 6)
        def _():
            run(st.at[p - 6])

    def launch(p):
        other_half(p, lambda ref: remote(ref, fb[0].at[p], fsem[0].at[p], fsem[1].at[p], c_peer).start())

    def rest_out(p, run):
        @pl.when(p < 4)
        def _():
            run(oi.at[:, pl.ds(pl.multiple_of(768 * p + 384 * c, 128), 384)])

        @pl.when(jnp.logical_and(p >= 4, p < 8))
        def _():
            run(o2.at[pl.ds(pl.multiple_of(ROW * (p - 4), 32), ROW), pl.ds(pl.multiple_of(384 * c, 128), 384)])

        @pl.when(p == 8)
        def _():
            run(oo.at[:, pl.ds(pl.multiple_of(384 * c, 128), 384)])

    def fold(p):
        return Fold(where, lambda sel: acc.at[(p,) + sel], fb, fsem, (p,), KEEP_REST)

    def any_first(p):
        return remote(fb[0].at[p], fb[0].at[p], fsem[0].at[p], fsem[1].at[p], c_peer)

    def step(p, name):
        ok_p = jnp.logical_and(p >= 0, p < REST)

        @pl.when(ok_p)
        def _():
            if name == "over_x":
                fold(p).over_x(any_first(p))
            elif name == "write":
                rest_out(p, lambda view: fold(p).write(view))
            elif name == "drain":
                rest_out(p, lambda view: fold(p).drain(view))
            else:
                getattr(fold(p), name)()

    def gfold(g, w):
        cols = pl.ds(pl.multiple_of(GCOLS * w + 128 * c, 128), 128)
        return Fold(where, lambda sel: dwg.at[(g,) + sel + (cols,)], gb, gsem, (g, w), KEEP_GROUP)

    def gfirst(g, w):
        cols = pl.ds(pl.multiple_of(GCOLS * w + 128 * (1 - c), 128), 128)
        return remote(dwg.at[g, :, :, :, cols], gb[0].at[g, w], gsem[0].at[g, w], gsem[1].at[g, w], c_peer)

    def gstep(g, name):
        for w, o in enumerate((oq, ok, ov)):
            view = o.at[:, pl.ds(pl.multiple_of(GCOLS * g + 128 * c, 128), 128)]
            if name == "start":
                gfirst(g, w).start()
            elif name == "over_x":
                gfold(g, w).over_x(gfirst(g, w))
            elif name == "write":
                gfold(g, w).write(view)
            elif name == "drain":
                gfold(g, w).drain(view)
                gfirst(g, w).wait_send()
            else:
                getattr(gfold(g, w), name)()

    stages = (("over_x", 0), ("over_y", 4), ("over_z", 9), ("inside", 14), ("total", 18), ("write", 22))
    pace = 3
    last = pace * (REST + GROUPS - 1) + stages[-1][1] + 1

    def tick(t):
        for name, late in stages:
            n = t - late
            p = lax.div(n, pace)

            @pl.when(jnp.logical_and(n >= 0, jnp.logical_and(lax.rem(n, pace) == 0, p < REST + GROUPS)))
            def _():
                step(p, name)

                @pl.when(p >= REST)
                def _():
                    gstep(p - REST, name)

    firsts = [
        pltpu.make_async_copy(src, dst, lsem.at[i])
        for i, (src, dst) in enumerate(
            ((gout_h, gout), (hid_h, hid), (gm2_h, accs), (n1_h, n1b), (r1_h, r1s), (go_h, go), (c_h, c_v))
        )
    ]

    def row_block(start, size):
        return pl.ds(pl.multiple_of(start, 256), size)

    def slot(kind, j):
        return pool.at[row_block((2 * kind + lax.rem(j, 2)) * n, n), :]

    def chunk_loads(j):
        return [
            pltpu.make_async_copy(src.at[j], slot(kind, j), msem.at[kind, lax.rem(j, 2)])
            for kind, src in enumerate((gi_h, g2_h, act_h, dd_h))
        ]

    seconds = [
        pltpu.make_async_copy(src, pool.at[pl.ds(start, src.shape[0]), :], ssem.at[i])
        for i, (src, start) in enumerate(
            ((q_h, at_q), (k_h, at_k), (v_h, at_v), (gq_h, at_gq), (gk_h, at_gk), (gv_h, at_gv))
        )
    ] + [
        pltpu.make_async_copy(x_h.at[page, pl.ds(0, own), :], hid.at[pl.ds(page * own, own), :], ssem.at[6 + page])
        for page in range(pages)
    ]

    def p_copy(it, half):
        g, page = lax.div(it, pages), lax.rem(it, pages)
        return pltpu.make_async_copy(p_h.at[page, pl.ds(4 * g + 2 * half, 2)], pbuf.at[half], ps.at[half])

    pages_mine = pl.ds(pages * x, pages)
    back_out = remote(out_h.at[:, pl.ds(blk, blk), :], fin_out.at[pages_mine], bs.at[0], br.at[0], x_peer)
    stay_in = pltpu.make_async_copy(out_h.at[:, pl.ds(0, blk), :], stay, bl.at[0])
    stay_out = pltpu.make_async_copy(stay, fin_out.at[pages_mine], bl.at[1])
    back_out.start()
    begin_with = chunk_loads(0)
    for copy in firsts[:1] + [begin_with[1], begin_with[3]] + firsts[1:2] + [begin_with[0]] + firsts[2:3] + [begin_with[2]]:
        copy.start()
    for copy in firsts[3:]:
        copy.start()
    for copy in chunk_loads(1):
        copy.start()
    for half in range(2):
        p_copy(0, half).start()
    stay_in.start()
    gvs[...] = gvf[...]

    def halves(value):
        low, high = value[..., :384], value[..., 384:]
        return jnp.where(c == 0, low, high), jnp.where(c == 0, high, low)

    n_chunks = gi_h.shape[0]
    firsts[0].wait()

    def down(j, carry):
        wi_in, w2_in, act_in, dd_in = chunk_loads(j)
        w2_in.wait()
        dd_in.wait()
        cols = pl.ds(pl.multiple_of(j * d, d), d)
        di = (dot(gout[...], slot(1, j)[...], NT) * slot(3, j)[...].astype(F32)).astype(BF)

        @pl.when(j == 0)
        def _():
            firsts[1].wait()

        keep, pass_on = halves(dot(hid[...], di, TN).astype(BF))
        acc[j] = keep.reshape(4, 2, ROW, 384)
        other_half(j, lambda ref: ref.__setitem__(Ellipsis, pass_on.reshape(4, 2, ROW, 384)))
        launch(j)

        @pl.when(j == 0)
        def _():
            firsts[2].wait()

        @pl.when(j > 0)
        def _():
            tick(pace * j - 2)
            tick(pace * j - 1)

        wi_in.wait()
        accs[...] += dot(di, slot(0, j)[...], NT)
        gbin[:, cols] = jnp.sum(di.astype(F32), 0, keepdims=True)
        act_in.wait()
        keep, pass_on = halves(dot(slot(2, j)[...], gout[...], TN).astype(BF))
        keep, pass_on = keep.reshape(2, 4, ROW, 384), pass_on.reshape(2, 4, ROW, 384)
        for p in range(4):
            acc[4 + p, j] = keep[:, p]
            if p < 2:
                dwg[2, j, :, :, 384 * p : 384 * p + 384] = pass_on[:, p]
            else:
                st[p - 2, j] = pass_on[:, p]

        @pl.when(j + 2 < n_chunks)
        def _():
            for copy in chunk_loads(j + 2):
                copy.start()

        tick(pace * j)
        return carry

    lax.fori_loop(0, n_chunks, down, 0)
    for p in range(4):
        launch(4 + p)
    stay_in.wait()
    stay_out.start()
    for copy in seconds:
        copy.start()
    for copy in firsts[3:]:
        copy.wait()

    def add(row, value):
        gvs[row : row + 1, :] += jnp.sum(value, 0, keepdims=True)

    before = pace * (n_chunks - 1) + 1
    for page in range(pages):
        r = slice(page * own, (page + 1) * own)
        gh = accs[r, :]
        n1 = n1b[r, :].astype(F32)
        gm1 = norm_back(gh * vec[3:4, :], n1, r1s[r, 0:1])
        accs[r, :] = gm1
        ga = gm1.astype(BF)
        gout[r, :] = ga
        dc_v[page] = dot(ga, go[...], NT).astype(BF)
        add(2, ga.astype(F32))
        add(3, gh * n1)
        add(4, gh)
        tick(before + page)
    before += pages
    keep, pass_on = halves(dot(c_v[...].reshape(n, d), gout[...], TN).astype(BF))
    acc[8] = keep.reshape(4, 2, ROW, 384)
    st[2] = pass_on.reshape(4, 2, ROW, 384)
    launch(8)
    for copy in seconds:
        copy.wait()

    low_lane = lax.broadcasted_iota(jnp.int32, (own, PAIR), 1) < HEAD_DIM
    scale = 1.0 / math.sqrt(HEAD_DIM)

    def kv_send(it):
        g, page = lax.div(it, pages), lax.rem(it, pages)
        gcols = pl.ds(pl.multiple_of(g * GCOLS, GCOLS), GCOLS)
        return [
            remote(s_ref.at[page], r_ref.at[page, :, gcols], ks.at[g, page, i], kr.at[g, page, i], c_peer)
            for i, (s_ref, r_ref) in enumerate(((sk, rk), (sv, rv)))
        ]

    def attend(it, half):
        g, page = lax.div(it, pages), lax.rem(it, pages)
        here = pl.ds(pl.multiple_of(page * own, own), own)
        p_copy(it, half).wait()
        local = slice(half * PAIR, (half + 1) * PAIR)
        cols = pl.ds(pl.multiple_of(g * GCOLS + half * PAIR, PAIR), PAIR)
        qp = pool[row_block(at_q + page * own, own), cols] * jnp.array(scale, BF)
        kp = pool[row_block(at_k + page * rows, rows), cols]
        kt = kp.T
        vp = pool[row_block(at_v + page * rows, rows), cols]
        dc = dc_v[page, :, cols]
        prod = (dc.astype(F32) * c_v[page, :, cols].astype(F32)).T
        dk = None
        dv = None
        dqs = []
        for h in range(2):
            keep = low_lane if h == 0 else jnp.logical_not(low_lane)
            feats = slice(h * HEAD_DIM, (h + 1) * HEAD_DIM)
            dch = jnp.where(keep, dc, jnp.zeros_like(dc))
            qh = jnp.where(keep, qp, jnp.zeros_like(qp))
            pt = pbuf[half, h]
            delta = jnp.sum(prod[feats], axis=0, keepdims=True)
            dpt = dot(vp, dch, NT)
            dst = (pt.astype(F32) * (dpt - delta)).astype(BF)
            dvh = dot(pt, dch)
            dkh = dot(dst, qh)
            dk = dkh if dk is None else dk + dkh
            dv = dvh if dv is None else dv + dvh
            dqs.append(dot(kt[feats], dst))
        dq_all[here, cols] = (jnp.concatenate(dqs, axis=0) * scale).T.astype(BF)
        dk_all[here, cols] = dk[:own].astype(BF)
        sk[page, :, local] = dk[own:].astype(BF)
        dv_all[here, cols] = dv[:own].astype(BF)
        sv[page, :, local] = dv[own:].astype(BF)

        @pl.when(it + 1 < GROUPS * pages)
        def _():
            p_copy(it + 1, half).start()

    def group_grads(g):
        for i in range(2):
            any_first(2 * g + i).wait_send()
        gcols = pl.ds(pl.multiple_of(g * GCOLS, GCOLS), GCOLS)
        for page in range(pages):
            here = pl.ds(page * own, own)
            for copy in kv_send(g * pages + page):
                copy.wait_recv()
            dk_all[here, gcols] = dk_all[here, gcols] + rk[page, :, gcols]
            dv_all[here, gcols] = dv_all[here, gcols] + rv[page, :, gcols]
        for w, grad in enumerate((dq_all, dk_all, dv_all)):
            value = grad[:, gcols]
            dwg[g, :, :, :, w * GCOLS : (w + 1) * GCOLS] = (
                dot(hid[...], value, TN).astype(BF).reshape(4, 2, ROW, GCOLS)
            )
            if w != 1:
                brow[w : w + 1, gcols] = jnp.sum(value.astype(F32), 0, keepdims=True)
        gstep(g, "start")

    def gx_send(page):
        return remote(go.at[pl.ds(pl.multiple_of(page * blk, 128), blk), :], rgx.at[page], gs.at[page], gr.at[page], x_peer)

    def input_grads(page):
        here = pl.ds(pl.multiple_of(page * own, own), own)
        total = accs[here, :]
        for grad, start in ((dq_all, at_gq), (dk_all, at_gk), (dv_all, at_gv)):
            total = total + dot(grad[here, :], pool[pl.ds(start, d), :], NT)
        accs[here, :] = total
        go[pl.ds(pl.multiple_of(page * blk, 128), blk), :] = total[blk:].astype(BF)
        gx_send(page).start()
        gx_store(page, 0).start()

    def gx_store(page, side):
        src = accs.at[pl.ds(pl.multiple_of(page * own + side * blk, 128), blk), :]
        return pltpu.make_async_copy(src, gx.at[pages * (x if side == 0 else 1 - x) + page], os.at[page, side])

    n_it = GROUPS * pages

    def unit(it, carry):
        @pl.when(it == n_it)
        def _():
            group_grads(GROUPS - 1)

        for half in range(2):

            if half == 0:

                @pl.when(jnp.logical_and(it >= pages, it < n_it))
                def _():
                    for copy in kv_send(it - pages):
                        copy.wait_send()

            @pl.when(it < n_it)
            def _():
                attend(it, half)

            if half == 1:

                @pl.when(it < n_it)
                def _():
                    for copy in kv_send(it):
                        copy.start()

            tick(before + 2 * it + half)

        @pl.when(jnp.logical_and(it > 0, jnp.logical_and(lax.rem(it, pages) == 0, it < n_it)))
        def _():
            group_grads(lax.div(it, pages) - 1)

        page = it - n_it

        @pl.when(jnp.logical_and(page >= 0, page < pages))
        def _():
            input_grads(page)

        return carry

    def vec_send(k):
        to = lax.rem(f + k + 1, 8)
        return remote(pack.at[to], vecin.at[k], vs.at[k], vr.at[k], {"fsdp": to})

    vec_x = lambda: remote(vtot, vx.at[0], us.at[0], ur.at[0], x_peer)
    vec_c = lambda: remote(vx.at[1], vx.at[2], us.at[1], ur.at[1], c_peer)

    def small_pack():
        for i in range(8):
            row = brow[0:1, :] if i == 0 else brow[2:3, :] if i == 1 else gvs[i : i + 1, :]
            for j in range(8):
                pack[j, i : i + 1, :ROW] = row[:, ROW * j : ROW * (j + 1)]
        for j in range(8):
            for i in range(3):
                pack[j, 8 + i : 9 + i, :] = gbin[:, (3 * j + i) * 128 : (3 * j + i + 1) * 128]
        for k in range(7):
            vec_send(k).start()

    def small_sum():
        total = pack[f]
        for k in range(7):
            vec_send(k).wait_recv()
            total = total + vecin[k]
        vtot[...] = total
        vec_x().start()

    def small_pair():
        vec_x().wait_recv()
        vx[1] = vtot[...] + vx[0]
        vec_c().start()

    def all_steps(it, carry):
        unit(it, carry)
        for when, run in ((n_it, small_pack), (n_it + 3, small_sum), (n_it + 6, small_pair)):
            pl.when(it == when)(run)
        return carry

    lax.fori_loop(0, (last - before + 2) // 2, all_steps, 0)
    for page in range(pages):
        gx_send(page).wait_recv()
        accs[page * own + blk : (page + 1) * own, :] = rgx[page].astype(F32)
        gx_store(page, 1).start()
    vec_c().wait_recv()
    ovec[...] = vx[1] + vx[2]

    def finish(p, carry):
        step(p, "drain")
        return carry

    lax.fori_loop(0, REST, finish, 0)
    for g in range(GROUPS):
        gstep(g, "drain")
    for p in range(6, REST):
        any_first(p).wait_send()
    for it in range(n_it - pages, n_it):
        for copy in kv_send(it):
            copy.wait_send()
    for page in range(pages):
        gx_send(page).wait_send()
        gx_store(page, 0).wait()
        gx_store(page, 1).wait()
    for k in range(7):
        vec_send(k).wait_send()
    back_out.wait()
    stay_out.wait()
    vec_x().wait_send()
    vec_c().wait_send()


def bwd(kept, shards):
    (gq, gk, gv, xall, q, k, v, ctx, p, go, gi, g2, act, dd, hid, gout, n1, gm2, r1, out, gvs, vec) = kept
    pages, own, d = ctx.shape
    rows, blk = 2 * own, own // 2
    n = pages * own
    dma = pltpu.SemaphoreType.DMA
    vm = pltpu.VMEM
    sds = jax.ShapeDtypeStruct
    n_chunks = act.shape[0]
    flat = lambda a: a.reshape(-1, d)
    args = (
        flat(gq), flat(gk), flat(gv), xall, flat(q), flat(k), flat(v), ctx, p, flat(go),
        gi.reshape(n_chunks, d, d), g2.reshape(n_chunks, d, d), act, dd, hid, gout, n1, gm2, r1, out, gvs, vec,
    )
    res = call(
        bwd_body,
        (24 * n * d * d + pages * 10 * own * rows * d, 60 << 20, 0),
        in_specs=[ANY] * 20 + [VM, VM],
        out_specs=[VM] * 6 + [ANY, ANY, VM],
        out_shape=[sds(shape, F32) for shape in shards]
        + [sds((2 * pages, blk, d), F32), sds((2 * pages, blk, d), BF), sds((16, 128), F32)],
        scratch_shapes=[
            vm((8 * n, d), BF), vm((n, d), BF), vm((n, d), BF), vm((d, d), BF), vm((n, d), BF), vm((n, d), F32),
            vm((n, 128), F32), vm((pages, own, d), BF), vm((pages, own, d), BF),
            vm((REST, 4, 2, ROW, 384), BF), vm((GROUPS, 4, 2, ROW, 3 * GCOLS), BF), vm((3, 4, 2, ROW, 384), BF),
            vm((n, d), BF), vm((n, d), BF), vm((n, d), BF),
            vm((pages, own, d), BF), vm((pages, own, d), BF), vm((pages, own, GCOLS), BF), vm((pages, own, GCOLS), BF),
            vm((2, 2, rows, own), BF), vm((pages, blk, d), BF),
            vm((8, 16, 128), F32), vm((7, 16, 128), F32), vm((16, 128), F32), vm((3, 16, 128), F32), vm((8, d), F32),
            vm((8, d), F32), vm((1, n_chunks * d), F32), vm((pages, blk, d), BF),
        ]
        + fold_bufs(384, KEEP_REST, REST)
        + fold_bufs(128, KEEP_GROUP, GROUPS, 3)
        + fold_sems(REST)
        + fold_sems(GROUPS, 3)
        + [
            dma((7,)), dma((4, 2)), dma((6 + pages,)), dma((2,)), dma((GROUPS, pages, 2)), dma((GROUPS, pages, 2)),
            dma((pages,)), dma((pages,)), dma((pages, 2)), dma((7,)), dma((7,)), dma((2,)), dma((2,)),
            dma((1,)), dma((1,)), dma((2,)),
        ],
        params=dict(collective_id=1, has_side_effects=True, vmem_limit_bytes=64 << 20),
        name="backward_reduce",
    )(*args)
    return res[:6], res[6], res[7], res[8]


def finish_body(*refs):
    n = 8
    src, small, dst, lows = refs[:n], refs[n], refs[n + 1 : 2 * n + 1], refs[2 * n + 1 : 2 * n + 10]
    held, sem_in, sem_out = refs[2 * n + 10 : 3 * n + 10], refs[-2], refs[-1]
    loads = [pltpu.make_async_copy(src[i], held[i], sem_in.at[i]) for i in range(n)]
    stores = [pltpu.make_async_copy(held[i], dst[i], sem_out.at[i]) for i in range(n)]
    for copy in loads:
        copy.start()
    width = lows[0].shape[0]
    for i in range(8):
        lows[i][...] = small[i, :width]
    for i in range(3):
        lows[8][128 * i : 128 * (i + 1)] = small[8 + i, :]
    for load, store in zip(loads, stores):
        load.wait()
        store.start()
    for copy in stores:
        copy.wait()


def finish(arrays, small, width, wide):
    sds = jax.ShapeDtypeStruct
    dma = pltpu.SemaphoreType.DMA
    n = len(arrays)
    return call(
        finish_body,
        (0, 2 * sum(a.size * a.dtype.itemsize for a in arrays), 0),
        in_specs=[ANY] * n + [VM],
        out_specs=[ANY] * n + [VM] * 9,
        out_shape=[sds(a.shape, a.dtype) for a in arrays] + [sds((width,), F32)] * 8 + [sds((wide,), F32)],
        scratch_shapes=[pltpu.VMEM(a.shape, a.dtype) for a in arrays] + [dma((n,)), dma((n,))],
        name="finish",
    )(*arrays, small)


SWAP_X = [(0, 2), (2, 0), (1, 3), (3, 1)]
SWAP_C = [(0, 1), (1, 0), (2, 3), (3, 2)]


def swap(value, pairs):
    return lax.ppermute(value, "seq", pairs)


def per_device(
    fsdp, inputs, lengths, w_query, b_query, w_key, w_value, b_value, w_out, b_out,
    gain_one, shift_one, w_inner, b_inner, w_outer, b_outer, gain_two, shift_two, cotangent,
):
    pages_all, blk, d = inputs.shape
    pages = pages_all // 2
    s = lax.axis_index("seq")
    x_at = lax.div(s, 2)
    direct = fsdp == 8
    ws = (w_query, w_key, w_value, w_out, w_inner, w_outer)
    shards = [w.shape for w in ws]
    width = b_query.shape[0]
    names = (b_query, b_value, b_out, gain_one, shift_one, b_outer, gain_two, shift_two)

    def pages_of(array, side):
        return lax.dynamic_slice_in_dim(array, side * pages, pages, 0)

    order = jnp.stack([s, s ^ 2, s ^ 1, s ^ 3]).astype(jnp.int32)
    thr = pages_of(lengths, x_at).astype(jnp.int32)[:, None] - order[None, :] * blk
    if direct:
        kept = fwd(lengths.astype(jnp.int32), inputs, cotangent, ws, names + (b_inner,))
    else:
        wq, wk, wv, wo, wi, w2 = [lax.all_gather(w, "fsdp", axis=0, tiled=True) for w in ws]
        vec = jnp.concatenate(names + (b_inner,)).reshape(12, width)
        gvec = lax.all_gather(vec, "fsdp", axis=0)
        vec_full = jnp.swapaxes(gvec[:, :8], 0, 1).reshape(8, d).astype(F32)
        bin_full = gvec[:, 8:].reshape(1, -1).astype(F32)

        def own_rows(array):
            other = swap(pages_of(array, 1 - x_at), SWAP_X)
            return jnp.concatenate([pages_of(array, x_at), other], axis=1)

        xown, cown = own_rows(inputs), own_rows(cotangent)
        xall = jnp.concatenate([xown, swap(xown, SWAP_C)], axis=1)
        q, k, v, p, ctx = attn_fwd(thr, xall, wq, wk, wv, vec_full)
    if direct:
        tot, grad_inputs, output, tvec = bwd(kept, shards)
        res = finish((output, grad_inputs) + tuple(tot), tvec, width, b_inner.shape[0])
        output, grad_inputs, tot, small, g_bi = res[0], res[1], res[2:8], res[8:16], res[16]
    else:
        out, gm1, dctx, dwo, dwi, dw2, gv_ffn, gbin = ffn(ctx, xall, cown, wo, wi, w2, vec_full, bin_full)
        dq, dk, dk_send, dv, dv_send = attn_bwd(q, k, v, p, ctx, dctx)
        dkr, dvr = swap(dk_send, SWAP_C), swap(dv_send, SWAP_C)
        gx_a, gx_b, dwq, dwk, dwv, gv_proj = proj(xall, dq, dk, dkr, dv, dvr, gm1, wq, wk, wv)
        gv = jnp.concatenate([gv_proj[:2], gv_ffn[2:]], axis=0)
        by_owner = jnp.concatenate(
            [jnp.swapaxes(gv.reshape(8, fsdp, width), 0, 1), gbin.reshape(fsdp, 4, width)], axis=1
        )
        tot = [
            lax.psum(lax.psum_scatter(g, "fsdp", scatter_dimension=0, tiled=True), "seq").astype(F32)
            for g in (dwq, dwk, dwv, dwo, dwi, dw2)
        ]
        tvec = lax.psum(lax.psum_scatter(by_owner, "fsdp", scatter_dimension=0, tiled=True)[0], "seq")

        def joined(mine, other):
            here = lax.dynamic_update_slice_in_dim(
                jnp.zeros((pages_all, blk, d), mine.dtype), mine, x_at * pages, 0
            )
            return lax.dynamic_update_slice_in_dim(here, other, (1 - x_at) * pages, 0)

        output = joined(out[:, :blk], swap(out[:, blk:], SWAP_X))
        grad_inputs = joined(gx_a, swap(gx_b, SWAP_X).astype(F32))
        small = [tvec[i] for i in range(8)]
        g_bi = tvec[8:].reshape(-1)
    g_bq, g_bv, g_bo, g_g1, g_s1, g_bo2, g_g2, g_s2 = small
    t_q, t_k, t_v, t_o, t_i, t_2 = tot
    return (
        output, grad_inputs, t_q, g_bq, t_k, t_v, g_bv, t_o, g_bo, g_g1, g_s1,
        t_i, g_bi, t_2, g_bo2, g_g2, g_s2,
    )


def solution(mesh):
    vec, mat, act = P("fsdp"), P("fsdp", None), P("fsdp", "seq", None)
    return jax.shard_map(
        functools.partial(per_device, mesh.shape["fsdp"]),
        mesh=mesh,
        in_specs=(act, vec, mat, vec, mat, mat, vec, mat, vec, vec, vec, mat, vec, mat, vec, vec, vec, act),
        out_specs=(act, act, mat, vec, mat, mat, vec, mat, vec, vec, vec, mat, vec, mat, vec, vec, vec),
        check_vma=False,
    )
```
